32 devices in a mesh: dp: 4 (over y, x), ctx: 8 (over z, core).
Axes of the slice: x: 2, y: 2, z: 4, core: 2. Of those that a mesh axis runs over, the one named last changes fastest.
Arguments:
- tokens: bfloat16 [4, 2048, 768], P('dp', 'ctx'), may hold values from -6 to 6
- segment_ids: int32 [4, 2048], P('dp', 'ctx'), may hold values from 0 to 7, never falling along the last dimension, each value on 1 to 1024 neighbouring positions
- live_blocks: int32 [4, 16, 16], P('dp'), may hold values 0 or 1
- norm1_gain: bfloat16 [768], P(('dp', 'ctx')), may hold values from 0.25 to 1.75
- norm1_bias: bfloat16 [768], P(('dp', 'ctx')), may hold values from -1.5 to 1.5
- qkv_weight: bfloat16 [768, 2304], P(('dp', 'ctx')), may hold values from -0.3125 to 0.3125
- qv_bias: bfloat16 [1536], P(('dp', 'ctx')), may hold values from -2.5 to 2.5
- out_weight: bfloat16 [768, 768], P(('dp', 'ctx')), may hold values from -1.25 to 1.25
- out_bias: bfloat16 [768], P(('dp', 'ctx')), may hold values from -1.5 to 1.5
- norm2_gain: bfloat16 [768], P(('dp', 'ctx')), may hold values from 0.25 to 1.75
- norm2_bias: bfloat16 [768], P(('dp', 'ctx')), may hold values from -1.5 to 1.5
- up_weight: bfloat16 [768, 3072], P(('dp', 'ctx')), may hold values from -0.21875 to 0.21875
- up_bias: bfloat16 [3072], P(('dp', 'ctx')), may hold values from -2.5 to 2.5
- down_weight: bfloat16 [3072, 768], P(('dp', 'ctx')), may hold values from -0.15625 to 0.15625
- down_bias: bfloat16 [768], P(('dp', 'ctx')), may hold values from -1.5 to 1.5
- grad_out: bfloat16 [4, 2048, 768], P('dp', 'ctx'), may hold values from -6 to 6
Outputs:
- output: bfloat16 [4, 2048, 768], P('dp', 'ctx')
- grad_tokens: float32 [4, 2048, 768], P('dp', 'ctx')
- grad_norm1_gain: float32 [768], P(('dp', 'ctx'))
- grad_norm1_bias: float32 [768], P(('dp', 'ctx'))
- grad_qkv_weight: float32 [768, 2304], P(('dp', 'ctx'))
- grad_qv_bias: float32 [1536], P(('dp', 'ctx'))
- grad_out_weight: float32 [768, 768], P(('dp', 'ctx'))
- grad_out_bias: float32 [768], P(('dp', 'ctx'))
- grad_norm2_gain: float32 [768], P(('dp', 'ctx'))
- grad_norm2_bias: float32 [768], P(('dp', 'ctx'))
- grad_up_weight: float32 [768, 3072], P(('dp', 'ctx'))
- grad_up_bias: float32 [3072], P(('dp', 'ctx'))
- grad_down_weight: float32 [3072, 768], P(('dp', 'ctx'))
- grad_down_bias: float32 [768], P(('dp', 'ctx'))
The draws below stay inside these ranges and needn't reach their ends.
Inputs may be any that keep to these rules, and one draw needn't show every extreme that they name: `segment_ids`: segment numbers never fall along a sequence; a document holds 1 to 1024 positions and one holds exactly 1024.
All inputs are finite; a program needn't handle non-finite values. No bound on the sum of `live_blocks` on one device may be relied on, other than what follows from the above.
Results may differ from the reference program's by a relative error of at most 0.019.
Values may be sent and summed in bfloat16 or wider, within the bound.
No kernel may reach another device: no remote copies, remote signals or barrier semaphores. Data moves between devices by JAX's collectives and lax.ppermute only.
A program may use at most 192 MiB of HBM per device.

```python
import math
import jax
import jax.numpy as jnp
import numpy as np
from jax import lax

D = 768
HEADS = 12
HEAD_DIM = 64
FF = 3072
BLOCK = 128
LENGTH = 2048
SEQS = 4
NB = 16
DOCS = 8
DOC_MOST = 1024


def plant(drawn, rng, low, high):
    index_at = [jax.random.randint(jax.random.fold_in(rng, axis), (), 0, length) for axis, length in enumerate(drawn.shape)]
    longest = drawn.shape.index(max(drawn.shape))
    beside = index_at[:longest] + [(index_at[longest] + 1) % drawn.shape[longest]] + index_at[longest + 1:]
    return drawn.at[tuple(index_at)].set(low).at[tuple(beside)].set(high)


def levels(stream_key, shape, split, low, top_value):
    factor_of, own = 1.0, jax.random.fold_in(stream_key, 6)
    for position, blocks in split:
        draws = jnp.exp(jax.random.uniform(jax.random.fold_in(own, position), (blocks,), jnp.float32, low / len(split), top_value / len(split)))
        factor_of = factor_of * jnp.repeat(draws, shape[position] // blocks).reshape([-1 if axis == position else 1 for axis in range(len(shape))])
    return factor_of


def profile(amount, total, limit, skew):
    weights = [(1 << 20) // math.isqrt(standing ** skew) + 1 for standing in range(2, amount + 1)]
    surplus, holding = total - limit - (amount - 1), [1] * (amount - 1)
    while surplus > 0:
        free = [i for i in range(amount - 1) if holding[i] < limit]
        mass, left = sum([weights[i] for i in free]), surplus
        for i in free:
            more = min(limit - holding[i], max(1, left * weights[i] // mass), surplus)
            holding[i] = holding[i] + more
            surplus = surplus - more
    return np.array([limit] + holding)


def uneven_parts(rng, count, total, bound, skew):
    if count == 2:
        one = jax.random.randint(rng, (), max(1, total - bound), min(bound, total - 1) + 1)
        return jnp.stack([one, total - one])
    sizes = jnp.asarray(profile(count, total, bound, skew), jnp.int32)
    twos = (count - 1) // 2
    donor, taker = sizes[1:1 + 2 * twos:2], sizes[2:2 + 2 * twos:2]
    margin = jnp.minimum(donor - 1, bound - taker)
    passed = jax.random.randint(jax.random.fold_in(rng, 1), (twos,), 0, 1 << 20) % (margin + 1)
    sizes = sizes.at[1:1 + 2 * twos:2].set(donor - passed).at[2:2 + 2 * twos:2].set(taker + passed)
    return sizes[jax.random.permutation(jax.random.fold_in(rng, 2), count)]


def noise(rng, dims, scale, bound, cuts=(), held_as=jnp.bfloat16):
    values = jax.random.normal(rng, dims, jnp.float32) * scale
    if len(cuts) > 0:
        values = levels(rng, dims, cuts, -0.22, 0.18) * values
    return jnp.clip(values, min=-bound, max=bound).astype(held_as)


def setup_inputs(seed: int = 0) -> dict:
    seeds = jax.random.split(jax.random.key(seed), 17)
    return {
        "tokens": noise(seeds[0], (SEQS, LENGTH, D), 1.0, 6.0, ((0, 4), (1, 8))),
        "segment_ids": jax.vmap(lambda own: jnp.searchsorted(jnp.cumsum(uneven_parts(own, DOCS, LENGTH, DOC_MOST, 2)), jnp.arange(LENGTH), side="right"))(jax.random.split(seeds[1], SEQS)).reshape((SEQS, LENGTH)).astype(jnp.int32),
        "live_blocks": plant((jax.random.randint(seeds[2], (SEQS, NB, NB), 0, 4) < 3).astype(jnp.int32), jax.random.fold_in(seeds[2], 1), 0, 1),
        "norm1_gain": jnp.clip(1.0 + 0.15 * jax.random.normal(seeds[3], (D,), jnp.float32), 0.25, 1.75).astype(jnp.bfloat16),
        "norm1_bias": noise(seeds[4], (D,), 0.3, 1.5, ((0, 32),)),
        "qkv_weight": noise(seeds[5], (D, 3 * D), (D // 2) ** -0.5, 0.3125, ((0, 32),)),
        "qv_bias": noise(seeds[6], (2 * D,), 0.5, 2.5, ((0, 32),)),
        "out_weight": noise(seeds[7], (D, D), (D // 32) ** -0.5, 1.25, ((0, 32),)),
        "out_bias": noise(seeds[8], (D,), 0.3, 1.5, ((0, 32),)),
        "norm2_gain": jnp.clip(1.0 + 0.15 * jax.random.normal(seeds[9], (D,), jnp.float32), 0.25, 1.75).astype(jnp.bfloat16),
        "norm2_bias": noise(seeds[10], (D,), 0.3, 1.5, ((0, 32),)),
        "up_weight": noise(seeds[11], (D, FF), D ** -0.5, 0.21875, ((0, 32),)),
        "up_bias": noise(seeds[12], (FF,), 0.5, 2.5, ((0, 32),)),
        "down_weight": noise(seeds[13], (FF, D), (FF // 2) ** -0.5, 0.15625, ((0, 32),)),
        "down_bias": noise(seeds[14], (D,), 0.3, 1.5, ((0, 32),)),
        "grad_out": noise(seeds[15], (SEQS, LENGTH, D), 1.0, 6.0, ((0, 4), (1, 8))),
    }


@jax.custom_vjp
def low(v):
    return lax.optimization_barrier(v.astype(jnp.bfloat16)).astype(jnp.float32)

@jax.custom_vjp
def low_back(v):
    return v

def low_keep(v):
    return (low(v), None)

def low_pass(kept, grad):
    return (grad,)

def back_keep(v):
    return (v, None)

def back_low(kept, grad):
    return (low(grad),)
low.defvjp(low_keep, low_pass)
low_back.defvjp(back_keep, back_low)
PRECISE = lax.Precision.HIGHEST

def rounded(value_in):
    return low(low_back(value_in))

def layer_norm(value_in, norm_gain, norm_shift):
    center = value_in - lax.optimization_barrier(jnp.mean(value_in, axis=-1, keepdims=True))
    spread = lax.optimization_barrier(jnp.mean(center * center, axis=-1, keepdims=True))
    return center * lax.rsqrt(spread + 1e-05) * norm_gain + norm_shift

def product(left_side, right_side):
    return jnp.dot(left_side, right_side, precision=PRECISE)

def attention(queries, key_rows, value_rows, segments, live_row):
    rows_block = min(512, LENGTH)
    key_pos = jnp.arange(LENGTH, dtype=jnp.int32)
    key_block = key_pos // BLOCK
    live_keys = live_row[:, key_block]
    key_heads = key_rows.reshape(LENGTH, HEADS, HEAD_DIM)
    value_heads = value_rows.reshape(LENGTH, HEADS, HEAD_DIM)

    def one_block(block_index):
        row_start = block_index * rows_block
        query_heads = lax.dynamic_slice_in_dim(queries, row_start, rows_block, 0).reshape(rows_block, HEADS, HEAD_DIM)
        query_pos = row_start + jnp.arange(rows_block, dtype=jnp.int32)
        query_block = query_pos // BLOCK
        seg_rows = lax.dynamic_slice_in_dim(segments, row_start, rows_block, 0)
        live_rows = live_keys[query_block]
        allowed = (seg_rows[:, None] == segments[None, :]) & ((live_rows > 0) | (query_block[:, None] == key_block[None, :]))
        scores = jnp.einsum('qhd,khd->hqk', query_heads, key_heads, precision=PRECISE) * 0.125
        scores = low_back(jnp.where(allowed[None], scores, -1e+30))
        row_max = lax.optimization_barrier(jnp.max(scores, axis=-1, keepdims=True))
        row_total = lax.optimization_barrier(jnp.sum(jnp.exp(scores - row_max), axis=-1, keepdims=True))
        attn_probs = low(jnp.exp(scores - row_max - jnp.log(row_total)))
        attended = jnp.einsum('hqk,khd->qhd', attn_probs, value_heads, precision=PRECISE)
        return attended.reshape(rows_block, HEADS * HEAD_DIM)
    blocks = lax.map(jax.checkpoint(one_block), jnp.arange(LENGTH // rows_block, dtype=jnp.int32))
    return blocks.reshape(LENGTH, HEADS * HEAD_DIM)

def encoder_layer(tokens, params, segments, live_all):
    gain_first, shift_first, qkv_weight, qv_bias, out_weight, out_bias, gain_second, shift_second, up_weight, up_bias, down_weight, down_bias = params

    def one_sequence(inputs):
        seq_rows, seg_row, live_row = inputs
        normed = low(layer_norm(seq_rows, gain_first, shift_first))
        projected = product(normed, qkv_weight)
        queries = rounded(projected[:, :D] + qv_bias[:D])
        key_rows = rounded(projected[:, D:2 * D])
        value_rows = rounded(projected[:, 2 * D:] + qv_bias[D:])
        attended = rounded(attention(queries, key_rows, value_rows, seg_row, live_row))
        branch = low_back(product(attended, out_weight) + out_bias)
        hidden = seq_rows + branch
        normed_two = low(layer_norm(hidden, gain_second, shift_second))
        before = low_back(product(normed_two, up_weight) + up_bias)
        activated = low(jax.nn.gelu(before, approximate=False))
        feed_out = low_back(product(activated, down_weight) + down_bias)
        return hidden + feed_out
    return lax.map(one_sequence, (tokens, segments, live_all))

def reference(tokens, segment_ids, live_blocks, norm1_gain, norm1_bias, qkv_weight, qv_bias, out_weight, out_bias, norm2_gain, norm2_bias, up_weight, up_bias, down_weight, down_bias, grad_out):
    params = tuple((element.astype(jnp.float32) for element in (norm1_gain, norm1_bias, qkv_weight, qv_bias, out_weight, out_bias, norm2_gain, norm2_bias, up_weight, up_bias, down_weight, down_bias)))

    def forward(token_rows, weights):
        return encoder_layer(token_rows, weights, segment_ids, live_blocks)
    output, pullback = jax.vjp(forward, tokens.astype(jnp.float32), params)
    grad_rows, grad_params = pullback(grad_out.astype(jnp.float32))
    return (output.astype(jnp.bfloat16), grad_rows, grad_params[0], grad_params[1], grad_params[2], grad_params[3], grad_params[4], grad_params[5], grad_params[6], grad_params[7], grad_params[8], grad_params[9], grad_params[10], grad_params[11])
```

```python
import math

import jax
import jax.numpy as jnp
from jax import lax
from jax.sharding import PartitionSpec as P

HEADS = 12
HEAD_DIM = 64
BLOCK = 128


NEG_FILL = -1e30
SCORE_SCALE = 0.125


def layer_norm(value_in, norm_gain, norm_shift):
    center = value_in - jnp.mean(value_in, axis=-1, keepdims=True)
    spread = jnp.mean(center * center, axis=-1, keepdims=True)
    return center * lax.rsqrt(spread + 1e-05) * norm_gain + norm_shift


def exact_gelu(value_in):
    return jax.nn.gelu(value_in, approximate=False)


def matmul_low(left_side, right_side):
    return jnp.dot(left_side, right_side, preferred_element_type=jnp.float32)


def inner_rows(left_side, right_side):
    return lax.dot_general(
        left_side, right_side, (((0,), (0,)), ((), ())), preferred_element_type=jnp.float32
    )


def times_transpose(left_side, right_side):
    return lax.dot_general(
        left_side, right_side, (((1,), (1,)), ((), ())), preferred_element_type=jnp.float32
    )


def sweep_blocks(count_rows, step_fn, carry_state):
    span_rows = math.gcd(count_rows, 512)
    return lax.fori_loop(
        0,
        count_rows // span_rows,
        lambda loop_index, loop_state: step_fn(loop_index * span_rows, span_rows, loop_state),
        carry_state,
    )


def allowed_pairs(live_table, query_pos, key_pos, query_seg, key_seg):
    block_slots = jnp.arange(live_table.shape[-1], dtype=jnp.int32)
    query_block = query_pos // BLOCK
    key_block = key_pos // BLOCK
    pick_query = (query_block[:, None] == block_slots[None, :]).astype(jnp.bfloat16)
    pick_key = (key_block[:, None] == block_slots[None, :]).astype(jnp.bfloat16)
    live_rows = jnp.einsum(
        "qa,sab->sqb", pick_query, live_table, preferred_element_type=jnp.float32
    )
    live_grid = jnp.einsum(
        "sqb,kb->sqk", live_rows.astype(jnp.bfloat16), pick_key, preferred_element_type=jnp.float32
    )
    same_block = query_block[:, None] == key_block[None, :]
    same_doc = query_seg[:, :, None] == key_seg[:, None, :]
    return same_doc & ((live_grid > 0.5) | same_block[None])


def pair_grads(
    live_table,
    query_heads,
    dout_heads,
    lse_heads,
    delta_heads,
    query_pos,
    query_seg,
    key_heads,
    value_heads,
    key_pos,
    key_seg,
):
    scores = (
        jnp.einsum("sqhd,skhd->shqk", query_heads, key_heads, preferred_element_type=jnp.float32)
        * SCORE_SCALE
    )
    permit = allowed_pairs(live_table, query_pos, key_pos, query_seg, key_seg)[:, None]
    attn_probs = jnp.where(permit, jnp.exp(scores - lse_heads[..., None]), 0.0)
    grad_prob = jnp.einsum(
        "sqhd,skhd->shqk", dout_heads, value_heads, preferred_element_type=jnp.float32
    )
    grad_score = (attn_probs * (grad_prob - delta_heads[..., None])).astype(jnp.bfloat16)
    grad_query = (
        jnp.einsum("shqk,skhd->sqhd", grad_score, key_heads, preferred_element_type=jnp.float32)
        * SCORE_SCALE
    )
    grad_key = (
        jnp.einsum("shqk,sqhd->skhd", grad_score, query_heads, preferred_element_type=jnp.float32)
        * SCORE_SCALE
    )
    grad_value = jnp.einsum(
        "shqk,sqhd->skhd",
        attn_probs.astype(jnp.bfloat16),
        dout_heads,
        preferred_element_type=jnp.float32,
    )
    return (grad_query, grad_key, grad_value)


def local(
    tokens,
    segment_ids,
    live_blocks,
    norm1_gain,
    norm1_bias,
    qkv_weight,
    qv_bias,
    out_weight,
    out_bias,
    norm2_gain,
    norm2_bias,
    up_weight,
    up_bias,
    down_weight,
    down_bias,
    grad_out,
):
    shards = (
        norm1_gain,
        norm1_bias,
        qkv_weight,
        qv_bias,
        out_weight,
        out_bias,
        norm2_gain,
        norm2_bias,
        up_weight,
        up_bias,
        down_weight,
        down_bias,
    )
    gathered = (
        lax.all_gather(shards[0], ("dp", "ctx"), axis=0, tiled=True),
        lax.all_gather(shards[1], ("dp", "ctx"), axis=0, tiled=True),
        lax.all_gather(shards[2], ("dp", "ctx"), axis=0, tiled=True),
        lax.all_gather(shards[3], ("dp", "ctx"), axis=0, tiled=True),
        lax.all_gather(shards[4], ("dp", "ctx"), axis=0, tiled=True),
        lax.all_gather(shards[5], ("dp", "ctx"), axis=0, tiled=True),
        lax.all_gather(shards[6], ("dp", "ctx"), axis=0, tiled=True),
        lax.all_gather(shards[7], ("dp", "ctx"), axis=0, tiled=True),
        lax.all_gather(shards[8], ("dp", "ctx"), axis=0, tiled=True),
        lax.all_gather(shards[9], ("dp", "ctx"), axis=0, tiled=True),
        lax.all_gather(shards[10], ("dp", "ctx"), axis=0, tiled=True),
        lax.all_gather(shards[11], ("dp", "ctx"), axis=0, tiled=True),
    )
    (
        gain_first,
        shift_first,
        full_qkv,
        bias_qv,
        full_out,
        bias_out,
        gain_second,
        shift_second,
        full_up,
        bias_up,
        full_down,
        bias_down,
    ) = gathered
    seq_count, tok_rows, model_width = tokens.shape
    head_count = HEADS
    head_size = HEAD_DIM
    flat_rows = seq_count * tok_rows
    query_pos = lax.axis_index("ctx") * tok_rows + jnp.arange(tok_rows, dtype=jnp.int32)
    live_table = live_blocks.astype(jnp.bfloat16)
    seg_low = segment_ids.astype(jnp.bfloat16)
    inputs_wide = tokens.reshape(flat_rows, model_width).astype(jnp.float32)
    normed_wide, norm_pull_one = jax.vjp(
        layer_norm, inputs_wide, gain_first.astype(jnp.float32), shift_first.astype(jnp.float32)
    )
    normed_one = normed_wide.astype(jnp.bfloat16)
    projected = matmul_low(normed_one, full_qkv)
    bias_wide = bias_qv.astype(jnp.float32)
    query_low = (projected[:, :model_width] + bias_wide[:model_width]).astype(jnp.bfloat16)
    key_low = projected[:, model_width : 2 * model_width].astype(jnp.bfloat16)
    value_low = (projected[:, 2 * model_width :] + bias_wide[model_width:]).astype(jnp.bfloat16)
    query_heads = query_low.reshape(seq_count, tok_rows, head_count, head_size)
    key_seq = key_low.reshape(seq_count, tok_rows, model_width)
    value_seq = value_low.reshape(seq_count, tok_rows, model_width)
    initial = (
        jnp.full((seq_count, head_count, tok_rows), NEG_FILL, jnp.float32),
        jnp.zeros((seq_count, head_count, tok_rows), jnp.float32),
        jnp.zeros((seq_count, tok_rows, head_count, head_size), jnp.float32),
    )
    key_part = lax.all_gather(key_seq, "ctx", axis=1, tiled=True)
    value_part = lax.all_gather(value_seq, "ctx", axis=1, tiled=True)
    seg_part = lax.all_gather(seg_low, "ctx", axis=1, tiled=True)

    def step_fn(offset, span_rows, inner_state):
        run_max, run_total, accum_out = inner_state
        key_heads = lax.dynamic_slice_in_dim(key_part, offset, span_rows, 1).reshape(
            seq_count, span_rows, head_count, head_size
        )
        value_heads = lax.dynamic_slice_in_dim(value_part, offset, span_rows, 1).reshape(
            seq_count, span_rows, head_count, head_size
        )
        key_seg = lax.dynamic_slice_in_dim(seg_part, offset, span_rows, 1)
        key_pos = offset + jnp.arange(span_rows, dtype=jnp.int32)
        scores = (
            jnp.einsum(
                "sqhd,skhd->shqk", query_heads, key_heads, preferred_element_type=jnp.float32
            )
            * SCORE_SCALE
        )
        permit = allowed_pairs(live_table, query_pos, key_pos, seg_low, key_seg)[:, None]
        scores = jnp.where(permit, scores, NEG_FILL)
        new_max = jnp.maximum(run_max, jnp.max(scores, axis=-1))
        exp_scores = jnp.where(permit, jnp.exp(scores - new_max[..., None]), 0.0)
        factor = jnp.exp(run_max - new_max)
        run_total = run_total * factor + jnp.sum(exp_scores, axis=-1)
        weighted = jnp.einsum(
            "shqk,skhd->sqhd",
            exp_scores.astype(jnp.bfloat16),
            value_heads,
            preferred_element_type=jnp.float32,
        )
        accum_out = accum_out * jnp.transpose(factor, (0, 2, 1))[..., None] + weighted
        return (new_max, run_total, accum_out)

    run_max, run_total, accum_out = sweep_blocks(key_part.shape[1], step_fn, initial)
    attn_wide = accum_out / jnp.transpose(run_total, (0, 2, 1))[..., None]
    lse_heads = run_max + jnp.log(run_total)
    attn_low = attn_wide.reshape(flat_rows, model_width).astype(jnp.bfloat16)
    hidden = inputs_wide + matmul_low(attn_low, full_out) + bias_out.astype(jnp.float32)
    normed_two_wide, norm_pull_two = jax.vjp(
        layer_norm, hidden, gain_second.astype(jnp.float32), shift_second.astype(jnp.float32)
    )
    normed_two = normed_two_wide.astype(jnp.bfloat16)
    before = matmul_low(normed_two, full_up) + bias_up.astype(jnp.float32)
    activated_wide, gelu_pull = jax.vjp(exact_gelu, before)
    activated = activated_wide.astype(jnp.bfloat16)
    output = (hidden + matmul_low(activated, full_down) + bias_down.astype(jnp.float32)).astype(
        jnp.bfloat16
    )
    back_params = (
        lax.all_gather(shards[0], ("dp", "ctx"), axis=0, tiled=True),
        lax.all_gather(shards[1], ("dp", "ctx"), axis=0, tiled=True),
        lax.all_gather(shards[2], ("dp", "ctx"), axis=0, tiled=True),
        lax.all_gather(shards[3], ("dp", "ctx"), axis=0, tiled=True),
        lax.all_gather(shards[4], ("dp", "ctx"), axis=0, tiled=True),
        lax.all_gather(shards[5], ("dp", "ctx"), axis=0, tiled=True),
        lax.all_gather(shards[6], ("dp", "ctx"), axis=0, tiled=True),
        lax.all_gather(shards[7], ("dp", "ctx"), axis=0, tiled=True),
        lax.all_gather(shards[8], ("dp", "ctx"), axis=0, tiled=True),
        lax.all_gather(shards[9], ("dp", "ctx"), axis=0, tiled=True),
        lax.all_gather(shards[10], ("dp", "ctx"), axis=0, tiled=True),
        lax.all_gather(shards[11], ("dp", "ctx"), axis=0, tiled=True),
    )
    back_qkv = back_params[2]
    back_out = back_params[4]
    back_up = back_params[8]
    back_down = back_params[10]
    grad_low = grad_out.reshape(flat_rows, model_width)
    grad_down = inner_rows(activated, grad_low)
    grad_bias_down = jnp.sum(grad_low.astype(jnp.float32), axis=0)
    grad_act = times_transpose(grad_low, back_down)
    grad_before = gelu_pull(grad_act)[0].astype(jnp.bfloat16)
    grad_up = inner_rows(normed_two, grad_before)
    grad_bias_up = jnp.sum(grad_before.astype(jnp.float32), axis=0)
    grad_normed_two = times_transpose(grad_before, back_up)
    grad_hidden_part, grad_gain_two, grad_shift_two = norm_pull_two(grad_normed_two)
    grad_hidden = grad_low.astype(jnp.float32) + grad_hidden_part
    grad_branch = grad_hidden.astype(jnp.bfloat16)
    grad_out_full = inner_rows(attn_low, grad_branch)
    grad_bias_out = jnp.sum(grad_branch.astype(jnp.float32), axis=0)
    grad_attn = times_transpose(grad_branch, back_out).astype(jnp.bfloat16)
    dout_heads = grad_attn.reshape(seq_count, tok_rows, head_count, head_size)
    delta_rows = jnp.sum(dout_heads.astype(jnp.float32) * attn_wide, axis=-1)
    delta_heads = jnp.transpose(delta_rows, (0, 2, 1))
    key_all, value_all, seg_all = (
        lax.all_gather(key_seq, "ctx", axis=1, tiled=True),
        lax.all_gather(value_seq, "ctx", axis=1, tiled=True),
        lax.all_gather(seg_low, "ctx", axis=1, tiled=True),
    )

    def key_step(offset, span_rows, inner_state):
        grad_query_acc, grad_key_all, grad_value_all = inner_state
        key_heads = lax.dynamic_slice_in_dim(key_all, offset, span_rows, 1).reshape(
            seq_count, span_rows, head_count, head_size
        )
        value_heads = lax.dynamic_slice_in_dim(value_all, offset, span_rows, 1).reshape(
            seq_count, span_rows, head_count, head_size
        )
        key_seg = lax.dynamic_slice_in_dim(seg_all, offset, span_rows, 1)
        key_pos = offset + jnp.arange(span_rows, dtype=jnp.int32)
        grad_query, grad_key, grad_value = pair_grads(
            live_table,
            query_heads,
            dout_heads,
            lse_heads,
            delta_heads,
            query_pos,
            seg_low,
            key_heads,
            value_heads,
            key_pos,
            key_seg,
        )
        grad_key_all = lax.dynamic_update_slice_in_dim(
            grad_key_all, grad_key.reshape(seq_count, span_rows, model_width), offset, 1
        )
        grad_value_all = lax.dynamic_update_slice_in_dim(
            grad_value_all, grad_value.reshape(seq_count, span_rows, model_width), offset, 1
        )
        return (grad_query_acc + grad_query, grad_key_all, grad_value_all)

    length_rows = key_all.shape[1]
    zero_query = jnp.zeros((seq_count, tok_rows, head_count, head_size), jnp.float32)
    zero_keys = jnp.zeros((seq_count, length_rows, model_width), jnp.float32)
    grad_query_heads, grad_key_all, grad_value_all = sweep_blocks(
        length_rows, key_step, (zero_query, zero_keys, zero_keys)
    )
    grad_key_seq, grad_value_seq = (
        lax.psum_scatter(
            grad_key_all.astype(jnp.bfloat16), "ctx", scatter_dimension=1, tiled=True
        ).astype(jnp.float32),
        lax.psum_scatter(
            grad_value_all.astype(jnp.bfloat16), "ctx", scatter_dimension=1, tiled=True
        ).astype(jnp.float32),
    )
    grad_query_low = grad_query_heads.reshape(flat_rows, model_width).astype(jnp.bfloat16)
    grad_key_low = grad_key_seq.reshape(flat_rows, model_width).astype(jnp.bfloat16)
    grad_value_low = grad_value_seq.reshape(flat_rows, model_width).astype(jnp.bfloat16)
    grad_proj_low = jnp.concatenate([grad_query_low, grad_key_low, grad_value_low], axis=1)
    grad_qkv_full = inner_rows(normed_one, grad_proj_low)
    grad_bias_qv = jnp.concatenate(
        [
            jnp.sum(grad_query_low.astype(jnp.float32), axis=0),
            jnp.sum(grad_value_low.astype(jnp.float32), axis=0),
        ]
    )
    grad_normed_one = times_transpose(grad_proj_low, back_qkv)
    grad_input_part, grad_gain_one, grad_shift_one = norm_pull_one(grad_normed_one)
    grad_tokens = (grad_hidden + grad_input_part).reshape(seq_count, tok_rows, model_width)
    summed = (
        lax.psum_scatter(grad_gain_one, ("dp", "ctx"), scatter_dimension=0, tiled=True),
        lax.psum_scatter(grad_shift_one, ("dp", "ctx"), scatter_dimension=0, tiled=True),
        lax.psum_scatter(grad_qkv_full.astype(jnp.bfloat16), ("dp", "ctx"), scatter_dimension=0, tiled=True).astype(jnp.float32),
        lax.psum_scatter(grad_bias_qv, ("dp", "ctx"), scatter_dimension=0, tiled=True),
        lax.psum_scatter(grad_out_full.astype(jnp.bfloat16), ("dp", "ctx"), scatter_dimension=0, tiled=True).astype(jnp.float32),
        lax.psum_scatter(grad_bias_out, ("dp", "ctx"), scatter_dimension=0, tiled=True),
        lax.psum_scatter(grad_gain_two, ("dp", "ctx"), scatter_dimension=0, tiled=True),
        lax.psum_scatter(grad_shift_two, ("dp", "ctx"), scatter_dimension=0, tiled=True),
        lax.psum_scatter(grad_up.astype(jnp.bfloat16), ("dp", "ctx"), scatter_dimension=0, tiled=True).astype(jnp.float32),
        lax.psum_scatter(grad_bias_up, ("dp", "ctx"), scatter_dimension=0, tiled=True),
        lax.psum_scatter(grad_down.astype(jnp.bfloat16), ("dp", "ctx"), scatter_dimension=0, tiled=True).astype(jnp.float32),
        lax.psum_scatter(grad_bias_down, ("dp", "ctx"), scatter_dimension=0, tiled=True),
    )
    return (
        output.reshape(seq_count, tok_rows, model_width),
        grad_tokens,
        summed[0],
        summed[1],
        summed[2],
        summed[3],
        summed[4],
        summed[5],
        summed[6],
        summed[7],
        summed[8],
        summed[9],
        summed[10],
        summed[11],
    )


def solution(mesh):
    return jax.shard_map(
        local,
        mesh=mesh,
        in_specs=(
            P("dp", "ctx", None),
            P("dp", "ctx"),
            P("dp", None, None),
            P(("dp", "ctx")),
            P(("dp", "ctx")),
            P(("dp", "ctx"), None),
            P(("dp", "ctx")),
            P(("dp", "ctx"), None),
            P(("dp", "ctx")),
            P(("dp", "ctx")),
            P(("dp", "ctx")),
            P(("dp", "ctx"), None),
            P(("dp", "ctx")),
            P(("dp", "ctx"), None),
            P(("dp", "ctx")),
            P("dp", "ctx", None),
        ),
        out_specs=(
            P("dp", "ctx", None),
            P("dp", "ctx", None),
            P(("dp", "ctx")),
            P(("dp", "ctx")),
            P(("dp", "ctx"), None),
            P(("dp", "ctx")),
            P(("dp", "ctx"), None),
            P(("dp", "ctx")),
            P(("dp", "ctx")),
            P(("dp", "ctx")),
            P(("dp", "ctx"), None),
            P(("dp", "ctx")),
            P(("dp", "ctx"), None),
            P(("dp", "ctx")),
        ),
        check_vma=False,
    )
```

```python
import math

import jax
import jax.numpy as jnp
from jax import lax
from jax.experimental import pallas as pl
from jax.experimental.pallas import tpu as pltpu
from jax.sharding import Mesh, PartitionSpec as P

HEADS = 12
HEAD_DIM = 64
BLOCK = 128


NEG_FILL = -1e30
SCORE_SCALE = 0.125


def layer_norm(value_in, norm_gain, norm_shift):
    center = value_in - jnp.mean(value_in, axis=-1, keepdims=True)
    spread = jnp.mean(center * center, axis=-1, keepdims=True)
    return center * lax.rsqrt(spread + 1e-05) * norm_gain + norm_shift


def exact_gelu(value_in):
    return jax.nn.gelu(value_in, approximate=False)


def matmul_low(left_side, right_side):
    return jnp.dot(left_side, right_side, preferred_element_type=jnp.float32)


def inner_rows(left_side, right_side):
    return lax.dot_general(
        left_side, right_side, (((0,), (0,)), ((), ())), preferred_element_type=jnp.float32
    )


def times_transpose(left_side, right_side):
    return lax.dot_general(
        left_side, right_side, (((1,), (1,)), ((), ())), preferred_element_type=jnp.float32
    )


def sweep_blocks(count_rows, step_fn, carry_state):
    span_rows = math.gcd(count_rows, 512)
    return lax.fori_loop(
        0,
        count_rows // span_rows,
        lambda loop_index, loop_state: step_fn(loop_index * span_rows, span_rows, loop_state),
        carry_state,
    )


def allowed_pairs(live_table, query_pos, key_pos, query_seg, key_seg):
    block_slots = jnp.arange(live_table.shape[-1], dtype=jnp.int32)
    query_block = query_pos // BLOCK
    key_block = key_pos // BLOCK
    pick_query = (query_block[:, None] == block_slots[None, :]).astype(jnp.bfloat16)
    pick_key = (key_block[:, None] == block_slots[None, :]).astype(jnp.bfloat16)
    live_rows = jnp.einsum(
        "qa,sab->sqb", pick_query, live_table, preferred_element_type=jnp.float32
    )
    live_grid = jnp.einsum(
        "sqb,kb->sqk", live_rows.astype(jnp.bfloat16), pick_key, preferred_element_type=jnp.float32
    )
    same_block = query_block[:, None] == key_block[None, :]
    same_doc = query_seg[:, :, None] == key_seg[:, None, :]
    return same_doc & ((live_grid > 0.5) | same_block[None])


def pair_grads(
    live_table,
    query_heads,
    dout_heads,
    lse_heads,
    delta_heads,
    query_pos,
    query_seg,
    key_heads,
    value_heads,
    key_pos,
    key_seg,
):
    scores = (
        jnp.einsum("sqhd,skhd->shqk", query_heads, key_heads, preferred_element_type=jnp.float32)
        * SCORE_SCALE
    )
    permit = allowed_pairs(live_table, query_pos, key_pos, query_seg, key_seg)[:, None]
    attn_probs = jnp.where(permit, jnp.exp(scores - lse_heads[..., None]), 0.0)
    grad_prob = jnp.einsum(
        "sqhd,skhd->shqk", dout_heads, value_heads, preferred_element_type=jnp.float32
    )
    grad_score = (attn_probs * (grad_prob - delta_heads[..., None])).astype(jnp.bfloat16)
    grad_query = (
        jnp.einsum("shqk,skhd->sqhd", grad_score, key_heads, preferred_element_type=jnp.float32)
        * SCORE_SCALE
    )
    grad_key = (
        jnp.einsum("shqk,sqhd->skhd", grad_score, query_heads, preferred_element_type=jnp.float32)
        * SCORE_SCALE
    )
    grad_value = jnp.einsum(
        "shqk,sqhd->skhd",
        attn_probs.astype(jnp.bfloat16),
        dout_heads,
        preferred_element_type=jnp.float32,
    )
    return (grad_query, grad_key, grad_value)


def local(
    tokens,
    segment_ids,
    live_blocks,
    norm1_gain,
    norm1_bias,
    qkv_weight,
    qv_bias,
    out_weight,
    out_bias,
    norm2_gain,
    norm2_bias,
    up_weight,
    up_bias,
    down_weight,
    down_bias,
    grad_out,
):
    shards = (
        norm1_gain,
        norm1_bias,
        qkv_weight,
        qv_bias,
        out_weight,
        out_bias,
        norm2_gain,
        norm2_bias,
        up_weight,
        up_bias,
        down_weight,
        down_bias,
    )
    gathered = (
        lax.all_gather(shards[0], ("dp", "ctx"), axis=0, tiled=True),
        lax.all_gather(shards[1], ("dp", "ctx"), axis=0, tiled=True),
        lax.all_gather(shards[2], ("dp", "ctx"), axis=0, tiled=True),
        lax.all_gather(shards[3], ("dp", "ctx"), axis=0, tiled=True),
        lax.all_gather(shards[4], ("dp", "ctx"), axis=0, tiled=True),
        lax.all_gather(shards[5], ("dp", "ctx"), axis=0, tiled=True),
        lax.all_gather(shards[6], ("dp", "ctx"), axis=0, tiled=True),
        lax.all_gather(shards[7], ("dp", "ctx"), axis=0, tiled=True),
        lax.all_gather(shards[8], ("dp", "ctx"), axis=0, tiled=True),
        lax.all_gather(shards[9], ("dp", "ctx"), axis=0, tiled=True),
        lax.all_gather(shards[10], ("dp", "ctx"), axis=0, tiled=True),
        lax.all_gather(shards[11], ("dp", "ctx"), axis=0, tiled=True),
    )
    (
        gain_first,
        shift_first,
        full_qkv,
        bias_qv,
        full_out,
        bias_out,
        gain_second,
        shift_second,
        full_up,
        bias_up,
        full_down,
        bias_down,
    ) = gathered
    seq_count, tok_rows, model_width = tokens.shape
    head_count = HEADS
    head_size = HEAD_DIM
    flat_rows = seq_count * tok_rows
    query_pos = lax.axis_index("ctx") * tok_rows + jnp.arange(tok_rows, dtype=jnp.int32)
    live_table = live_blocks.astype(jnp.bfloat16)
    seg_low = segment_ids.astype(jnp.bfloat16)
    inputs_wide = tokens.reshape(flat_rows, model_width).astype(jnp.float32)
    normed_wide, norm_pull_one = jax.vjp(
        layer_norm, inputs_wide, gain_first.astype(jnp.float32), shift_first.astype(jnp.float32)
    )
    normed_one = normed_wide.astype(jnp.bfloat16)
    projected = matmul_low(normed_one, full_qkv)
    bias_wide = bias_qv.astype(jnp.float32)
    query_low = (projected[:, :model_width] + bias_wide[:model_width]).astype(jnp.bfloat16)
    key_low = projected[:, model_width : 2 * model_width].astype(jnp.bfloat16)
    value_low = (projected[:, 2 * model_width :] + bias_wide[model_width:]).astype(jnp.bfloat16)
    query_heads = query_low.reshape(seq_count, tok_rows, head_count, head_size)
    key_seq = key_low.reshape(seq_count, tok_rows, model_width)
    value_seq = value_low.reshape(seq_count, tok_rows, model_width)
    initial = (
        jnp.full((seq_count, head_count, tok_rows), NEG_FILL, jnp.float32),
        jnp.zeros((seq_count, head_count, tok_rows), jnp.float32),
        jnp.zeros((seq_count, tok_rows, head_count, head_size), jnp.float32),
    )
    key_part = lax.all_gather(key_seq, "ctx", axis=1, tiled=True)
    value_part = lax.all_gather(value_seq, "ctx", axis=1, tiled=True)
    seg_part = lax.all_gather(seg_low, "ctx", axis=1, tiled=True)

    def step_fn(offset, span_rows, inner_state):
        run_max, run_total, accum_out = inner_state
        key_heads = lax.dynamic_slice_in_dim(key_part, offset, span_rows, 1).reshape(
            seq_count, span_rows, head_count, head_size
        )
        value_heads = lax.dynamic_slice_in_dim(value_part, offset, span_rows, 1).reshape(
            seq_count, span_rows, head_count, head_size
        )
        key_seg = lax.dynamic_slice_in_dim(seg_part, offset, span_rows, 1)
        key_pos = offset + jnp.arange(span_rows, dtype=jnp.int32)
        scores = (
            jnp.einsum(
                "sqhd,skhd->shqk", query_heads, key_heads, preferred_element_type=jnp.float32
            )
            * SCORE_SCALE
        )
        permit = allowed_pairs(live_table, query_pos, key_pos, seg_low, key_seg)[:, None]
        scores = jnp.where(permit, scores, NEG_FILL)
        new_max = jnp.maximum(run_max, jnp.max(scores, axis=-1))
        exp_scores = jnp.where(permit, jnp.exp(scores - new_max[..., None]), 0.0)
        factor = jnp.exp(run_max - new_max)
        run_total = run_total * factor + jnp.sum(exp_scores, axis=-1)
        weighted = jnp.einsum(
            "shqk,skhd->sqhd",
            exp_scores.astype(jnp.bfloat16),
            value_heads,
            preferred_element_type=jnp.float32,
        )
        accum_out = accum_out * jnp.transpose(factor, (0, 2, 1))[..., None] + weighted
        return (new_max, run_total, accum_out)

    run_max, run_total, accum_out = sweep_blocks(key_part.shape[1], step_fn, initial)
    attn_wide = accum_out / jnp.transpose(run_total, (0, 2, 1))[..., None]
    lse_heads = run_max + jnp.log(run_total)
    attn_low = attn_wide.reshape(flat_rows, model_width).astype(jnp.bfloat16)
    hidden = inputs_wide + matmul_low(attn_low, full_out) + bias_out.astype(jnp.float32)
    normed_two_wide, norm_pull_two = jax.vjp(
        layer_norm, hidden, gain_second.astype(jnp.float32), shift_second.astype(jnp.float32)
    )
    normed_two = normed_two_wide.astype(jnp.bfloat16)
    before = matmul_low(normed_two, full_up) + bias_up.astype(jnp.float32)
    activated_wide, gelu_pull = jax.vjp(exact_gelu, before)
    activated = activated_wide.astype(jnp.bfloat16)
    output = (hidden + matmul_low(activated, full_down) + bias_down.astype(jnp.float32)).astype(
        jnp.bfloat16
    )
    back_params = (
        lax.all_gather(shards[0], ("dp", "ctx"), axis=0, tiled=True),
        lax.all_gather(shards[1], ("dp", "ctx"), axis=0, tiled=True),
        lax.all_gather(shards[2], ("dp", "ctx"), axis=0, tiled=True),
        lax.all_gather(shards[3], ("dp", "ctx"), axis=0, tiled=True),
        lax.all_gather(shards[4], ("dp", "ctx"), axis=0, tiled=True),
        lax.all_gather(shards[5], ("dp", "ctx"), axis=0, tiled=True),
        lax.all_gather(shards[6], ("dp", "ctx"), axis=0, tiled=True),
        lax.all_gather(shards[7], ("dp", "ctx"), axis=0, tiled=True),
        lax.all_gather(shards[8], ("dp", "ctx"), axis=0, tiled=True),
        lax.all_gather(shards[9], ("dp", "ctx"), axis=0, tiled=True),
        lax.all_gather(shards[10], ("dp", "ctx"), axis=0, tiled=True),
        lax.all_gather(shards[11], ("dp", "ctx"), axis=0, tiled=True),
    )
    back_qkv = back_params[2]
    back_out = back_params[4]
    back_up = back_params[8]
    back_down = back_params[10]
    grad_low = grad_out.reshape(flat_rows, model_width)
    grad_down = inner_rows(activated, grad_low)
    grad_bias_down = jnp.sum(grad_low.astype(jnp.float32), axis=0)
    grad_act = times_transpose(grad_low, back_down)
    grad_before = gelu_pull(grad_act)[0].astype(jnp.bfloat16)
    grad_up = inner_rows(normed_two, grad_before)
    grad_bias_up = jnp.sum(grad_before.astype(jnp.float32), axis=0)
    grad_normed_two = times_transpose(grad_before, back_up)
    grad_hidden_part, grad_gain_two, grad_shift_two = norm_pull_two(grad_normed_two)
    grad_hidden = grad_low.astype(jnp.float32) + grad_hidden_part
    grad_branch = grad_hidden.astype(jnp.bfloat16)
    grad_out_full = inner_rows(attn_low, grad_branch)
    grad_bias_out = jnp.sum(grad_branch.astype(jnp.float32), axis=0)
    grad_attn = times_transpose(grad_branch, back_out).astype(jnp.bfloat16)
    dout_heads = grad_attn.reshape(seq_count, tok_rows, head_count, head_size)
    delta_rows = jnp.sum(dout_heads.astype(jnp.float32) * attn_wide, axis=-1)
    delta_heads = jnp.transpose(delta_rows, (0, 2, 1))
    key_all, value_all, seg_all = (
        lax.all_gather(key_seq, "ctx", axis=1, tiled=True),
        lax.all_gather(value_seq, "ctx", axis=1, tiled=True),
        lax.all_gather(seg_low, "ctx", axis=1, tiled=True),
    )

    def key_step(offset, span_rows, inner_state):
        grad_query_acc, grad_key_all, grad_value_all = inner_state
        key_heads = lax.dynamic_slice_in_dim(key_all, offset, span_rows, 1).reshape(
            seq_count, span_rows, head_count, head_size
        )
        value_heads = lax.dynamic_slice_in_dim(value_all, offset, span_rows, 1).reshape(
            seq_count, span_rows, head_count, head_size
        )
        key_seg = lax.dynamic_slice_in_dim(seg_all, offset, span_rows, 1)
        key_pos = offset + jnp.arange(span_rows, dtype=jnp.int32)
        grad_query, grad_key, grad_value = pair_grads(
            live_table,
            query_heads,
            dout_heads,
            lse_heads,
            delta_heads,
            query_pos,
            seg_low,
            key_heads,
            value_heads,
            key_pos,
            key_seg,
        )
        grad_key_all = lax.dynamic_update_slice_in_dim(
            grad_key_all, grad_key.reshape(seq_count, span_rows, model_width), offset, 1
        )
        grad_value_all = lax.dynamic_update_slice_in_dim(
            grad_value_all, grad_value.reshape(seq_count, span_rows, model_width), offset, 1
        )
        return (grad_query_acc + grad_query, grad_key_all, grad_value_all)

    length_rows = key_all.shape[1]
    zero_query = jnp.zeros((seq_count, tok_rows, head_count, head_size), jnp.float32)
    zero_keys = jnp.zeros((seq_count, length_rows, model_width), jnp.float32)
    grad_query_heads, grad_key_all, grad_value_all = sweep_blocks(
        length_rows, key_step, (zero_query, zero_keys, zero_keys)
    )
    grad_key_seq, grad_value_seq = (
        lax.psum_scatter(
            grad_key_all.astype(jnp.bfloat16), "ctx", scatter_dimension=1, tiled=True
        ).astype(jnp.float32),
        lax.psum_scatter(
            grad_value_all.astype(jnp.bfloat16), "ctx", scatter_dimension=1, tiled=True
        ).astype(jnp.float32),
    )
    grad_query_low = grad_query_heads.reshape(flat_rows, model_width).astype(jnp.bfloat16)
    grad_key_low = grad_key_seq.reshape(flat_rows, model_width).astype(jnp.bfloat16)
    grad_value_low = grad_value_seq.reshape(flat_rows, model_width).astype(jnp.bfloat16)
    grad_proj_low = jnp.concatenate([grad_query_low, grad_key_low, grad_value_low], axis=1)
    grad_qkv_full = inner_rows(normed_one, grad_proj_low)
    grad_bias_qv = jnp.concatenate(
        [
            jnp.sum(grad_query_low.astype(jnp.float32), axis=0),
            jnp.sum(grad_value_low.astype(jnp.float32), axis=0),
        ]
    )
    grad_normed_one = times_transpose(grad_proj_low, back_qkv)
    grad_input_part, grad_gain_one, grad_shift_one = norm_pull_one(grad_normed_one)
    grad_tokens = (grad_hidden + grad_input_part).reshape(seq_count, tok_rows, model_width)
    summed = (
        lax.psum_scatter(grad_gain_one, ("dp", "ctx"), scatter_dimension=0, tiled=True),
        lax.psum_scatter(grad_shift_one, ("dp", "ctx"), scatter_dimension=0, tiled=True),
        lax.psum_scatter(grad_qkv_full.astype(jnp.bfloat16), ("dp", "ctx"), scatter_dimension=0, tiled=True).astype(jnp.float32),
        lax.psum_scatter(grad_bias_qv, ("dp", "ctx"), scatter_dimension=0, tiled=True),
        lax.psum_scatter(grad_out_full.astype(jnp.bfloat16), ("dp", "ctx"), scatter_dimension=0, tiled=True).astype(jnp.float32),
        lax.psum_scatter(grad_bias_out, ("dp", "ctx"), scatter_dimension=0, tiled=True),
        lax.psum_scatter(grad_gain_two, ("dp", "ctx"), scatter_dimension=0, tiled=True),
        lax.psum_scatter(grad_shift_two, ("dp", "ctx"), scatter_dimension=0, tiled=True),
        lax.psum_scatter(grad_up.astype(jnp.bfloat16), ("dp", "ctx"), scatter_dimension=0, tiled=True).astype(jnp.float32),
        lax.psum_scatter(grad_bias_up, ("dp", "ctx"), scatter_dimension=0, tiled=True),
        lax.psum_scatter(grad_down.astype(jnp.bfloat16), ("dp", "ctx"), scatter_dimension=0, tiled=True).astype(jnp.float32),
        lax.psum_scatter(grad_bias_down, ("dp", "ctx"), scatter_dimension=0, tiled=True),
    )
    return (
        output.reshape(seq_count, tok_rows, model_width),
        grad_tokens,
        summed[0],
        summed[1],
        summed[2],
        summed[3],
        summed[4],
        summed[5],
        summed[6],
        summed[7],
        summed[8],
        summed[9],
        summed[10],
        summed[11],
    )


NZ = 4
GROUP = HEADS // NZ
GW = GROUP * HEAD_DIM
CHUNK = 256


def pick(array, index, axis=0):
    return lax.dynamic_index_in_dim(array, index, axis, keepdims=False)


def shift(array, axis, size, hop):
    return lax.ppermute(array, axis, [(i, (i + hop) % size) for i in range(size)])


def swap(array, axis):
    return shift(array, axis, 2, 1)


def in_order(own, received, index, axis):
    first = jnp.where(index == 0, own, received)
    second = jnp.where(index == 0, received, own)
    return jnp.stack([first, second], axis=axis)


def z_spread(block, z):
    up = lax.ppermute(block, "z", [(0, 1), (1, 2), (2, 3)])
    down = lax.ppermute(block, "z", [(1, 0), (2, 1), (3, 2)])
    far = shift(block, "z", NZ, 2)
    last = lax.ppermute(far, "z", [(2, 3), (1, 0)])
    return jnp.stack(
        [
            lax.select_n(z, block, up, far, last),
            lax.select_n(z, down, block, up, far),
            lax.select_n(z, far, down, block, up),
            lax.select_n(z, last, far, down, block),
        ]
    )


def z_order(pieces, z):
    return jnp.stack([lax.select_n((z - a) % NZ, *pieces) for a in range(NZ)])


def z_exchange(array, z):
    return [pick(array, z)] + [shift(pick(array, (z + j) % NZ), "z", NZ, j) for j in range(1, NZ)]


def xy_gather(line, y, x):
    a, b = line[:2], line[2:]
    a = in_order(a, swap(a, "x"), x, 0)
    b = in_order(b, swap(b, "y"), y, 0)
    a = in_order(a, swap(a, "y"), y, 0)
    b = in_order(b, swap(b, "x"), x, 1)
    return jnp.concatenate([a, b], axis=2)


def xy_scatter(blocks, y, x, wire):
    def halve(array, axis, name, index):
        sent = swap(pick(array, 1 - index, axis).astype(wire), name)
        return pick(array, index, axis).astype(jnp.float32) + sent.astype(jnp.float32)

    a, b = blocks[:, :, :2], blocks[:, :, 2:]
    a = halve(a, 0, "y", y)
    b = halve(b, 1, "x", x)
    a = halve(a, 0, "x", x)
    b = halve(b, 0, "y", y)
    return jnp.concatenate([a, b], axis=0)


def z_collect(line, z, wire):
    own, *rest = z_exchange_wide(line, z, wire)
    total = own.astype(jnp.float32)
    for piece in rest:
        total = total + piece.astype(jnp.float32)
    return total


def z_exchange_wide(array, z, wire):
    return [pick(array, z)] + [
        shift(pick(array, (z + j) % NZ).astype(wire), "z", NZ, j) for j in range(1, NZ)
    ]


def norm_stats(values):
    center = values - jnp.mean(values, axis=-1, keepdims=True)
    scale = lax.rsqrt(jnp.mean(center * center, axis=-1, keepdims=True) + 1e-05)
    return center * scale, scale


def norm_back(grad, gain, unit, scale):
    c = grad * gain
    return scale * (
        c - jnp.mean(c, axis=-1, keepdims=True) - unit * jnp.mean(c * unit, axis=-1, keepdims=True)
    )


def dot_nt(a, b):
    return lax.dot_general(a, b, (((1,), (1,)), ((), ())), preferred_element_type=jnp.float32)


def dot_tn(a, b):
    return lax.dot_general(a, b, (((0,), (0,)), ((), ())), preferred_element_type=jnp.float32)


def dot_nn(a, b):
    return lax.dot_general(a, b, (((1,), (0,)), ((), ())), preferred_element_type=jnp.float32)


def attend_kernel(
    act_ref, q_ref, kv_ref, qseg_ref, kseg_ref, o_ref, low_ref, lse_ref, k_s, v_s, m_s, l_s, acc_s
):
    i = pl.program_id(0)
    chunks = kv_ref.shape[0] // CHUNK

    @pl.when(i == 0)
    def _():
        for h in range(GROUP):
            k_s[h] = kv_ref[:, HEAD_DIM * h : HEAD_DIM * (h + 1)]
            v_s[h] = kv_ref[:, GW + HEAD_DIM * h : GW + HEAD_DIM * (h + 1)]

    m_s[...] = jnp.full(m_s.shape, NEG_FILL, jnp.float32)
    l_s[...] = jnp.zeros(l_s.shape, jnp.float32)
    acc_s[...] = jnp.zeros(acc_s.shape, jnp.float32)
    q_heads = [q_ref[:, HEAD_DIM * h : HEAD_DIM * (h + 1)] for h in range(GROUP)]
    q_seg = qseg_ref[...]

    def one_chunk(j, carry):
        @pl.when(act_ref[i, j] != 0)
        def _():
            at = pl.ds(pl.multiple_of(j * CHUNK, CHUNK), CHUNK)
            permit = q_seg == kseg_ref[0, :, at]
            for h in range(GROUP):
                s = jnp.where(permit, dot_nt(q_heads[h], k_s[h, at]), NEG_FILL)
                old = m_s[h]
                new = jnp.maximum(old, jnp.max(s, axis=-1, keepdims=True))
                p = jnp.exp(s - new)
                fade = jnp.exp(old - new)
                l_s[h] = l_s[h] * fade + jnp.sum(p, axis=-1, keepdims=True)
                acc_s[h] = acc_s[h] * fade + dot_nn(p.astype(jnp.bfloat16), v_s[h, at])
                m_s[h] = new

        return carry

    lax.fori_loop(0, chunks, one_chunk, 0)
    rows = q_ref.shape[0]
    outs, logs = [], []
    for h in range(GROUP):
        outs.append(acc_s[h] / l_s[h])
        lse = m_s[h] + jnp.log(l_s[h])
        logs.append(jnp.transpose(jnp.broadcast_to(lse, (rows, rows)))[0:1])
    out = jnp.concatenate(outs, axis=1)
    o_ref[...] = out
    low_ref[...] = out.astype(jnp.bfloat16)
    lse_ref[...] = jnp.concatenate(logs + [logs[0]] * (8 - GROUP), axis=0)


def attend(active, q, kv, q_seg, k_seg):
    rows, keys = q.shape[0], kv.shape[0]
    grid = rows // BLOCK
    return pl.pallas_call(
        attend_kernel,
        out_shape=(
            jax.ShapeDtypeStruct((rows, GW), jnp.float32),
            jax.ShapeDtypeStruct((rows, GW), jnp.bfloat16),
            jax.ShapeDtypeStruct((8, rows), jnp.float32),
        ),
        grid_spec=pltpu.PrefetchScalarGridSpec(
            num_scalar_prefetch=1,
            grid=(grid,),
            in_specs=[
                pl.BlockSpec((BLOCK, GW), lambda i, t: (i, 0)),
                pl.BlockSpec((keys, 2 * GW), lambda i, t: (0, 0)),
                pl.BlockSpec((BLOCK, 1), lambda i, t: (i, 0)),
                pl.BlockSpec((1, 1, keys), lambda i, t: (i, 0, 0)),
            ],
            out_specs=[
                pl.BlockSpec((BLOCK, GW), lambda i, t: (i, 0)),
                pl.BlockSpec((BLOCK, GW), lambda i, t: (i, 0)),
                pl.BlockSpec((8, BLOCK), lambda i, t: (0, i)),
            ],
            scratch_shapes=[
                pltpu.VMEM((GROUP, keys, HEAD_DIM), jnp.bfloat16),
                pltpu.VMEM((GROUP, keys, HEAD_DIM), jnp.bfloat16),
                pltpu.VMEM((GROUP, BLOCK, 1), jnp.float32),
                pltpu.VMEM((GROUP, BLOCK, 1), jnp.float32),
                pltpu.VMEM((GROUP, BLOCK, HEAD_DIM), jnp.float32),
            ],
        ),
        compiler_params=pltpu.CompilerParams(vmem_limit_bytes=32 << 20),
        cost_estimate=pl.CostEstimate(
            flops=2 * rows * keys * GW, bytes_accessed=4 * keys * GW, transcendentals=rows * keys
        ),
        name="attend",
    )(active, q, kv, q_seg, k_seg)


def attend_back_kernel(
    act_ref, q_ref, do_ref, o_ref, kv_ref, lse_ref, qseg_ref, kseg_ref, dq_ref, dkv_ref,
    q_s, do_s, dq_s, delta_s, dk_s, dv_s,
):
    kb = pl.program_id(0)
    rows = q_ref.shape[0]

    @pl.when(kb == 0)
    def _():
        ones = jnp.ones((8, HEAD_DIM), jnp.float32)
        for h in range(GROUP):
            lanes = slice(HEAD_DIM * h, HEAD_DIM * (h + 1))
            q_s[h] = q_ref[:, lanes]
            do_s[h] = do_ref[:, lanes]
            both = do_ref[:, lanes].astype(jnp.float32) * o_ref[:, lanes]
            delta_s[h] = lax.dot_general(
                ones, both, (((1,), (1,)), ((), ())), precision=lax.Precision.HIGHEST,
                preferred_element_type=jnp.float32,
            )[0:1]
        dq_s[...] = jnp.zeros(dq_s.shape, jnp.float32)

    dk_s[...] = jnp.zeros(dk_s.shape, jnp.float32)
    dv_s[...] = jnp.zeros(dv_s.shape, jnp.float32)
    k_heads = [kv_ref[:, HEAD_DIM * h : HEAD_DIM * (h + 1)] for h in range(GROUP)]
    v_heads = [kv_ref[:, GW + HEAD_DIM * h : GW + HEAD_DIM * (h + 1)] for h in range(GROUP)]
    k_seg = kseg_ref[...]

    def one_chunk(j, carry):
        @pl.when(act_ref[kb, j] != 0)
        def _():
            at = pl.ds(pl.multiple_of(j * CHUNK, CHUNK), CHUNK)
            permit = k_seg == qseg_ref[0, :, at]
            for h in range(GROUP):
                q, do = q_s[h, at], do_s[h, at]
                s = dot_nt(k_heads[h], q)
                p = jnp.where(permit, jnp.exp(s - lse_ref[h : h + 1, at]), 0.0)
                dp = dot_nt(v_heads[h], do)
                ds = (p * (dp - delta_s[h, :, at])).astype(jnp.bfloat16)
                dv_s[h] += dot_nn(p.astype(jnp.bfloat16), do)
                dk_s[h] += dot_nn(ds, q)
                dq_s[h, at] += dot_tn(ds, k_heads[h])

        return carry

    lax.fori_loop(0, rows // CHUNK, one_chunk, 0)
    dkv_ref[...] = jnp.concatenate(
        [dk_s[h] for h in range(GROUP)] + [dv_s[h] for h in range(GROUP)], axis=1
    ).astype(jnp.bfloat16)

    @pl.when(kb == pl.num_programs(0) - 1)
    def _():
        dq_ref[...] = jnp.concatenate(
            [dq_s[h] * SCORE_SCALE for h in range(GROUP)], axis=1
        ).astype(jnp.bfloat16)


def attend_back(active, q, dout, out, kv, lse, q_seg, k_seg):
    rows, keys = q.shape[0], kv.shape[0]
    whole = lambda shape: pl.BlockSpec(shape, lambda i, t: (0,) * len(shape))
    return pl.pallas_call(
        attend_back_kernel,
        out_shape=(
            jax.ShapeDtypeStruct((rows, GW), jnp.bfloat16),
            jax.ShapeDtypeStruct((keys, 2 * GW), jnp.bfloat16),
        ),
        grid_spec=pltpu.PrefetchScalarGridSpec(
            num_scalar_prefetch=1,
            grid=(keys // BLOCK,),
            in_specs=[
                whole((rows, GW)),
                whole((rows, GW)),
                whole((rows, GW)),
                pl.BlockSpec((BLOCK, 2 * GW), lambda i, t: (i, 0)),
                whole((8, rows)),
                pl.BlockSpec((1, 1, rows), lambda i, t: (i, 0, 0)),
                pl.BlockSpec((BLOCK, 1), lambda i, t: (i, 0)),
            ],
            out_specs=[
                whole((rows, GW)),
                pl.BlockSpec((BLOCK, 2 * GW), lambda i, t: (i, 0)),
            ],
            scratch_shapes=[
                pltpu.VMEM((GROUP, rows, HEAD_DIM), jnp.bfloat16),
                pltpu.VMEM((GROUP, rows, HEAD_DIM), jnp.bfloat16),
                pltpu.VMEM((GROUP, rows, HEAD_DIM), jnp.float32),
                pltpu.VMEM((GROUP, 1, rows), jnp.float32),
                pltpu.VMEM((GROUP, BLOCK, HEAD_DIM), jnp.float32),
                pltpu.VMEM((GROUP, BLOCK, HEAD_DIM), jnp.float32),
            ],
        ),
        compiler_params=pltpu.CompilerParams(vmem_limit_bytes=32 << 20),
        cost_estimate=pl.CostEstimate(
            flops=5 * rows * keys * GW, bytes_accessed=8 * keys * GW, transcendentals=rows * keys
        ),
        name="attend_back",
    )(active, q, dout, out, kv, lse, q_seg, k_seg)


def fast_local(
    tokens, segment_ids, live_blocks, norm1_gain, norm1_bias, qkv_weight, qv_bias, out_weight, out_bias,
    norm2_gain, norm2_bias, up_weight, up_bias, down_weight, down_bias, grad_out,
):
    y, x, z, c = (lax.axis_index(name) for name in ("y", "x", "z", "c"))
    wide, low = jnp.float32, jnp.bfloat16
    _, rows, width = tokens.shape
    own_rows, units = qkv_weight.shape[0], down_weight.shape[0]
    ff = up_weight.shape[1]
    half = ff // 2
    devices = width // own_rows
    seq_rows = rows * NZ
    keys = 2 * seq_rows
    blocks = keys // BLOCK

    own_tokens = tokens[0]
    line_tokens = z_spread(own_tokens, z).reshape(seq_rows, width)
    own_seg = z_spread(segment_ids, z).reshape(NZ, rows)
    seg = in_order(own_seg, swap(own_seg, "c"), c, 1).reshape(keys)
    vectors = (norm1_gain, norm1_bias, qv_bias, out_bias, norm2_gain, norm2_bias, up_bias, down_bias)
    sizes = [v.shape[0] for v in vectors]
    packed = xy_gather(z_spread(jnp.concatenate(vectors)[None], z), y, x)
    packed = in_order(packed, swap(packed, "c"), c, 3).reshape(devices, sum(sizes)).astype(wide)
    cuts = [sum(sizes[:i]) for i in range(len(sizes) + 1)]
    gain1, shift1, bias_qv, bias_out, gain2, shift2, bias_up, bias_down = (
        packed[:, cuts[i] : cuts[i + 1]].reshape(-1) for i in range(len(sizes))
    )
    wz = qkv_weight.reshape(own_rows, 3, NZ, GW).transpose(2, 0, 1, 3).reshape(NZ, own_rows, 3 * GW)
    wz = xy_gather(z_order(z_exchange(wz, z), z), y, x)
    wz = in_order(wz, swap(wz, "c"), c, 3).reshape(width, 3 * GW)

    up_sets = up_weight.reshape(own_rows, ff // (2 * units), 2, units).transpose(2, 0, 1, 3)
    up_sets = up_sets.reshape(2, own_rows, half)
    up_chip = in_order(pick(up_sets, c), swap(pick(up_sets, 1 - c), "c"), c, 0)
    up_half = xy_gather(z_spread(up_chip.reshape(2 * own_rows, half), z), y, x).reshape(width, half)
    wo = xy_gather(z_spread(out_weight, z), y, x)
    wo = in_order(wo, swap(wo, "c"), c, 3).reshape(NZ, GW, width)
    down_half = xy_gather(z_spread(down_weight, z), y, x).reshape(half, width)
    up_bias_half = pick(bias_up.reshape(ff // (2 * units), 2, units), c, 1).reshape(half)

    own_blocks = seq_rows // BLOCK
    per = rows // BLOCK
    ids = jnp.arange(blocks, dtype=jnp.int32)
    own_ids = pick(ids.reshape(NZ, 2, per), c, 1).reshape(own_blocks)
    own_live = pick(live_blocks[0].reshape(NZ, 2, per, blocks), c, 1).reshape(own_blocks, blocks)
    seg_blocks = seg.reshape(blocks, BLOCK)
    first, last = seg_blocks[:, 0], seg_blocks[:, -1]
    own_seg_blocks = own_seg.reshape(own_blocks, BLOCK)
    own_first, own_last = own_seg_blocks[:, 0], own_seg_blocks[:, -1]
    may = (own_live > 0) | (own_ids[:, None] == ids[None, :])
    meet = may & (own_first[:, None] <= last[None, :]) & (first[None, :] <= own_last[:, None])
    per_chunk = CHUNK // BLOCK
    active = jnp.any(meet.reshape(own_blocks, blocks // per_chunk, per_chunk), axis=2).astype(jnp.int32)
    active_back = jnp.any(
        meet.reshape(own_blocks // per_chunk, per_chunk, blocks), axis=1
    ).T.astype(jnp.int32)
    key_seg = jnp.where(may[:, :, None], seg_blocks[None], -1).reshape(own_blocks, 1, keys)
    query_seg = jnp.where(may.T[:, :, None], own_seg_blocks[None], -1).reshape(blocks, 1, seq_rows)

    tokens_wide = line_tokens.astype(wide)
    unit1, scale1 = norm_stats(tokens_wide)
    n1 = (unit1 * gain1 + shift1).astype(low)
    projected = matmul_low(n1, wz)
    q_bias = pick(bias_qv[:width].reshape(NZ, GW), z)
    v_bias = pick(bias_qv[width:].reshape(NZ, GW), z)
    q = (projected[:, :GW] + q_bias).astype(low) * jnp.asarray(SCORE_SCALE, low)
    kv = jnp.concatenate(
        [projected[:, GW : 2 * GW].astype(low), (projected[:, 2 * GW :] + v_bias).astype(low)], axis=1
    )
    kv_line = kv.reshape(NZ, rows, 2 * GW)
    kv_all = in_order(kv_line, swap(kv_line, "c"), c, 1).reshape(keys, 2 * GW)
    att_wide, att_low, lse = attend(active, q, kv_all, own_seg.reshape(seq_rows, 1), key_seg)
    att = z_order(z_exchange(att_low.reshape(NZ, rows, GW), z), z)

    own_wide = own_tokens.astype(wide)
    branch = sum(matmul_low(att[g], wo[g]) for g in range(NZ))
    hidden = own_wide + branch + bias_out
    unit2, scale2 = norm_stats(hidden)
    n2 = (unit2 * gain2 + shift2).astype(low)

    go = grad_out[0]
    n2_both = jnp.concatenate([n2, swap(n2, "c")], axis=0)
    go_both = jnp.concatenate([go, swap(go, "c")], axis=0)
    before = matmul_low(n2_both, up_half) + up_bias_half
    cdf = 0.5 * (1.0 + lax.erf(before * 0.7071067811865476))
    slope = cdf + before * (0.3989422804014327 * jnp.exp(-0.5 * before * before))
    activated = (before * cdf).astype(low)
    out_part = matmul_low(activated, down_half)
    out_sum = out_part[:rows] + swap(out_part[rows:].astype(low), "c").astype(wide)
    output = (hidden + out_sum + bias_down).astype(low)
    grad_before = (dot_nt(go_both, down_half) * slope).astype(low)
    m_part = dot_nt(grad_before, up_half)
    m = m_part[:rows] + swap(m_part[rows:].astype(low), "c").astype(wide)
    grad_up = dot_tn(n2_both, grad_before).astype(low)
    grad_down = dot_tn(activated, go_both).astype(low)
    up_bias_part = jnp.sum(grad_before.astype(wide), axis=0)

    go_wide = go.astype(wide)
    grad_hidden = go_wide + norm_back(m, gain2, unit2, scale2)
    grad_branch = grad_hidden.astype(low)
    grad_att = jnp.stack([dot_nt(grad_branch, wo[g]).astype(low) for g in range(NZ)])
    dout = z_order(z_exchange(grad_att, z), z).reshape(seq_rows, GW)
    grad_wo = jnp.stack([dot_tn(att[g], grad_branch) for g in range(NZ)]).astype(low)

    dq, dkv = attend_back(
        active_back, q, dout, att_wide, kv_all, lse, query_seg, seg.reshape(keys, 1)
    )
    dkv = dkv.reshape(NZ, 2, rows, 2 * GW)
    dkv_sum = pick(dkv, c, 1).astype(wide) + swap(pick(dkv, 1 - c, 1), "c").astype(wide)
    dkv_low = dkv_sum.reshape(seq_rows, 2 * GW).astype(low)
    dqkv = jnp.concatenate([dq, dkv_low], axis=1)
    m1 = dot_nt(dqkv, wz)
    m1_line = m1.reshape(NZ, rows, width)
    m1_own = z_collect(m1_line, z, low)
    grad_wz = dot_tn(n1, dqkv).astype(low)
    own_unit1, own_scale1 = norm_stats(own_wide)
    grad_tokens = grad_hidden + norm_back(m1_own, gain1, own_unit1, own_scale1)

    grad_down = z_collect(xy_scatter(grad_down.reshape(2, 2, NZ, units, width), y, x, low), z, low)
    grad_up = z_collect(xy_scatter(grad_up.reshape(2, 2, NZ, 2 * own_rows, half), y, x, low), z, low)
    grad_up = grad_up.reshape(2, own_rows, half)
    up_other = swap(pick(grad_up, 1 - c).astype(low), "c").astype(wide)
    up_shape = (own_rows, ff // (2 * units), units)
    grad_up = in_order(pick(grad_up, c).reshape(up_shape), up_other.reshape(up_shape), c, 2)
    grad_up = grad_up.reshape(own_rows, ff)

    def over_cores(array, wire):
        return pick(array, c, 3).astype(wide) + swap(pick(array, 1 - c, 3).astype(wire), "c").astype(wide)

    grad_wo = over_cores(grad_wo.reshape(2, 2, NZ, 2, own_rows, width), low)
    grad_wo = z_collect(xy_scatter(grad_wo, y, x, low), z, low)
    grad_wz = over_cores(grad_wz.reshape(2, 2, NZ, 2, own_rows, 3 * GW), low)
    grad_wz = z_order(z_exchange(xy_scatter(grad_wz, y, x, low).astype(low), z), z)
    grad_qkv = grad_wz.reshape(NZ, own_rows, 3, GW).transpose(1, 2, 0, 3).reshape(own_rows, 3 * width)

    dqkv_sum = jnp.sum(dqkv.astype(wide), axis=0)
    at_group = (jnp.arange(NZ) == z)[:, None]
    qv_part = jnp.concatenate(
        [
            jnp.where(at_group, dqkv_sum[None, :GW], 0.0).reshape(width),
            jnp.where(at_group, dqkv_sum[None, 2 * GW :], 0.0).reshape(width),
        ]
    )
    at_core = (jnp.arange(2) == c)[None, :, None]
    up_bias_part = jnp.where(at_core, up_bias_part.reshape(ff // (2 * units), 1, units), 0.0)
    parts = (
        jnp.sum(m1 * unit1, axis=0),
        jnp.sum(m1, axis=0),
        qv_part,
        jnp.sum(grad_branch.astype(wide), axis=0),
        jnp.sum(m * unit2, axis=0),
        jnp.sum(m, axis=0),
        up_bias_part,
        jnp.sum(go_wide, axis=0),
    )
    vec = jnp.concatenate([p.reshape(devices, s) for p, s in zip(parts, sizes)], axis=1)
    vec = over_cores(vec.reshape(2, 2, NZ, 2, 1, sum(sizes)), wide)
    vec = z_collect(xy_scatter(vec, y, x, wide), z, wide)[0]
    v = [vec[cuts[i] : cuts[i + 1]] for i in range(len(sizes))]
    return (
        output[None], grad_tokens[None], v[0], v[1], grad_qkv.astype(wide), v[2], grad_wo, v[3],
        v[4], v[5], grad_up, v[6], grad_down, v[7],
    )


def build(body, mesh, dp, ctx):
    both = dp + ctx
    rows, vector, matrix = P(dp, ctx, None), P(both), P(both, None)
    return jax.shard_map(
        body,
        mesh=mesh,
        in_specs=(
            rows, P(dp, ctx), P(dp, None, None), vector, vector, matrix, vector, matrix, vector,
            vector, vector, matrix, vector, matrix, vector, rows,
        ),
        out_specs=(
            rows, rows, vector, vector, matrix, vector, matrix, vector, vector, vector, matrix,
            vector, matrix, vector,
        ),
        check_vma=False,
    )


def solution(mesh):
    if dict(mesh.shape) == {"dp": 4, "ctx": 2 * NZ}:
        grid = Mesh(mesh.devices.reshape(2, 2, NZ, 2), ("y", "x", "z", "c"))
        return build(fast_local, grid, ("y", "x"), ("z", "c"))
    return build(local, mesh, ("dp",), ("ctx",))
```

```python
import math

import jax
import jax.numpy as jnp
from jax import lax
from jax.experimental import pallas as pl
from jax.experimental.pallas import tpu as pltpu
from jax.sharding import Mesh, PartitionSpec as P

HEADS = 12
HEAD_DIM = 64
BLOCK = 128


NEG_FILL = -1e30
SCORE_SCALE = 0.125


def layer_norm(value_in, norm_gain, norm_shift):
    center = value_in - jnp.mean(value_in, axis=-1, keepdims=True)
    spread = jnp.mean(center * center, axis=-1, keepdims=True)
    return center * lax.rsqrt(spread + 1e-05) * norm_gain + norm_shift


def exact_gelu(value_in):
    return jax.nn.gelu(value_in, approximate=False)


def matmul_low(left_side, right_side):
    return jnp.dot(left_side, right_side, preferred_element_type=jnp.float32)


def inner_rows(left_side, right_side):
    return lax.dot_general(
        left_side, right_side, (((0,), (0,)), ((), ())), preferred_element_type=jnp.float32
    )


def times_transpose(left_side, right_side):
    return lax.dot_general(
        left_side, right_side, (((1,), (1,)), ((), ())), preferred_element_type=jnp.float32
    )


def sweep_blocks(count_rows, step_fn, carry_state):
    span_rows = math.gcd(count_rows, 512)
    return lax.fori_loop(
        0,
        count_rows // span_rows,
        lambda loop_index, loop_state: step_fn(loop_index * span_rows, span_rows, loop_state),
        carry_state,
    )


def allowed_pairs(live_table, query_pos, key_pos, query_seg, key_seg):
    block_slots = jnp.arange(live_table.shape[-1], dtype=jnp.int32)
    query_block = query_pos // BLOCK
    key_block = key_pos // BLOCK
    pick_query = (query_block[:, None] == block_slots[None, :]).astype(jnp.bfloat16)
    pick_key = (key_block[:, None] == block_slots[None, :]).astype(jnp.bfloat16)
    live_rows = jnp.einsum(
        "qa,sab->sqb", pick_query, live_table, preferred_element_type=jnp.float32
    )
    live_grid = jnp.einsum(
        "sqb,kb->sqk", live_rows.astype(jnp.bfloat16), pick_key, preferred_element_type=jnp.float32
    )
    same_block = query_block[:, None] == key_block[None, :]
    same_doc = query_seg[:, :, None] == key_seg[:, None, :]
    return same_doc & ((live_grid > 0.5) | same_block[None])


def pair_grads(
    live_table,
    query_heads,
    dout_heads,
    lse_heads,
    delta_heads,
    query_pos,
    query_seg,
    key_heads,
    value_heads,
    key_pos,
    key_seg,
):
    scores = (
        jnp.einsum("sqhd,skhd->shqk", query_heads, key_heads, preferred_element_type=jnp.float32)
        * SCORE_SCALE
    )
    permit = allowed_pairs(live_table, query_pos, key_pos, query_seg, key_seg)[:, None]
    attn_probs = jnp.where(permit, jnp.exp(scores - lse_heads[..., None]), 0.0)
    grad_prob = jnp.einsum(
        "sqhd,skhd->shqk", dout_heads, value_heads, preferred_element_type=jnp.float32
    )
    grad_score = (attn_probs * (grad_prob - delta_heads[..., None])).astype(jnp.bfloat16)
    grad_query = (
        jnp.einsum("shqk,skhd->sqhd", grad_score, key_heads, preferred_element_type=jnp.float32)
        * SCORE_SCALE
    )
    grad_key = (
        jnp.einsum("shqk,sqhd->skhd", grad_score, query_heads, preferred_element_type=jnp.float32)
        * SCORE_SCALE
    )
    grad_value = jnp.einsum(
        "shqk,sqhd->skhd",
        attn_probs.astype(jnp.bfloat16),
        dout_heads,
        preferred_element_type=jnp.float32,
    )
    return (grad_query, grad_key, grad_value)


def local(
    tokens,
    segment_ids,
    live_blocks,
    norm1_gain,
    norm1_bias,
    qkv_weight,
    qv_bias,
    out_weight,
    out_bias,
    norm2_gain,
    norm2_bias,
    up_weight,
    up_bias,
    down_weight,
    down_bias,
    grad_out,
):
    shards = (
        norm1_gain,
        norm1_bias,
        qkv_weight,
        qv_bias,
        out_weight,
        out_bias,
        norm2_gain,
        norm2_bias,
        up_weight,
        up_bias,
        down_weight,
        down_bias,
    )
    gathered = (
        lax.all_gather(shards[0], ("dp", "ctx"), axis=0, tiled=True),
        lax.all_gather(shards[1], ("dp", "ctx"), axis=0, tiled=True),
        lax.all_gather(shards[2], ("dp", "ctx"), axis=0, tiled=True),
        lax.all_gather(shards[3], ("dp", "ctx"), axis=0, tiled=True),
        lax.all_gather(shards[4], ("dp", "ctx"), axis=0, tiled=True),
        lax.all_gather(shards[5], ("dp", "ctx"), axis=0, tiled=True),
        lax.all_gather(shards[6], ("dp", "ctx"), axis=0, tiled=True),
        lax.all_gather(shards[7], ("dp", "ctx"), axis=0, tiled=True),
        lax.all_gather(shards[8], ("dp", "ctx"), axis=0, tiled=True),
        lax.all_gather(shards[9], ("dp", "ctx"), axis=0, tiled=True),
        lax.all_gather(shards[10], ("dp", "ctx"), axis=0, tiled=True),
        lax.all_gather(shards[11], ("dp", "ctx"), axis=0, tiled=True),
    )
    (
        gain_first,
        shift_first,
        full_qkv,
        bias_qv,
        full_out,
        bias_out,
        gain_second,
        shift_second,
        full_up,
        bias_up,
        full_down,
        bias_down,
    ) = gathered
    seq_count, tok_rows, model_width = tokens.shape
    head_count = HEADS
    head_size = HEAD_DIM
    flat_rows = seq_count * tok_rows
    query_pos = lax.axis_index("ctx") * tok_rows + jnp.arange(tok_rows, dtype=jnp.int32)
    live_table = live_blocks.astype(jnp.bfloat16)
    seg_low = segment_ids.astype(jnp.bfloat16)
    inputs_wide = tokens.reshape(flat_rows, model_width).astype(jnp.float32)
    normed_wide, norm_pull_one = jax.vjp(
        layer_norm, inputs_wide, gain_first.astype(jnp.float32), shift_first.astype(jnp.float32)
    )
    normed_one = normed_wide.astype(jnp.bfloat16)
    projected = matmul_low(normed_one, full_qkv)
    bias_wide = bias_qv.astype(jnp.float32)
    query_low = (projected[:, :model_width] + bias_wide[:model_width]).astype(jnp.bfloat16)
    key_low = projected[:, model_width : 2 * model_width].astype(jnp.bfloat16)
    value_low = (projected[:, 2 * model_width :] + bias_wide[model_width:]).astype(jnp.bfloat16)
    query_heads = query_low.reshape(seq_count, tok_rows, head_count, head_size)
    key_seq = key_low.reshape(seq_count, tok_rows, model_width)
    value_seq = value_low.reshape(seq_count, tok_rows, model_width)
    initial = (
        jnp.full((seq_count, head_count, tok_rows), NEG_FILL, jnp.float32),
        jnp.zeros((seq_count, head_count, tok_rows), jnp.float32),
        jnp.zeros((seq_count, tok_rows, head_count, head_size), jnp.float32),
    )
    key_part = lax.all_gather(key_seq, "ctx", axis=1, tiled=True)
    value_part = lax.all_gather(value_seq, "ctx", axis=1, tiled=True)
    seg_part = lax.all_gather(seg_low, "ctx", axis=1, tiled=True)

    def step_fn(offset, span_rows, inner_state):
        run_max, run_total, accum_out = inner_state
        key_heads = lax.dynamic_slice_in_dim(key_part, offset, span_rows, 1).reshape(
            seq_count, span_rows, head_count, head_size
        )
        value_heads = lax.dynamic_slice_in_dim(value_part, offset, span_rows, 1).reshape(
            seq_count, span_rows, head_count, head_size
        )
        key_seg = lax.dynamic_slice_in_dim(seg_part, offset, span_rows, 1)
        key_pos = offset + jnp.arange(span_rows, dtype=jnp.int32)
        scores = (
            jnp.einsum(
                "sqhd,skhd->shqk", query_heads, key_heads, preferred_element_type=jnp.float32
            )
            * SCORE_SCALE
        )
        permit = allowed_pairs(live_table, query_pos, key_pos, seg_low, key_seg)[:, None]
        scores = jnp.where(permit, scores, NEG_FILL)
        new_max = jnp.maximum(run_max, jnp.max(scores, axis=-1))
        exp_scores = jnp.where(permit, jnp.exp(scores - new_max[..., None]), 0.0)
        factor = jnp.exp(run_max - new_max)
        run_total = run_total * factor + jnp.sum(exp_scores, axis=-1)
        weighted = jnp.einsum(
            "shqk,skhd->sqhd",
            exp_scores.astype(jnp.bfloat16),
            value_heads,
            preferred_element_type=jnp.float32,
        )
        accum_out = accum_out * jnp.transpose(factor, (0, 2, 1))[..., None] + weighted
        return (new_max, run_total, accum_out)

    run_max, run_total, accum_out = sweep_blocks(key_part.shape[1], step_fn, initial)
    attn_wide = accum_out / jnp.transpose(run_total, (0, 2, 1))[..., None]
    lse_heads = run_max + jnp.log(run_total)
    attn_low = attn_wide.reshape(flat_rows, model_width).astype(jnp.bfloat16)
    hidden = inputs_wide + matmul_low(attn_low, full_out) + bias_out.astype(jnp.float32)
    normed_two_wide, norm_pull_two = jax.vjp(
        layer_norm, hidden, gain_second.astype(jnp.float32), shift_second.astype(jnp.float32)
    )
    normed_two = normed_two_wide.astype(jnp.bfloat16)
    before = matmul_low(normed_two, full_up) + bias_up.astype(jnp.float32)
    activated_wide, gelu_pull = jax.vjp(exact_gelu, before)
    activated = activated_wide.astype(jnp.bfloat16)
    output = (hidden + matmul_low(activated, full_down) + bias_down.astype(jnp.float32)).astype(
        jnp.bfloat16
    )
    back_params = (
        lax.all_gather(shards[0], ("dp", "ctx"), axis=0, tiled=True),
        lax.all_gather(shards[1], ("dp", "ctx"), axis=0, tiled=True),
        lax.all_gather(shards[2], ("dp", "ctx"), axis=0, tiled=True),
        lax.all_gather(shards[3], ("dp", "ctx"), axis=0, tiled=True),
        lax.all_gather(shards[4], ("dp", "ctx"), axis=0, tiled=True),
        lax.all_gather(shards[5], ("dp", "ctx"), axis=0, tiled=True),
        lax.all_gather(shards[6], ("dp", "ctx"), axis=0, tiled=True),
        lax.all_gather(shards[7], ("dp", "ctx"), axis=0, tiled=True),
        lax.all_gather(shards[8], ("dp", "ctx"), axis=0, tiled=True),
        lax.all_gather(shards[9], ("dp", "ctx"), axis=0, tiled=True),
        lax.all_gather(shards[10], ("dp", "ctx"), axis=0, tiled=True),
        lax.all_gather(shards[11], ("dp", "ctx"), axis=0, tiled=True),
    )
    back_qkv = back_params[2]
    back_out = back_params[4]
    back_up = back_params[8]
    back_down = back_params[10]
    grad_low = grad_out.reshape(flat_rows, model_width)
    grad_down = inner_rows(activated, grad_low)
    grad_bias_down = jnp.sum(grad_low.astype(jnp.float32), axis=0)
    grad_act = times_transpose(grad_low, back_down)
    grad_before = gelu_pull(grad_act)[0].astype(jnp.bfloat16)
    grad_up = inner_rows(normed_two, grad_before)
    grad_bias_up = jnp.sum(grad_before.astype(jnp.float32), axis=0)
    grad_normed_two = times_transpose(grad_before, back_up)
    grad_hidden_part, grad_gain_two, grad_shift_two = norm_pull_two(grad_normed_two)
    grad_hidden = grad_low.astype(jnp.float32) + grad_hidden_part
    grad_branch = grad_hidden.astype(jnp.bfloat16)
    grad_out_full = inner_rows(attn_low, grad_branch)
    grad_bias_out = jnp.sum(grad_branch.astype(jnp.float32), axis=0)
    grad_attn = times_transpose(grad_branch, back_out).astype(jnp.bfloat16)
    dout_heads = grad_attn.reshape(seq_count, tok_rows, head_count, head_size)
    delta_rows = jnp.sum(dout_heads.astype(jnp.float32) * attn_wide, axis=-1)
    delta_heads = jnp.transpose(delta_rows, (0, 2, 1))
    key_all, value_all, seg_all = (
        lax.all_gather(key_seq, "ctx", axis=1, tiled=True),
        lax.all_gather(value_seq, "ctx", axis=1, tiled=True),
        lax.all_gather(seg_low, "ctx", axis=1, tiled=True),
    )

    def key_step(offset, span_rows, inner_state):
        grad_query_acc, grad_key_all, grad_value_all = inner_state
        key_heads = lax.dynamic_slice_in_dim(key_all, offset, span_rows, 1).reshape(
            seq_count, span_rows, head_count, head_size
        )
        value_heads = lax.dynamic_slice_in_dim(value_all, offset, span_rows, 1).reshape(
            seq_count, span_rows, head_count, head_size
        )
        key_seg = lax.dynamic_slice_in_dim(seg_all, offset, span_rows, 1)
        key_pos = offset + jnp.arange(span_rows, dtype=jnp.int32)
        grad_query, grad_key, grad_value = pair_grads(
            live_table,
            query_heads,
            dout_heads,
            lse_heads,
            delta_heads,
            query_pos,
            seg_low,
            key_heads,
            value_heads,
            key_pos,
            key_seg,
        )
        grad_key_all = lax.dynamic_update_slice_in_dim(
            grad_key_all, grad_key.reshape(seq_count, span_rows, model_width), offset, 1
        )
        grad_value_all = lax.dynamic_update_slice_in_dim(
            grad_value_all, grad_value.reshape(seq_count, span_rows, model_width), offset, 1
        )
        return (grad_query_acc + grad_query, grad_key_all, grad_value_all)

    length_rows = key_all.shape[1]
    zero_query = jnp.zeros((seq_count, tok_rows, head_count, head_size), jnp.float32)
    zero_keys = jnp.zeros((seq_count, length_rows, model_width), jnp.float32)
    grad_query_heads, grad_key_all, grad_value_all = sweep_blocks(
        length_rows, key_step, (zero_query, zero_keys, zero_keys)
    )
    grad_key_seq, grad_value_seq = (
        lax.psum_scatter(
            grad_key_all.astype(jnp.bfloat16), "ctx", scatter_dimension=1, tiled=True
        ).astype(jnp.float32),
        lax.psum_scatter(
            grad_value_all.astype(jnp.bfloat16), "ctx", scatter_dimension=1, tiled=True
        ).astype(jnp.float32),
    )
    grad_query_low = grad_query_heads.reshape(flat_rows, model_width).astype(jnp.bfloat16)
    grad_key_low = grad_key_seq.reshape(flat_rows, model_width).astype(jnp.bfloat16)
    grad_value_low = grad_value_seq.reshape(flat_rows, model_width).astype(jnp.bfloat16)
    grad_proj_low = jnp.concatenate([grad_query_low, grad_key_low, grad_value_low], axis=1)
    grad_qkv_full = inner_rows(normed_one, grad_proj_low)
    grad_bias_qv = jnp.concatenate(
        [
            jnp.sum(grad_query_low.astype(jnp.float32), axis=0),
            jnp.sum(grad_value_low.astype(jnp.float32), axis=0),
        ]
    )
    grad_normed_one = times_transpose(grad_proj_low, back_qkv)
    grad_input_part, grad_gain_one, grad_shift_one = norm_pull_one(grad_normed_one)
    grad_tokens = (grad_hidden + grad_input_part).reshape(seq_count, tok_rows, model_width)
    summed = (
        lax.psum_scatter(grad_gain_one, ("dp", "ctx"), scatter_dimension=0, tiled=True),
        lax.psum_scatter(grad_shift_one, ("dp", "ctx"), scatter_dimension=0, tiled=True),
        lax.psum_scatter(grad_qkv_full.astype(jnp.bfloat16), ("dp", "ctx"), scatter_dimension=0, tiled=True).astype(jnp.float32),
        lax.psum_scatter(grad_bias_qv, ("dp", "ctx"), scatter_dimension=0, tiled=True),
        lax.psum_scatter(grad_out_full.astype(jnp.bfloat16), ("dp", "ctx"), scatter_dimension=0, tiled=True).astype(jnp.float32),
        lax.psum_scatter(grad_bias_out, ("dp", "ctx"), scatter_dimension=0, tiled=True),
        lax.psum_scatter(grad_gain_two, ("dp", "ctx"), scatter_dimension=0, tiled=True),
        lax.psum_scatter(grad_shift_two, ("dp", "ctx"), scatter_dimension=0, tiled=True),
        lax.psum_scatter(grad_up.astype(jnp.bfloat16), ("dp", "ctx"), scatter_dimension=0, tiled=True).astype(jnp.float32),
        lax.psum_scatter(grad_bias_up, ("dp", "ctx"), scatter_dimension=0, tiled=True),
        lax.psum_scatter(grad_down.astype(jnp.bfloat16), ("dp", "ctx"), scatter_dimension=0, tiled=True).astype(jnp.float32),
        lax.psum_scatter(grad_bias_down, ("dp", "ctx"), scatter_dimension=0, tiled=True),
    )
    return (
        output.reshape(seq_count, tok_rows, model_width),
        grad_tokens,
        summed[0],
        summed[1],
        summed[2],
        summed[3],
        summed[4],
        summed[5],
        summed[6],
        summed[7],
        summed[8],
        summed[9],
        summed[10],
        summed[11],
    )


NZ = 4
GROUP = HEADS // NZ
GW = GROUP * HEAD_DIM
CHUNK = 256


def pick(array, index, axis=0):
    return lax.dynamic_index_in_dim(array, index, axis, keepdims=False)


def shift(array, axis, size, hop):
    return lax.ppermute(array, axis, [(i, (i + hop) % size) for i in range(size)])


def swap(array, axis):
    return shift(array, axis, 2, 1)


def in_order(own, received, index, axis):
    first = jnp.where(index == 0, own, received)
    second = jnp.where(index == 0, received, own)
    return jnp.stack([first, second], axis=axis)


def z_pieces(block):
    up = lax.ppermute(block, "z", [(0, 1), (1, 2), (2, 3)])
    down = lax.ppermute(block, "z", [(1, 0), (2, 1), (3, 2)])
    far = shift(block, "z", NZ, 2)
    last = lax.ppermute(after(far, up, down), "z", [(2, 3), (1, 0)])
    return up, down, far, last


def z_select(block, pieces, z):
    up, down, far, last = pieces
    return jnp.stack(
        [
            lax.select_n(z, block, up, far, last),
            lax.select_n(z, down, block, up, far),
            lax.select_n(z, far, down, block, up),
            lax.select_n(z, last, far, down, block),
        ]
    )


def z_order(pieces, z):
    return jnp.stack([lax.select_n((z - a) % NZ, *pieces) for a in range(NZ)])


def z_exchange(array, z):
    return [pick(array, z)] + [shift(pick(array, (z + j) % NZ), "z", NZ, j) for j in range(1, NZ)]


def xy_gather(line, y, x, event=None):
    a, b = line[:2], line[2:]
    a = in_order(a, swap(a, "x"), x, 0)
    b = in_order(b, swap(b, "y"), y, 0)
    if event is not None:
        a, b = after(a, event), after(b, event)
    a = in_order(a, swap(a, "y"), y, 0)
    b = in_order(b, swap(b, "x"), x, 1)
    return jnp.concatenate([a, b], axis=2)


def xy_scatter(blocks, y, x, wire, event=None):
    def halve(array, axis, name, index):
        sent = swap(pick(array, 1 - index, axis).astype(wire), name)
        return pick(array, index, axis).astype(jnp.float32) + sent.astype(jnp.float32)

    a, b = blocks[:, :, :2], blocks[:, :, 2:]
    a = halve(a, 0, "y", y)
    b = halve(b, 1, "x", x)
    if event is not None:
        a, b = after(a, event), after(b, event)
    a = halve(a, 0, "x", x)
    b = halve(b, 0, "y", y)
    return jnp.concatenate([a, b], axis=0)


def after(value, *events):
    flag = sum(e[(slice(0, 1),) * e.ndim].reshape(()).astype(jnp.float32) * 0.0 for e in events)
    return jnp.where(flag != 0.0, jnp.zeros_like(value), value)


def z_collect(line, z, wire):
    own, *rest = z_exchange_wide(line, z, wire)
    total = own.astype(jnp.float32)
    for piece in rest:
        total = total + piece.astype(jnp.float32)
    return total


def z_exchange_wide(array, z, wire):
    return [pick(array, z)] + [
        shift(pick(array, (z + j) % NZ).astype(wire), "z", NZ, j) for j in range(1, NZ)
    ]


def norm_back(grad, gain, unit, scale):
    c = grad * gain
    return scale * (
        c - jnp.mean(c, axis=-1, keepdims=True) - unit * jnp.mean(c * unit, axis=-1, keepdims=True)
    )


def dot_nt(a, b):
    return lax.dot_general(a, b, (((1,), (1,)), ((), ())), preferred_element_type=jnp.float32)


def dot_tn(a, b):
    return lax.dot_general(a, b, (((0,), (0,)), ((), ())), preferred_element_type=jnp.float32)


def dot_nn(a, b):
    return lax.dot_general(a, b, (((1,), (0,)), ((), ())), preferred_element_type=jnp.float32)


def column_of(row):
    return jnp.transpose(jnp.broadcast_to(row, (8, row.shape[1])))[:, 0:1]


def query_row(may_ref, tile, block, seg_row):
    per = CHUNK // BLOCK
    lane = lax.broadcasted_iota(jnp.int32, (1, CHUNK), 1)
    flag = jnp.full((1, CHUNK), may_ref[tile * per, block], jnp.int32)
    for b in range(1, per):
        flag = jnp.where(lane >= b * BLOCK, may_ref[tile * per + b, block], flag)
    return jnp.where(flag > 0, seg_row, -1.0)


def permit_of(may_ref, tile, chunk, seg_row, key_column):
    per = CHUNK // BLOCK
    return jnp.concatenate(
        [
            key_column[b * BLOCK : (b + 1) * BLOCK]
            == query_row(may_ref, tile, chunk * per + b, seg_row)
            for b in range(per)
        ],
        axis=0,
    )


def whole_spec(shape):
    return pl.BlockSpec(shape, lambda *_: (0,) * len(shape))


def kernel_call(body, place, arrays, in_specs, outs, out_specs, grid, scratch, flops, name, more=()):
    prefetch = (place,) + tuple(more)
    moved = sum(a.size * a.dtype.itemsize for a in arrays)
    return pl.pallas_call(
        body,
        out_shape=tuple(jax.ShapeDtypeStruct(shape, dtype) for shape, dtype in outs),
        grid_spec=pltpu.PrefetchScalarGridSpec(
            num_scalar_prefetch=len(prefetch),
            grid=grid,
            in_specs=in_specs,
            out_specs=out_specs,
            scratch_shapes=scratch,
        ),
        compiler_params=pltpu.CompilerParams(vmem_limit_bytes=40 << 20),
        cost_estimate=pl.CostEstimate(flops=flops, bytes_accessed=moved, transcendentals=0),
        name=name,
    )(*prefetch, *arrays)


def lane_groups(lanes, size):
    lane = lax.broadcasted_iota(jnp.int32, (1, lanes), 1).astype(jnp.float32)
    group = jnp.floor((lane + 0.5) * (1.0 / size))
    return group, lane - group * size


def one_hot_rows(place_row, count):
    rows = lax.broadcasted_iota(jnp.int32, (count, place_row.shape[1]), 0).astype(jnp.float32)
    return (rows == place_row).astype(jnp.float32).astype(jnp.bfloat16)


VEC_ROWS = 16


def unpack_kernel(place_ref, packed_ref, vec_ref):
    devices = packed_ref.shape[0]
    width = vec_ref.shape[1]
    size = width // devices
    c = place_ref[1]
    device = lax.broadcasted_iota(jnp.int32, (devices, 1), 0)
    parity = lax.rem(device, 2)
    pair = lax.div(device, 2).astype(jnp.float32)
    device = device.astype(jnp.float32)
    vec_ref[...] = jnp.zeros(vec_ref.shape, jnp.float32)

    def spread(start, n, lanes, owner, keep):
        group, at = lane_groups(lanes, n)
        tiled = dot_nn(packed_ref[:, start : start + n], one_hot_rows(at, n))
        mine = (owner == group) if keep is None else (owner == group) & keep
        return jnp.sum(jnp.where(mine, tiled, 0.0), axis=0, keepdims=True)

    vec_ref[0:1] = spread(0, size, width, device, None)
    vec_ref[1:2] = spread(size, size, width, device, None)
    qv = spread(2 * size, 2 * size, 2 * width, device, None)
    vec_ref[2:3] = qv[:, :width]
    vec_ref[3:4] = qv[:, width:]
    vec_ref[4:5] = spread(4 * size, size, width, device, None)
    vec_ref[5:6] = spread(5 * size, size, width, device, None)
    vec_ref[6:7] = spread(6 * size, size, width, device, None)
    up = spread(7 * size, 4 * size, 2 * width, pair, parity == c)
    vec_ref[8:9] = up[:, :width]
    vec_ref[9:10] = up[:, width:]
    vec_ref[7:8] = spread(11 * size, size, width, device, None)


def pack_kernel(place_ref, grads_ref, mid_ref, qkv_ref, up_ref, packed_ref):
    devices = packed_ref.shape[0]
    width = grads_ref.shape[1]
    size = width // devices
    z, c = place_ref[0], place_ref[1]
    device = lax.broadcasted_iota(jnp.int32, (devices, 1), 0)
    parity = lax.rem(device, 2)
    pair = lax.div(device, 2).astype(jnp.float32)
    device = device.astype(jnp.float32)
    packed_ref[...] = jnp.zeros(packed_ref.shape, jnp.bfloat16)

    def gather(row, n, owner, keep):
        group, at = lane_groups(row.shape[1], n)
        mine = (owner == group) if keep is None else (owner == group) & keep
        return dot_nt(jnp.where(mine, row, 0.0).astype(jnp.bfloat16), one_hot_rows(at, n))

    def place_group(row):
        wide = jnp.concatenate([row] * NZ, axis=1)
        group, _ = lane_groups(wide.shape[1], GW)
        return jnp.where(group == z.astype(jnp.float32), wide, 0.0)

    qkv = qkv_ref[0:1]
    qv = jnp.concatenate([place_group(qkv[:, :GW]), place_group(qkv[:, 2 * GW :])], axis=1)
    parts = [
        gather(grads_ref[0:1], size, device, None),
        gather(grads_ref[1:2], size, device, None),
        gather(qv, 2 * size, device, None),
        gather(mid_ref[2:3], size, device, None),
        gather(mid_ref[0:1], size, device, None),
        gather(mid_ref[1:2], size, device, None),
        gather(up_ref[0:1], 4 * size, pair, parity == c),
        gather(mid_ref[3:4], size, device, None),
    ]
    packed_ref[:, 0 : 12 * size] = jnp.concatenate(parts, axis=1).astype(jnp.bfloat16)


def norm_rows(x):
    center = x - jnp.mean(x, axis=-1, keepdims=True)
    scale = lax.rsqrt(jnp.mean(center * center, axis=-1, keepdims=True) + 1e-05)
    return center * scale, scale


def project_kernel(
    place_ref, own_ref, up_ref, down_ref, far_ref, last_ref, vec_ref, wz_ref, line_ref, n1_ref, q_ref, kv_ref
):
    a = pl.program_id(0)
    z = place_ref[0]
    away = a - z
    x = jnp.where(away == 0, own_ref[...].astype(jnp.float32), far_ref[...].astype(jnp.float32))
    x = jnp.where(away == 1, down_ref[...].astype(jnp.float32), x)
    x = jnp.where(away == -1, up_ref[...].astype(jnp.float32), x)
    x = jnp.where(jnp.abs(away) == 3, last_ref[...].astype(jnp.float32), x)
    line_ref[...] = x.astype(jnp.bfloat16)
    unit, _ = norm_rows(x)
    n1 = (unit * vec_ref[0:1] + vec_ref[1:2]).astype(jnp.bfloat16)
    n1_ref[...] = n1
    y = dot_nn(n1, wz_ref[...])
    q_bias, v_bias = vec_ref[2:3, 0:GW], vec_ref[3:4, 0:GW]
    for g in range(1, NZ):
        q_bias = jnp.where(z == g, vec_ref[2:3, g * GW : (g + 1) * GW], q_bias)
        v_bias = jnp.where(z == g, vec_ref[3:4, g * GW : (g + 1) * GW], v_bias)
    q = (y[:, :GW] + q_bias).astype(jnp.bfloat16)
    q_ref[...] = q * jnp.asarray(SCORE_SCALE, jnp.bfloat16)
    kv_ref[:, :GW] = y[:, GW : 2 * GW].astype(jnp.bfloat16)
    kv_ref[:, GW:] = (y[:, 2 * GW :] + v_bias).astype(jnp.bfloat16)


def project(place, own, up, down, far, last, vec, wz):
    rows, width = own.shape
    low = jnp.bfloat16
    tall = lambda w: pl.BlockSpec((rows, w), lambda a, *_: (a, 0))
    return kernel_call(
        project_kernel, place, (own, up, down, far, last, vec, wz),
        [whole_spec((rows, width))] * 5 + [whole_spec(vec.shape), whole_spec(wz.shape)],
        [((NZ * rows, width), low), ((NZ * rows, width), low), ((NZ * rows, GW), low), ((NZ * rows, 2 * GW), low)],
        [tall(width), tall(width), tall(GW), tall(2 * GW)],
        (NZ,), [], 8 * NZ * rows * width * 3 * GW, "project",
    )


def branch_kernel(place_ref, a0_ref, a1_ref, a2_ref, a3_ref, wo_ref, own_ref, vec_ref, hidden_ref, n2_ref):
    z = place_ref[0]
    total = own_ref[...].astype(jnp.float32) + vec_ref[4:5]
    branch = None
    for j, ref in enumerate((a0_ref, a1_ref, a2_ref, a3_ref)):
        start = pl.multiple_of(lax.rem(z - j + NZ, NZ) * GW, GW)
        part = dot_nn(ref[...], wo_ref[pl.ds(start, GW), :])
        branch = part if branch is None else branch + part
    hidden = total + branch
    hidden_ref[...] = hidden
    unit, _ = norm_rows(hidden)
    n2_ref[...] = (unit * vec_ref[5:6] + vec_ref[6:7]).astype(jnp.bfloat16)


def branch_call(place, pieces, wo, own, vec):
    rows, width = own.shape
    arrays = (*pieces, wo, own, vec)
    return kernel_call(
        branch_kernel, place, arrays, [whole_spec(a.shape) for a in arrays],
        [((rows, width), jnp.float32), ((rows, width), jnp.bfloat16)],
        [whole_spec((rows, width))] * 2, (1,), [], 8 * rows * width * width, "branch",
    )


FF_STEP = 512


def feed_kernel(
    place_ref, na_ref, nb_ref, ga_ref, gb_ref, up_ref, down_ref, bias_ref,
    act_ref, grad_ref, out_ref, m_ref, sums_ref, bias_out_ref, n_s, g_s, out_s, m_s,
):
    k = pl.program_id(0)
    rows = na_ref.shape[0]

    @pl.when(k == 0)
    def _():
        n_s[:rows], n_s[rows:] = na_ref[...], nb_ref[...]
        g_s[:rows], g_s[rows:] = ga_ref[...], gb_ref[...]
        out_s[...] = jnp.zeros(out_s.shape, jnp.float32)
        m_s[...] = jnp.zeros(m_s.shape, jnp.float32)

    up, down = up_ref[...], down_ref[...]
    v = dot_nn(n_s[...], up) + bias_ref[...]
    cdf = 0.5 * (1.0 + lax.erf(v * 0.7071067811865476))
    slope = cdf + v * (0.3989422804014327 * jnp.exp(-0.5 * v * v))
    act = (v * cdf).astype(jnp.bfloat16)
    act_ref[...] = act
    grad = dot_nt(g_s[...], down) * slope
    grad = grad.astype(jnp.bfloat16)
    grad_ref[...] = grad
    bias_out_ref[...] = jnp.sum(grad.astype(jnp.float32), axis=0, keepdims=True)
    out_s[...] += dot_nn(act, down)
    m_s[...] += dot_nt(grad, up)

    @pl.when(k == pl.num_programs(0) - 1)
    def _():
        out_ref[...] = out_s[:rows]
        m_ref[...] = m_s[:rows]
        sums_ref[0] = m_s[rows:].astype(jnp.bfloat16)
        sums_ref[1] = out_s[rows:].astype(jnp.bfloat16)


def feed(place, na, nb, ga, gb, up, down, bias):
    rows, width = na.shape
    half = up.shape[1]
    low, wide = jnp.bfloat16, jnp.float32
    one = whole_spec((rows, width))
    across = lambda r: pl.BlockSpec((r, FF_STEP), lambda k, *_: (0, k))
    return kernel_call(
        feed_kernel, place, (na, nb, ga, gb, up, down, bias),
        [one] * 4 + [across(width), pl.BlockSpec((FF_STEP, width), lambda k, *_: (k, 0)), across(1)],
        [
            ((2 * rows, half), low), ((2 * rows, half), low), ((rows, width), wide), ((rows, width), wide),
            ((2, rows, width), low), ((1, half), wide),
        ],
        [across(2 * rows), across(2 * rows), one, one, whole_spec((2, rows, width)), across(1)],
        (half // FF_STEP,),
        [
            pltpu.VMEM((2 * rows, width), low), pltpu.VMEM((2 * rows, width), low),
            pltpu.VMEM((2 * rows, width), wide), pltpu.VMEM((2 * rows, width), wide),
        ],
        32 * rows * width * half, "feed",
    )


def middle_kernel(
    place_ref, m_ref, out_ref, sums_ref, hidden_ref, go_ref, vec_ref, wo_ref,
    output_ref, gh_ref, branch_ref, d0_ref, d1_ref, d2_ref, d3_ref, cols_ref,
):
    z = place_ref[0]
    hidden, go = hidden_ref[...], go_ref[...].astype(jnp.float32)
    output_ref[...] = (hidden + out_ref[...] + sums_ref[1].astype(jnp.float32) + vec_ref[7:8]).astype(
        jnp.bfloat16
    )
    m = m_ref[...] + sums_ref[0].astype(jnp.float32)
    unit, scale = norm_rows(hidden)
    grad_hidden = go + norm_back(m, vec_ref[5:6], unit, scale)
    gh_ref[...] = grad_hidden
    branch = grad_hidden.astype(jnp.bfloat16)
    branch_ref[...] = branch
    for j, ref in enumerate((d0_ref, d1_ref, d2_ref, d3_ref)):
        start = pl.multiple_of(lax.rem(z + j, NZ) * GW, GW)
        ref[...] = dot_nt(branch, wo_ref[pl.ds(start, GW), :]).astype(jnp.bfloat16)
    cols_ref[...] = jnp.zeros(cols_ref.shape, jnp.float32)
    cols_ref[0:1] = jnp.sum(m * unit, axis=0, keepdims=True)
    cols_ref[1:2] = jnp.sum(m, axis=0, keepdims=True)
    cols_ref[2:3] = jnp.sum(branch.astype(jnp.float32), axis=0, keepdims=True)
    cols_ref[3:4] = jnp.sum(go, axis=0, keepdims=True)


def middle(place, m, out, sums, hidden, go, vec, wo):
    rows, width = m.shape
    arrays = (m, out, sums, hidden, go, vec, wo)
    low, wide = jnp.bfloat16, jnp.float32
    outs = [((rows, width), low), ((rows, width), wide), ((rows, width), low)]
    outs += [((rows, GW), low)] * NZ + [((8, width), wide)]
    return kernel_call(
        middle_kernel, place, arrays, [whole_spec(a.shape) for a in arrays], outs,
        [whole_spec(shape) for shape, _ in outs], (1,), [], 8 * rows * width * width, "middle",
    )


def inward_kernel(
    place_ref, dq_ref, mine_ref, theirs_ref, line_ref, wz_ref, dqkv_ref, keep_ref, sent_ref, cols_ref, sums_ref
):
    j = pl.program_id(0)
    dq = dq_ref[...]
    dkv = (mine_ref[...].astype(jnp.float32) + theirs_ref[...].astype(jnp.float32)).astype(jnp.bfloat16)
    dqkv = jnp.concatenate([dq, dkv], axis=1)
    dqkv_ref[...] = dqkv
    m1 = dot_nt(dqkv, wz_ref[...])
    sent_ref[0] = m1.astype(jnp.bfloat16)
    unit, _ = norm_rows(line_ref[...].astype(jnp.float32))

    @pl.when(j == 0)
    def _():
        cols_ref[...] = jnp.zeros(cols_ref.shape, jnp.float32)
        sums_ref[...] = jnp.zeros(sums_ref.shape, jnp.float32)

    cols_ref[0:1] += jnp.sum(m1 * unit, axis=0, keepdims=True)
    cols_ref[1:2] += jnp.sum(m1, axis=0, keepdims=True)
    sums_ref[0:1] += jnp.sum(dqkv.astype(jnp.float32), axis=0, keepdims=True)

    @pl.when(j == pl.num_programs(0) - 1)
    def _():
        keep_ref[...] = m1


def inward(place, dq, mine, theirs, line, wz):
    total, width = line.shape
    rows = total // NZ
    low, wide = jnp.bfloat16, jnp.float32
    turned = lambda w: pl.BlockSpec((rows, w), lambda j, p: (lax.rem(p[0] + 1 + j, NZ), 0))
    return kernel_call(
        inward_kernel, place, (dq, mine, theirs, line, wz),
        [turned(GW), turned(2 * GW), turned(2 * GW), turned(width), whole_spec(wz.shape)],
        [((total, 3 * GW), low), ((rows, width), wide), ((NZ, rows, width), low), ((8, width), wide), ((8, 3 * GW), wide)],
        [
            turned(3 * GW), whole_spec((rows, width)),
            pl.BlockSpec((1, rows, width), lambda j, p: (j, 0, 0)),
            whole_spec((8, width)), whole_spec((8, 3 * GW)),
        ],
        (NZ,), [], 8 * total * width * 3 * GW, "inward",
    )


def finish_kernel(place_ref, m_ref, r1_ref, r2_ref, r3_ref, own_ref, gh_ref, vec_ref, out_ref):
    m = m_ref[...]
    for ref in (r1_ref, r2_ref, r3_ref):
        m = m + ref[...].astype(jnp.float32)
    unit, scale = norm_rows(own_ref[...].astype(jnp.float32))
    out_ref[...] = gh_ref[...] + norm_back(m, vec_ref[0:1], unit, scale)


def finish(place, m, pieces, own, grad_hidden, vec):
    rows, width = own.shape
    arrays = (m, *pieces, own, grad_hidden, vec)
    return kernel_call(
        finish_kernel, place, arrays, [whole_spec(a.shape) for a in arrays],
        [((rows, width), jnp.float32)], [whole_spec((rows, width))], (1,), [], 100 * rows * width, "finish",
    )[0]


def owners_kernel(
    place_ref, a0_ref, a1_ref, a2_ref, a3_ref, branch_ref, n1_ref, dqkv_ref, cols_ref, mid_ref, sums_ref, up_ref,
    mine_ref, theirs_ref, wo_s, wz_s, vec_s,
):
    z, c = place_ref[0], place_ref[1]
    width = branch_ref.shape[1]
    for j, ref in enumerate((a0_ref, a1_ref, a2_ref, a3_ref)):
        start = pl.multiple_of(lax.rem(z - j + NZ, NZ) * GW, GW)
        wo_s[pl.ds(start, GW), :] = dot_tn(ref[...], branch_ref[...]).astype(jnp.bfloat16)
    wz_s[...] = dot_tn(n1_ref[...], dqkv_ref[...]).astype(jnp.bfloat16)
    pack_kernel(place_ref, cols_ref, mid_ref, sums_ref, up_ref, vec_s)
    chips, tall, span = mine_ref.shape
    devices = 2 * chips
    rows = width // devices
    pad = jnp.zeros((tall - rows, span), jnp.bfloat16)
    first_row = lax.broadcasted_iota(jnp.int32, (tall - rows, span), 0) == 0
    for pair in range(chips):
        blocks = []
        for core in range(2):
            at = slice((2 * pair + core) * rows, (2 * pair + core + 1) * rows)
            vec = vec_s[2 * pair + core : 2 * pair + core + 1]
            vec = jnp.where(first_row, jnp.broadcast_to(vec.astype(jnp.float32), pad.shape), 0.0)
            top = jnp.concatenate([wo_s[at], wz_s[at]], axis=1)
            blocks.append((top, vec.astype(jnp.bfloat16)))
        mine_ref[pair, :rows] = jnp.where(c == 0, blocks[0][0], blocks[1][0])
        mine_ref[pair, rows:] = jnp.where(c == 0, blocks[0][1], blocks[1][1])
        theirs_ref[pair, :rows] = jnp.where(c == 0, blocks[1][0], blocks[0][0])
        theirs_ref[pair, rows:] = jnp.where(c == 0, blocks[1][1], blocks[0][1])


def owners(place, pieces, branch, n1, dqkv, cols, mid, sums, up, devices, tall):
    width, span = n1.shape[1], n1.shape[1] + dqkv.shape[1]
    low = jnp.bfloat16
    arrays = (*pieces, branch, n1, dqkv, cols, mid, sums, up)
    shape = (devices // 2, tall, span)
    return kernel_call(
        owners_kernel, place, arrays, [whole_spec(a.shape) for a in arrays], [(shape, low), (shape, low)],
        [whole_spec(shape)] * 2, (1,),
        [pltpu.VMEM((width, width), low), pltpu.VMEM((width, dqkv.shape[1]), low), pltpu.VMEM((devices, span), low)],
        1 << 20, "owners",
    )


def attend_kernel(
    act_ref, may_ref, place_ref, q_ref, mine_ref, theirs_ref, qseg_ref, kseg_ref, o_ref, low_ref, lse_ref,
    k_s, vt_s, col_s, m_s, l_s, acc_s,
):
    i = pl.program_id(0)
    chunks = kseg_ref.shape[0]

    @pl.when(i == 0)
    def _():
        for line, ref in enumerate((mine_ref, theirs_ref)):
            core = place_ref[1] if line == 0 else 1 - place_ref[1]
            for a in range(chunks // 2):
                rows = slice(a * CHUNK, (a + 1) * CHUNK)
                at = pl.ds(pl.multiple_of((2 * a + core) * CHUNK, CHUNK), CHUNK)
                for h in range(GROUP):
                    k_s[h, at] = ref[rows, HEAD_DIM * h : HEAD_DIM * (h + 1)]
                    vt_s[h, :, at] = jnp.transpose(ref[rows, GW + HEAD_DIM * h : GW + HEAD_DIM * (h + 1)])
        for j in range(chunks):
            col_s[j * CHUNK : (j + 1) * CHUNK] = column_of(kseg_ref[j : j + 1])

    m_s[...] = jnp.full(m_s.shape, NEG_FILL, jnp.float32)
    l_s[...] = jnp.zeros(l_s.shape, jnp.float32)
    acc_s[...] = jnp.zeros(acc_s.shape, jnp.float32)
    q_heads = [q_ref[:, HEAD_DIM * h : HEAD_DIM * (h + 1)] for h in range(GROUP)]
    q_seg = qseg_ref[pl.ds(i, 1)]

    def one_chunk(j, carry):
        @pl.when(act_ref[i, j] != 0)
        def _():
            at = pl.ds(pl.multiple_of(j * CHUNK, CHUNK), CHUNK)
            permit = permit_of(may_ref, i, j, q_seg, col_s[at])
            for h in range(GROUP):
                s = jnp.where(permit, dot_nt(k_s[h, at], q_heads[h]), NEG_FILL)
                old = m_s[h]
                new = jnp.maximum(old, jnp.max(s, axis=0, keepdims=True))
                p = jnp.exp(s - new)
                fade = jnp.exp(old - new)
                l_s[h] = l_s[h] * fade + jnp.sum(p, axis=0, keepdims=True)
                acc_s[h] = acc_s[h] * fade + dot_nn(vt_s[h, :, at], p.astype(jnp.bfloat16))
                m_s[h] = new

        return carry

    lax.fori_loop(0, chunks, one_chunk, 0)
    out = jnp.concatenate([jnp.transpose(acc_s[h] / l_s[h]) for h in range(GROUP)], axis=1)
    o_ref[...] = out
    low_ref[...] = out.astype(jnp.bfloat16)
    logs = [m_s[h] + jnp.log(l_s[h]) for h in range(GROUP)]
    lse_ref[...] = jnp.concatenate(logs + [logs[0]] * (8 - GROUP), axis=0)


def attend(active, may, place, q, mine, theirs, q_seg, k_seg):
    rows, keys = q.shape[0], 2 * mine.shape[0]
    tall = pl.BlockSpec((CHUNK, GW), lambda i, *_: (i, 0))
    return pl.pallas_call(
        attend_kernel,
        out_shape=(
            jax.ShapeDtypeStruct((rows, GW), jnp.float32),
            jax.ShapeDtypeStruct((rows, GW), jnp.bfloat16),
            jax.ShapeDtypeStruct((8, rows), jnp.float32),
        ),
        grid_spec=pltpu.PrefetchScalarGridSpec(
            num_scalar_prefetch=3,
            grid=(rows // CHUNK,),
            in_specs=[
                tall, whole_spec(mine.shape), whole_spec(theirs.shape), whole_spec(q_seg.shape),
                whole_spec(k_seg.shape),
            ],
            out_specs=[tall, tall, pl.BlockSpec((8, CHUNK), lambda i, *_: (0, i))],
            scratch_shapes=[
                pltpu.VMEM((GROUP, keys, HEAD_DIM), jnp.bfloat16),
                pltpu.VMEM((GROUP, HEAD_DIM, keys), jnp.bfloat16),
                pltpu.VMEM((keys, 1), jnp.float32),
                pltpu.VMEM((GROUP, 1, CHUNK), jnp.float32),
                pltpu.VMEM((GROUP, 1, CHUNK), jnp.float32),
                pltpu.VMEM((GROUP, HEAD_DIM, CHUNK), jnp.float32),
            ],
        ),
        compiler_params=pltpu.CompilerParams(vmem_limit_bytes=32 << 20),
        cost_estimate=pl.CostEstimate(
            flops=48 * rows * keys * GW, bytes_accessed=16 * keys * GW, transcendentals=4 * rows * keys
        ),
        name="attend",
    )(active, may, place, q, mine, theirs, q_seg, k_seg)


def attend_back_kernel(
    act_ref, may_ref, place_ref, q_ref, d0_ref, d1_ref, d2_ref, d3_ref, o_ref, mine_ref, theirs_ref, lse_ref,
    qseg_ref, kseg_ref, dq_ref, dmine_ref, dtheirs_ref, q_s, do_s, dqt_s, delta_s, dk_s, dv_s,
):
    step = pl.program_id(0)
    rows = q_ref.shape[0]
    lines = rows // CHUNK
    z, c = place_ref[0], place_ref[1]
    j = jnp.where(step < lines, 2 * step + 1 - c, 2 * (step - lines) + c)

    @pl.when(step == 0)
    def _():
        for r, ref in enumerate((d0_ref, d1_ref, d2_ref, d3_ref)):
            at = pl.ds(pl.multiple_of(lax.rem(z - r + NZ, NZ) * CHUNK, CHUNK), CHUNK)
            for h in range(GROUP):
                do_s[h, at] = ref[:, HEAD_DIM * h : HEAD_DIM * (h + 1)]
        ones = jnp.ones((8, HEAD_DIM), jnp.float32)
        for h in range(GROUP):
            lanes = slice(HEAD_DIM * h, HEAD_DIM * (h + 1))
            q_s[h] = q_ref[:, lanes]
            both = do_s[h].astype(jnp.float32) * o_ref[:, lanes]
            delta_s[h] = lax.dot_general(
                ones, both, (((1,), (1,)), ((), ())), precision=lax.Precision.HIGHEST,
                preferred_element_type=jnp.float32,
            )[0:1]
        dqt_s[...] = jnp.zeros(dqt_s.shape, jnp.float32)

    dk_s[...] = jnp.zeros(dk_s.shape, jnp.float32)
    dv_s[...] = jnp.zeros(dv_s.shape, jnp.float32)
    kv = jnp.where(step < lines, theirs_ref[...], mine_ref[...])
    k_heads = [kv[:, HEAD_DIM * h : HEAD_DIM * (h + 1)] for h in range(GROUP)]
    v_heads = [kv[:, GW + HEAD_DIM * h : GW + HEAD_DIM * (h + 1)] for h in range(GROUP)]
    k_turned = [jnp.transpose(k) for k in k_heads]
    k_column = column_of(kseg_ref[pl.ds(j, 1)])

    def one_tile(i, carry):
        @pl.when(act_ref[i, j] != 0)
        def _():
            at = pl.ds(pl.multiple_of(i * CHUNK, CHUNK), CHUNK)
            permit = permit_of(may_ref, i, j, qseg_ref[pl.ds(i, 1)], k_column)
            for h in range(GROUP):
                q, do = q_s[h, at], do_s[h, at]
                s = dot_nt(k_heads[h], q)
                p = jnp.where(permit, jnp.exp(s - lse_ref[h : h + 1, at]), 0.0)
                dp = dot_nt(v_heads[h], do)
                ds = (p * (dp - delta_s[h, :, at])).astype(jnp.bfloat16)
                dv_s[h] += dot_nn(p.astype(jnp.bfloat16), do)
                dk_s[h] += dot_nn(ds, q)
                dqt_s[h, :, at] += dot_nn(k_turned[h], ds)

        return carry

    lax.fori_loop(0, lines, one_tile, 0)
    dkv = jnp.concatenate(
        [dk_s[h] for h in range(GROUP)] + [dv_s[h] for h in range(GROUP)], axis=1
    ).astype(jnp.bfloat16)

    @pl.when(step < lines)
    def _():
        dtheirs_ref[...] = dkv

    @pl.when(step >= lines)
    def _():
        dmine_ref[...] = dkv

    @pl.when(step == pl.num_programs(0) - 1)
    def _():
        dq_ref[...] = jnp.concatenate(
            [jnp.transpose(dqt_s[h] * SCORE_SCALE) for h in range(GROUP)], axis=1
        ).astype(jnp.bfloat16)


def attend_back(active, may, place, q, pieces, out, mine, theirs, lse, q_seg, k_seg):
    rows, keys = q.shape[0], 2 * mine.shape[0]
    lines = rows // CHUNK
    late = pl.BlockSpec((CHUNK, 2 * GW), lambda s, *_: (jnp.maximum(s - lines, 0), 0))
    early = pl.BlockSpec((CHUNK, 2 * GW), lambda s, *_: (jnp.minimum(s, lines - 1), 0))
    return pl.pallas_call(
        attend_back_kernel,
        out_shape=(
            jax.ShapeDtypeStruct((rows, GW), jnp.bfloat16),
            jax.ShapeDtypeStruct((rows, 2 * GW), jnp.bfloat16),
            jax.ShapeDtypeStruct((rows, 2 * GW), jnp.bfloat16),
        ),
        grid_spec=pltpu.PrefetchScalarGridSpec(
            num_scalar_prefetch=3,
            grid=(keys // CHUNK,),
            in_specs=[
                whole_spec((rows, GW)), *[whole_spec(p.shape) for p in pieces], whole_spec((rows, GW)),
                late, early, whole_spec((8, rows)), whole_spec(q_seg.shape), whole_spec(k_seg.shape),
            ],
            out_specs=[whole_spec((rows, GW)), late, early],
            scratch_shapes=[
                pltpu.VMEM((GROUP, rows, HEAD_DIM), jnp.bfloat16),
                pltpu.VMEM((GROUP, rows, HEAD_DIM), jnp.bfloat16),
                pltpu.VMEM((GROUP, HEAD_DIM, rows), jnp.float32),
                pltpu.VMEM((GROUP, 1, rows), jnp.float32),
                pltpu.VMEM((GROUP, CHUNK, HEAD_DIM), jnp.float32),
                pltpu.VMEM((GROUP, CHUNK, HEAD_DIM), jnp.float32),
            ],
        ),
        compiler_params=pltpu.CompilerParams(vmem_limit_bytes=32 << 20),
        cost_estimate=pl.CostEstimate(
            flops=56 * rows * keys * GW, bytes_accessed=32 * keys * GW, transcendentals=4 * rows * keys
        ),
        name="attend_back",
    )(active, may, place, q, *pieces, out, mine, theirs, lse, q_seg, k_seg)


def fast_local(
    tokens, segment_ids, live_blocks, norm1_gain, norm1_bias, qkv_weight, qv_bias, out_weight, out_bias,
    norm2_gain, norm2_bias, up_weight, up_bias, down_weight, down_bias, grad_out,
):
    y, x, z, c = (lax.axis_index(name) for name in ("y", "x", "z", "c"))
    place = jnp.stack([z, c]).astype(jnp.int32)
    wide, low = jnp.float32, jnp.bfloat16
    _, rows, width = tokens.shape
    own_rows, units = qkv_weight.shape[0], down_weight.shape[0]
    ff = up_weight.shape[1]
    half, pairs = ff // 2, ff // (2 * units)
    devices = width // own_rows
    seq_rows = rows * NZ
    keys = 2 * seq_rows
    blocks = keys // BLOCK
    per = CHUNK // BLOCK

    own = tokens[0]
    line_pieces = z_pieces(own)

    vectors = (norm1_gain, norm1_bias, qv_bias, out_bias, norm2_gain, norm2_bias, up_bias, down_bias)
    sizes = [v.shape[0] for v in vectors]
    cuts = [sum(sizes[:i]) for i in range(len(sizes) + 1)]
    extra = jnp.concatenate(vectors + (segment_ids[0].astype(low),))[None]
    span = width + 3 * GW
    tall = own_rows + 8
    extra = jnp.pad(extra, ((0, 7), (0, span - extra.shape[1])))
    wz = qkv_weight.reshape(own_rows, 3, NZ, GW).transpose(2, 0, 1, 3).reshape(NZ, own_rows, 3 * GW)
    group1 = jnp.concatenate(
        [jnp.broadcast_to(out_weight[None], (NZ, own_rows, width)), wz], axis=2
    )
    group1 = jnp.concatenate([group1, jnp.broadcast_to(extra[None], (NZ, 8, span))], axis=1)
    group1 = group1
    group1 = z_order(z_exchange(group1, z), z)
    own_seg = group1[:, own_rows, cuts[-1] : cuts[-1] + rows].astype(wide)
    seg = in_order(own_seg, swap(own_seg, "c"), c, 1).reshape(keys // CHUNK, CHUNK)
    group1 = xy_gather(group1, y, x)
    group1 = in_order(group1, swap(group1, "c"), c, 3)
    wo = group1[..., :own_rows, :width].reshape(width, width)
    wz = group1[..., :own_rows, width:].reshape(width, 3 * GW)
    packed = group1[..., own_rows, : cuts[-1]].reshape(devices, cuts[-1])
    vec = kernel_call(
        unpack_kernel, place, (packed,), [whole_spec(packed.shape)], [((VEC_ROWS, width), wide)],
        [whole_spec((VEC_ROWS, width))], (1,), [], 1 << 20, "unpack",
    )[0]

    up_sets = up_weight.reshape(own_rows, pairs, 2, units).transpose(2, 0, 1, 3)
    up_sets = up_sets.reshape(2, own_rows, half)
    up_chip = in_order(pick(up_sets, c), swap(pick(up_sets, 1 - c), "c"), c, 0)
    up_chip = up_chip.reshape(2 * own_rows, half)
    up_pieces = z_pieces(up_chip)
    down_chip = after(down_weight, line_pieces[2])
    up_line = z_select(up_chip, up_pieces, z)
    down_line = z_select(down_chip, z_pieces(down_chip), z)
    own_blocks = seq_rows // BLOCK
    ids = jnp.arange(blocks, dtype=jnp.int32)
    own_ids = pick(ids.reshape(NZ, 2, rows // BLOCK), c, 1).reshape(own_blocks)
    own_live = pick(live_blocks[0].reshape(NZ, 2, rows // BLOCK, blocks), c, 1)
    own_live = own_live.reshape(own_blocks, blocks)
    seg_blocks = seg.reshape(blocks, BLOCK)
    own_seg_blocks = own_seg.reshape(own_blocks, BLOCK)
    may = (own_live > 0) | (own_ids[:, None] == ids[None, :])
    meet = (
        may
        & (own_seg_blocks[:, :1] <= seg_blocks[:, -1][None])
        & (seg_blocks[:, 0][None] <= own_seg_blocks[:, -1:])
    )
    active = jnp.any(meet.reshape(own_blocks // per, per, blocks // per, per), axis=(1, 3))
    active, may = active.astype(jnp.int32), may.astype(jnp.int32)

    line, n1, q, kv = project(place, own, *line_pieces, vec, wz)
    kv_theirs = swap(kv, "c")
    up_half = xy_gather(up_line, y, x, q).reshape(width, half)
    att_wide, att_low, lse = attend(active, may, place, q, kv, kv_theirs, own_seg, seg)
    att = z_exchange(att_low.reshape(NZ, rows, GW), z)
    down_half = xy_gather(after(down_line, q), y, x, att_low).reshape(half, width)

    hidden, n2 = branch_call(place, att, wo, own, vec)
    go = grad_out[0]
    n2_theirs, go_theirs = swap(n2, "c"), swap(go, "c")
    up_bias_half = vec[8:10].reshape(1, half)
    activated, grad_before, out_part, m_part, sums, up_bias_part = feed(
        place, n2, n2_theirs, go, go_theirs, up_half, down_half, up_bias_half
    )
    sums = swap(sums, "c")
    output, grad_hidden, grad_branch, *grad_att, mid = middle(
        place, m_part, out_part, sums, hidden, go, vec, wo
    )
    dout = [grad_att[0]] + [shift(grad_att[j], "z", NZ, j) for j in range(1, NZ)]
    n2_both = jnp.concatenate([n2, n2_theirs], axis=0)
    go_both = jnp.concatenate([go, go_theirs], axis=0)
    grad_down = dot_tn(activated, go_both).astype(low)
    grad_up = dot_tn(n2_both, grad_before).astype(low)
    down_line = xy_scatter(grad_down.reshape(2, 2, NZ, units, width), y, x, low, grad_branch)
    up_line = xy_scatter(grad_up.reshape(2, 2, NZ, 2 * own_rows, half), y, x, low, dout[3])

    dq, dkv_mine, dkv_theirs = attend_back(
        active, may, place, q, dout, att_wide, kv, kv_theirs, lse, own_seg, seg
    )
    dqkv, m1_own, m1_sent, cols, dqkv_sum = inward(place, dq, dkv_mine, swap(dkv_theirs, "c"), line, wz)
    m1_pieces = [shift(m1_sent[j - 1], "z", NZ, j) for j in range(1, NZ)]

    grad_down = z_collect(down_line, z, low)
    grad_up = z_collect(up_line, z, low).reshape(2, own_rows, half)
    up_other = swap(pick(grad_up, 1 - c).astype(low), "c").astype(wide)
    up_shape = (own_rows, pairs, units)
    grad_up = in_order(pick(grad_up, c).reshape(up_shape), up_other.reshape(up_shape), c, 2)
    grad_up = grad_up.reshape(own_rows, ff)

    mine, theirs = owners(
        place, att, grad_branch, n1, dqkv, cols, mid, dqkv_sum, up_bias_part, devices, tall
    )
    group1 = mine.astype(wide) + swap(theirs, "c").astype(wide)
    group1 = group1.reshape(2, 2, NZ, tall, span)
    group1 = xy_scatter(group1, y, x, low)
    pieces = z_exchange(group1.astype(low), z)
    grad_wz = z_order([p[:own_rows, width:] for p in pieces], z)
    grad_qkv = grad_wz.reshape(NZ, own_rows, 3, GW).transpose(1, 2, 0, 3).reshape(own_rows, 3 * width)
    total = sum([p.astype(wide) for p in pieces[1:]], pick(group1, z))
    grad_wo = total[:own_rows, :width]
    v = [total[own_rows, cuts[i] : cuts[i + 1]] for i in range(len(sizes))]
    grad_tokens = finish(place, m1_own, m1_pieces, own, grad_hidden, vec)
    return (
        output[None], grad_tokens[None], v[0], v[1], grad_qkv.astype(wide), v[2], grad_wo, v[3],
        v[4], v[5], grad_up, v[6], grad_down, v[7],
    )


def build(body, mesh, dp, ctx):
    both = dp + ctx
    rows, vector, matrix = P(dp, ctx, None), P(both), P(both, None)
    return jax.shard_map(
        body,
        mesh=mesh,
        in_specs=(
            rows, P(dp, ctx), P(dp, None, None), vector, vector, matrix, vector, matrix, vector,
            vector, vector, matrix, vector, matrix, vector, rows,
        ),
        out_specs=(
            rows, rows, vector, vector, matrix, vector, matrix, vector, vector, vector, matrix,
            vector, matrix, vector,
        ),
        check_vma=False,
    )


def solution(mesh):
    if dict(mesh.shape) == {"dp": 4, "ctx": 2 * NZ}:
        grid = Mesh(mesh.devices.reshape(2, 2, NZ, 2), ("y", "x", "z", "c"))
        return build(fast_local, grid, ("y", "x"), ("z", "c"))
    return build(local, mesh, ("dp",), ("ctx",))
```

```python
import functools
import math

import jax
import jax.numpy as jnp
from jax import lax
from jax.experimental import pallas as pl
from jax.experimental.pallas import tpu as pltpu
from jax.sharding import Mesh, PartitionSpec as P

HEADS = 12
HEAD_DIM = 64
BLOCK = 128


NEG_FILL = -1e30
SCORE_SCALE = 0.125


def layer_norm(value_in, norm_gain, norm_shift):
    center = value_in - jnp.mean(value_in, axis=-1, keepdims=True)
    spread = jnp.mean(center * center, axis=-1, keepdims=True)
    return center * lax.rsqrt(spread + 1e-05) * norm_gain + norm_shift


def exact_gelu(value_in):
    return jax.nn.gelu(value_in, approximate=False)


def matmul_low(left_side, right_side):
    return jnp.dot(left_side, right_side, preferred_element_type=jnp.float32)


def inner_rows(left_side, right_side):
    return lax.dot_general(
        left_side, right_side, (((0,), (0,)), ((), ())), preferred_element_type=jnp.float32
    )


def times_transpose(left_side, right_side):
    return lax.dot_general(
        left_side, right_side, (((1,), (1,)), ((), ())), preferred_element_type=jnp.float32
    )


def sweep_blocks(count_rows, step_fn, carry_state):
    span_rows = math.gcd(count_rows, 512)
    return lax.fori_loop(
        0,
        count_rows // span_rows,
        lambda loop_index, loop_state: step_fn(loop_index * span_rows, span_rows, loop_state),
        carry_state,
    )


def allowed_pairs(live_table, query_pos, key_pos, query_seg, key_seg):
    block_slots = jnp.arange(live_table.shape[-1], dtype=jnp.int32)
    query_block = query_pos // BLOCK
    key_block = key_pos // BLOCK
    pick_query = (query_block[:, None] == block_slots[None, :]).astype(jnp.bfloat16)
    pick_key = (key_block[:, None] == block_slots[None, :]).astype(jnp.bfloat16)
    live_rows = jnp.einsum(
        "qa,sab->sqb", pick_query, live_table, preferred_element_type=jnp.float32
    )
    live_grid = jnp.einsum(
        "sqb,kb->sqk", live_rows.astype(jnp.bfloat16), pick_key, preferred_element_type=jnp.float32
    )
    same_block = query_block[:, None] == key_block[None, :]
    same_doc = query_seg[:, :, None] == key_seg[:, None, :]
    return same_doc & ((live_grid > 0.5) | same_block[None])


def pair_grads(
    live_table,
    query_heads,
    dout_heads,
    lse_heads,
    delta_heads,
    query_pos,
    query_seg,
    key_heads,
    value_heads,
    key_pos,
    key_seg,
):
    scores = (
        jnp.einsum("sqhd,skhd->shqk", query_heads, key_heads, preferred_element_type=jnp.float32)
        * SCORE_SCALE
    )
    permit = allowed_pairs(live_table, query_pos, key_pos, query_seg, key_seg)[:, None]
    attn_probs = jnp.where(permit, jnp.exp(scores - lse_heads[..., None]), 0.0)
    grad_prob = jnp.einsum(
        "sqhd,skhd->shqk", dout_heads, value_heads, preferred_element_type=jnp.float32
    )
    grad_score = (attn_probs * (grad_prob - delta_heads[..., None])).astype(jnp.bfloat16)
    grad_query = (
        jnp.einsum("shqk,skhd->sqhd", grad_score, key_heads, preferred_element_type=jnp.float32)
        * SCORE_SCALE
    )
    grad_key = (
        jnp.einsum("shqk,sqhd->skhd", grad_score, query_heads, preferred_element_type=jnp.float32)
        * SCORE_SCALE
    )
    grad_value = jnp.einsum(
        "shqk,sqhd->skhd",
        attn_probs.astype(jnp.bfloat16),
        dout_heads,
        preferred_element_type=jnp.float32,
    )
    return (grad_query, grad_key, grad_value)


def local(
    tokens,
    segment_ids,
    live_blocks,
    norm1_gain,
    norm1_bias,
    qkv_weight,
    qv_bias,
    out_weight,
    out_bias,
    norm2_gain,
    norm2_bias,
    up_weight,
    up_bias,
    down_weight,
    down_bias,
    grad_out,
):
    shards = (
        norm1_gain,
        norm1_bias,
        qkv_weight,
        qv_bias,
        out_weight,
        out_bias,
        norm2_gain,
        norm2_bias,
        up_weight,
        up_bias,
        down_weight,
        down_bias,
    )
    gathered = (
        lax.all_gather(shards[0], ("dp", "ctx"), axis=0, tiled=True),
        lax.all_gather(shards[1], ("dp", "ctx"), axis=0, tiled=True),
        lax.all_gather(shards[2], ("dp", "ctx"), axis=0, tiled=True),
        lax.all_gather(shards[3], ("dp", "ctx"), axis=0, tiled=True),
        lax.all_gather(shards[4], ("dp", "ctx"), axis=0, tiled=True),
        lax.all_gather(shards[5], ("dp", "ctx"), axis=0, tiled=True),
        lax.all_gather(shards[6], ("dp", "ctx"), axis=0, tiled=True),
        lax.all_gather(shards[7], ("dp", "ctx"), axis=0, tiled=True),
        lax.all_gather(shards[8], ("dp", "ctx"), axis=0, tiled=True),
        lax.all_gather(shards[9], ("dp", "ctx"), axis=0, tiled=True),
        lax.all_gather(shards[10], ("dp", "ctx"), axis=0, tiled=True),
        lax.all_gather(shards[11], ("dp", "ctx"), axis=0, tiled=True),
    )
    (
        gain_first,
        shift_first,
        full_qkv,
        bias_qv,
        full_out,
        bias_out,
        gain_second,
        shift_second,
        full_up,
        bias_up,
        full_down,
        bias_down,
    ) = gathered
    seq_count, tok_rows, model_width = tokens.shape
    head_count = HEADS
    head_size = HEAD_DIM
    flat_rows = seq_count * tok_rows
    query_pos = lax.axis_index("ctx") * tok_rows + jnp.arange(tok_rows, dtype=jnp.int32)
    live_table = live_blocks.astype(jnp.bfloat16)
    seg_low = segment_ids.astype(jnp.bfloat16)
    inputs_wide = tokens.reshape(flat_rows, model_width).astype(jnp.float32)
    normed_wide, norm_pull_one = jax.vjp(
        layer_norm, inputs_wide, gain_first.astype(jnp.float32), shift_first.astype(jnp.float32)
    )
    normed_one = normed_wide.astype(jnp.bfloat16)
    projected = matmul_low(normed_one, full_qkv)
    bias_wide = bias_qv.astype(jnp.float32)
    query_low = (projected[:, :model_width] + bias_wide[:model_width]).astype(jnp.bfloat16)
    key_low = projected[:, model_width : 2 * model_width].astype(jnp.bfloat16)
    value_low = (projected[:, 2 * model_width :] + bias_wide[model_width:]).astype(jnp.bfloat16)
    query_heads = query_low.reshape(seq_count, tok_rows, head_count, head_size)
    key_seq = key_low.reshape(seq_count, tok_rows, model_width)
    value_seq = value_low.reshape(seq_count, tok_rows, model_width)
    initial = (
        jnp.full((seq_count, head_count, tok_rows), NEG_FILL, jnp.float32),
        jnp.zeros((seq_count, head_count, tok_rows), jnp.float32),
        jnp.zeros((seq_count, tok_rows, head_count, head_size), jnp.float32),
    )
    key_part = lax.all_gather(key_seq, "ctx", axis=1, tiled=True)
    value_part = lax.all_gather(value_seq, "ctx", axis=1, tiled=True)
    seg_part = lax.all_gather(seg_low, "ctx", axis=1, tiled=True)

    def step_fn(offset, span_rows, inner_state):
        run_max, run_total, accum_out = inner_state
        key_heads = lax.dynamic_slice_in_dim(key_part, offset, span_rows, 1).reshape(
            seq_count, span_rows, head_count, head_size
        )
        value_heads = lax.dynamic_slice_in_dim(value_part, offset, span_rows, 1).reshape(
            seq_count, span_rows, head_count, head_size
        )
        key_seg = lax.dynamic_slice_in_dim(seg_part, offset, span_rows, 1)
        key_pos = offset + jnp.arange(span_rows, dtype=jnp.int32)
        scores = (
            jnp.einsum(
                "sqhd,skhd->shqk", query_heads, key_heads, preferred_element_type=jnp.float32
            )
            * SCORE_SCALE
        )
        permit = allowed_pairs(live_table, query_pos, key_pos, seg_low, key_seg)[:, None]
        scores = jnp.where(permit, scores, NEG_FILL)
        new_max = jnp.maximum(run_max, jnp.max(scores, axis=-1))
        exp_scores = jnp.where(permit, jnp.exp(scores - new_max[..., None]), 0.0)
        factor = jnp.exp(run_max - new_max)
        run_total = run_total * factor + jnp.sum(exp_scores, axis=-1)
        weighted = jnp.einsum(
            "shqk,skhd->sqhd",
            exp_scores.astype(jnp.bfloat16),
            value_heads,
            preferred_element_type=jnp.float32,
        )
        accum_out = accum_out * jnp.transpose(factor, (0, 2, 1))[..., None] + weighted
        return (new_max, run_total, accum_out)

    run_max, run_total, accum_out = sweep_blocks(key_part.shape[1], step_fn, initial)
    attn_wide = accum_out / jnp.transpose(run_total, (0, 2, 1))[..., None]
    lse_heads = run_max + jnp.log(run_total)
    attn_low = attn_wide.reshape(flat_rows, model_width).astype(jnp.bfloat16)
    hidden = inputs_wide + matmul_low(attn_low, full_out) + bias_out.astype(jnp.float32)
    normed_two_wide, norm_pull_two = jax.vjp(
        layer_norm, hidden, gain_second.astype(jnp.float32), shift_second.astype(jnp.float32)
    )
    normed_two = normed_two_wide.astype(jnp.bfloat16)
    before = matmul_low(normed_two, full_up) + bias_up.astype(jnp.float32)
    activated_wide, gelu_pull = jax.vjp(exact_gelu, before)
    activated = activated_wide.astype(jnp.bfloat16)
    output = (hidden + matmul_low(activated, full_down) + bias_down.astype(jnp.float32)).astype(
        jnp.bfloat16
    )
    back_params = (
        lax.all_gather(shards[0], ("dp", "ctx"), axis=0, tiled=True),
        lax.all_gather(shards[1], ("dp", "ctx"), axis=0, tiled=True),
        lax.all_gather(shards[2], ("dp", "ctx"), axis=0, tiled=True),
        lax.all_gather(shards[3], ("dp", "ctx"), axis=0, tiled=True),
        lax.all_gather(shards[4], ("dp", "ctx"), axis=0, tiled=True),
        lax.all_gather(shards[5], ("dp", "ctx"), axis=0, tiled=True),
        lax.all_gather(shards[6], ("dp", "ctx"), axis=0, tiled=True),
        lax.all_gather(shards[7], ("dp", "ctx"), axis=0, tiled=True),
        lax.all_gather(shards[8], ("dp", "ctx"), axis=0, tiled=True),
        lax.all_gather(shards[9], ("dp", "ctx"), axis=0, tiled=True),
        lax.all_gather(shards[10], ("dp", "ctx"), axis=0, tiled=True),
        lax.all_gather(shards[11], ("dp", "ctx"), axis=0, tiled=True),
    )
    back_qkv = back_params[2]
    back_out = back_params[4]
    back_up = back_params[8]
    back_down = back_params[10]
    grad_low = grad_out.reshape(flat_rows, model_width)
    grad_down = inner_rows(activated, grad_low)
    grad_bias_down = jnp.sum(grad_low.astype(jnp.float32), axis=0)
    grad_act = times_transpose(grad_low, back_down)
    grad_before = gelu_pull(grad_act)[0].astype(jnp.bfloat16)
    grad_up = inner_rows(normed_two, grad_before)
    grad_bias_up = jnp.sum(grad_before.astype(jnp.float32), axis=0)
    grad_normed_two = times_transpose(grad_before, back_up)
    grad_hidden_part, grad_gain_two, grad_shift_two = norm_pull_two(grad_normed_two)
    grad_hidden = grad_low.astype(jnp.float32) + grad_hidden_part
    grad_branch = grad_hidden.astype(jnp.bfloat16)
    grad_out_full = inner_rows(attn_low, grad_branch)
    grad_bias_out = jnp.sum(grad_branch.astype(jnp.float32), axis=0)
    grad_attn = times_transpose(grad_branch, back_out).astype(jnp.bfloat16)
    dout_heads = grad_attn.reshape(seq_count, tok_rows, head_count, head_size)
    delta_rows = jnp.sum(dout_heads.astype(jnp.float32) * attn_wide, axis=-1)
    delta_heads = jnp.transpose(delta_rows, (0, 2, 1))
    key_all, value_all, seg_all = (
        lax.all_gather(key_seq, "ctx", axis=1, tiled=True),
        lax.all_gather(value_seq, "ctx", axis=1, tiled=True),
        lax.all_gather(seg_low, "ctx", axis=1, tiled=True),
    )

    def key_step(offset, span_rows, inner_state):
        grad_query_acc, grad_key_all, grad_value_all = inner_state
        key_heads = lax.dynamic_slice_in_dim(key_all, offset, span_rows, 1).reshape(
            seq_count, span_rows, head_count, head_size
        )
        value_heads = lax.dynamic_slice_in_dim(value_all, offset, span_rows, 1).reshape(
            seq_count, span_rows, head_count, head_size
        )
        key_seg = lax.dynamic_slice_in_dim(seg_all, offset, span_rows, 1)
        key_pos = offset + jnp.arange(span_rows, dtype=jnp.int32)
        grad_query, grad_key, grad_value = pair_grads(
            live_table,
            query_heads,
            dout_heads,
            lse_heads,
            delta_heads,
            query_pos,
            seg_low,
            key_heads,
            value_heads,
            key_pos,
            key_seg,
        )
        grad_key_all = lax.dynamic_update_slice_in_dim(
            grad_key_all, grad_key.reshape(seq_count, span_rows, model_width), offset, 1
        )
        grad_value_all = lax.dynamic_update_slice_in_dim(
            grad_value_all, grad_value.reshape(seq_count, span_rows, model_width), offset, 1
        )
        return (grad_query_acc + grad_query, grad_key_all, grad_value_all)

    length_rows = key_all.shape[1]
    zero_query = jnp.zeros((seq_count, tok_rows, head_count, head_size), jnp.float32)
    zero_keys = jnp.zeros((seq_count, length_rows, model_width), jnp.float32)
    grad_query_heads, grad_key_all, grad_value_all = sweep_blocks(
        length_rows, key_step, (zero_query, zero_keys, zero_keys)
    )
    grad_key_seq, grad_value_seq = (
        lax.psum_scatter(
            grad_key_all.astype(jnp.bfloat16), "ctx", scatter_dimension=1, tiled=True
        ).astype(jnp.float32),
        lax.psum_scatter(
            grad_value_all.astype(jnp.bfloat16), "ctx", scatter_dimension=1, tiled=True
        ).astype(jnp.float32),
    )
    grad_query_low = grad_query_heads.reshape(flat_rows, model_width).astype(jnp.bfloat16)
    grad_key_low = grad_key_seq.reshape(flat_rows, model_width).astype(jnp.bfloat16)
    grad_value_low = grad_value_seq.reshape(flat_rows, model_width).astype(jnp.bfloat16)
    grad_proj_low = jnp.concatenate([grad_query_low, grad_key_low, grad_value_low], axis=1)
    grad_qkv_full = inner_rows(normed_one, grad_proj_low)
    grad_bias_qv = jnp.concatenate(
        [
            jnp.sum(grad_query_low.astype(jnp.float32), axis=0),
            jnp.sum(grad_value_low.astype(jnp.float32), axis=0),
        ]
    )
    grad_normed_one = times_transpose(grad_proj_low, back_qkv)
    grad_input_part, grad_gain_one, grad_shift_one = norm_pull_one(grad_normed_one)
    grad_tokens = (grad_hidden + grad_input_part).reshape(seq_count, tok_rows, model_width)
    summed = (
        lax.psum_scatter(grad_gain_one, ("dp", "ctx"), scatter_dimension=0, tiled=True),
        lax.psum_scatter(grad_shift_one, ("dp", "ctx"), scatter_dimension=0, tiled=True),
        lax.psum_scatter(grad_qkv_full.astype(jnp.bfloat16), ("dp", "ctx"), scatter_dimension=0, tiled=True).astype(jnp.float32),
        lax.psum_scatter(grad_bias_qv, ("dp", "ctx"), scatter_dimension=0, tiled=True),
        lax.psum_scatter(grad_out_full.astype(jnp.bfloat16), ("dp", "ctx"), scatter_dimension=0, tiled=True).astype(jnp.float32),
        lax.psum_scatter(grad_bias_out, ("dp", "ctx"), scatter_dimension=0, tiled=True),
        lax.psum_scatter(grad_gain_two, ("dp", "ctx"), scatter_dimension=0, tiled=True),
        lax.psum_scatter(grad_shift_two, ("dp", "ctx"), scatter_dimension=0, tiled=True),
        lax.psum_scatter(grad_up.astype(jnp.bfloat16), ("dp", "ctx"), scatter_dimension=0, tiled=True).astype(jnp.float32),
        lax.psum_scatter(grad_bias_up, ("dp", "ctx"), scatter_dimension=0, tiled=True),
        lax.psum_scatter(grad_down.astype(jnp.bfloat16), ("dp", "ctx"), scatter_dimension=0, tiled=True).astype(jnp.float32),
        lax.psum_scatter(grad_bias_down, ("dp", "ctx"), scatter_dimension=0, tiled=True),
    )
    return (
        output.reshape(seq_count, tok_rows, model_width),
        grad_tokens,
        summed[0],
        summed[1],
        summed[2],
        summed[3],
        summed[4],
        summed[5],
        summed[6],
        summed[7],
        summed[8],
        summed[9],
        summed[10],
        summed[11],
    )


NZ = 4
GROUP = HEADS // NZ
GW = GROUP * HEAD_DIM
CHUNK = 256


def pick(array, index, axis=0):
    return lax.dynamic_index_in_dim(array, index, axis, keepdims=False)


def shift(array, axis, size, hop):
    return lax.ppermute(array, axis, [(i, (i + hop) % size) for i in range(size)])


def swap(array, axis):
    return shift(array, axis, 2, 1)


def in_order(own, received, index, axis):
    first = jnp.where(index == 0, own, received)
    second = jnp.where(index == 0, received, own)
    return jnp.stack([first, second], axis=axis)


def z_pieces(block):
    return [block] + [shift(block, "z", NZ, j) for j in range(1, NZ)]


def z_order(pieces, z):
    return jnp.stack([lax.select_n((z - a) % NZ, *pieces) for a in range(NZ)])


def z_exchange(array, z):
    return [pick(array, z)] + [shift(pick(array, (z + j) % NZ), "z", NZ, j) for j in range(1, NZ)]


def xy_gather(line, y, x):
    a, b = line[: NZ // 2], line[NZ // 2 :]
    a = in_order(a, swap(a, "x"), x, 0)
    b = in_order(b, swap(b, "y"), y, 0)
    return (a, swap(a, "y"), y, 0), (b, swap(b, "x"), x, 1)


def add_up(kept, sent, name):
    return kept.astype(jnp.float32) + swap(sent, name).astype(jnp.float32)


def halve(array, name, index, wire):
    return add_up(pick(array, index), pick(array, 1 - index).astype(wire), name)


def after(value, event):
    flag = event[(slice(0, 1),) * event.ndim].reshape(()).astype(jnp.float32)
    return jnp.where(flag != flag, jnp.zeros_like(value), value)


def meet(*values):
    return lax.optimization_barrier(values)


def z_collect(line, z, wire):
    own, *rest = z_exchange_wide(line, z, wire)
    total = own.astype(jnp.float32)
    for piece in rest:
        total = total + piece.astype(jnp.float32)
    return total


def z_exchange_wide(array, z, wire):
    return [pick(array, z)] + [
        shift(pick(array, (z + j) % NZ).astype(wire), "z", NZ, j) for j in range(1, NZ)
    ]


def norm_back(grad, gain, unit, scale):
    c = grad * gain
    return scale * (
        c - jnp.mean(c, axis=-1, keepdims=True) - unit * jnp.mean(c * unit, axis=-1, keepdims=True)
    )


def dot_nt(a, b):
    return lax.dot_general(a, b, (((1,), (1,)), ((), ())), preferred_element_type=jnp.float32)


def dot_tn(a, b):
    return lax.dot_general(a, b, (((0,), (0,)), ((), ())), preferred_element_type=jnp.float32)


def dot_nn(a, b):
    return lax.dot_general(a, b, (((1,), (0,)), ((), ())), preferred_element_type=jnp.float32)


def column_of(row):
    return jnp.transpose(jnp.broadcast_to(row, (8, row.shape[1])))[:, 0:1]


def query_row(may_ref, tile, block, seg_row, alive):
    per = CHUNK // BLOCK
    lane = lax.broadcasted_iota(jnp.int32, (1, CHUNK), 1)
    flag = jnp.full((1, CHUNK), may_ref[tile * per, block] * alive, jnp.int32)
    for b in range(1, per):
        flag = jnp.where(lane >= b * BLOCK, may_ref[tile * per + b, block] * alive, flag)
    return jnp.where(flag > 0, seg_row, -1.0)


def permit_of(may_ref, tile, chunk, seg_row, key_column, alive):
    per = CHUNK // BLOCK
    return jnp.concatenate(
        [
            key_column[b * BLOCK : (b + 1) * BLOCK]
            == query_row(may_ref, tile, chunk * per + b, seg_row, alive)
            for b in range(per)
        ],
        axis=0,
    )


def list_live(live, list_ref):
    count = jnp.int32(0)
    for number, flag in enumerate(live):
        list_ref[count] = number
        count = count + flag
    list_ref[count] = list_ref[jnp.maximum(count - 1, 0)]
    return count


def pair_at(list_ref, count, step):
    return (
        (list_ref[2 * step], jnp.int32(1)),
        (list_ref[2 * step + 1], (2 * step + 1 < count).astype(jnp.int32)),
    )


def whole_spec(shape):
    return pl.BlockSpec(shape, lambda *_: (0,) * len(shape))


def held(specs, arrays):
    return [
        pl.BlockSpec(memory_space=pltpu.VMEM) if tuple(spec.block_shape) == a.shape else spec
        for spec, a in zip(specs, arrays)
    ]


VMEM_MIB = {
    "unpack": 4, "pack": 4, "project": 14, "branch": 10, "feed": 28, "feed_weights": 24, "middle": 16,
    "inward": 14, "owners": 20, "finish": 10,
}


def kernel_call(body, place, arrays, in_specs, outs, out_specs, grid, scratch, flops, name, more=()):
    prefetch = (place,) + tuple(more)
    moved = sum(a.size * a.dtype.itemsize for a in arrays)
    return pl.pallas_call(
        body,
        out_shape=tuple(jax.ShapeDtypeStruct(shape, dtype) for shape, dtype in outs),
        grid_spec=pltpu.PrefetchScalarGridSpec(
            num_scalar_prefetch=len(prefetch),
            grid=grid,
            in_specs=held(in_specs, arrays),
            out_specs=out_specs,
            scratch_shapes=scratch,
        ),
        compiler_params=pltpu.CompilerParams(vmem_limit_bytes=VMEM_MIB[name] << 20),
        cost_estimate=pl.CostEstimate(flops=flops, bytes_accessed=moved, transcendentals=0),
        name=name,
    )(*prefetch, *arrays)


def lane_groups(lanes, size):
    lane = lax.broadcasted_iota(jnp.int32, (1, lanes), 1).astype(jnp.float32)
    group = jnp.floor((lane + 0.5) * (1.0 / size))
    return group, lane - group * size


def one_hot_rows(place_row, count):
    rows = lax.broadcasted_iota(jnp.int32, (count, place_row.shape[1]), 0).astype(jnp.float32)
    return (rows == place_row).astype(jnp.float32).astype(jnp.bfloat16)


VEC_ROWS = 16


def unpack_kernel(place_ref, packed_ref, vec_ref):
    devices = packed_ref.shape[0]
    width = vec_ref.shape[1]
    size = width // devices
    c = place_ref[1]
    device = lax.broadcasted_iota(jnp.int32, (devices, 1), 0)
    parity = lax.rem(device, 2)
    pair = lax.div(device, 2).astype(jnp.float32)
    device = device.astype(jnp.float32)
    vec_ref[...] = jnp.zeros(vec_ref.shape, jnp.float32)

    def spread(start, n, lanes, owner, keep):
        group, at = lane_groups(lanes, n)
        tiled = dot_nn(packed_ref[:, start : start + n], one_hot_rows(at, n))
        mine = (owner == group) if keep is None else (owner == group) & keep
        return jnp.sum(jnp.where(mine, tiled, 0.0), axis=0, keepdims=True)

    vec_ref[0:1] = spread(0, size, width, device, None)
    vec_ref[1:2] = spread(size, size, width, device, None)
    qv = spread(2 * size, 2 * size, 2 * width, device, None)
    vec_ref[2:3] = qv[:, :width]
    vec_ref[3:4] = qv[:, width:]
    vec_ref[4:5] = spread(4 * size, size, width, device, None)
    vec_ref[5:6] = spread(5 * size, size, width, device, None)
    vec_ref[6:7] = spread(6 * size, size, width, device, None)
    up = spread(7 * size, 4 * size, 2 * width, pair, parity == c)
    vec_ref[8:9] = up[:, :width]
    vec_ref[9:10] = up[:, width:]
    vec_ref[7:8] = spread(11 * size, size, width, device, None)


def pack_kernel(place_ref, grads_ref, mid_ref, qkv_ref, up_ref, packed_ref):
    devices = packed_ref.shape[0]
    width = grads_ref.shape[1]
    size = width // devices
    z, c = place_ref[0], place_ref[1]
    device = lax.broadcasted_iota(jnp.int32, (devices, 1), 0)
    parity = lax.rem(device, 2)
    pair = lax.div(device, 2).astype(jnp.float32)
    device = device.astype(jnp.float32)
    packed_ref[...] = jnp.zeros(packed_ref.shape, jnp.bfloat16)

    def gather(row, n, owner, keep):
        group, at = lane_groups(row.shape[1], n)
        mine = (owner == group) if keep is None else (owner == group) & keep
        return dot_nt(jnp.where(mine, row, 0.0).astype(jnp.bfloat16), one_hot_rows(at, n))

    def place_group(row):
        wide = jnp.concatenate([row] * NZ, axis=1)
        group, _ = lane_groups(wide.shape[1], GW)
        return jnp.where(group == z.astype(jnp.float32), wide, 0.0)

    qkv = qkv_ref[0:1]
    qv = jnp.concatenate([place_group(qkv[:, :GW]), place_group(qkv[:, 2 * GW :])], axis=1)
    parts = [
        gather(grads_ref[0:1], size, device, None),
        gather(grads_ref[1:2], size, device, None),
        gather(qv, 2 * size, device, None),
        gather(mid_ref[2:3], size, device, None),
        gather(mid_ref[0:1], size, device, None),
        gather(mid_ref[1:2], size, device, None),
        gather(up_ref[0:1], 4 * size, pair, parity == c),
        gather(mid_ref[3:4], size, device, None),
    ]
    packed_ref[:, 0 : 12 * size] = jnp.concatenate(parts, axis=1).astype(jnp.bfloat16)


def norm_rows(x):
    center = x - jnp.mean(x, axis=-1, keepdims=True)
    scale = lax.rsqrt(jnp.mean(center * center, axis=-1, keepdims=True) + 1e-05)
    return center * scale, scale


def project_kernel(place_ref, t0_ref, t1_ref, t2_ref, t3_ref, vec_ref, wz_ref, line_ref, n1_ref, q_ref, kv_ref):
    a = pl.program_id(0)
    z = place_ref[0]
    away = lax.rem(z - a + NZ, NZ)
    x = t0_ref[...].astype(jnp.float32)
    for j, ref in enumerate((t1_ref, t2_ref, t3_ref), 1):
        x = jnp.where(away == j, ref[...].astype(jnp.float32), x)
    line_ref[...] = x.astype(jnp.bfloat16)
    unit, _ = norm_rows(x)
    n1 = (unit * vec_ref[0:1] + vec_ref[1:2]).astype(jnp.bfloat16)
    n1_ref[...] = n1
    y = dot_nn(n1, wz_ref[...])
    q_bias, v_bias = vec_ref[2:3, 0:GW], vec_ref[3:4, 0:GW]
    for g in range(1, NZ):
        q_bias = jnp.where(z == g, vec_ref[2:3, g * GW : (g + 1) * GW], q_bias)
        v_bias = jnp.where(z == g, vec_ref[3:4, g * GW : (g + 1) * GW], v_bias)
    q = (y[:, :GW] + q_bias).astype(jnp.bfloat16)
    q_ref[...] = q * jnp.asarray(SCORE_SCALE, jnp.bfloat16)
    kv_ref[:, :GW] = y[:, GW : 2 * GW].astype(jnp.bfloat16)
    kv_ref[:, GW:] = (y[:, 2 * GW :] + v_bias).astype(jnp.bfloat16)


def project(place, pieces, vec, wz):
    rows, width = pieces[0].shape
    low = jnp.bfloat16
    tall = lambda w: pl.BlockSpec((rows, w), lambda a, *_: (a, 0))
    return kernel_call(
        project_kernel, place, (*pieces, vec, wz),
        [whole_spec((rows, width))] * NZ + [whole_spec(vec.shape), whole_spec(wz.shape)],
        [((NZ * rows, width), low), ((NZ * rows, width), low), ((NZ * rows, GW), low), ((NZ * rows, 2 * GW), low)],
        [tall(width), tall(width), tall(GW), tall(2 * GW)],
        (NZ,), [], 8 * NZ * rows * width * 3 * GW, "project",
    )


def branch_kernel(place_ref, a0_ref, a1_ref, a2_ref, a3_ref, wo_ref, own_ref, vec_ref, hidden_ref, n2_ref):
    z = place_ref[0]
    total = own_ref[...].astype(jnp.float32) + vec_ref[4:5]
    branch = None
    for j, ref in enumerate((a0_ref, a1_ref, a2_ref, a3_ref)):
        start = pl.multiple_of(lax.rem(z - j + NZ, NZ) * GW, GW)
        part = dot_nn(ref[...], wo_ref[pl.ds(start, GW), :])
        branch = part if branch is None else branch + part
    hidden = total + branch
    hidden_ref[...] = hidden
    unit, _ = norm_rows(hidden)
    n2_ref[...] = (unit * vec_ref[5:6] + vec_ref[6:7]).astype(jnp.bfloat16)


def branch_call(place, pieces, wo, own, vec):
    rows, width = own.shape
    arrays = (*pieces, wo, own, vec)
    return kernel_call(
        branch_kernel, place, arrays, [whole_spec(a.shape) for a in arrays],
        [((rows, width), jnp.float32), ((rows, width), jnp.bfloat16)],
        [whole_spec((rows, width))] * 2, (1,), [], 8 * rows * width * width, "branch",
    )


def feed_kernel(
    place_ref, na_ref, nb_ref, ga_ref, gb_ref, up_ref, down_ref, bias_ref,
    act_ref, grad_ref, out_ref, m_ref, sums_ref, bias_out_ref, n_s, g_s, out_s, m_s,
):
    k = pl.program_id(0)
    rows, width = na_ref.shape

    @pl.when(k == 0)
    def _():
        n_s[:rows], n_s[rows:] = na_ref[...], nb_ref[...]
        g_s[:rows], g_s[rows:] = ga_ref[...], gb_ref[...]
        out_s[...] = jnp.zeros(out_s.shape, jnp.float32)
        m_s[...] = jnp.zeros(m_s.shape, jnp.float32)

    up, down = up_ref[...].reshape(width, width), down_ref[...].reshape(width, width)
    v = dot_nn(n_s[...], up) + bias_ref[...]
    cdf = 0.5 * (1.0 + lax.erf(v * 0.7071067811865476))
    slope = cdf + v * (0.3989422804014327 * jnp.exp(-0.5 * v * v))
    act = (v * cdf).astype(jnp.bfloat16)
    act_ref[...] = act
    grad = dot_nt(g_s[...], down) * slope
    grad = grad.astype(jnp.bfloat16)
    grad_ref[...] = grad
    bias_out_ref[...] = jnp.sum(grad.astype(jnp.float32), axis=0, keepdims=True)
    out_s[...] += dot_nn(act, down)
    m_s[...] += dot_nt(grad, up)

    @pl.when(k == pl.num_programs(0) - 1)
    def _():
        out_ref[...] = out_s[:rows]
        m_ref[...] = m_s[:rows]
        sums_ref[0] = m_s[rows:].astype(jnp.bfloat16)
        sums_ref[1] = out_s[rows:].astype(jnp.bfloat16)


def feed(place, na, nb, ga, gb, both, bias):
    rows, width = na.shape
    chips, tall, _ = both.shape
    half = bias.shape[1]
    low, wide = jnp.bfloat16, jnp.float32
    one = whole_spec((rows, width))
    across = lambda r: pl.BlockSpec((r, width), lambda k, *_: (0, k))
    return kernel_call(
        feed_kernel, place, (na, nb, ga, gb, both, both, bias),
        [one] * 4 + [
            pl.BlockSpec((chips, tall // 4, width), lambda k, *_: (0, k, 0)),
            pl.BlockSpec((chips // 2, tall // 2, width), lambda k, *_: (k, 1, 0)),
            across(1),
        ],
        [
            ((2 * rows, half), low), ((2 * rows, half), low), ((rows, width), wide), ((rows, width), wide),
            ((2, rows, width), low), ((1, half), wide),
        ],
        [across(2 * rows), across(2 * rows), one, one, whole_spec((2, rows, width)), across(1)],
        (2,),
        [
            pltpu.VMEM((2 * rows, width), low), pltpu.VMEM((2 * rows, width), low),
            pltpu.VMEM((2 * rows, width), wide), pltpu.VMEM((2 * rows, width), wide),
        ],
        32 * rows * width * half, "feed",
    )


def feed_weights_kernel(
    place_ref, na_ref, nb_ref, ga_ref, gb_ref, act_ref, grad_ref, ak_ref, as_ref, bk_ref, bs_ref, n_s, g_s
):
    rows, width = na_ref.shape
    y, x = place_ref[2], place_ref[3]
    n_s[:rows], n_s[rows:] = na_ref[...], nb_ref[...]
    g_s[:rows], g_s[rows:] = ga_ref[...], gb_ref[...]
    tall = ak_ref.shape[2]
    quarter = tall // 4
    span = NZ * quarter

    def put(py, px, pz, row, value):
        count = value.shape[0]
        near, far = (ak_ref, as_ref) if pz < NZ // 2 else (bk_ref, bs_ref)
        index, mine = (px, py == y) if pz < NZ // 2 else (py, px == x)

        @pl.when(mine)
        def _():
            near[index, pz % (NZ // 2), row : row + count] = value

        @pl.when(jnp.logical_not(mine))
        def _():
            far[index, pz % (NZ // 2), row : row + count] = value

    n, g = n_s[...], g_s[...]
    for py in range(2):
        for px in range(2):
            at = (2 * py + px) * span
            up = dot_tn(n[:, at : at + span], grad_ref[...]).astype(jnp.bfloat16)
            down = dot_tn(act_ref[:, 2 * at : 2 * (at + span)], g).astype(jnp.bfloat16)
            for pz in range(NZ):
                here = slice(pz * quarter, (pz + 1) * quarter)
                put(py, px, pz, 0, up[here, :width])
                put(py, px, pz, quarter, up[here, width:])
                put(py, px, pz, 2 * quarter, down[2 * pz * quarter : 2 * (pz + 1) * quarter])


def feed_weights(place, na, nb, ga, gb, act, grad, tall):
    rows, width = na.shape
    low = jnp.bfloat16
    arrays = (na, nb, ga, gb, act, grad)
    shape = (2, NZ // 2, tall, width)
    return kernel_call(
        feed_weights_kernel, place, arrays, [whole_spec(a.shape) for a in arrays], [(shape, low)] * 4,
        [whole_spec(shape)] * 4, (1,),
        [pltpu.VMEM((2 * rows, width), low), pltpu.VMEM((2 * rows, width), low)],
        8 * rows * width * act.shape[1], "feed_weights",
    )


def middle_kernel(
    place_ref, m_ref, out_ref, sums_ref, hidden_ref, go_ref, vec_ref, wo_ref,
    output_ref, gh_ref, branch_ref, d0_ref, d1_ref, d2_ref, d3_ref, cols_ref,
):
    z = place_ref[0]
    hidden, go = hidden_ref[...], go_ref[...].astype(jnp.float32)
    output_ref[...] = (hidden + out_ref[...] + sums_ref[1].astype(jnp.float32) + vec_ref[7:8]).astype(
        jnp.bfloat16
    )
    m = m_ref[...] + sums_ref[0].astype(jnp.float32)
    unit, scale = norm_rows(hidden)
    grad_hidden = go + norm_back(m, vec_ref[5:6], unit, scale)
    gh_ref[...] = grad_hidden
    branch = grad_hidden.astype(jnp.bfloat16)
    branch_ref[...] = branch
    for j, ref in enumerate((d0_ref, d1_ref, d2_ref, d3_ref)):
        start = pl.multiple_of(lax.rem(z + j, NZ) * GW, GW)
        ref[...] = dot_nt(branch, wo_ref[pl.ds(start, GW), :]).astype(jnp.bfloat16)
    cols_ref[...] = jnp.zeros(cols_ref.shape, jnp.float32)
    cols_ref[0:1] = jnp.sum(m * unit, axis=0, keepdims=True)
    cols_ref[1:2] = jnp.sum(m, axis=0, keepdims=True)
    cols_ref[2:3] = jnp.sum(branch.astype(jnp.float32), axis=0, keepdims=True)
    cols_ref[3:4] = jnp.sum(go, axis=0, keepdims=True)


def middle(place, m, out, sums, hidden, go, vec, wo):
    rows, width = m.shape
    arrays = (m, out, sums, hidden, go, vec, wo)
    low, wide = jnp.bfloat16, jnp.float32
    outs = [((rows, width), low), ((rows, width), wide), ((rows, width), low)]
    outs += [((rows, GW), low)] * NZ + [((8, width), wide)]
    return kernel_call(
        middle_kernel, place, arrays, [whole_spec(a.shape) for a in arrays], outs,
        [whole_spec(shape) for shape, _ in outs], (1,), [], 8 * rows * width * width, "middle",
    )


def inward_kernel(
    place_ref, dq_ref, mine_ref, theirs_ref, line_ref, wz_ref, dqkv_ref, keep_ref, sent_ref, cols_ref, sums_ref
):
    j = pl.program_id(0)
    dq = dq_ref[...]
    dkv = (mine_ref[...].astype(jnp.float32) + theirs_ref[...].astype(jnp.float32)).astype(jnp.bfloat16)
    dqkv = jnp.concatenate([dq, dkv], axis=1)
    dqkv_ref[...] = dqkv
    m1 = dot_nt(dqkv, wz_ref[...])
    sent_ref[0] = m1.astype(jnp.bfloat16)
    unit, _ = norm_rows(line_ref[...].astype(jnp.float32))

    @pl.when(j == 0)
    def _():
        cols_ref[...] = jnp.zeros(cols_ref.shape, jnp.float32)
        sums_ref[...] = jnp.zeros(sums_ref.shape, jnp.float32)

    cols_ref[0:1] += jnp.sum(m1 * unit, axis=0, keepdims=True)
    cols_ref[1:2] += jnp.sum(m1, axis=0, keepdims=True)
    sums_ref[0:1] += jnp.sum(dqkv.astype(jnp.float32), axis=0, keepdims=True)

    @pl.when(j == pl.num_programs(0) - 1)
    def _():
        keep_ref[...] = m1


def inward(place, dq, mine, theirs, line, wz):
    total, width = line.shape
    rows = total // NZ
    low, wide = jnp.bfloat16, jnp.float32
    turned = lambda w: pl.BlockSpec((rows, w), lambda j, p: (lax.rem(p[0] + 1 + j, NZ), 0))
    return kernel_call(
        inward_kernel, place, (dq, mine, theirs, line, wz),
        [turned(GW), turned(2 * GW), turned(2 * GW), turned(width), whole_spec(wz.shape)],
        [((total, 3 * GW), low), ((rows, width), wide), ((NZ, rows, width), low), ((8, width), wide), ((8, 3 * GW), wide)],
        [
            turned(3 * GW), whole_spec((rows, width)),
            pl.BlockSpec((1, rows, width), lambda j, p: (j, 0, 0)),
            whole_spec((8, width)), whole_spec((8, 3 * GW)),
        ],
        (NZ,), [], 8 * total * width * 3 * GW, "inward",
    )


def finish_kernel(place_ref, m_ref, r1_ref, r2_ref, r3_ref, own_ref, gh_ref, vec_ref, out_ref):
    m = m_ref[...]
    for ref in (r1_ref, r2_ref, r3_ref):
        m = m + ref[...].astype(jnp.float32)
    unit, scale = norm_rows(own_ref[...].astype(jnp.float32))
    out_ref[...] = gh_ref[...] + norm_back(m, vec_ref[0:1], unit, scale)


def finish(place, m, pieces, own, grad_hidden, vec):
    rows, width = own.shape
    arrays = (m, *pieces, own, grad_hidden, vec)
    return kernel_call(
        finish_kernel, place, arrays, [whole_spec(a.shape) for a in arrays],
        [((rows, width), jnp.float32)], [whole_spec((rows, width))], (1,), [], 100 * rows * width, "finish",
    )[0]


def owners_kernel(
    place_ref, a0_ref, a1_ref, a2_ref, a3_ref, branch_ref, n1_ref, dqkv_ref, cols_ref, mid_ref, sums_ref, up_ref,
    mine_ref, theirs_ref, wo_s, wz_s, vec_s,
):
    z, c = place_ref[0], place_ref[1]
    width = branch_ref.shape[1]
    for j, ref in enumerate((a0_ref, a1_ref, a2_ref, a3_ref)):
        start = pl.multiple_of(lax.rem(z - j + NZ, NZ) * GW, GW)
        wo_s[pl.ds(start, GW), :] = dot_tn(ref[...], branch_ref[...]).astype(jnp.bfloat16)
    wz_s[...] = dot_tn(n1_ref[...], dqkv_ref[...]).astype(jnp.bfloat16)
    pack_kernel(place_ref, cols_ref, mid_ref, sums_ref, up_ref, vec_s)
    chips, tall, span = mine_ref.shape
    devices = 2 * chips
    rows = width // devices
    pad = jnp.zeros((tall - rows, span), jnp.bfloat16)
    first_row = lax.broadcasted_iota(jnp.int32, (tall - rows, span), 0) == 0
    for pair in range(chips):
        blocks = []
        for core in range(2):
            at = slice((2 * pair + core) * rows, (2 * pair + core + 1) * rows)
            vec = vec_s[2 * pair + core : 2 * pair + core + 1]
            vec = jnp.where(first_row, jnp.broadcast_to(vec.astype(jnp.float32), pad.shape), 0.0)
            top = jnp.concatenate([wo_s[at], wz_s[at]], axis=1)
            blocks.append((top, vec.astype(jnp.bfloat16)))
        mine_ref[pair, :rows] = jnp.where(c == 0, blocks[0][0], blocks[1][0])
        mine_ref[pair, rows:] = jnp.where(c == 0, blocks[0][1], blocks[1][1])
        theirs_ref[pair, :rows] = jnp.where(c == 0, blocks[1][0], blocks[0][0])
        theirs_ref[pair, rows:] = jnp.where(c == 0, blocks[1][1], blocks[0][1])


def owners(place, pieces, branch, n1, dqkv, cols, mid, sums, up, devices, tall):
    width, span = n1.shape[1], n1.shape[1] + dqkv.shape[1]
    low = jnp.bfloat16
    arrays = (*pieces, branch, n1, dqkv, cols, mid, sums, up)
    shape = (devices // 2, tall, span)
    return kernel_call(
        owners_kernel, place, arrays, [whole_spec(a.shape) for a in arrays], [(shape, low), (shape, low)],
        [whole_spec(shape)] * 2, (1,),
        [pltpu.VMEM((width, width), low), pltpu.VMEM((width, dqkv.shape[1]), low), pltpu.VMEM((devices, span), low)],
        1 << 20, "owners",
    )


def attend_kernel(
    act_ref, may_ref, place_ref, q_ref, mine_ref, theirs_ref, qseg_ref, kseg_ref, o_ref, low_ref, lse_ref,
    k_s, vt_s, col_s, m_s, l_s, acc_s, list_s,
):
    i = pl.program_id(0)
    chunks = kseg_ref.shape[0]

    @pl.when(i == 0)
    def _():
        for line, ref in enumerate((mine_ref, theirs_ref)):
            core = place_ref[1] if line == 0 else 1 - place_ref[1]
            for a in range(chunks // 2):
                rows = slice(a * CHUNK, (a + 1) * CHUNK)
                at = pl.ds(pl.multiple_of((2 * a + core) * CHUNK, CHUNK), CHUNK)
                for h in range(GROUP):
                    k_s[h, at] = ref[rows, HEAD_DIM * h : HEAD_DIM * (h + 1)]
                    vt_s[h, :, at] = jnp.transpose(ref[rows, GW + HEAD_DIM * h : GW + HEAD_DIM * (h + 1)])
        for j in range(chunks):
            col_s[j * CHUNK : (j + 1) * CHUNK] = column_of(kseg_ref[j : j + 1])

    m_s[...] = jnp.full(m_s.shape, NEG_FILL, jnp.float32)
    l_s[...] = jnp.zeros(l_s.shape, jnp.float32)
    acc_s[...] = jnp.zeros(acc_s.shape, jnp.float32)
    q_heads = [q_ref[:, HEAD_DIM * h : HEAD_DIM * (h + 1)] for h in range(GROUP)]
    q_seg = qseg_ref[pl.ds(i, 1)]

    count = list_live([act_ref[i, j] for j in range(chunks)], list_s)

    def two_chunks(step, carry):
        heads, pair = range(GROUP), pair_at(list_s, count, step)
        at = [pl.ds(pl.multiple_of(j * CHUNK, CHUNK), CHUNK) for j, _ in pair]
        permit = [permit_of(may_ref, i, j, q_seg, col_s[at[u]], alive) for u, (j, alive) in enumerate(pair)]
        s = [[jnp.where(permit[u], dot_nt(k_s[h, at[u]], q_heads[h]), NEG_FILL) for u in range(2)] for h in heads]
        old = [m_s[h] for h in heads]
        top = [[jnp.max(part, axis=0, keepdims=True) for part in s[h]] for h in heads]
        new = [jnp.maximum(old[h], jnp.maximum(*top[h])) for h in heads]
        p = [[jnp.exp(part - new[h]) for part in s[h]] for h in heads]
        fade = [jnp.exp(old[h] - new[h]) for h in heads]
        for h in heads:
            l_s[h] = l_s[h] * fade[h] + sum(jnp.sum(part, axis=0, keepdims=True) for part in p[h])
            added = [dot_nn(vt_s[h, :, at[u]], p[h][u].astype(jnp.bfloat16)) for u in range(2)]
            acc_s[h] = acc_s[h] * fade[h] + (added[0] + added[1])
            m_s[h] = new[h]
        return carry

    lax.fori_loop(0, lax.div(count + 1, 2), two_chunks, 0)
    out = jnp.concatenate([jnp.transpose(acc_s[h] / l_s[h]) for h in range(GROUP)], axis=1)
    o_ref[...] = out
    low_ref[...] = out.astype(jnp.bfloat16)
    logs = [m_s[h] + jnp.log(l_s[h]) for h in range(GROUP)]
    lse_ref[...] = jnp.concatenate(logs + [logs[0]] * (8 - GROUP), axis=0)


def attend(active, may, place, q, mine, theirs, q_seg, k_seg):
    rows, keys = q.shape[0], 2 * mine.shape[0]
    tall = pl.BlockSpec((CHUNK, GW), lambda i, *_: (i, 0))
    return pl.pallas_call(
        attend_kernel,
        out_shape=(
            jax.ShapeDtypeStruct((rows, GW), jnp.float32),
            jax.ShapeDtypeStruct((rows, GW), jnp.bfloat16),
            jax.ShapeDtypeStruct((8, rows), jnp.float32),
        ),
        grid_spec=pltpu.PrefetchScalarGridSpec(
            num_scalar_prefetch=3,
            grid=(rows // CHUNK,),
            in_specs=held(
                [tall, *[whole_spec(a.shape) for a in (mine, theirs, q_seg, k_seg)]], (q, mine, theirs, q_seg, k_seg)
            ),
            out_specs=[tall, tall, pl.BlockSpec((8, CHUNK), lambda i, *_: (0, i))],
            scratch_shapes=[
                pltpu.VMEM((GROUP, keys, HEAD_DIM), jnp.bfloat16),
                pltpu.VMEM((GROUP, HEAD_DIM, keys), jnp.bfloat16),
                pltpu.VMEM((keys, 1), jnp.float32),
                pltpu.VMEM((GROUP, 1, CHUNK), jnp.float32),
                pltpu.VMEM((GROUP, 1, CHUNK), jnp.float32),
                pltpu.VMEM((GROUP, HEAD_DIM, CHUNK), jnp.float32),
                pltpu.SMEM((keys // CHUNK + 1,), jnp.int32),
            ],
        ),
        compiler_params=pltpu.CompilerParams(vmem_limit_bytes=18 << 20),
        cost_estimate=pl.CostEstimate(
            flops=48 * rows * keys * GW, bytes_accessed=16 * keys * GW, transcendentals=4 * rows * keys
        ),
        name="attend",
    )(active, may, place, q, mine, theirs, q_seg, k_seg)


def attend_back_kernel(first, *refs):
    (act_ref, may_ref, place_ref, q_ref, d0_ref, d1_ref, d2_ref, d3_ref, kv_ref, lse_ref, qseg_ref,
     kseg_ref, from_ref, *refs) = refs
    if first:
        dqt_ref, delta_ref, dkv_ref, list_s, q_s, do_s, dk_s, dv_s = refs
    else:
        old_ref, dq_ref, dkv_ref, list_s, q_s, do_s, dk_s, dv_s, dqt_ref = refs
        delta_ref = from_ref
    step = pl.program_id(0)
    rows = q_ref.shape[0]
    z, c = place_ref[0], place_ref[1]
    j = 2 * step + (1 - c if first else c)

    @pl.when(step == 0)
    def _():
        for r, ref in enumerate((d0_ref, d1_ref, d2_ref, d3_ref)):
            at = pl.ds(pl.multiple_of(lax.rem(z - r + NZ, NZ) * CHUNK, CHUNK), CHUNK)
            for h in range(GROUP):
                do_s[h, at] = ref[:, HEAD_DIM * h : HEAD_DIM * (h + 1)]
        ones = jnp.ones((8, HEAD_DIM), jnp.float32)
        for h in range(GROUP):
            lanes = slice(HEAD_DIM * h, HEAD_DIM * (h + 1))
            q_s[h] = q_ref[:, lanes]
            if first:
                both = do_s[h].astype(jnp.float32) * from_ref[:, lanes]
                delta_ref[h : h + 1] = lax.dot_general(
                    ones, both, (((1,), (1,)), ((), ())), precision=lax.Precision.HIGHEST,
                    preferred_element_type=jnp.float32,
                )[0:1]
        dqt_ref[...] = jnp.zeros(dqt_ref.shape, jnp.float32) if first else old_ref[...]
        if first:
            delta_ref[GROUP:] = jnp.zeros((8 - GROUP, rows), jnp.float32)

    dk_s[...] = jnp.zeros(dk_s.shape, jnp.float32)
    dv_s[...] = jnp.zeros(dv_s.shape, jnp.float32)
    k_heads = [kv_ref[:, HEAD_DIM * h : HEAD_DIM * (h + 1)] for h in range(GROUP)]
    v_heads = [kv_ref[:, GW + HEAD_DIM * h : GW + HEAD_DIM * (h + 1)] for h in range(GROUP)]
    k_turned = [jnp.transpose(k) for k in k_heads]
    k_column = column_of(kseg_ref[pl.ds(j, 1)])

    count = list_live([act_ref[i, j] for i in range(rows // CHUNK)], list_s)

    def two_tiles(turn, carry):
        heads, pair, low = range(GROUP), pair_at(list_s, count, turn), jnp.bfloat16
        both = [(h, u) for h in heads for u in range(2)]
        at = [pl.ds(pl.multiple_of(i * CHUNK, CHUNK), CHUNK) for i, _ in pair]
        permit = [
            permit_of(may_ref, i, j, qseg_ref[pl.ds(i, 1)], k_column, alive) for i, alive in pair
        ]
        s = {(h, u): dot_nt(k_heads[h], q_s[h, at[u]]) for h, u in both}
        dp = {(h, u): dot_nt(v_heads[h], do_s[h, at[u]]) for h, u in both}
        p = {
            (h, u): jnp.where(permit[u], jnp.exp(s[h, u] - lse_ref[h : h + 1, at[u]]), 0.0) for h, u in both
        }
        ds = {(h, u): (p[h, u] * (dp[h, u] - delta_ref[h : h + 1, at[u]])).astype(low) for h, u in both}
        for h in heads:
            dv_s[h] += dot_nn(p[h, 0].astype(low), do_s[h, at[0]]) + dot_nn(p[h, 1].astype(low), do_s[h, at[1]])
            dk_s[h] += dot_nn(ds[h, 0], q_s[h, at[0]]) + dot_nn(ds[h, 1], q_s[h, at[1]])
            for u in range(2):
                dqt_ref[h, :, at[u]] += dot_nn(k_turned[h], ds[h, u])
        return carry

    lax.fori_loop(0, lax.div(count + 1, 2), two_tiles, 0)
    dkv_ref[...] = jnp.concatenate(
        [dk_s[h] for h in range(GROUP)] + [dv_s[h] for h in range(GROUP)], axis=1
    ).astype(jnp.bfloat16)
    if not first:

        @pl.when(step == pl.num_programs(0) - 1)
        def _():
            dq_ref[...] = jnp.concatenate(
                [jnp.transpose(dqt_ref[h] * SCORE_SCALE) for h in range(GROUP)], axis=1
            ).astype(jnp.bfloat16)


def attend_back(first, active, may, place, q, pieces, kv, lse, q_seg, k_seg, *carried):
    rows = q.shape[0]
    low, wide = jnp.bfloat16, jnp.float32
    tall = pl.BlockSpec((CHUNK, 2 * GW), lambda s, *_: (s, 0))
    turned = (GROUP, HEAD_DIM, rows)
    outs = [(turned, wide), ((8, rows), wide)] if first else [((rows, GW), low)]
    scratch = [pltpu.SMEM((rows // CHUNK + 1,), jnp.int32)] + [pltpu.VMEM((GROUP, rows, HEAD_DIM), low)] * 2 + [pltpu.VMEM((GROUP, CHUNK, HEAD_DIM), wide)] * 2
    if not first:
        scratch.append(pltpu.VMEM(turned, wide))
    return pl.pallas_call(
        functools.partial(attend_back_kernel, first),
        out_shape=tuple(jax.ShapeDtypeStruct(*o) for o in outs + [((rows, 2 * GW), low)]),
        grid_spec=pltpu.PrefetchScalarGridSpec(
            num_scalar_prefetch=3,
            grid=(rows // CHUNK,),
            in_specs=held(
                [
                    whole_spec((rows, GW)), *[whole_spec(p.shape) for p in pieces], tall, whole_spec((8, rows)),
                    whole_spec(q_seg.shape), whole_spec(k_seg.shape), *[whole_spec(a.shape) for a in carried],
                ],
                (q, *pieces, kv, lse, q_seg, k_seg, *carried),
            ),
            out_specs=[whole_spec(shape) for shape, _ in outs] + [tall],
            scratch_shapes=scratch,
        ),
        compiler_params=pltpu.CompilerParams(vmem_limit_bytes=20 << 20),
        cost_estimate=pl.CostEstimate(
            flops=56 * rows * rows * GW, bytes_accessed=32 * rows * GW, transcendentals=4 * rows * rows
        ),
        name="attend_back_first" if first else "attend_back_last",
    )(active, may, place, q, *pieces, kv, lse, q_seg, k_seg, *carried)


def fast_local(
    tokens, segment_ids, live_blocks, norm1_gain, norm1_bias, qkv_weight, qv_bias, out_weight, out_bias,
    norm2_gain, norm2_bias, up_weight, up_bias, down_weight, down_bias, grad_out,
):
    y, x, z, c = (lax.axis_index(name) for name in ("y", "x", "z", "c"))
    place = jnp.stack([z, c, y, x]).astype(jnp.int32)
    wide, low = jnp.float32, jnp.bfloat16
    _, rows, width = tokens.shape
    own_rows, units = qkv_weight.shape[0], down_weight.shape[0]
    ff = up_weight.shape[1]
    half, pairs = ff // 2, ff // (2 * units)
    devices = width // own_rows
    seq_rows = rows * NZ
    keys = 2 * seq_rows
    blocks = keys // BLOCK
    per = CHUNK // BLOCK

    vectors = (norm1_gain, norm1_bias, qv_bias, out_bias, norm2_gain, norm2_bias, up_bias, down_bias)
    sizes = [v.shape[0] for v in vectors]
    cuts = [sum(sizes[:i]) for i in range(len(sizes) + 1)]
    span = width + 3 * GW
    tall = own_rows + 8
    parts = vectors + (segment_ids[0].astype(low),)
    extra = sum(
        jnp.pad(p, (start, span - start - p.shape[0])) for p, start in zip(parts, cuts)
    )
    extra = jnp.pad(extra[None], ((0, 7), (0, 0)))
    wz = qkv_weight.reshape(own_rows, 3, NZ, GW).transpose(2, 0, 1, 3).reshape(NZ, own_rows, 3 * GW)
    group1 = jnp.concatenate(
        [jnp.broadcast_to(out_weight[None], (NZ, own_rows, width)), wz], axis=2
    )
    group1 = jnp.concatenate([group1, jnp.broadcast_to(extra[None], (NZ, 8, span))], axis=1)
    pieces1 = z_exchange(group1, z)

    up_sets = up_weight.reshape(own_rows, pairs, 2, units).transpose(2, 0, 1, 3)
    up_sets = up_sets.reshape(2, own_rows, half)
    up_chip = in_order(pick(up_sets, c), swap(pick(up_sets, 1 - c), "c"), c, 0)
    up_chip = up_chip.reshape(2 * own_rows, half)
    group2 = jnp.concatenate([up_chip[:, :width], up_chip[:, width:], down_weight], axis=0)
    pieces2 = z_pieces(group2)

    own, pieces2[1], pieces2[3] = meet(tokens[0], pieces2[1], pieces2[3])
    line_pieces = z_pieces(own)
    group1 = z_order(pieces1, z)
    own_seg = group1[:, own_rows, cuts[-1] : cuts[-1] + rows].astype(wide)
    seg = in_order(own_seg, swap(own_seg, "c"), c, 1).reshape(keys // CHUNK, CHUNK)
    group1 = jnp.concatenate([in_order(*half) for half in xy_gather(group1, y, x)], axis=2)
    group1 = in_order(group1, swap(group1, "c"), c, 3)
    wo = group1[..., :own_rows, :width].reshape(width, width)
    wz = group1[..., :own_rows, width:].reshape(width, 3 * GW)
    packed = group1[..., own_rows, : cuts[-1]].reshape(devices, cuts[-1])
    vec = kernel_call(
        unpack_kernel, place, (packed,), [whole_spec(packed.shape)], [((VEC_ROWS, width), wide)],
        [whole_spec((VEC_ROWS, width))], (1,), [], 1 << 20, "unpack",
    )[0]
    group2, vec = meet(z_order(pieces2, z), vec)
    group2 = xy_gather(group2, y, x)

    own_blocks = seq_rows // BLOCK
    ids = jnp.arange(blocks, dtype=jnp.int32)
    own_ids = pick(ids.reshape(NZ, 2, rows // BLOCK), c, 1).reshape(own_blocks)
    own_live = pick(live_blocks[0].reshape(NZ, 2, rows // BLOCK, blocks), c, 1)
    own_live = own_live.reshape(own_blocks, blocks)
    seg_blocks = seg.reshape(blocks, BLOCK)
    own_seg_blocks = own_seg.reshape(own_blocks, BLOCK)
    may = (own_live > 0) | (own_ids[:, None] == ids[None, :])
    touch = (
        may
        & (own_seg_blocks[:, :1] <= seg_blocks[:, -1][None])
        & (seg_blocks[:, 0][None] <= own_seg_blocks[:, -1:])
    )
    active = jnp.any(touch.reshape(own_blocks // per, per, blocks // per, per), axis=(1, 3))
    active, may = active.astype(jnp.int32), may.astype(jnp.int32)

    line, n1, q, kv = project(place, line_pieces, vec, wz)
    kv_theirs = swap(kv, "c")
    att_wide, att_low, lse = attend(active, may, place, q, kv, kv_theirs, own_seg, seg)
    att = z_exchange(att_low.reshape(NZ, rows, GW), z)
    group2 = [in_order(own_half, after(other, att_low), at, axis) for own_half, other, at, axis in group2]
    group2 = jnp.concatenate(group2, axis=2)

    hidden, n2 = branch_call(place, att, wo, own, vec)
    go = grad_out[0]
    n2_theirs, go_theirs = swap(n2, "c"), swap(go, "c")
    up_bias_half = vec[8:10].reshape(1, half)
    chips = devices // 2
    group2 = group2.reshape(chips, 2 * units, width)
    activated, grad_before, out_part, m_part, sums, up_bias_part = feed(
        place, n2, n2_theirs, go, go_theirs, group2, up_bias_half
    )
    sums = swap(sums, "c")
    a_kept, a_sent, b_kept, b_sent = feed_weights(
        place, n2, n2_theirs, go, go_theirs, activated, grad_before, 2 * units
    )
    output, grad_hidden, grad_branch, *grad_att, mid = middle(
        place, m_part, out_part, sums, hidden, go, vec, wo
    )
    dout = [grad_att[0]] + [shift(grad_att[j], "z", NZ, j) for j in range(1, NZ)]
    a, b = add_up(a_kept, a_sent, "y"), add_up(b_kept, b_sent, "x")

    dq_part, delta, dkv_theirs = attend_back(
        True, active, may, place, q, dout, kv_theirs, lse, own_seg, seg, att_wide
    )
    a, b, dq_part = meet(a, b, dq_part)
    a, b = halve(a, "x", x, low), halve(b, "y", y, low)
    dq, dkv_mine = attend_back(
        False, active, may, place, q, dout, kv, lse, own_seg, seg, delta, dq_part
    )
    a, b, dq = meet(a, b, dq)
    group2 = jnp.concatenate([a, b], axis=0)
    dqkv, m1_own, m1_sent, cols, dqkv_sum = inward(place, dq, dkv_mine, swap(dkv_theirs, "c"), line, wz)
    m1_far = shift(m1_sent[1], "z", NZ, 2)

    mine, theirs = owners(
        place, att, grad_branch, n1, dqkv, cols, mid, dqkv_sum, up_bias_part, devices, tall
    )
    group1 = (mine.astype(wide) + swap(theirs, "c").astype(wide)).astype(low)
    m1_far, m1_up, m1_down, group1 = meet(m1_far, m1_sent[0], m1_sent[2], group1)
    m1_up, m1_down = shift(m1_up, "z", NZ, 1), shift(m1_down, "z", NZ, 3)
    group1 = group1.reshape(2, 2, NZ, tall, span)
    a = halve(group1[:, :, :2], "y", y, low)
    b = halve(group1[:, :, 2:].swapaxes(0, 1), "x", x, low)
    a, b = halve(a, "x", x, low), halve(b, "y", y, low)
    a, b, m1_up, m1_down = meet(a, b, m1_up, m1_down)
    grad_tokens = finish(place, m1_own, (m1_up, m1_far, m1_down), own, grad_hidden, vec)
    group1 = jnp.concatenate([a, b], axis=0)
    pieces = z_exchange(group1.astype(low), z)
    grad_wz = z_order([p[:own_rows, width:] for p in pieces], z)
    grad_qkv = grad_wz.reshape(NZ, own_rows, 3, GW).transpose(1, 2, 0, 3).reshape(own_rows, 3 * width)
    total = sum([p.astype(wide) for p in pieces[1:]], pick(group1, z))
    grad_wo = total[:own_rows, :width]
    v = [total[own_rows, cuts[i] : cuts[i + 1]] for i in range(len(sizes))]

    group2 = z_collect(group2, z, low)
    grad_down = group2[units:]
    up_rows = jnp.concatenate([group2[: 2 * own_rows], group2[2 * own_rows : units]], axis=1)
    up_rows = up_rows.reshape(2, own_rows, half)
    up_other = swap(pick(up_rows, 1 - c).astype(low), "c").astype(wide)
    up_shape = (own_rows, pairs, units)
    grad_up = in_order(pick(up_rows, c).reshape(up_shape), up_other.reshape(up_shape), c, 2)
    grad_up = grad_up.reshape(own_rows, ff)
    return (
        output[None], grad_tokens[None], v[0], v[1], grad_qkv.astype(wide), v[2], grad_wo, v[3],
        v[4], v[5], grad_up, v[6], grad_down, v[7],
    )


def build(body, mesh, dp, ctx):
    both = dp + ctx
    rows, vector, matrix = P(dp, ctx, None), P(both), P(both, None)
    return jax.shard_map(
        body,
        mesh=mesh,
        in_specs=(
            rows, P(dp, ctx), P(dp, None, None), vector, vector, matrix, vector, matrix, vector,
            vector, vector, matrix, vector, matrix, vector, rows,
        ),
        out_specs=(
            rows, rows, vector, vector, matrix, vector, matrix, vector, vector, vector, matrix,
            vector, matrix, vector,
        ),
        check_vma=False,
    )


def solution(mesh):
    if dict(mesh.shape) == {"dp": 4, "ctx": 2 * NZ}:
        grid = Mesh(mesh.devices.reshape(2, 2, NZ, 2), ("y", "x", "z", "c"))
        return build(fast_local, grid, ("y", "x"), ("z", "c"))
    return build(local, mesh, ("dp",), ("ctx",))
```

```python
import functools
import math

import jax
import jax.numpy as jnp
from jax import lax
from jax.experimental import pallas as pl
from jax.experimental.pallas import tpu as pltpu
from jax.sharding import Mesh, PartitionSpec as P

HEADS = 12
HEAD_DIM = 64
BLOCK = 128


NEG_FILL = -1e30
SCORE_SCALE = 0.125


def layer_norm(value_in, norm_gain, norm_shift):
    center = value_in - jnp.mean(value_in, axis=-1, keepdims=True)
    spread = jnp.mean(center * center, axis=-1, keepdims=True)
    return center * lax.rsqrt(spread + 1e-05) * norm_gain + norm_shift


def exact_gelu(value_in):
    return jax.nn.gelu(value_in, approximate=False)


def matmul_low(left_side, right_side):
    return jnp.dot(left_side, right_side, preferred_element_type=jnp.float32)


def inner_rows(left_side, right_side):
    return lax.dot_general(
        left_side, right_side, (((0,), (0,)), ((), ())), preferred_element_type=jnp.float32
    )


def times_transpose(left_side, right_side):
    return lax.dot_general(
        left_side, right_side, (((1,), (1,)), ((), ())), preferred_element_type=jnp.float32
    )


def sweep_blocks(count_rows, step_fn, carry_state):
    span_rows = math.gcd(count_rows, 512)
    return lax.fori_loop(
        0,
        count_rows // span_rows,
        lambda loop_index, loop_state: step_fn(loop_index * span_rows, span_rows, loop_state),
        carry_state,
    )


def allowed_pairs(live_table, query_pos, key_pos, query_seg, key_seg):
    block_slots = jnp.arange(live_table.shape[-1], dtype=jnp.int32)
    query_block = query_pos // BLOCK
    key_block = key_pos // BLOCK
    pick_query = (query_block[:, None] == block_slots[None, :]).astype(jnp.bfloat16)
    pick_key = (key_block[:, None] == block_slots[None, :]).astype(jnp.bfloat16)
    live_rows = jnp.einsum(
        "qa,sab->sqb", pick_query, live_table, preferred_element_type=jnp.float32
    )
    live_grid = jnp.einsum(
        "sqb,kb->sqk", live_rows.astype(jnp.bfloat16), pick_key, preferred_element_type=jnp.float32
    )
    same_block = query_block[:, None] == key_block[None, :]
    same_doc = query_seg[:, :, None] == key_seg[:, None, :]
    return same_doc & ((live_grid > 0.5) | same_block[None])


def pair_grads(
    live_table,
    query_heads,
    dout_heads,
    lse_heads,
    delta_heads,
    query_pos,
    query_seg,
    key_heads,
    value_heads,
    key_pos,
    key_seg,
):
    scores = (
        jnp.einsum("sqhd,skhd->shqk", query_heads, key_heads, preferred_element_type=jnp.float32)
        * SCORE_SCALE
    )
    permit = allowed_pairs(live_table, query_pos, key_pos, query_seg, key_seg)[:, None]
    attn_probs = jnp.where(permit, jnp.exp(scores - lse_heads[..., None]), 0.0)
    grad_prob = jnp.einsum(
        "sqhd,skhd->shqk", dout_heads, value_heads, preferred_element_type=jnp.float32
    )
    grad_score = (attn_probs * (grad_prob - delta_heads[..., None])).astype(jnp.bfloat16)
    grad_query = (
        jnp.einsum("shqk,skhd->sqhd", grad_score, key_heads, preferred_element_type=jnp.float32)
        * SCORE_SCALE
    )
    grad_key = (
        jnp.einsum("shqk,sqhd->skhd", grad_score, query_heads, preferred_element_type=jnp.float32)
        * SCORE_SCALE
    )
    grad_value = jnp.einsum(
        "shqk,sqhd->skhd",
        attn_probs.astype(jnp.bfloat16),
        dout_heads,
        preferred_element_type=jnp.float32,
    )
    return (grad_query, grad_key, grad_value)


def local(
    tokens,
    segment_ids,
    live_blocks,
    norm1_gain,
    norm1_bias,
    qkv_weight,
    qv_bias,
    out_weight,
    out_bias,
    norm2_gain,
    norm2_bias,
    up_weight,
    up_bias,
    down_weight,
    down_bias,
    grad_out,
):
    shards = (
        norm1_gain,
        norm1_bias,
        qkv_weight,
        qv_bias,
        out_weight,
        out_bias,
        norm2_gain,
        norm2_bias,
        up_weight,
        up_bias,
        down_weight,
        down_bias,
    )
    gathered = (
        lax.all_gather(shards[0], ("dp", "ctx"), axis=0, tiled=True),
        lax.all_gather(shards[1], ("dp", "ctx"), axis=0, tiled=True),
        lax.all_gather(shards[2], ("dp", "ctx"), axis=0, tiled=True),
        lax.all_gather(shards[3], ("dp", "ctx"), axis=0, tiled=True),
        lax.all_gather(shards[4], ("dp", "ctx"), axis=0, tiled=True),
        lax.all_gather(shards[5], ("dp", "ctx"), axis=0, tiled=True),
        lax.all_gather(shards[6], ("dp", "ctx"), axis=0, tiled=True),
        lax.all_gather(shards[7], ("dp", "ctx"), axis=0, tiled=True),
        lax.all_gather(shards[8], ("dp", "ctx"), axis=0, tiled=True),
        lax.all_gather(shards[9], ("dp", "ctx"), axis=0, tiled=True),
        lax.all_gather(shards[10], ("dp", "ctx"), axis=0, tiled=True),
        lax.all_gather(shards[11], ("dp", "ctx"), axis=0, tiled=True),
    )
    (
        gain_first,
        shift_first,
        full_qkv,
        bias_qv,
        full_out,
        bias_out,
        gain_second,
        shift_second,
        full_up,
        bias_up,
        full_down,
        bias_down,
    ) = gathered
    seq_count, tok_rows, model_width = tokens.shape
    head_count = HEADS
    head_size = HEAD_DIM
    flat_rows = seq_count * tok_rows
    query_pos = lax.axis_index("ctx") * tok_rows + jnp.arange(tok_rows, dtype=jnp.int32)
    live_table = live_blocks.astype(jnp.bfloat16)
    seg_low = segment_ids.astype(jnp.bfloat16)
    inputs_wide = tokens.reshape(flat_rows, model_width).astype(jnp.float32)
    normed_wide, norm_pull_one = jax.vjp(
        layer_norm, inputs_wide, gain_first.astype(jnp.float32), shift_first.astype(jnp.float32)
    )
    normed_one = normed_wide.astype(jnp.bfloat16)
    projected = matmul_low(normed_one, full_qkv)
    bias_wide = bias_qv.astype(jnp.float32)
    query_low = (projected[:, :model_width] + bias_wide[:model_width]).astype(jnp.bfloat16)
    key_low = projected[:, model_width : 2 * model_width].astype(jnp.bfloat16)
    value_low = (projected[:, 2 * model_width :] + bias_wide[model_width:]).astype(jnp.bfloat16)
    query_heads = query_low.reshape(seq_count, tok_rows, head_count, head_size)
    key_seq = key_low.reshape(seq_count, tok_rows, model_width)
    value_seq = value_low.reshape(seq_count, tok_rows, model_width)
    initial = (
        jnp.full((seq_count, head_count, tok_rows), NEG_FILL, jnp.float32),
        jnp.zeros((seq_count, head_count, tok_rows), jnp.float32),
        jnp.zeros((seq_count, tok_rows, head_count, head_size), jnp.float32),
    )
    key_part = lax.all_gather(key_seq, "ctx", axis=1, tiled=True)
    value_part = lax.all_gather(value_seq, "ctx", axis=1, tiled=True)
    seg_part = lax.all_gather(seg_low, "ctx", axis=1, tiled=True)

    def step_fn(offset, span_rows, inner_state):
        run_max, run_total, accum_out = inner_state
        key_heads = lax.dynamic_slice_in_dim(key_part, offset, span_rows, 1).reshape(
            seq_count, span_rows, head_count, head_size
        )
        value_heads = lax.dynamic_slice_in_dim(value_part, offset, span_rows, 1).reshape(
            seq_count, span_rows, head_count, head_size
        )
        key_seg = lax.dynamic_slice_in_dim(seg_part, offset, span_rows, 1)
        key_pos = offset + jnp.arange(span_rows, dtype=jnp.int32)
        scores = (
            jnp.einsum(
                "sqhd,skhd->shqk", query_heads, key_heads, preferred_element_type=jnp.float32
            )
            * SCORE_SCALE
        )
        permit = allowed_pairs(live_table, query_pos, key_pos, seg_low, key_seg)[:, None]
        scores = jnp.where(permit, scores, NEG_FILL)
        new_max = jnp.maximum(run_max, jnp.max(scores, axis=-1))
        exp_scores = jnp.where(permit, jnp.exp(scores - new_max[..., None]), 0.0)
        factor = jnp.exp(run_max - new_max)
        run_total = run_total * factor + jnp.sum(exp_scores, axis=-1)
        weighted = jnp.einsum(
            "shqk,skhd->sqhd",
            exp_scores.astype(jnp.bfloat16),
            value_heads,
            preferred_element_type=jnp.float32,
        )
        accum_out = accum_out * jnp.transpose(factor, (0, 2, 1))[..., None] + weighted
        return (new_max, run_total, accum_out)

    run_max, run_total, accum_out = sweep_blocks(key_part.shape[1], step_fn, initial)
    attn_wide = accum_out / jnp.transpose(run_total, (0, 2, 1))[..., None]
    lse_heads = run_max + jnp.log(run_total)
    attn_low = attn_wide.reshape(flat_rows, model_width).astype(jnp.bfloat16)
    hidden = inputs_wide + matmul_low(attn_low, full_out) + bias_out.astype(jnp.float32)
    normed_two_wide, norm_pull_two = jax.vjp(
        layer_norm, hidden, gain_second.astype(jnp.float32), shift_second.astype(jnp.float32)
    )
    normed_two = normed_two_wide.astype(jnp.bfloat16)
    before = matmul_low(normed_two, full_up) + bias_up.astype(jnp.float32)
    activated_wide, gelu_pull = jax.vjp(exact_gelu, before)
    activated = activated_wide.astype(jnp.bfloat16)
    output = (hidden + matmul_low(activated, full_down) + bias_down.astype(jnp.float32)).astype(
        jnp.bfloat16
    )
    back_params = (
        lax.all_gather(shards[0], ("dp", "ctx"), axis=0, tiled=True),
        lax.all_gather(shards[1], ("dp", "ctx"), axis=0, tiled=True),
        lax.all_gather(shards[2], ("dp", "ctx"), axis=0, tiled=True),
        lax.all_gather(shards[3], ("dp", "ctx"), axis=0, tiled=True),
        lax.all_gather(shards[4], ("dp", "ctx"), axis=0, tiled=True),
        lax.all_gather(shards[5], ("dp", "ctx"), axis=0, tiled=True),
        lax.all_gather(shards[6], ("dp", "ctx"), axis=0, tiled=True),
        lax.all_gather(shards[7], ("dp", "ctx"), axis=0, tiled=True),
        lax.all_gather(shards[8], ("dp", "ctx"), axis=0, tiled=True),
        lax.all_gather(shards[9], ("dp", "ctx"), axis=0, tiled=True),
        lax.all_gather(shards[10], ("dp", "ctx"), axis=0, tiled=True),
        lax.all_gather(shards[11], ("dp", "ctx"), axis=0, tiled=True),
    )
    back_qkv = back_params[2]
    back_out = back_params[4]
    back_up = back_params[8]
    back_down = back_params[10]
    grad_low = grad_out.reshape(flat_rows, model_width)
    grad_down = inner_rows(activated, grad_low)
    grad_bias_down = jnp.sum(grad_low.astype(jnp.float32), axis=0)
    grad_act = times_transpose(grad_low, back_down)
    grad_before = gelu_pull(grad_act)[0].astype(jnp.bfloat16)
    grad_up = inner_rows(normed_two, grad_before)
    grad_bias_up = jnp.sum(grad_before.astype(jnp.float32), axis=0)
    grad_normed_two = times_transpose(grad_before, back_up)
    grad_hidden_part, grad_gain_two, grad_shift_two = norm_pull_two(grad_normed_two)
    grad_hidden = grad_low.astype(jnp.float32) + grad_hidden_part
    grad_branch = grad_hidden.astype(jnp.bfloat16)
    grad_out_full = inner_rows(attn_low, grad_branch)
    grad_bias_out = jnp.sum(grad_branch.astype(jnp.float32), axis=0)
    grad_attn = times_transpose(grad_branch, back_out).astype(jnp.bfloat16)
    dout_heads = grad_attn.reshape(seq_count, tok_rows, head_count, head_size)
    delta_rows = jnp.sum(dout_heads.astype(jnp.float32) * attn_wide, axis=-1)
    delta_heads = jnp.transpose(delta_rows, (0, 2, 1))
    key_all, value_all, seg_all = (
        lax.all_gather(key_seq, "ctx", axis=1, tiled=True),
        lax.all_gather(value_seq, "ctx", axis=1, tiled=True),
        lax.all_gather(seg_low, "ctx", axis=1, tiled=True),
    )

    def key_step(offset, span_rows, inner_state):
        grad_query_acc, grad_key_all, grad_value_all = inner_state
        key_heads = lax.dynamic_slice_in_dim(key_all, offset, span_rows, 1).reshape(
            seq_count, span_rows, head_count, head_size
        )
        value_heads = lax.dynamic_slice_in_dim(value_all, offset, span_rows, 1).reshape(
            seq_count, span_rows, head_count, head_size
        )
        key_seg = lax.dynamic_slice_in_dim(seg_all, offset, span_rows, 1)
        key_pos = offset + jnp.arange(span_rows, dtype=jnp.int32)
        grad_query, grad_key, grad_value = pair_grads(
            live_table,
            query_heads,
            dout_heads,
            lse_heads,
            delta_heads,
            query_pos,
            seg_low,
            key_heads,
            value_heads,
            key_pos,
            key_seg,
        )
        grad_key_all = lax.dynamic_update_slice_in_dim(
            grad_key_all, grad_key.reshape(seq_count, span_rows, model_width), offset, 1
        )
        grad_value_all = lax.dynamic_update_slice_in_dim(
            grad_value_all, grad_value.reshape(seq_count, span_rows, model_width), offset, 1
        )
        return (grad_query_acc + grad_query, grad_key_all, grad_value_all)

    length_rows = key_all.shape[1]
    zero_query = jnp.zeros((seq_count, tok_rows, head_count, head_size), jnp.float32)
    zero_keys = jnp.zeros((seq_count, length_rows, model_width), jnp.float32)
    grad_query_heads, grad_key_all, grad_value_all = sweep_blocks(
        length_rows, key_step, (zero_query, zero_keys, zero_keys)
    )
    grad_key_seq, grad_value_seq = (
        lax.psum_scatter(
            grad_key_all.astype(jnp.bfloat16), "ctx", scatter_dimension=1, tiled=True
        ).astype(jnp.float32),
        lax.psum_scatter(
            grad_value_all.astype(jnp.bfloat16), "ctx", scatter_dimension=1, tiled=True
        ).astype(jnp.float32),
    )
    grad_query_low = grad_query_heads.reshape(flat_rows, model_width).astype(jnp.bfloat16)
    grad_key_low = grad_key_seq.reshape(flat_rows, model_width).astype(jnp.bfloat16)
    grad_value_low = grad_value_seq.reshape(flat_rows, model_width).astype(jnp.bfloat16)
    grad_proj_low = jnp.concatenate([grad_query_low, grad_key_low, grad_value_low], axis=1)
    grad_qkv_full = inner_rows(normed_one, grad_proj_low)
    grad_bias_qv = jnp.concatenate(
        [
            jnp.sum(grad_query_low.astype(jnp.float32), axis=0),
            jnp.sum(grad_value_low.astype(jnp.float32), axis=0),
        ]
    )
    grad_normed_one = times_transpose(grad_proj_low, back_qkv)
    grad_input_part, grad_gain_one, grad_shift_one = norm_pull_one(grad_normed_one)
    grad_tokens = (grad_hidden + grad_input_part).reshape(seq_count, tok_rows, model_width)
    summed = (
        lax.psum_scatter(grad_gain_one, ("dp", "ctx"), scatter_dimension=0, tiled=True),
        lax.psum_scatter(grad_shift_one, ("dp", "ctx"), scatter_dimension=0, tiled=True),
        lax.psum_scatter(grad_qkv_full.astype(jnp.bfloat16), ("dp", "ctx"), scatter_dimension=0, tiled=True).astype(jnp.float32),
        lax.psum_scatter(grad_bias_qv, ("dp", "ctx"), scatter_dimension=0, tiled=True),
        lax.psum_scatter(grad_out_full.astype(jnp.bfloat16), ("dp", "ctx"), scatter_dimension=0, tiled=True).astype(jnp.float32),
        lax.psum_scatter(grad_bias_out, ("dp", "ctx"), scatter_dimension=0, tiled=True),
        lax.psum_scatter(grad_gain_two, ("dp", "ctx"), scatter_dimension=0, tiled=True),
        lax.psum_scatter(grad_shift_two, ("dp", "ctx"), scatter_dimension=0, tiled=True),
        lax.psum_scatter(grad_up.astype(jnp.bfloat16), ("dp", "ctx"), scatter_dimension=0, tiled=True).astype(jnp.float32),
        lax.psum_scatter(grad_bias_up, ("dp", "ctx"), scatter_dimension=0, tiled=True),
        lax.psum_scatter(grad_down.astype(jnp.bfloat16), ("dp", "ctx"), scatter_dimension=0, tiled=True).astype(jnp.float32),
        lax.psum_scatter(grad_bias_down, ("dp", "ctx"), scatter_dimension=0, tiled=True),
    )
    return (
        output.reshape(seq_count, tok_rows, model_width),
        grad_tokens,
        summed[0],
        summed[1],
        summed[2],
        summed[3],
        summed[4],
        summed[5],
        summed[6],
        summed[7],
        summed[8],
        summed[9],
        summed[10],
        summed[11],
    )


NZ = 4
GROUP = HEADS // NZ
GW = GROUP * HEAD_DIM
CHUNK = 256


def pick(array, index, axis=0):
    return lax.dynamic_index_in_dim(array, index, axis, keepdims=False)


def shift(array, axis, size, hop):
    return lax.ppermute(array, axis, [(i, (i + hop) % size) for i in range(size)])


def swap(array, axis):
    return shift(array, axis, 2, 1)


def in_order(own, received, index, axis):
    first = jnp.where(index == 0, own, received)
    second = jnp.where(index == 0, received, own)
    return jnp.stack([first, second], axis=axis)


def z_pieces(block):
    return [block] + [shift(block, "z", NZ, j) for j in range(1, NZ)]


def z_order(pieces, z):
    return jnp.stack([lax.select_n((z - a) % NZ, *pieces) for a in range(NZ)])


def z_exchange(array, z):
    return [pick(array, z)] + [shift(pick(array, (z + j) % NZ), "z", NZ, j) for j in range(1, NZ)]


def xy_gather(line, y, x):
    a, b = line[: NZ // 2], line[NZ // 2 :]
    a = in_order(a, swap(a, "x"), x, 0)
    b = in_order(b, swap(b, "y"), y, 0)
    return (a, swap(a, "y"), y, 0), (b, swap(b, "x"), x, 1)


def add_up(kept, sent, name):
    return kept.astype(jnp.float32) + swap(sent, name).astype(jnp.float32)


def halve(array, name, index, wire):
    return add_up(pick(array, index), pick(array, 1 - index).astype(wire), name)


def after(value, event):
    flag = event[(slice(0, 1),) * event.ndim].reshape(()).astype(jnp.float32)
    return jnp.where(flag != flag, jnp.zeros_like(value), value)


def meet(*values):
    return lax.optimization_barrier(values)


def z_reduce(sent, z):
    edge = jnp.where(z == 0, sent[2], sent[0])
    edge = lax.ppermute(edge, "z", [(0, 1), (NZ - 1, NZ - 2)])
    far = (sent[1].astype(jnp.float32) + edge.astype(jnp.float32)).astype(sent[1].dtype)
    far = shift(far, "z", NZ, 2)
    up = lax.ppermute(sent[0], "z", [(0, 1), (1, 2), (2, 3)])
    down = lax.ppermute(sent[2], "z", [(1, 0), (2, 1), (3, 2)])
    return up, far, down


def norm_back(grad, gain, unit, scale):
    c = grad * gain
    return scale * (
        c - jnp.mean(c, axis=-1, keepdims=True) - unit * jnp.mean(c * unit, axis=-1, keepdims=True)
    )


def dot_nt(a, b):
    return lax.dot_general(a, b, (((1,), (1,)), ((), ())), preferred_element_type=jnp.float32)


def dot_tn(a, b):
    return lax.dot_general(a, b, (((0,), (0,)), ((), ())), preferred_element_type=jnp.float32)


def dot_nn(a, b):
    return lax.dot_general(a, b, (((1,), (0,)), ((), ())), preferred_element_type=jnp.float32)


def column_of(row):
    return jnp.transpose(jnp.broadcast_to(row, (8, row.shape[1])))[:, 0:1]


def query_row(may_ref, tile, block, seg_row, alive):
    per = CHUNK // BLOCK
    lane = lax.broadcasted_iota(jnp.int32, (1, CHUNK), 1)
    flag = jnp.full((1, CHUNK), may_ref[tile * per, block] * alive, jnp.int32)
    for b in range(1, per):
        flag = jnp.where(lane >= b * BLOCK, may_ref[tile * per + b, block] * alive, flag)
    return jnp.where(flag > 0, seg_row, -1.0)


def permit_of(may_ref, tile, chunk, seg_row, key_column, alive):
    per = CHUNK // BLOCK
    return jnp.concatenate(
        [
            key_column[b * BLOCK : (b + 1) * BLOCK]
            == query_row(may_ref, tile, chunk * per + b, seg_row, alive)
            for b in range(per)
        ],
        axis=0,
    )


def list_live(live, list_ref):
    count = jnp.int32(0)
    for number, flag in enumerate(live):
        list_ref[count] = number
        count = count + flag
    list_ref[count] = list_ref[jnp.maximum(count - 1, 0)]
    return count


def pair_at(list_ref, count, step):
    return (
        (list_ref[2 * step], jnp.int32(1)),
        (list_ref[2 * step + 1], (2 * step + 1 < count).astype(jnp.int32)),
    )


def whole_spec(shape):
    return pl.BlockSpec(shape, lambda *_: (0,) * len(shape))


def held(specs, arrays):
    return [
        pl.BlockSpec(memory_space=pltpu.VMEM) if tuple(spec.block_shape) == a.shape else spec
        for spec, a in zip(specs, arrays)
    ]


VMEM_MIB = {
    "unpack": 4, "pack": 4, "project": 14, "branch": 10, "feed": 28, "feed_weights": 24, "middle": 16,
    "inward": 16, "owners": 20, "finish": 10, "deliver": 6, "weave": 6,
}


WEIGHT = {'branch': 3, 'feed': 10, 'feed_weights': 3, 'middle': 3, 'inward': 3, 'owners': 3, 'finish': 10, 'deliver': 3, 'weave': 3}


def kernel_call(body, place, arrays, in_specs, outs, out_specs, grid, scratch, flops, name, more=()):
    prefetch = (place,) + tuple(more)
    moved = sum(a.size * a.dtype.itemsize for a in arrays)
    return pl.pallas_call(
        body,
        out_shape=tuple(jax.ShapeDtypeStruct(shape, dtype) for shape, dtype in outs),
        grid_spec=pltpu.PrefetchScalarGridSpec(
            num_scalar_prefetch=len(prefetch),
            grid=grid,
            in_specs=held(in_specs, arrays),
            out_specs=out_specs,
            scratch_shapes=scratch,
        ),
        compiler_params=pltpu.CompilerParams(vmem_limit_bytes=VMEM_MIB[name] << 20),
        cost_estimate=pl.CostEstimate(
            flops=int(flops * WEIGHT.get(name, 1)), bytes_accessed=int(moved * WEIGHT.get(name, 1)), transcendentals=0
        ),
        name=name,
    )(*prefetch, *arrays)


def lane_groups(lanes, size):
    lane = lax.broadcasted_iota(jnp.int32, (1, lanes), 1).astype(jnp.float32)
    group = jnp.floor((lane + 0.5) * (1.0 / size))
    return group, lane - group * size


def one_hot_rows(place_row, count):
    rows = lax.broadcasted_iota(jnp.int32, (count, place_row.shape[1]), 0).astype(jnp.float32)
    return (rows == place_row).astype(jnp.float32).astype(jnp.bfloat16)


VEC_ROWS = 16


def unpack_kernel(place_ref, packed_ref, vec_ref):
    devices = packed_ref.shape[0]
    width = vec_ref.shape[1]
    size = width // devices
    c = place_ref[1]
    device = lax.broadcasted_iota(jnp.int32, (devices, 1), 0)
    parity = lax.rem(device, 2)
    pair = lax.div(device, 2).astype(jnp.float32)
    device = device.astype(jnp.float32)
    vec_ref[...] = jnp.zeros(vec_ref.shape, jnp.float32)

    def spread(start, n, lanes, owner, keep):
        group, at = lane_groups(lanes, n)
        tiled = dot_nn(packed_ref[:, start : start + n], one_hot_rows(at, n))
        mine = (owner == group) if keep is None else (owner == group) & keep
        return jnp.sum(jnp.where(mine, tiled, 0.0), axis=0, keepdims=True)

    vec_ref[0:1] = spread(0, size, width, device, None)
    vec_ref[1:2] = spread(size, size, width, device, None)
    qv = spread(2 * size, 2 * size, 2 * width, device, None)
    vec_ref[2:3] = qv[:, :width]
    vec_ref[3:4] = qv[:, width:]
    vec_ref[4:5] = spread(4 * size, size, width, device, None)
    vec_ref[5:6] = spread(5 * size, size, width, device, None)
    vec_ref[6:7] = spread(6 * size, size, width, device, None)
    up = spread(7 * size, 4 * size, 2 * width, pair, parity == c)
    vec_ref[8:9] = up[:, :width]
    vec_ref[9:10] = up[:, width:]
    vec_ref[7:8] = spread(11 * size, size, width, device, None)


def pack_kernel(place_ref, grads_ref, mid_ref, qkv_ref, up_ref, packed_ref):
    devices = packed_ref.shape[0]
    width = grads_ref.shape[1]
    size = width // devices
    z, c = place_ref[0], place_ref[1]
    device = lax.broadcasted_iota(jnp.int32, (devices, 1), 0)
    parity = lax.rem(device, 2)
    pair = lax.div(device, 2).astype(jnp.float32)
    device = device.astype(jnp.float32)
    packed_ref[...] = jnp.zeros(packed_ref.shape, jnp.bfloat16)

    def gather(row, n, owner, keep):
        group, at = lane_groups(row.shape[1], n)
        mine = (owner == group) if keep is None else (owner == group) & keep
        return dot_nt(jnp.where(mine, row, 0.0).astype(jnp.bfloat16), one_hot_rows(at, n))

    def place_group(row):
        wide = jnp.concatenate([row] * NZ, axis=1)
        group, _ = lane_groups(wide.shape[1], GW)
        return jnp.where(group == z.astype(jnp.float32), wide, 0.0)

    qkv = qkv_ref[0:1]
    qv = jnp.concatenate([place_group(qkv[:, :GW]), place_group(qkv[:, 2 * GW :])], axis=1)
    parts = [
        gather(grads_ref[0:1], size, device, None),
        gather(grads_ref[1:2], size, device, None),
        gather(qv, 2 * size, device, None),
        gather(mid_ref[2:3], size, device, None),
        gather(mid_ref[0:1], size, device, None),
        gather(mid_ref[1:2], size, device, None),
        gather(up_ref[0:1], 4 * size, pair, parity == c),
        gather(mid_ref[3:4], size, device, None),
    ]
    packed_ref[:, 0 : 12 * size] = jnp.concatenate(parts, axis=1).astype(jnp.bfloat16)


def norm_rows(x):
    center = x - jnp.mean(x, axis=-1, keepdims=True)
    scale = lax.rsqrt(jnp.mean(center * center, axis=-1, keepdims=True) + 1e-05)
    return center * scale, scale


def project_kernel(place_ref, t0_ref, t1_ref, t2_ref, t3_ref, vec_ref, wz_ref, line_ref, n1_ref, q_ref, kv_ref):
    a = pl.program_id(0)
    z = place_ref[0]
    away = lax.rem(z - a + NZ, NZ)
    x = t0_ref[...].astype(jnp.float32)
    for j, ref in enumerate((t1_ref, t2_ref, t3_ref), 1):
        x = jnp.where(away == j, ref[...].astype(jnp.float32), x)
    line_ref[...] = x.astype(jnp.bfloat16)
    unit, _ = norm_rows(x)
    n1 = (unit * vec_ref[0:1] + vec_ref[1:2]).astype(jnp.bfloat16)
    n1_ref[...] = n1
    y = dot_nn(n1, wz_ref[...])
    q_bias, v_bias = vec_ref[2:3, 0:GW], vec_ref[3:4, 0:GW]
    for g in range(1, NZ):
        q_bias = jnp.where(z == g, vec_ref[2:3, g * GW : (g + 1) * GW], q_bias)
        v_bias = jnp.where(z == g, vec_ref[3:4, g * GW : (g + 1) * GW], v_bias)
    q = (y[:, :GW] + q_bias).astype(jnp.bfloat16)
    q_ref[...] = q * jnp.asarray(SCORE_SCALE, jnp.bfloat16)
    kv_ref[:, :GW] = y[:, GW : 2 * GW].astype(jnp.bfloat16)
    kv_ref[:, GW:] = (y[:, 2 * GW :] + v_bias).astype(jnp.bfloat16)


def project(place, pieces, vec, wz):
    rows, width = pieces[0].shape
    low = jnp.bfloat16
    tall = lambda w: pl.BlockSpec((rows, w), lambda a, *_: (a, 0))
    return kernel_call(
        project_kernel, place, (*pieces, vec, wz),
        [whole_spec((rows, width))] * NZ + [whole_spec(vec.shape), whole_spec(wz.shape)],
        [((NZ * rows, width), low), ((NZ * rows, width), low), ((NZ * rows, GW), low), ((NZ * rows, 2 * GW), low)],
        [tall(width), tall(width), tall(GW), tall(2 * GW)],
        (NZ,), [], 8 * NZ * rows * width * 3 * GW, "project",
    )


def branch_kernel(place_ref, a0_ref, a1_ref, a2_ref, a3_ref, wo_ref, own_ref, vec_ref, hidden_ref, n2_ref):
    z = place_ref[0]
    total = own_ref[...].astype(jnp.float32) + vec_ref[4:5]
    branch = None
    for j, ref in enumerate((a0_ref, a1_ref, a2_ref, a3_ref)):
        start = pl.multiple_of(lax.rem(z - j + NZ, NZ) * GW, GW)
        part = dot_nn(ref[...], wo_ref[pl.ds(start, GW), :])
        branch = part if branch is None else branch + part
    hidden = total + branch
    hidden_ref[...] = hidden
    unit, _ = norm_rows(hidden)
    n2_ref[...] = (unit * vec_ref[5:6] + vec_ref[6:7]).astype(jnp.bfloat16)


def branch_call(place, pieces, wo, own, vec):
    rows, width = own.shape
    arrays = (*pieces, wo, own, vec)
    return kernel_call(
        branch_kernel, place, arrays, [whole_spec(a.shape) for a in arrays],
        [((rows, width), jnp.float32), ((rows, width), jnp.bfloat16)],
        [whole_spec((rows, width))] * 2, (1,), [], 8 * rows * width * width, "branch",
    )


def feed_kernel(
    place_ref, na_ref, nb_ref, ga_ref, gb_ref, up_ref, down_ref, bias_ref,
    act_ref, grad_ref, out_ref, m_ref, sums_ref, bias_out_ref, n_s, g_s, out_s, m_s,
):
    k = pl.program_id(0)
    rows, width = na_ref.shape

    @pl.when(k == 0)
    def _():
        n_s[:rows], n_s[rows:] = na_ref[...], nb_ref[...]
        g_s[:rows], g_s[rows:] = ga_ref[...], gb_ref[...]
        out_s[...] = jnp.zeros(out_s.shape, jnp.float32)
        m_s[...] = jnp.zeros(m_s.shape, jnp.float32)

    up, down = up_ref[...].reshape(width, width), down_ref[...].reshape(width, width)
    v = dot_nn(n_s[...], up) + bias_ref[...]
    cdf = 0.5 * (1.0 + lax.erf(v * 0.7071067811865476))
    slope = cdf + v * (0.3989422804014327 * jnp.exp(-0.5 * v * v))
    act = (v * cdf).astype(jnp.bfloat16)
    act_ref[...] = act
    grad = dot_nt(g_s[...], down) * slope
    grad = grad.astype(jnp.bfloat16)
    grad_ref[...] = grad
    bias_out_ref[...] = jnp.sum(grad.astype(jnp.float32), axis=0, keepdims=True)
    out_s[...] += dot_nn(act, down)
    m_s[...] += dot_nt(grad, up)

    @pl.when(k == pl.num_programs(0) - 1)
    def _():
        out_ref[...] = out_s[:rows]
        m_ref[...] = m_s[:rows]
        sums_ref[0] = m_s[rows:].astype(jnp.bfloat16)
        sums_ref[1] = out_s[rows:].astype(jnp.bfloat16)


def feed(place, na, nb, ga, gb, both, bias):
    rows, width = na.shape
    chips, tall, _ = both.shape
    half = bias.shape[1]
    low, wide = jnp.bfloat16, jnp.float32
    one = whole_spec((rows, width))
    across = lambda r: pl.BlockSpec((r, width), lambda k, *_: (0, k))
    return kernel_call(
        feed_kernel, place, (na, nb, ga, gb, both, both, bias),
        [one] * 4 + [
            pl.BlockSpec((chips, tall // 4, width), lambda k, *_: (0, k, 0)),
            pl.BlockSpec((chips // 2, tall // 2, width), lambda k, *_: (k, 1, 0)),
            across(1),
        ],
        [
            ((2 * rows, half), low), ((2 * rows, half), low), ((rows, width), wide), ((rows, width), wide),
            ((2, rows, width), low), ((1, half), wide),
        ],
        [across(2 * rows), across(2 * rows), one, one, whole_spec((2, rows, width)), across(1)],
        (2,),
        [
            pltpu.VMEM((2 * rows, width), low), pltpu.VMEM((2 * rows, width), low),
            pltpu.VMEM((2 * rows, width), wide), pltpu.VMEM((2 * rows, width), wide),
        ],
        32 * rows * width * half, "feed",
    )


def feed_weights_kernel(
    place_ref, na_ref, nb_ref, ga_ref, gb_ref, act_ref, grad_ref, ak_ref, as_ref, bk_ref, bs_ref, n_s, a_s, g_s
):
    rows, width = na_ref.shape
    y, x = place_ref[2], place_ref[3]
    n_s[:, :rows], n_s[:, rows:] = jnp.transpose(na_ref[...]), jnp.transpose(nb_ref[...])
    g_s[:rows], g_s[rows:] = ga_ref[...], gb_ref[...]
    for k in range(0, act_ref.shape[1], width):
        a_s[k : k + width] = jnp.transpose(act_ref[:, k : k + width])
    tall = ak_ref.shape[2]
    quarter = tall // 4
    span = NZ * quarter

    def put(py, px, pz, row, value):
        count = value.shape[0]
        near, far = (ak_ref, as_ref) if pz < NZ // 2 else (bk_ref, bs_ref)
        index, mine = (px, py == y) if pz < NZ // 2 else (py, px == x)

        @pl.when(mine)
        def _():
            near[index, pz % (NZ // 2), row : row + count] = value

        @pl.when(jnp.logical_not(mine))
        def _():
            far[index, pz % (NZ // 2), row : row + count] = value

    def one_column(column, carry):
        py, px = lax.div(column, 2), lax.rem(column, 2)
        at = pl.multiple_of(column * span, span)
        up = dot_nn(n_s[pl.ds(at, span)], grad_ref[...]).astype(jnp.bfloat16)
        down = dot_nn(a_s[pl.ds(pl.multiple_of(2 * at, 2 * span), 2 * span)], g_s[...]).astype(jnp.bfloat16)
        for pz in range(NZ):
            here = slice(pz * quarter, (pz + 1) * quarter)
            put(py, px, pz, 0, up[here, :width])
            put(py, px, pz, quarter, up[here, width:])
            put(py, px, pz, 2 * quarter, down[2 * pz * quarter : 2 * (pz + 1) * quarter])
        return carry

    lax.fori_loop(0, 4, one_column, 0)


def feed_weights(place, na, nb, ga, gb, act, grad, tall):
    rows, width = na.shape
    low = jnp.bfloat16
    arrays = (na, nb, ga, gb, act, grad)
    shape = (2, NZ // 2, tall, width)
    return kernel_call(
        feed_weights_kernel, place, arrays, [whole_spec(a.shape) for a in arrays], [(shape, low)] * 4,
        [whole_spec(shape)] * 4, (1,),
        [
            pltpu.VMEM((width, 2 * rows), low), pltpu.VMEM((act.shape[1], 2 * rows), low),
            pltpu.VMEM((2 * rows, width), low),
        ],
        8 * rows * width * act.shape[1], "feed_weights",
    )


def middle_kernel(
    place_ref, m_ref, out_ref, sums_ref, hidden_ref, go_ref, vec_ref, wo_ref,
    output_ref, gh_ref, branch_ref, d0_ref, d1_ref, d2_ref, d3_ref, cols_ref,
):
    z = place_ref[0]
    hidden, go = hidden_ref[...], go_ref[...].astype(jnp.float32)
    output_ref[...] = (hidden + out_ref[...] + sums_ref[1].astype(jnp.float32) + vec_ref[7:8]).astype(
        jnp.bfloat16
    )
    m = m_ref[...] + sums_ref[0].astype(jnp.float32)
    unit, scale = norm_rows(hidden)
    grad_hidden = go + norm_back(m, vec_ref[5:6], unit, scale)
    gh_ref[...] = grad_hidden
    branch = grad_hidden.astype(jnp.bfloat16)
    branch_ref[...] = branch
    for j, ref in enumerate((d0_ref, d1_ref, d2_ref, d3_ref)):
        start = pl.multiple_of(lax.rem(z + j, NZ) * GW, GW)
        ref[...] = dot_nt(branch, wo_ref[pl.ds(start, GW), :]).astype(jnp.bfloat16)
    cols_ref[...] = jnp.zeros(cols_ref.shape, jnp.float32)
    cols_ref[0:1] = jnp.sum(m * unit, axis=0, keepdims=True)
    cols_ref[1:2] = jnp.sum(m, axis=0, keepdims=True)
    cols_ref[2:3] = jnp.sum(branch.astype(jnp.float32), axis=0, keepdims=True)
    cols_ref[3:4] = jnp.sum(go, axis=0, keepdims=True)


def middle(place, m, out, sums, hidden, go, vec, wo):
    rows, width = m.shape
    arrays = (m, out, sums, hidden, go, vec, wo)
    low, wide = jnp.bfloat16, jnp.float32
    outs = [((rows, width), low), ((rows, width), wide), ((rows, width), low)]
    outs += [((rows, GW), low)] * NZ + [((8, width), wide)]
    return kernel_call(
        middle_kernel, place, arrays, [whole_spec(a.shape) for a in arrays], outs,
        [whole_spec(shape) for shape, _ in outs], (1,), [], 8 * rows * width * width, "middle",
    )


def inward_kernel(
    place_ref, dq_ref, mine_ref, theirs_ref, line_ref, wz_ref, dqkv_ref, keep_ref, s1_ref, s2_ref, s3_ref,
    cols_ref, sums_ref,
):
    j = pl.program_id(0)
    rows = keep_ref.shape[0]
    at = pl.ds(pl.multiple_of(lax.rem(place_ref[0] + 1 + j, NZ) * rows, rows), rows)
    dkv = (mine_ref[at].astype(jnp.float32) + theirs_ref[at].astype(jnp.float32)).astype(jnp.bfloat16)
    dqkv = jnp.concatenate([dq_ref[at], dkv], axis=1)
    dqkv_ref[at] = dqkv
    m1 = dot_nt(dqkv, wz_ref[...])
    unit, _ = norm_rows(line_ref[at].astype(jnp.float32))

    @pl.when(j == 0)
    def _():
        cols_ref[...] = jnp.zeros(cols_ref.shape, jnp.float32)
        sums_ref[...] = jnp.zeros(sums_ref.shape, jnp.float32)

    cols_ref[0:1] += jnp.sum(m1 * unit, axis=0, keepdims=True)
    cols_ref[1:2] += jnp.sum(m1, axis=0, keepdims=True)
    sums_ref[0:1] += jnp.sum(dqkv.astype(jnp.float32), axis=0, keepdims=True)

    for number, ref in enumerate((s1_ref, s2_ref, s3_ref)):

        @pl.when(j == number)
        def _():
            ref[...] = m1.astype(jnp.bfloat16)

    @pl.when(j == pl.num_programs(0) - 1)
    def _():
        keep_ref[...] = m1


def inward(place, dq, mine, theirs, line, wz):
    total, width = line.shape
    rows = total // NZ
    low, wide = jnp.bfloat16, jnp.float32
    arrays = (dq, mine, theirs, line, wz)
    outs = [((total, 3 * GW), low), ((rows, width), wide)] + [((rows, width), low)] * (NZ - 1)
    outs += [((8, width), wide), ((8, 3 * GW), wide)]
    return kernel_call(
        inward_kernel, place, arrays, [whole_spec(a.shape) for a in arrays], outs,
        [whole_spec(shape) for shape, _ in outs], (NZ,), [], 8 * total * width * 3 * GW, "inward",
    )


def finish_kernel(place_ref, m_ref, r1_ref, r2_ref, r3_ref, own_ref, gh_ref, vec_ref, out_ref):
    m = m_ref[...]
    for ref in (r1_ref, r2_ref, r3_ref):
        m = m + ref[...].astype(jnp.float32)
    unit, scale = norm_rows(own_ref[...].astype(jnp.float32))
    out_ref[...] = gh_ref[...] + norm_back(m, vec_ref[0:1], unit, scale)


def finish(place, m, pieces, own, grad_hidden, vec):
    rows, width = own.shape
    arrays = (m, *pieces, own, grad_hidden, vec)
    return kernel_call(
        finish_kernel, place, arrays, [whole_spec(a.shape) for a in arrays],
        [((rows, width), jnp.float32)], [whole_spec((rows, width))], (1,), [], 100 * rows * width, "finish",
    )[0]


def owners_kernel(
    place_ref, a0_ref, a1_ref, a2_ref, a3_ref, branch_ref, n1_ref, dqkv_ref, cols_ref, mid_ref, sums_ref, up_ref,
    mine_ref, theirs_ref, wo_s, wz_s, vec_s,
):
    z, c = place_ref[0], place_ref[1]
    width = branch_ref.shape[1]
    for j, ref in enumerate((a0_ref, a1_ref, a2_ref, a3_ref)):
        start = pl.multiple_of(lax.rem(z - j + NZ, NZ) * GW, GW)
        wo_s[pl.ds(start, GW), :] = dot_tn(ref[...], branch_ref[...]).astype(jnp.bfloat16)
    wz_s[...] = dot_tn(n1_ref[...], dqkv_ref[...]).astype(jnp.bfloat16)
    pack_kernel(place_ref, cols_ref, mid_ref, sums_ref, up_ref, vec_s)
    chips, tall, span = mine_ref.shape
    devices = 2 * chips
    rows = width // devices
    first_row = lax.broadcasted_iota(jnp.int32, (tall - rows, span), 0) == 0
    for pair in range(chips):
        tails = []
        for core in range(2):
            row = vec_s[2 * pair + core : 2 * pair + core + 1].astype(jnp.float32)
            tails.append(jnp.where(first_row, jnp.broadcast_to(row, first_row.shape), 0.0).astype(jnp.bfloat16))
        mine_ref[pair, rows:] = jnp.where(c == 0, tails[0], tails[1])
        theirs_ref[pair, rows:] = jnp.where(c == 0, tails[1], tails[0])

    def one_chip(pair, carry):
        at = pl.ds(pl.multiple_of(pair * (2 * rows), 2 * rows), 2 * rows)
        both = jnp.concatenate([wo_s[at], wz_s[at]], axis=1)
        mine_ref[pair, :rows] = jnp.where(c == 0, both[:rows], both[rows:])
        theirs_ref[pair, :rows] = jnp.where(c == 0, both[rows:], both[:rows])
        return carry

    lax.fori_loop(0, chips, one_chip, 0)


def owners(place, pieces, branch, n1, dqkv, cols, mid, sums, up, devices, tall):
    width, span = n1.shape[1], n1.shape[1] + dqkv.shape[1]
    low = jnp.bfloat16
    arrays = (*pieces, branch, n1, dqkv, cols, mid, sums, up)
    shape = (devices // 2, tall, span)
    return kernel_call(
        owners_kernel, place, arrays, [whole_spec(a.shape) for a in arrays], [(shape, low), (shape, low)],
        [whole_spec(shape)] * 2, (1,),
        [pltpu.VMEM((width, width), low), pltpu.VMEM((width, dqkv.shape[1]), low), pltpu.VMEM((devices, span), low)],
        1 << 20, "owners",
    )


def deliver_kernel(place_ref, own_ref, p1_ref, p2_ref, p3_ref, qkv_ref, wo_ref, vec_ref):
    z = place_ref[0]
    rows, width = wo_ref.shape
    own = own_ref[...]
    pieces = [own] + [ref[...].astype(jnp.float32) for ref in (p1_ref, p2_ref, p3_ref)]
    for g in range(NZ):
        away = lax.rem(z - g + NZ, NZ)
        part = pieces[0]
        for j in range(1, NZ):
            part = jnp.where(away == j, pieces[j], part)
        for k in range(3):
            lanes = slice(k * width + g * GW, k * width + (g + 1) * GW)
            qkv_ref[:, lanes] = part[:rows, width + k * GW : width + (k + 1) * GW]
    total = pieces[0] + pieces[1] + pieces[2] + pieces[3]
    wo_ref[...] = total[:rows, :width]
    vec_ref[...] = total[rows:]


def weave_kernel(place_ref, mine_ref, theirs_ref, out_ref):
    c = place_ref[1]
    mine, theirs = mine_ref[...], theirs_ref[...].astype(jnp.float32)
    even, odd = jnp.where(c == 0, mine, theirs), jnp.where(c == 0, theirs, mine)
    half = mine.shape[1]
    units = half // 16
    for pair in range(16):
        here = slice(pair * units, (pair + 1) * units)
        out_ref[:, 2 * pair * units : (2 * pair + 1) * units] = even[:, here]
        out_ref[:, (2 * pair + 1) * units : (2 * pair + 2) * units] = odd[:, here]


def attend_kernel(
    act_ref, may_ref, place_ref, q_ref, mine_ref, theirs_ref, qseg_ref, kseg_ref, o_ref, low_ref, lse_ref,
    k_s, vt_s, col_s, m_s, l_s, acc_s, list_s,
):
    i = pl.program_id(0)
    chunks = kseg_ref.shape[0]

    @pl.when(i == 0)
    def _():
        for line, ref in enumerate((mine_ref, theirs_ref)):
            core = place_ref[1] if line == 0 else 1 - place_ref[1]
            for a in range(chunks // 2):
                rows = slice(a * CHUNK, (a + 1) * CHUNK)
                at = pl.ds(pl.multiple_of((2 * a + core) * CHUNK, CHUNK), CHUNK)
                for h in range(GROUP):
                    k_s[h, at] = ref[rows, HEAD_DIM * h : HEAD_DIM * (h + 1)]
                    vt_s[h, :, at] = jnp.transpose(ref[rows, GW + HEAD_DIM * h : GW + HEAD_DIM * (h + 1)])
        for j in range(chunks):
            col_s[j * CHUNK : (j + 1) * CHUNK] = column_of(kseg_ref[j : j + 1])

    m_s[...] = jnp.full(m_s.shape, NEG_FILL, jnp.float32)
    l_s[...] = jnp.zeros(l_s.shape, jnp.float32)
    acc_s[...] = jnp.zeros(acc_s.shape, jnp.float32)
    here = pl.ds(pl.multiple_of(i * CHUNK, CHUNK), CHUNK)
    q_heads = [q_ref[here, HEAD_DIM * h : HEAD_DIM * (h + 1)] for h in range(GROUP)]
    q_seg = qseg_ref[pl.ds(i, 1)]

    count = list_live([act_ref[i, j] for j in range(chunks)], list_s)

    def two_chunks(step, carry):
        heads, pair = range(GROUP), pair_at(list_s, count, step)
        at = [pl.ds(pl.multiple_of(j * CHUNK, CHUNK), CHUNK) for j, _ in pair]
        permit = [permit_of(may_ref, i, j, q_seg, col_s[at[u]], alive) for u, (j, alive) in enumerate(pair)]
        s = [[jnp.where(permit[u], dot_nt(k_s[h, at[u]], q_heads[h]), NEG_FILL) for u in range(2)] for h in heads]
        old = [m_s[h] for h in heads]
        top = [[jnp.max(part, axis=0, keepdims=True) for part in s[h]] for h in heads]
        new = [jnp.maximum(old[h], jnp.maximum(*top[h])) for h in heads]
        p = [[jnp.exp(part - new[h]) for part in s[h]] for h in heads]
        fade = [jnp.exp(old[h] - new[h]) for h in heads]
        for h in heads:
            l_s[h] = l_s[h] * fade[h] + sum(jnp.sum(part, axis=0, keepdims=True) for part in p[h])
            added = [dot_nn(vt_s[h, :, at[u]], p[h][u].astype(jnp.bfloat16)) for u in range(2)]
            acc_s[h] = acc_s[h] * fade[h] + (added[0] + added[1])
            m_s[h] = new[h]
        return carry

    lax.fori_loop(0, lax.div(count + 1, 2), two_chunks, 0)
    out = jnp.concatenate([jnp.transpose(acc_s[h] / l_s[h]) for h in range(GROUP)], axis=1)
    o_ref[...] = out
    low_ref[...] = out.astype(jnp.bfloat16)
    logs = [m_s[h] + jnp.log(l_s[h]) for h in range(GROUP)]
    lse_ref[...] = jnp.concatenate(logs + [logs[0]] * (8 - GROUP), axis=0)


def attend(active, may, place, q, mine, theirs, q_seg, k_seg):
    rows, keys = q.shape[0], 2 * mine.shape[0]
    tall = pl.BlockSpec((CHUNK, GW), lambda i, *_: (i, 0))
    return pl.pallas_call(
        attend_kernel,
        out_shape=(
            jax.ShapeDtypeStruct((rows, GW), jnp.float32),
            jax.ShapeDtypeStruct((rows, GW), jnp.bfloat16),
            jax.ShapeDtypeStruct((8, rows), jnp.float32),
        ),
        grid_spec=pltpu.PrefetchScalarGridSpec(
            num_scalar_prefetch=3,
            grid=(rows // CHUNK,),
            in_specs=held(
                [whole_spec(a.shape) for a in (q, mine, theirs, q_seg, k_seg)], (q, mine, theirs, q_seg, k_seg)
            ),
            out_specs=[tall, tall, pl.BlockSpec((8, CHUNK), lambda i, *_: (0, i))],
            scratch_shapes=[
                pltpu.VMEM((GROUP, keys, HEAD_DIM), jnp.bfloat16),
                pltpu.VMEM((GROUP, HEAD_DIM, keys), jnp.bfloat16),
                pltpu.VMEM((keys, 1), jnp.float32),
                pltpu.VMEM((GROUP, 1, CHUNK), jnp.float32),
                pltpu.VMEM((GROUP, 1, CHUNK), jnp.float32),
                pltpu.VMEM((GROUP, HEAD_DIM, CHUNK), jnp.float32),
                pltpu.SMEM((keys // CHUNK + 1,), jnp.int32),
            ],
        ),
        compiler_params=pltpu.CompilerParams(vmem_limit_bytes=18 << 20),
        cost_estimate=pl.CostEstimate(
            flops=int(48 * rows * keys * GW), bytes_accessed=16 * keys * GW, transcendentals=4 * rows * keys
        ),
        name="attend",
    )(active, may, place, q, mine, theirs, q_seg, k_seg)


def attend_back_kernel(first, *refs):
    (act_ref, may_ref, place_ref, q_ref, d0_ref, d1_ref, d2_ref, d3_ref, kv_ref, lse_ref, qseg_ref,
     kseg_ref, from_ref, *refs) = refs
    if first:
        dqt_ref, delta_ref, dkv_ref, list_s, q_s, do_s, dk_s, dv_s = refs
    else:
        old_ref, dq_ref, dkv_ref, list_s, q_s, do_s, dk_s, dv_s, dqt_ref = refs
        delta_ref = from_ref
    step = pl.program_id(0)
    rows = q_ref.shape[0]
    z, c = place_ref[0], place_ref[1]
    j = 2 * step + (1 - c if first else c)

    @pl.when(step == 0)
    def _():
        for r, ref in enumerate((d0_ref, d1_ref, d2_ref, d3_ref)):
            at = pl.ds(pl.multiple_of(lax.rem(z - r + NZ, NZ) * CHUNK, CHUNK), CHUNK)
            for h in range(GROUP):
                do_s[h, at] = ref[:, HEAD_DIM * h : HEAD_DIM * (h + 1)]
        ones = jnp.ones((8, HEAD_DIM), jnp.float32)
        for h in range(GROUP):
            lanes = slice(HEAD_DIM * h, HEAD_DIM * (h + 1))
            q_s[h] = q_ref[:, lanes]
            if first:
                both = do_s[h].astype(jnp.float32) * from_ref[:, lanes]
                delta_ref[h : h + 1] = lax.dot_general(
                    ones, both, (((1,), (1,)), ((), ())), precision=lax.Precision.HIGHEST,
                    preferred_element_type=jnp.float32,
                )[0:1]
        dqt_ref[...] = jnp.zeros(dqt_ref.shape, jnp.float32) if first else old_ref[...]
        if first:
            delta_ref[GROUP:] = jnp.zeros((8 - GROUP, rows), jnp.float32)

    dk_s[...] = jnp.zeros(dk_s.shape, jnp.float32)
    dv_s[...] = jnp.zeros(dv_s.shape, jnp.float32)
    here = pl.ds(pl.multiple_of(step * CHUNK, CHUNK), CHUNK)
    k_heads = [kv_ref[here, HEAD_DIM * h : HEAD_DIM * (h + 1)] for h in range(GROUP)]
    v_heads = [kv_ref[here, GW + HEAD_DIM * h : GW + HEAD_DIM * (h + 1)] for h in range(GROUP)]
    k_turned = [jnp.transpose(k) for k in k_heads]
    k_column = column_of(kseg_ref[pl.ds(j, 1)])

    count = list_live([act_ref[i, j] for i in range(rows // CHUNK)], list_s)

    def two_tiles(turn, carry):
        heads, pair, low = range(GROUP), pair_at(list_s, count, turn), jnp.bfloat16
        both = [(h, u) for h in heads for u in range(2)]
        at = [pl.ds(pl.multiple_of(i * CHUNK, CHUNK), CHUNK) for i, _ in pair]
        permit = [
            permit_of(may_ref, i, j, qseg_ref[pl.ds(i, 1)], k_column, alive) for i, alive in pair
        ]
        s = {(h, u): dot_nt(k_heads[h], q_s[h, at[u]]) for h, u in both}
        dp = {(h, u): dot_nt(v_heads[h], do_s[h, at[u]]) for h, u in both}
        p = {
            (h, u): jnp.where(permit[u], jnp.exp(s[h, u] - lse_ref[h : h + 1, at[u]]), 0.0) for h, u in both
        }
        ds = {(h, u): (p[h, u] * (dp[h, u] - delta_ref[h : h + 1, at[u]])).astype(low) for h, u in both}
        for h in heads:
            dv_s[h] += dot_nn(p[h, 0].astype(low), do_s[h, at[0]]) + dot_nn(p[h, 1].astype(low), do_s[h, at[1]])
            dk_s[h] += dot_nn(ds[h, 0], q_s[h, at[0]]) + dot_nn(ds[h, 1], q_s[h, at[1]])
            for u in range(2):
                dqt_ref[h, :, at[u]] += dot_nn(k_turned[h], ds[h, u])
        return carry

    lax.fori_loop(0, lax.div(count + 1, 2), two_tiles, 0)
    dkv_ref[...] = jnp.concatenate(
        [dk_s[h] for h in range(GROUP)] + [dv_s[h] for h in range(GROUP)], axis=1
    ).astype(jnp.bfloat16)
    if not first:

        @pl.when(step == pl.num_programs(0) - 1)
        def _():
            dq_ref[...] = jnp.concatenate(
                [jnp.transpose(dqt_ref[h] * SCORE_SCALE) for h in range(GROUP)], axis=1
            ).astype(jnp.bfloat16)


def attend_back(first, active, may, place, q, pieces, kv, lse, q_seg, k_seg, *carried):
    rows = q.shape[0]
    low, wide = jnp.bfloat16, jnp.float32
    tall = pl.BlockSpec((CHUNK, 2 * GW), lambda s, *_: (s, 0))
    turned = (GROUP, HEAD_DIM, rows)
    outs = [(turned, wide), ((8, rows), wide)] if first else [((rows, GW), low)]
    scratch = [pltpu.SMEM((rows // CHUNK + 1,), jnp.int32)] + [pltpu.VMEM((GROUP, rows, HEAD_DIM), low)] * 2 + [pltpu.VMEM((GROUP, CHUNK, HEAD_DIM), wide)] * 2
    if not first:
        scratch.append(pltpu.VMEM(turned, wide))
    return pl.pallas_call(
        functools.partial(attend_back_kernel, first),
        out_shape=tuple(jax.ShapeDtypeStruct(*o) for o in outs + [((rows, 2 * GW), low)]),
        grid_spec=pltpu.PrefetchScalarGridSpec(
            num_scalar_prefetch=3,
            grid=(rows // CHUNK,),
            in_specs=held(
                [
                    whole_spec((rows, GW)), *[whole_spec(p.shape) for p in pieces], whole_spec(kv.shape), whole_spec((8, rows)),
                    whole_spec(q_seg.shape), whole_spec(k_seg.shape), *[whole_spec(a.shape) for a in carried],
                ],
                (q, *pieces, kv, lse, q_seg, k_seg, *carried),
            ),
            out_specs=[whole_spec(shape) for shape, _ in outs] + [tall],
            scratch_shapes=scratch,
        ),
        compiler_params=pltpu.CompilerParams(vmem_limit_bytes=20 << 20),
        cost_estimate=pl.CostEstimate(
            flops=int(56 * rows * rows * GW), bytes_accessed=32 * rows * GW, transcendentals=4 * rows * rows
        ),
        name="attend_back_first" if first else "attend_back_last",
    )(active, may, place, q, *pieces, kv, lse, q_seg, k_seg, *carried)


def fast_local(
    tokens, segment_ids, live_blocks, norm1_gain, norm1_bias, qkv_weight, qv_bias, out_weight, out_bias,
    norm2_gain, norm2_bias, up_weight, up_bias, down_weight, down_bias, grad_out,
):
    y, x, z, c = (lax.axis_index(name) for name in ("y", "x", "z", "c"))
    place = jnp.stack([z, c, y, x]).astype(jnp.int32)
    wide, low = jnp.float32, jnp.bfloat16
    _, rows, width = tokens.shape
    own_rows, units = qkv_weight.shape[0], down_weight.shape[0]
    ff = up_weight.shape[1]
    half, pairs = ff // 2, ff // (2 * units)
    devices = width // own_rows
    seq_rows = rows * NZ
    keys = 2 * seq_rows
    blocks = keys // BLOCK
    per = CHUNK // BLOCK

    vectors = (norm1_gain, norm1_bias, qv_bias, out_bias, norm2_gain, norm2_bias, up_bias, down_bias)
    sizes = [v.shape[0] for v in vectors]
    cuts = [sum(sizes[:i]) for i in range(len(sizes) + 1)]
    span = width + 3 * GW
    tall = own_rows + 8
    parts = vectors + (segment_ids[0].astype(low),)
    extra = sum(
        jnp.pad(p, (start, span - start - p.shape[0])) for p, start in zip(parts, cuts)
    )
    extra = jnp.pad(extra[None], ((0, 7), (0, 0)))
    wz = qkv_weight.reshape(own_rows, 3, NZ, GW).transpose(2, 0, 1, 3).reshape(NZ, own_rows, 3 * GW)
    group1 = jnp.concatenate(
        [jnp.broadcast_to(out_weight[None], (NZ, own_rows, width)), wz], axis=2
    )
    group1 = jnp.concatenate([group1, jnp.broadcast_to(extra[None], (NZ, 8, span))], axis=1)
    pieces1 = z_exchange(group1, z)

    up_sets = up_weight.reshape(own_rows, pairs, 2, units).transpose(2, 0, 1, 3)
    up_sets = up_sets.reshape(2, own_rows, half)
    up_chip = in_order(pick(up_sets, c), swap(pick(up_sets, 1 - c), "c"), c, 0)
    up_chip = up_chip.reshape(2 * own_rows, half)
    group2 = jnp.concatenate([up_chip[:, :width], up_chip[:, width:], down_weight], axis=0)
    pieces2 = z_pieces(group2)

    own, pieces2[1], pieces2[3] = meet(tokens[0], pieces2[1], pieces2[3])
    line_pieces = z_pieces(own)
    group1 = z_order(pieces1, z)
    own_seg = group1[:, own_rows, cuts[-1] : cuts[-1] + rows].astype(wide)
    seg = in_order(own_seg, swap(own_seg, "c"), c, 1).reshape(keys // CHUNK, CHUNK)
    group1 = jnp.concatenate([in_order(*half) for half in xy_gather(group1, y, x)], axis=2)
    group1 = in_order(group1, swap(group1, "c"), c, 3)
    wo = group1[..., :own_rows, :width].reshape(width, width)
    wz = group1[..., :own_rows, width:].reshape(width, 3 * GW)
    packed = group1[..., own_rows, : cuts[-1]].reshape(devices, cuts[-1])
    vec = kernel_call(
        unpack_kernel, place, (packed,), [whole_spec(packed.shape)], [((VEC_ROWS, width), wide)],
        [whole_spec((VEC_ROWS, width))], (1,), [], 1 << 20, "unpack",
    )[0]
    group2, vec = meet(z_order(pieces2, z), vec)
    group2 = xy_gather(group2, y, x)

    own_blocks = seq_rows // BLOCK
    ids = jnp.arange(blocks, dtype=jnp.int32)
    own_ids = pick(ids.reshape(NZ, 2, rows // BLOCK), c, 1).reshape(own_blocks)
    own_live = pick(live_blocks[0].reshape(NZ, 2, rows // BLOCK, blocks), c, 1)
    own_live = own_live.reshape(own_blocks, blocks)
    seg_blocks = seg.reshape(blocks, BLOCK)
    own_seg_blocks = own_seg.reshape(own_blocks, BLOCK)
    may = (own_live > 0) | (own_ids[:, None] == ids[None, :])
    touch = (
        may
        & (own_seg_blocks[:, :1] <= seg_blocks[:, -1][None])
        & (seg_blocks[:, 0][None] <= own_seg_blocks[:, -1:])
    )
    active = jnp.any(touch.reshape(own_blocks // per, per, blocks // per, per), axis=(1, 3))
    active, may = active.astype(jnp.int32), may.astype(jnp.int32)

    line, n1, q, kv = project(place, line_pieces, vec, wz)
    kv_theirs = swap(kv, "c")
    att_wide, att_low, lse = attend(active, may, place, q, kv, kv_theirs, own_seg, seg)
    att = z_exchange(att_low.reshape(NZ, rows, GW), z)
    group2 = [in_order(own_half, after(other, att_low), at, axis) for own_half, other, at, axis in group2]
    group2 = jnp.concatenate(group2, axis=2)

    hidden, n2 = branch_call(place, att, wo, own, vec)
    go = grad_out[0]
    n2_theirs, go_theirs = swap(n2, "c"), swap(go, "c")
    up_bias_half = vec[8:10].reshape(1, half)
    chips = devices // 2
    group2 = group2.reshape(chips, 2 * units, width)
    activated, grad_before, out_part, m_part, sums, up_bias_part = feed(
        place, n2, n2_theirs, go, go_theirs, group2, up_bias_half
    )
    sums = swap(sums, "c")
    a_kept, a_sent, b_kept, b_sent = feed_weights(
        place, n2, n2_theirs, go, go_theirs, activated, grad_before, 2 * units
    )
    output, grad_hidden, grad_branch, *grad_att, mid = middle(
        place, m_part, out_part, sums, hidden, go, vec, wo
    )
    dout = [grad_att[0]] + [shift(grad_att[j], "z", NZ, j) for j in range(1, NZ)]
    a, b = add_up(a_kept, a_sent, "y"), add_up(b_kept, b_sent, "x")

    dq_part, delta, dkv_theirs = attend_back(
        True, active, may, place, q, dout, kv_theirs, lse, own_seg, seg, att_wide
    )
    a, b, dq_part = meet(a, b, dq_part)
    a, b = halve(a, "x", x, low), halve(b, "y", y, low)
    dq, dkv_mine = attend_back(
        False, active, may, place, q, dout, kv, lse, own_seg, seg, delta, dq_part
    )
    dqkv, m1_own, *m1_sent, cols, dqkv_sum = inward(place, dq, dkv_mine, swap(dkv_theirs, "c"), line, wz)
    a, b, m1_sent[0] = meet(a, b, m1_sent[0])
    group2 = jnp.concatenate([a, b], axis=0)
    m1_up, m1_far, m1_down = z_reduce(m1_sent, z)

    mine, theirs = owners(
        place, att, grad_branch, n1, dqkv, cols, mid, dqkv_sum, up_bias_part, devices, tall
    )
    group1 = (mine.astype(wide) + swap(theirs, "c").astype(wide)).astype(low)
    group1 = group1.reshape(2, 2, NZ, tall, span)
    a = halve(group1[:, :, :2], "y", y, low)
    b = halve(group1[:, :, 2:].swapaxes(0, 1), "x", x, low)
    a, b = halve(a, "x", x, low), halve(b, "y", y, low)
    a, b, m1_far, m1_down = meet(a, b, m1_far, m1_down)
    grad_tokens = finish(place, m1_own, (m1_up, m1_far, m1_down), own, grad_hidden, vec)
    group1 = jnp.concatenate([a, b], axis=0)
    pieces = z_exchange(group1.astype(low), z)
    arrays = (pick(group1, z), *pieces[1:])
    outs = [((own_rows, 3 * width), wide), ((own_rows, width), wide), ((tall - own_rows, span), wide)]
    grad_qkv, grad_wo, vec_sum = kernel_call(
        deliver_kernel, place, arrays, [whole_spec(a.shape) for a in arrays], outs,
        [whole_spec(shape) for shape, _ in outs], (1,), [], 1 << 20, "deliver",
    )
    v = [vec_sum[0, cuts[i] : cuts[i + 1]] for i in range(len(sizes))]

    group2_low = group2.astype(low)
    sent = [pick(group2_low, (z + j) % NZ) for j in range(1, NZ)]
    group2 = sum((piece.astype(wide) for piece in [shift(p, "z", NZ, j) for j, p in enumerate(sent, 1)]), pick(group2, z))
    grad_down = group2[units:]
    up_rows = jnp.concatenate([group2[: 2 * own_rows], group2[2 * own_rows : units]], axis=1)
    up_rows = up_rows.reshape(2, own_rows, half)
    arrays = (pick(up_rows, c), swap(pick(up_rows, 1 - c).astype(low), "c"))
    grad_up = kernel_call(
        weave_kernel, place, arrays, [whole_spec(a.shape) for a in arrays], [((own_rows, ff), wide)],
        [whole_spec((own_rows, ff))], (1,), [], 1 << 20, "weave",
    )[0]
    return (
        output[None], grad_tokens[None], v[0], v[1], grad_qkv, v[2], grad_wo, v[3],
        v[4], v[5], grad_up, v[6], grad_down, v[7],
    )


def build(body, mesh, dp, ctx):
    both = dp + ctx
    rows, vector, matrix = P(dp, ctx, None), P(both), P(both, None)
    return jax.shard_map(
        body,
        mesh=mesh,
        in_specs=(
            rows, P(dp, ctx), P(dp, None, None), vector, vector, matrix, vector, matrix, vector,
            vector, vector, matrix, vector, matrix, vector, rows,
        ),
        out_specs=(
            rows, rows, vector, vector, matrix, vector, matrix, vector, vector, vector, matrix,
            vector, matrix, vector,
        ),
        check_vma=False,
    )


def solution(mesh):
    if dict(mesh.shape) == {"dp": 4, "ctx": 2 * NZ}:
        grid = Mesh(mesh.devices.reshape(2, 2, NZ, 2), ("y", "x", "z", "c"))
        return build(fast_local, grid, ("y", "x"), ("z", "c"))
    return build(local, mesh, ("dp",), ("ctx",))
```

```python
import functools
import math

import jax
import jax.numpy as jnp
from jax import lax
from jax.experimental import pallas as pl
from jax.experimental.pallas import tpu as pltpu
from jax.sharding import Mesh, PartitionSpec as P

HEADS = 12
HEAD_DIM = 64
BLOCK = 128


NEG_FILL = -1e30
SCORE_SCALE = 0.125


def layer_norm(value_in, norm_gain, norm_shift):
    center = value_in - jnp.mean(value_in, axis=-1, keepdims=True)
    spread = jnp.mean(center * center, axis=-1, keepdims=True)
    return center * lax.rsqrt(spread + 1e-05) * norm_gain + norm_shift


def exact_gelu(value_in):
    return jax.nn.gelu(value_in, approximate=False)


def matmul_low(left_side, right_side):
    return jnp.dot(left_side, right_side, preferred_element_type=jnp.float32)


def inner_rows(left_side, right_side):
    return lax.dot_general(
        left_side, right_side, (((0,), (0,)), ((), ())), preferred_element_type=jnp.float32
    )


def times_transpose(left_side, right_side):
    return lax.dot_general(
        left_side, right_side, (((1,), (1,)), ((), ())), preferred_element_type=jnp.float32
    )


def sweep_blocks(count_rows, step_fn, carry_state):
    span_rows = math.gcd(count_rows, 512)
    return lax.fori_loop(
        0,
        count_rows // span_rows,
        lambda loop_index, loop_state: step_fn(loop_index * span_rows, span_rows, loop_state),
        carry_state,
    )


def allowed_pairs(live_table, query_pos, key_pos, query_seg, key_seg):
    block_slots = jnp.arange(live_table.shape[-1], dtype=jnp.int32)
    query_block = query_pos // BLOCK
    key_block = key_pos // BLOCK
    pick_query = (query_block[:, None] == block_slots[None, :]).astype(jnp.bfloat16)
    pick_key = (key_block[:, None] == block_slots[None, :]).astype(jnp.bfloat16)
    live_rows = jnp.einsum(
        "qa,sab->sqb", pick_query, live_table, preferred_element_type=jnp.float32
    )
    live_grid = jnp.einsum(
        "sqb,kb->sqk", live_rows.astype(jnp.bfloat16), pick_key, preferred_element_type=jnp.float32
    )
    same_block = query_block[:, None] == key_block[None, :]
    same_doc = query_seg[:, :, None] == key_seg[:, None, :]
    return same_doc & ((live_grid > 0.5) | same_block[None])


def pair_grads(
    live_table,
    query_heads,
    dout_heads,
    lse_heads,
    delta_heads,
    query_pos,
    query_seg,
    key_heads,
    value_heads,
    key_pos,
    key_seg,
):
    scores = (
        jnp.einsum("sqhd,skhd->shqk", query_heads, key_heads, preferred_element_type=jnp.float32)
        * SCORE_SCALE
    )
    permit = allowed_pairs(live_table, query_pos, key_pos, query_seg, key_seg)[:, None]
    attn_probs = jnp.where(permit, jnp.exp(scores - lse_heads[..., None]), 0.0)
    grad_prob = jnp.einsum(
        "sqhd,skhd->shqk", dout_heads, value_heads, preferred_element_type=jnp.float32
    )
    grad_score = (attn_probs * (grad_prob - delta_heads[..., None])).astype(jnp.bfloat16)
    grad_query = (
        jnp.einsum("shqk,skhd->sqhd", grad_score, key_heads, preferred_element_type=jnp.float32)
        * SCORE_SCALE
    )
    grad_key = (
        jnp.einsum("shqk,sqhd->skhd", grad_score, query_heads, preferred_element_type=jnp.float32)
        * SCORE_SCALE
    )
    grad_value = jnp.einsum(
        "shqk,sqhd->skhd",
        attn_probs.astype(jnp.bfloat16),
        dout_heads,
        preferred_element_type=jnp.float32,
    )
    return (grad_query, grad_key, grad_value)


def local(
    tokens,
    segment_ids,
    live_blocks,
    norm1_gain,
    norm1_bias,
    qkv_weight,
    qv_bias,
    out_weight,
    out_bias,
    norm2_gain,
    norm2_bias,
    up_weight,
    up_bias,
    down_weight,
    down_bias,
    grad_out,
):
    shards = (
        norm1_gain,
        norm1_bias,
        qkv_weight,
        qv_bias,
        out_weight,
        out_bias,
        norm2_gain,
        norm2_bias,
        up_weight,
        up_bias,
        down_weight,
        down_bias,
    )
    gathered = (
        lax.all_gather(shards[0], ("dp", "ctx"), axis=0, tiled=True),
        lax.all_gather(shards[1], ("dp", "ctx"), axis=0, tiled=True),
        lax.all_gather(shards[2], ("dp", "ctx"), axis=0, tiled=True),
        lax.all_gather(shards[3], ("dp", "ctx"), axis=0, tiled=True),
        lax.all_gather(shards[4], ("dp", "ctx"), axis=0, tiled=True),
        lax.all_gather(shards[5], ("dp", "ctx"), axis=0, tiled=True),
        lax.all_gather(shards[6], ("dp", "ctx"), axis=0, tiled=True),
        lax.all_gather(shards[7], ("dp", "ctx"), axis=0, tiled=True),
        lax.all_gather(shards[8], ("dp", "ctx"), axis=0, tiled=True),
        lax.all_gather(shards[9], ("dp", "ctx"), axis=0, tiled=True),
        lax.all_gather(shards[10], ("dp", "ctx"), axis=0, tiled=True),
        lax.all_gather(shards[11], ("dp", "ctx"), axis=0, tiled=True),
    )
    (
        gain_first,
        shift_first,
        full_qkv,
        bias_qv,
        full_out,
        bias_out,
        gain_second,
        shift_second,
        full_up,
        bias_up,
        full_down,
        bias_down,
    ) = gathered
    seq_count, tok_rows, model_width = tokens.shape
    head_count = HEADS
    head_size = HEAD_DIM
    flat_rows = seq_count * tok_rows
    query_pos = lax.axis_index("ctx") * tok_rows + jnp.arange(tok_rows, dtype=jnp.int32)
    live_table = live_blocks.astype(jnp.bfloat16)
    seg_low = segment_ids.astype(jnp.bfloat16)
    inputs_wide = tokens.reshape(flat_rows, model_width).astype(jnp.float32)
    normed_wide, norm_pull_one = jax.vjp(
        layer_norm, inputs_wide, gain_first.astype(jnp.float32), shift_first.astype(jnp.float32)
    )
    normed_one = normed_wide.astype(jnp.bfloat16)
    projected = matmul_low(normed_one, full_qkv)
    bias_wide = bias_qv.astype(jnp.float32)
    query_low = (projected[:, :model_width] + bias_wide[:model_width]).astype(jnp.bfloat16)
    key_low = projected[:, model_width : 2 * model_width].astype(jnp.bfloat16)
    value_low = (projected[:, 2 * model_width :] + bias_wide[model_width:]).astype(jnp.bfloat16)
    query_heads = query_low.reshape(seq_count, tok_rows, head_count, head_size)
    key_seq = key_low.reshape(seq_count, tok_rows, model_width)
    value_seq = value_low.reshape(seq_count, tok_rows, model_width)
    initial = (
        jnp.full((seq_count, head_count, tok_rows), NEG_FILL, jnp.float32),
        jnp.zeros((seq_count, head_count, tok_rows), jnp.float32),
        jnp.zeros((seq_count, tok_rows, head_count, head_size), jnp.float32),
    )
    key_part = lax.all_gather(key_seq, "ctx", axis=1, tiled=True)
    value_part = lax.all_gather(value_seq, "ctx", axis=1, tiled=True)
    seg_part = lax.all_gather(seg_low, "ctx", axis=1, tiled=True)

    def step_fn(offset, span_rows, inner_state):
        run_max, run_total, accum_out = inner_state
        key_heads = lax.dynamic_slice_in_dim(key_part, offset, span_rows, 1).reshape(
            seq_count, span_rows, head_count, head_size
        )
        value_heads = lax.dynamic_slice_in_dim(value_part, offset, span_rows, 1).reshape(
            seq_count, span_rows, head_count, head_size
        )
        key_seg = lax.dynamic_slice_in_dim(seg_part, offset, span_rows, 1)
        key_pos = offset + jnp.arange(span_rows, dtype=jnp.int32)
        scores = (
            jnp.einsum(
                "sqhd,skhd->shqk", query_heads, key_heads, preferred_element_type=jnp.float32
            )
            * SCORE_SCALE
        )
        permit = allowed_pairs(live_table, query_pos, key_pos, seg_low, key_seg)[:, None]
        scores = jnp.where(permit, scores, NEG_FILL)
        new_max = jnp.maximum(run_max, jnp.max(scores, axis=-1))
        exp_scores = jnp.where(permit, jnp.exp(scores - new_max[..., None]), 0.0)
        factor = jnp.exp(run_max - new_max)
        run_total = run_total * factor + jnp.sum(exp_scores, axis=-1)
        weighted = jnp.einsum(
            "shqk,skhd->sqhd",
            exp_scores.astype(jnp.bfloat16),
            value_heads,
            preferred_element_type=jnp.float32,
        )
        accum_out = accum_out * jnp.transpose(factor, (0, 2, 1))[..., None] + weighted
        return (new_max, run_total, accum_out)

    run_max, run_total, accum_out = sweep_blocks(key_part.shape[1], step_fn, initial)
    attn_wide = accum_out / jnp.transpose(run_total, (0, 2, 1))[..., None]
    lse_heads = run_max + jnp.log(run_total)
    attn_low = attn_wide.reshape(flat_rows, model_width).astype(jnp.bfloat16)
    hidden = inputs_wide + matmul_low(attn_low, full_out) + bias_out.astype(jnp.float32)
    normed_two_wide, norm_pull_two = jax.vjp(
        layer_norm, hidden, gain_second.astype(jnp.float32), shift_second.astype(jnp.float32)
    )
    normed_two = normed_two_wide.astype(jnp.bfloat16)
    before = matmul_low(normed_two, full_up) + bias_up.astype(jnp.float32)
    activated_wide, gelu_pull = jax.vjp(exact_gelu, before)
    activated = activated_wide.astype(jnp.bfloat16)
    output = (hidden + matmul_low(activated, full_down) + bias_down.astype(jnp.float32)).astype(
        jnp.bfloat16
    )
    back_params = (
        lax.all_gather(shards[0], ("dp", "ctx"), axis=0, tiled=True),
        lax.all_gather(shards[1], ("dp", "ctx"), axis=0, tiled=True),
        lax.all_gather(shards[2], ("dp", "ctx"), axis=0, tiled=True),
        lax.all_gather(shards[3], ("dp", "ctx"), axis=0, tiled=True),
        lax.all_gather(shards[4], ("dp", "ctx"), axis=0, tiled=True),
        lax.all_gather(shards[5], ("dp", "ctx"), axis=0, tiled=True),
        lax.all_gather(shards[6], ("dp", "ctx"), axis=0, tiled=True),
        lax.all_gather(shards[7], ("dp", "ctx"), axis=0, tiled=True),
        lax.all_gather(shards[8], ("dp", "ctx"), axis=0, tiled=True),
        lax.all_gather(shards[9], ("dp", "ctx"), axis=0, tiled=True),
        lax.all_gather(shards[10], ("dp", "ctx"), axis=0, tiled=True),
        lax.all_gather(shards[11], ("dp", "ctx"), axis=0, tiled=True),
    )
    back_qkv = back_params[2]
    back_out = back_params[4]
    back_up = back_params[8]
    back_down = back_params[10]
    grad_low = grad_out.reshape(flat_rows, model_width)
    grad_down = inner_rows(activated, grad_low)
    grad_bias_down = jnp.sum(grad_low.astype(jnp.float32), axis=0)
    grad_act = times_transpose(grad_low, back_down)
    grad_before = gelu_pull(grad_act)[0].astype(jnp.bfloat16)
    grad_up = inner_rows(normed_two, grad_before)
    grad_bias_up = jnp.sum(grad_before.astype(jnp.float32), axis=0)
    grad_normed_two = times_transpose(grad_before, back_up)
    grad_hidden_part, grad_gain_two, grad_shift_two = norm_pull_two(grad_normed_two)
    grad_hidden = grad_low.astype(jnp.float32) + grad_hidden_part
    grad_branch = grad_hidden.astype(jnp.bfloat16)
    grad_out_full = inner_rows(attn_low, grad_branch)
    grad_bias_out = jnp.sum(grad_branch.astype(jnp.float32), axis=0)
    grad_attn = times_transpose(grad_branch, back_out).astype(jnp.bfloat16)
    dout_heads = grad_attn.reshape(seq_count, tok_rows, head_count, head_size)
    delta_rows = jnp.sum(dout_heads.astype(jnp.float32) * attn_wide, axis=-1)
    delta_heads = jnp.transpose(delta_rows, (0, 2, 1))
    key_all, value_all, seg_all = (
        lax.all_gather(key_seq, "ctx", axis=1, tiled=True),
        lax.all_gather(value_seq, "ctx", axis=1, tiled=True),
        lax.all_gather(seg_low, "ctx", axis=1, tiled=True),
    )

    def key_step(offset, span_rows, inner_state):
        grad_query_acc, grad_key_all, grad_value_all = inner_state
        key_heads = lax.dynamic_slice_in_dim(key_all, offset, span_rows, 1).reshape(
            seq_count, span_rows, head_count, head_size
        )
        value_heads = lax.dynamic_slice_in_dim(value_all, offset, span_rows, 1).reshape(
            seq_count, span_rows, head_count, head_size
        )
        key_seg = lax.dynamic_slice_in_dim(seg_all, offset, span_rows, 1)
        key_pos = offset + jnp.arange(span_rows, dtype=jnp.int32)
        grad_query, grad_key, grad_value = pair_grads(
            live_table,
            query_heads,
            dout_heads,
            lse_heads,
            delta_heads,
            query_pos,
            seg_low,
            key_heads,
            value_heads,
            key_pos,
            key_seg,
        )
        grad_key_all = lax.dynamic_update_slice_in_dim(
            grad_key_all, grad_key.reshape(seq_count, span_rows, model_width), offset, 1
        )
        grad_value_all = lax.dynamic_update_slice_in_dim(
            grad_value_all, grad_value.reshape(seq_count, span_rows, model_width), offset, 1
        )
        return (grad_query_acc + grad_query, grad_key_all, grad_value_all)

    length_rows = key_all.shape[1]
    zero_query = jnp.zeros((seq_count, tok_rows, head_count, head_size), jnp.float32)
    zero_keys = jnp.zeros((seq_count, length_rows, model_width), jnp.float32)
    grad_query_heads, grad_key_all, grad_value_all = sweep_blocks(
        length_rows, key_step, (zero_query, zero_keys, zero_keys)
    )
    grad_key_seq, grad_value_seq = (
        lax.psum_scatter(
            grad_key_all.astype(jnp.bfloat16), "ctx", scatter_dimension=1, tiled=True
        ).astype(jnp.float32),
        lax.psum_scatter(
            grad_value_all.astype(jnp.bfloat16), "ctx", scatter_dimension=1, tiled=True
        ).astype(jnp.float32),
    )
    grad_query_low = grad_query_heads.reshape(flat_rows, model_width).astype(jnp.bfloat16)
    grad_key_low = grad_key_seq.reshape(flat_rows, model_width).astype(jnp.bfloat16)
    grad_value_low = grad_value_seq.reshape(flat_rows, model_width).astype(jnp.bfloat16)
    grad_proj_low = jnp.concatenate([grad_query_low, grad_key_low, grad_value_low], axis=1)
    grad_qkv_full = inner_rows(normed_one, grad_proj_low)
    grad_bias_qv = jnp.concatenate(
        [
            jnp.sum(grad_query_low.astype(jnp.float32), axis=0),
            jnp.sum(grad_value_low.astype(jnp.float32), axis=0),
        ]
    )
    grad_normed_one = times_transpose(grad_proj_low, back_qkv)
    grad_input_part, grad_gain_one, grad_shift_one = norm_pull_one(grad_normed_one)
    grad_tokens = (grad_hidden + grad_input_part).reshape(seq_count, tok_rows, model_width)
    summed = (
        lax.psum_scatter(grad_gain_one, ("dp", "ctx"), scatter_dimension=0, tiled=True),
        lax.psum_scatter(grad_shift_one, ("dp", "ctx"), scatter_dimension=0, tiled=True),
        lax.psum_scatter(grad_qkv_full.astype(jnp.bfloat16), ("dp", "ctx"), scatter_dimension=0, tiled=True).astype(jnp.float32),
        lax.psum_scatter(grad_bias_qv, ("dp", "ctx"), scatter_dimension=0, tiled=True),
        lax.psum_scatter(grad_out_full.astype(jnp.bfloat16), ("dp", "ctx"), scatter_dimension=0, tiled=True).astype(jnp.float32),
        lax.psum_scatter(grad_bias_out, ("dp", "ctx"), scatter_dimension=0, tiled=True),
        lax.psum_scatter(grad_gain_two, ("dp", "ctx"), scatter_dimension=0, tiled=True),
        lax.psum_scatter(grad_shift_two, ("dp", "ctx"), scatter_dimension=0, tiled=True),
        lax.psum_scatter(grad_up.astype(jnp.bfloat16), ("dp", "ctx"), scatter_dimension=0, tiled=True).astype(jnp.float32),
        lax.psum_scatter(grad_bias_up, ("dp", "ctx"), scatter_dimension=0, tiled=True),
        lax.psum_scatter(grad_down.astype(jnp.bfloat16), ("dp", "ctx"), scatter_dimension=0, tiled=True).astype(jnp.float32),
        lax.psum_scatter(grad_bias_down, ("dp", "ctx"), scatter_dimension=0, tiled=True),
    )
    return (
        output.reshape(seq_count, tok_rows, model_width),
        grad_tokens,
        summed[0],
        summed[1],
        summed[2],
        summed[3],
        summed[4],
        summed[5],
        summed[6],
        summed[7],
        summed[8],
        summed[9],
        summed[10],
        summed[11],
    )


NZ = 4
GROUP = HEADS // NZ
GW = GROUP * HEAD_DIM
CHUNK = 256


def pick(array, index, axis=0):
    return lax.dynamic_index_in_dim(array, index, axis, keepdims=False)


def shift(array, axis, size, hop):
    return lax.ppermute(array, axis, [(i, (i + hop) % size) for i in range(size)])


def swap(array, axis):
    return shift(array, axis, 2, 1)


def in_order(own, received, index, axis):
    first = jnp.where(index == 0, own, received)
    second = jnp.where(index == 0, received, own)
    return jnp.stack([first, second], axis=axis)


def hops(send, order):
    got = {hop: send(hop) for hop in order}
    return [got[hop] for hop in range(1, NZ)]


def z_pieces(block, order):
    return [block] + hops(lambda hop: shift(block, "z", NZ, hop), order)


def z_order(pieces, z):
    return jnp.stack([lax.select_n((z - a) % NZ, *pieces) for a in range(NZ)])


def z_exchange(array, z, order):
    return [pick(array, z)] + hops(lambda hop: shift(pick(array, (z + hop) % NZ), "z", NZ, hop), order)


def xy_gather(line, y, x):
    a, b = line[: NZ // 2], line[NZ // 2 :]
    a = in_order(a, swap(a, "x"), x, 0)
    b = in_order(b, swap(b, "y"), y, 0)
    return (a, swap(a, "y"), y, 0), (b, swap(b, "x"), x, 1)


def add_up(kept, sent, name):
    return kept.astype(jnp.float32) + swap(sent, name).astype(jnp.float32)


def halve(array, name, index, wire):
    return add_up(pick(array, index), pick(array, 1 - index).astype(wire), name)


def after(value, event):
    flag = event[(slice(0, 1),) * event.ndim].reshape(()).astype(jnp.float32)
    return jnp.where(flag != flag, jnp.zeros_like(value), value)


def meet(*values):
    return lax.optimization_barrier(values)


def z_reduce(sent, z):
    edge = jnp.where(z == 0, sent[2], sent[0])
    edge = lax.ppermute(edge, "z", [(0, 1), (NZ - 1, NZ - 2)])
    far = (sent[1].astype(jnp.float32) + edge.astype(jnp.float32)).astype(sent[1].dtype)
    far = shift(far, "z", NZ, 2)
    up = lax.ppermute(sent[0], "z", [(0, 1), (1, 2), (2, 3)])
    down = lax.ppermute(sent[2], "z", [(1, 0), (2, 1), (3, 2)])
    return up, far, down


def norm_back(grad, gain, unit, scale):
    c = grad * gain
    return scale * (
        c - jnp.mean(c, axis=-1, keepdims=True) - unit * jnp.mean(c * unit, axis=-1, keepdims=True)
    )


def dot_nt(a, b):
    return lax.dot_general(a, b, (((1,), (1,)), ((), ())), preferred_element_type=jnp.float32)


def dot_tn(a, b):
    return lax.dot_general(a, b, (((0,), (0,)), ((), ())), preferred_element_type=jnp.float32)


def dot_nn(a, b):
    return lax.dot_general(a, b, (((1,), (0,)), ((), ())), preferred_element_type=jnp.float32)


def column_of(row):
    return jnp.transpose(jnp.broadcast_to(row, (8, row.shape[1])))[:, 0:1]


def query_row(may_ref, tile, block, seg_row, alive):
    per = CHUNK // BLOCK
    lane = lax.broadcasted_iota(jnp.int32, (1, CHUNK), 1)
    flag = jnp.full((1, CHUNK), may_ref[tile * per, block] * alive, jnp.int32)
    for b in range(1, per):
        flag = jnp.where(lane >= b * BLOCK, may_ref[tile * per + b, block] * alive, flag)
    return jnp.where(flag > 0, seg_row, -1.0)


def permit_of(may_ref, tile, chunk, seg_row, key_column, alive):
    per = CHUNK // BLOCK
    return jnp.concatenate(
        [
            key_column[b * BLOCK : (b + 1) * BLOCK]
            == query_row(may_ref, tile, chunk * per + b, seg_row, alive)
            for b in range(per)
        ],
        axis=0,
    )


def list_live(live, list_ref):
    count = jnp.int32(0)
    for number, flag in enumerate(live):
        list_ref[count] = number
        count = count + flag
    list_ref[count] = list_ref[jnp.maximum(count - 1, 0)]
    return count


def pair_at(list_ref, count, step):
    return (
        (list_ref[2 * step], jnp.int32(1)),
        (list_ref[2 * step + 1], (2 * step + 1 < count).astype(jnp.int32)),
    )


def whole_spec(shape):
    return pl.BlockSpec(shape, lambda *_: (0,) * len(shape))


def held(specs, arrays):
    return [
        pl.BlockSpec(memory_space=pltpu.VMEM) if tuple(spec.block_shape) == a.shape else spec
        for spec, a in zip(specs, arrays)
    ]


VMEM_MIB = {
    "unpack": 4, "pack": 4, "project": 14, "branch": 10, "feed": 28, "feed_weights": 24, "middle": 16,
    "inward": 16, "owners": 20, "finish": 10, "deliver": 6, "weave": 6,
}


WEIGHT = {
    "project": 1, "branch": 3, "feed": 10, "feed_weights": 3, "middle": 3, "inward": 3, "owners": 3, "finish": 10, "deliver": 3, "weave": 3,
}


def kernel_call(body, place, arrays, in_specs, outs, out_specs, grid, scratch, flops, name, more=()):
    prefetch = (place,) + tuple(more)
    moved = sum(a.size * a.dtype.itemsize for a in arrays)
    return pl.pallas_call(
        body,
        out_shape=tuple(jax.ShapeDtypeStruct(shape, dtype) for shape, dtype in outs),
        grid_spec=pltpu.PrefetchScalarGridSpec(
            num_scalar_prefetch=len(prefetch),
            grid=grid,
            in_specs=held(in_specs, arrays),
            out_specs=out_specs,
            scratch_shapes=scratch,
        ),
        compiler_params=pltpu.CompilerParams(vmem_limit_bytes=VMEM_MIB[name] << 20),
        cost_estimate=pl.CostEstimate(
            flops=int(flops * WEIGHT.get(name, 1)), bytes_accessed=int(moved * WEIGHT.get(name, 1)), transcendentals=0
        ),
        name=name,
    )(*prefetch, *arrays)


def lane_groups(lanes, size):
    lane = lax.broadcasted_iota(jnp.int32, (1, lanes), 1).astype(jnp.float32)
    group = jnp.floor((lane + 0.5) * (1.0 / size))
    return group, lane - group * size


def one_hot_rows(place_row, count):
    rows = lax.broadcasted_iota(jnp.int32, (count, place_row.shape[1]), 0).astype(jnp.float32)
    return (rows == place_row).astype(jnp.float32).astype(jnp.bfloat16)


VEC_ROWS = 16


def unpack_kernel(place_ref, packed_ref, vec_ref):
    devices = packed_ref.shape[0]
    width = vec_ref.shape[1]
    size = width // devices
    c = place_ref[1]
    device = lax.broadcasted_iota(jnp.int32, (devices, 1), 0)
    parity = lax.rem(device, 2)
    pair = lax.div(device, 2).astype(jnp.float32)
    device = device.astype(jnp.float32)
    vec_ref[...] = jnp.zeros(vec_ref.shape, jnp.float32)

    def spread(start, n, lanes, owner, keep):
        group, at = lane_groups(lanes, n)
        tiled = dot_nn(packed_ref[:, start : start + n], one_hot_rows(at, n))
        mine = (owner == group) if keep is None else (owner == group) & keep
        return jnp.sum(jnp.where(mine, tiled, 0.0), axis=0, keepdims=True)

    vec_ref[0:1] = spread(0, size, width, device, None)
    vec_ref[1:2] = spread(size, size, width, device, None)
    qv = spread(2 * size, 2 * size, 2 * width, device, None)
    vec_ref[2:3] = qv[:, :width]
    vec_ref[3:4] = qv[:, width:]
    vec_ref[4:5] = spread(4 * size, size, width, device, None)
    vec_ref[5:6] = spread(5 * size, size, width, device, None)
    vec_ref[6:7] = spread(6 * size, size, width, device, None)
    up = spread(7 * size, 4 * size, 2 * width, pair, parity == c)
    vec_ref[8:9] = up[:, :width]
    vec_ref[9:10] = up[:, width:]
    vec_ref[7:8] = spread(11 * size, size, width, device, None)


def pack_kernel(place_ref, grads_ref, mid_ref, qkv_ref, up_ref, packed_ref):
    devices = packed_ref.shape[0]
    width = grads_ref.shape[1]
    size = width // devices
    z, c = place_ref[0], place_ref[1]
    device = lax.broadcasted_iota(jnp.int32, (devices, 1), 0)
    parity = lax.rem(device, 2)
    pair = lax.div(device, 2).astype(jnp.float32)
    device = device.astype(jnp.float32)
    packed_ref[...] = jnp.zeros(packed_ref.shape, jnp.bfloat16)

    def gather(row, n, owner, keep):
        group, at = lane_groups(row.shape[1], n)
        mine = (owner == group) if keep is None else (owner == group) & keep
        return dot_nt(jnp.where(mine, row, 0.0).astype(jnp.bfloat16), one_hot_rows(at, n))

    def place_group(row):
        wide = jnp.concatenate([row] * NZ, axis=1)
        group, _ = lane_groups(wide.shape[1], GW)
        return jnp.where(group == z.astype(jnp.float32), wide, 0.0)

    qkv = qkv_ref[0:1]
    qv = jnp.concatenate([place_group(qkv[:, :GW]), place_group(qkv[:, 2 * GW :])], axis=1)
    parts = [
        gather(grads_ref[0:1], size, device, None),
        gather(grads_ref[1:2], size, device, None),
        gather(qv, 2 * size, device, None),
        gather(mid_ref[2:3], size, device, None),
        gather(mid_ref[0:1], size, device, None),
        gather(mid_ref[1:2], size, device, None),
        gather(up_ref[0:1], 4 * size, pair, parity == c),
        gather(mid_ref[3:4], size, device, None),
    ]
    packed_ref[:, 0 : 12 * size] = jnp.concatenate(parts, axis=1).astype(jnp.bfloat16)


def norm_rows(x):
    center = x - jnp.mean(x, axis=-1, keepdims=True)
    scale = lax.rsqrt(jnp.mean(center * center, axis=-1, keepdims=True) + 1e-05)
    return center * scale, scale


def project_kernel(place_ref, t0_ref, t1_ref, t2_ref, t3_ref, vec_ref, wz_ref, line_ref, n1_ref, q_ref, kv_ref):
    a = pl.program_id(0)
    z = place_ref[0]
    away = lax.rem(z - a + NZ, NZ)
    x = t0_ref[...].astype(jnp.float32)
    for j, ref in enumerate((t1_ref, t2_ref, t3_ref), 1):
        x = jnp.where(away == j, ref[...].astype(jnp.float32), x)
    line_ref[...] = x.astype(jnp.bfloat16)
    unit, _ = norm_rows(x)
    n1 = (unit * vec_ref[0:1] + vec_ref[1:2]).astype(jnp.bfloat16)
    n1_ref[...] = n1
    y = dot_nn(n1, wz_ref[...])
    q_bias, v_bias = vec_ref[2:3, 0:GW], vec_ref[3:4, 0:GW]
    for g in range(1, NZ):
        q_bias = jnp.where(z == g, vec_ref[2:3, g * GW : (g + 1) * GW], q_bias)
        v_bias = jnp.where(z == g, vec_ref[3:4, g * GW : (g + 1) * GW], v_bias)
    q = (y[:, :GW] + q_bias).astype(jnp.bfloat16)
    q_ref[...] = q * jnp.asarray(SCORE_SCALE, jnp.bfloat16)
    kv_ref[:, :GW] = y[:, GW : 2 * GW].astype(jnp.bfloat16)
    kv_ref[:, GW:] = (y[:, 2 * GW :] + v_bias).astype(jnp.bfloat16)


def project(place, pieces, vec, wz):
    rows, width = pieces[0].shape
    low = jnp.bfloat16
    tall = lambda w: pl.BlockSpec((rows, w), lambda a, *_: (a, 0))
    return kernel_call(
        project_kernel, place, (*pieces, vec, wz),
        [whole_spec((rows, width))] * NZ + [whole_spec(vec.shape), whole_spec(wz.shape)],
        [((NZ * rows, width), low), ((NZ * rows, width), low), ((NZ * rows, GW), low), ((NZ * rows, 2 * GW), low)],
        [tall(width), tall(width), tall(GW), tall(2 * GW)],
        (NZ,), [], 8 * NZ * rows * width * 3 * GW, "project",
    )


def branch_kernel(place_ref, a0_ref, a1_ref, a2_ref, a3_ref, wo_ref, own_ref, vec_ref, hidden_ref, n2_ref):
    z = place_ref[0]
    total = own_ref[...].astype(jnp.float32) + vec_ref[4:5]
    branch = None
    for j, ref in enumerate((a0_ref, a1_ref, a2_ref, a3_ref)):
        start = pl.multiple_of(lax.rem(z - j + NZ, NZ) * GW, GW)
        part = dot_nn(ref[...], wo_ref[pl.ds(start, GW), :])
        branch = part if branch is None else branch + part
    hidden = total + branch
    hidden_ref[...] = hidden
    unit, _ = norm_rows(hidden)
    n2_ref[...] = (unit * vec_ref[5:6] + vec_ref[6:7]).astype(jnp.bfloat16)


def branch_call(place, pieces, wo, own, vec):
    rows, width = own.shape
    arrays = (*pieces, wo, own, vec)
    return kernel_call(
        branch_kernel, place, arrays, [whole_spec(a.shape) for a in arrays],
        [((rows, width), jnp.float32), ((rows, width), jnp.bfloat16)],
        [whole_spec((rows, width))] * 2, (1,), [], 8 * rows * width * width, "branch",
    )


def feed_kernel(
    place_ref, na_ref, nb_ref, ga_ref, gb_ref, up_ref, down_ref, bias_ref,
    act_ref, grad_ref, out_ref, m_ref, sums_ref, bias_out_ref, n_s, g_s, out_s, m_s,
):
    k = pl.program_id(0)
    rows, width = na_ref.shape

    @pl.when(k == 0)
    def _():
        n_s[:rows], n_s[rows:] = na_ref[...], nb_ref[...]
        g_s[:rows], g_s[rows:] = ga_ref[...], gb_ref[...]
        out_s[...] = jnp.zeros(out_s.shape, jnp.float32)
        m_s[...] = jnp.zeros(m_s.shape, jnp.float32)

    up, down = up_ref[...].reshape(width, width), down_ref[...].reshape(width, width)
    v = dot_nn(n_s[...], up) + bias_ref[...]
    cdf = 0.5 * (1.0 + lax.erf(v * 0.7071067811865476))
    slope = cdf + v * (0.3989422804014327 * jnp.exp(-0.5 * v * v))
    act = (v * cdf).astype(jnp.bfloat16)
    act_ref[...] = act
    grad = dot_nt(g_s[...], down) * slope
    grad = grad.astype(jnp.bfloat16)
    grad_ref[...] = grad
    bias_out_ref[...] = jnp.sum(grad.astype(jnp.float32), axis=0, keepdims=True)
    out_s[...] += dot_nn(act, down)
    m_s[...] += dot_nt(grad, up)

    @pl.when(k == pl.num_programs(0) - 1)
    def _():
        out_ref[...] = out_s[:rows]
        m_ref[...] = m_s[:rows]
        sums_ref[0] = m_s[rows:].astype(jnp.bfloat16)
        sums_ref[1] = out_s[rows:].astype(jnp.bfloat16)


def feed(place, na, nb, ga, gb, both, bias):
    rows, width = na.shape
    chips, tall, _ = both.shape
    half = bias.shape[1]
    low, wide = jnp.bfloat16, jnp.float32
    one = whole_spec((rows, width))
    across = lambda r: pl.BlockSpec((r, width), lambda k, *_: (0, k))
    return kernel_call(
        feed_kernel, place, (na, nb, ga, gb, both, both, bias),
        [one] * 4 + [
            pl.BlockSpec((chips, tall // 4, width), lambda k, *_: (0, k, 0)),
            pl.BlockSpec((chips // 2, tall // 2, width), lambda k, *_: (k, 1, 0)),
            across(1),
        ],
        [
            ((2 * rows, half), low), ((2 * rows, half), low), ((rows, width), wide), ((rows, width), wide),
            ((2, rows, width), low), ((1, half), wide),
        ],
        [across(2 * rows), across(2 * rows), one, one, whole_spec((2, rows, width)), across(1)],
        (2,),
        [
            pltpu.VMEM((2 * rows, width), low), pltpu.VMEM((2 * rows, width), low),
            pltpu.VMEM((2 * rows, width), wide), pltpu.VMEM((2 * rows, width), wide),
        ],
        32 * rows * width * half, "feed",
    )


def feed_weights_kernel(
    place_ref, na_ref, nb_ref, ga_ref, gb_ref, act_ref, grad_ref, ak_ref, as_ref, bk_ref, bs_ref, n_s, a_s, g_s
):
    rows, width = na_ref.shape
    y, x = place_ref[2], place_ref[3]
    n_s[:, :rows], n_s[:, rows:] = jnp.transpose(na_ref[...]), jnp.transpose(nb_ref[...])
    g_s[:rows], g_s[rows:] = ga_ref[...], gb_ref[...]
    for k in range(0, act_ref.shape[1], width):
        a_s[k : k + width] = jnp.transpose(act_ref[:, k : k + width])
    tall = ak_ref.shape[2]
    quarter = tall // 4
    span = NZ * quarter

    def put(py, px, pz, row, value):
        count = value.shape[0]
        near, far = (ak_ref, as_ref) if pz < NZ // 2 else (bk_ref, bs_ref)
        index, mine = (px, py == y) if pz < NZ // 2 else (py, px == x)

        @pl.when(mine)
        def _():
            near[index, pz % (NZ // 2), row : row + count] = value

        @pl.when(jnp.logical_not(mine))
        def _():
            far[index, pz % (NZ // 2), row : row + count] = value

    def one_column(column, carry):
        py, px = lax.div(column, 2), lax.rem(column, 2)
        at = pl.multiple_of(column * span, span)
        up = dot_nn(n_s[pl.ds(at, span)], grad_ref[...]).astype(jnp.bfloat16)
        down = dot_nn(a_s[pl.ds(pl.multiple_of(2 * at, 2 * span), 2 * span)], g_s[...]).astype(jnp.bfloat16)
        for pz in range(NZ):
            here = slice(pz * quarter, (pz + 1) * quarter)
            put(py, px, pz, 0, up[here, :width])
            put(py, px, pz, quarter, up[here, width:])
            put(py, px, pz, 2 * quarter, down[2 * pz * quarter : 2 * (pz + 1) * quarter])
        return carry

    lax.fori_loop(0, 4, one_column, 0)


def feed_weights(place, na, nb, ga, gb, act, grad, tall):
    rows, width = na.shape
    low = jnp.bfloat16
    arrays = (na, nb, ga, gb, act, grad)
    shape = (2, NZ // 2, tall, width)
    return kernel_call(
        feed_weights_kernel, place, arrays, [whole_spec(a.shape) for a in arrays], [(shape, low)] * 4,
        [whole_spec(shape)] * 4, (1,),
        [
            pltpu.VMEM((width, 2 * rows), low), pltpu.VMEM((act.shape[1], 2 * rows), low),
            pltpu.VMEM((2 * rows, width), low),
        ],
        8 * rows * width * act.shape[1], "feed_weights",
    )


def middle_kernel(
    place_ref, m_ref, out_ref, sums_ref, hidden_ref, go_ref, vec_ref, wo_ref,
    output_ref, gh_ref, branch_ref, d0_ref, d1_ref, d2_ref, d3_ref, cols_ref,
):
    z = place_ref[0]
    hidden, go = hidden_ref[...], go_ref[...].astype(jnp.float32)
    output_ref[...] = (hidden + out_ref[...] + sums_ref[1].astype(jnp.float32) + vec_ref[7:8]).astype(
        jnp.bfloat16
    )
    m = m_ref[...] + sums_ref[0].astype(jnp.float32)
    unit, scale = norm_rows(hidden)
    grad_hidden = go + norm_back(m, vec_ref[5:6], unit, scale)
    gh_ref[...] = grad_hidden
    branch = grad_hidden.astype(jnp.bfloat16)
    branch_ref[...] = branch
    for j, ref in enumerate((d0_ref, d1_ref, d2_ref, d3_ref)):
        start = pl.multiple_of(lax.rem(z + j, NZ) * GW, GW)
        ref[...] = dot_nt(branch, wo_ref[pl.ds(start, GW), :]).astype(jnp.bfloat16)
    cols_ref[...] = jnp.zeros(cols_ref.shape, jnp.float32)
    cols_ref[0:1] = jnp.sum(m * unit, axis=0, keepdims=True)
    cols_ref[1:2] = jnp.sum(m, axis=0, keepdims=True)
    cols_ref[2:3] = jnp.sum(branch.astype(jnp.float32), axis=0, keepdims=True)
    cols_ref[3:4] = jnp.sum(go, axis=0, keepdims=True)


def middle(place, m, out, sums, hidden, go, vec, wo):
    rows, width = m.shape
    arrays = (m, out, sums, hidden, go, vec, wo)
    low, wide = jnp.bfloat16, jnp.float32
    outs = [((rows, width), low), ((rows, width), wide), ((rows, width), low)]
    outs += [((rows, GW), low)] * NZ + [((8, width), wide)]
    return kernel_call(
        middle_kernel, place, arrays, [whole_spec(a.shape) for a in arrays], outs,
        [whole_spec(shape) for shape, _ in outs], (1,), [], 8 * rows * width * width, "middle",
    )


def inward_kernel(
    place_ref, dq_ref, mine_ref, theirs_ref, line_ref, wz_ref, dqkv_ref, keep_ref, s1_ref, s2_ref, s3_ref,
    cols_ref, sums_ref,
):
    j = pl.program_id(0)
    rows = keep_ref.shape[0]
    at = pl.ds(pl.multiple_of(lax.rem(place_ref[0] + 1 + j, NZ) * rows, rows), rows)
    dkv = (mine_ref[at].astype(jnp.float32) + theirs_ref[at].astype(jnp.float32)).astype(jnp.bfloat16)
    dqkv = jnp.concatenate([dq_ref[at], dkv], axis=1)
    dqkv_ref[at] = dqkv
    m1 = dot_nt(dqkv, wz_ref[...])
    unit, _ = norm_rows(line_ref[at].astype(jnp.float32))

    @pl.when(j == 0)
    def _():
        cols_ref[...] = jnp.zeros(cols_ref.shape, jnp.float32)
        sums_ref[...] = jnp.zeros(sums_ref.shape, jnp.float32)

    cols_ref[0:1] += jnp.sum(m1 * unit, axis=0, keepdims=True)
    cols_ref[1:2] += jnp.sum(m1, axis=0, keepdims=True)
    sums_ref[0:1] += jnp.sum(dqkv.astype(jnp.float32), axis=0, keepdims=True)

    for number, ref in enumerate((s1_ref, s2_ref, s3_ref)):

        @pl.when(j == number)
        def _():
            ref[...] = m1.astype(jnp.bfloat16)

    @pl.when(j == pl.num_programs(0) - 1)
    def _():
        keep_ref[...] = m1


def inward(place, dq, mine, theirs, line, wz):
    total, width = line.shape
    rows = total // NZ
    low, wide = jnp.bfloat16, jnp.float32
    arrays = (dq, mine, theirs, line, wz)
    outs = [((total, 3 * GW), low), ((rows, width), wide)] + [((rows, width), low)] * (NZ - 1)
    outs += [((8, width), wide), ((8, 3 * GW), wide)]
    return kernel_call(
        inward_kernel, place, arrays, [whole_spec(a.shape) for a in arrays], outs,
        [whole_spec(shape) for shape, _ in outs], (NZ,), [], 8 * total * width * 3 * GW, "inward",
    )


def finish_kernel(place_ref, m_ref, r1_ref, r2_ref, r3_ref, own_ref, gh_ref, vec_ref, out_ref):
    m = m_ref[...]
    for ref in (r1_ref, r2_ref, r3_ref):
        m = m + ref[...].astype(jnp.float32)
    unit, scale = norm_rows(own_ref[...].astype(jnp.float32))
    out_ref[...] = gh_ref[...] + norm_back(m, vec_ref[0:1], unit, scale)


def finish(place, m, pieces, own, grad_hidden, vec):
    rows, width = own.shape
    arrays = (m, *pieces, own, grad_hidden, vec)
    return kernel_call(
        finish_kernel, place, arrays, [whole_spec(a.shape) for a in arrays],
        [((rows, width), jnp.float32)], [whole_spec((rows, width))], (1,), [], 100 * rows * width, "finish",
    )[0]


def owners_kernel(
    place_ref, a0_ref, a1_ref, a2_ref, a3_ref, branch_ref, n1_ref, dqkv_ref, cols_ref, mid_ref, sums_ref, up_ref,
    mine_ref, theirs_ref, wo_s, wz_s, vec_s,
):
    z, c = place_ref[0], place_ref[1]
    width = branch_ref.shape[1]
    for j, ref in enumerate((a0_ref, a1_ref, a2_ref, a3_ref)):
        start = pl.multiple_of(lax.rem(z - j + NZ, NZ) * GW, GW)
        wo_s[pl.ds(start, GW), :] = dot_tn(ref[...], branch_ref[...]).astype(jnp.bfloat16)
    wz_s[...] = dot_tn(n1_ref[...], dqkv_ref[...]).astype(jnp.bfloat16)
    pack_kernel(place_ref, cols_ref, mid_ref, sums_ref, up_ref, vec_s)
    chips, tall, span = mine_ref.shape
    devices = 2 * chips
    rows = width // devices
    first_row = lax.broadcasted_iota(jnp.int32, (tall - rows, span), 0) == 0
    for pair in range(chips):
        tails = []
        for core in range(2):
            row = vec_s[2 * pair + core : 2 * pair + core + 1].astype(jnp.float32)
            tails.append(jnp.where(first_row, jnp.broadcast_to(row, first_row.shape), 0.0).astype(jnp.bfloat16))
        mine_ref[pair, rows:] = jnp.where(c == 0, tails[0], tails[1])
        theirs_ref[pair, rows:] = jnp.where(c == 0, tails[1], tails[0])

    def one_chip(pair, carry):
        at = pl.ds(pl.multiple_of(pair * (2 * rows), 2 * rows), 2 * rows)
        both = jnp.concatenate([wo_s[at], wz_s[at]], axis=1)
        mine_ref[pair, :rows] = jnp.where(c == 0, both[:rows], both[rows:])
        theirs_ref[pair, :rows] = jnp.where(c == 0, both[rows:], both[:rows])
        return carry

    lax.fori_loop(0, chips, one_chip, 0)


def owners(place, pieces, branch, n1, dqkv, cols, mid, sums, up, devices, tall):
    width, span = n1.shape[1], n1.shape[1] + dqkv.shape[1]
    low = jnp.bfloat16
    arrays = (*pieces, branch, n1, dqkv, cols, mid, sums, up)
    shape = (devices // 2, tall, span)
    return kernel_call(
        owners_kernel, place, arrays, [whole_spec(a.shape) for a in arrays], [(shape, low), (shape, low)],
        [whole_spec(shape)] * 2, (1,),
        [pltpu.VMEM((width, width), low), pltpu.VMEM((width, dqkv.shape[1]), low), pltpu.VMEM((devices, span), low)],
        1 << 20, "owners",
    )


def deliver_kernel(place_ref, own_ref, p1_ref, p2_ref, p3_ref, qkv_ref, wo_ref, vec_ref):
    z = place_ref[0]
    rows, width = wo_ref.shape
    own = own_ref[...]
    pieces = [own] + [ref[...].astype(jnp.float32) for ref in (p1_ref, p2_ref, p3_ref)]
    for g in range(NZ):
        away = lax.rem(z - g + NZ, NZ)
        part = pieces[0]
        for j in range(1, NZ):
            part = jnp.where(away == j, pieces[j], part)
        for k in range(3):
            lanes = slice(k * width + g * GW, k * width + (g + 1) * GW)
            qkv_ref[:, lanes] = part[:rows, width + k * GW : width + (k + 1) * GW]
    total = pieces[0] + pieces[1] + pieces[2] + pieces[3]
    wo_ref[...] = total[:rows, :width]
    vec_ref[...] = total[rows:]


def weave_kernel(place_ref, mine_ref, theirs_ref, out_ref):
    c = place_ref[1]
    mine, theirs = mine_ref[...], theirs_ref[...].astype(jnp.float32)
    even, odd = jnp.where(c == 0, mine, theirs), jnp.where(c == 0, theirs, mine)
    half = mine.shape[1]
    units = half // 16
    for pair in range(16):
        here = slice(pair * units, (pair + 1) * units)
        out_ref[:, 2 * pair * units : (2 * pair + 1) * units] = even[:, here]
        out_ref[:, (2 * pair + 1) * units : (2 * pair + 2) * units] = odd[:, here]


def attend_kernel(
    act_ref, may_ref, place_ref, q_ref, mine_ref, theirs_ref, qseg_ref, kseg_ref, o_ref, low_ref, lse_ref,
    k_s, vt_s, col_s, m_s, l_s, acc_s, list_s,
):
    i = pl.program_id(0)
    chunks = kseg_ref.shape[0]

    @pl.when(i == 0)
    def _():
        for line, ref in enumerate((mine_ref, theirs_ref)):
            core = place_ref[1] if line == 0 else 1 - place_ref[1]
            for a in range(chunks // 2):
                rows = slice(a * CHUNK, (a + 1) * CHUNK)
                at = pl.ds(pl.multiple_of((2 * a + core) * CHUNK, CHUNK), CHUNK)
                for h in range(GROUP):
                    k_s[h, at] = ref[rows, HEAD_DIM * h : HEAD_DIM * (h + 1)]
                    vt_s[h, :, at] = jnp.transpose(ref[rows, GW + HEAD_DIM * h : GW + HEAD_DIM * (h + 1)])
        for j in range(chunks):
            col_s[j * CHUNK : (j + 1) * CHUNK] = column_of(kseg_ref[j : j + 1])

    m_s[...] = jnp.full(m_s.shape, NEG_FILL, jnp.float32)
    l_s[...] = jnp.zeros(l_s.shape, jnp.float32)
    acc_s[...] = jnp.zeros(acc_s.shape, jnp.float32)
    here = pl.ds(pl.multiple_of(i * CHUNK, CHUNK), CHUNK)
    q_heads = [q_ref[here, HEAD_DIM * h : HEAD_DIM * (h + 1)] for h in range(GROUP)]
    q_seg = qseg_ref[pl.ds(i, 1)]

    count = list_live([act_ref[i, j] for j in range(chunks)], list_s)

    def two_chunks(step, carry):
        heads, pair = range(GROUP), pair_at(list_s, count, step)
        at = [pl.ds(pl.multiple_of(j * CHUNK, CHUNK), CHUNK) for j, _ in pair]
        permit = [permit_of(may_ref, i, j, q_seg, col_s[at[u]], alive) for u, (j, alive) in enumerate(pair)]
        s = [[jnp.where(permit[u], dot_nt(k_s[h, at[u]], q_heads[h]), NEG_FILL) for u in range(2)] for h in heads]
        old = [m_s[h] for h in heads]
        top = [[jnp.max(part, axis=0, keepdims=True) for part in s[h]] for h in heads]
        new = [jnp.maximum(old[h], jnp.maximum(*top[h])) for h in heads]
        p = [[jnp.exp(part - new[h]) for part in s[h]] for h in heads]
        fade = [jnp.exp(old[h] - new[h]) for h in heads]
        for h in heads:
            l_s[h] = l_s[h] * fade[h] + sum(jnp.sum(part, axis=0, keepdims=True) for part in p[h])
            added = [dot_nn(vt_s[h, :, at[u]], p[h][u].astype(jnp.bfloat16)) for u in range(2)]
            acc_s[h] = acc_s[h] * fade[h] + (added[0] + added[1])
            m_s[h] = new[h]
        return carry

    lax.fori_loop(0, lax.div(count + 1, 2), two_chunks, 0)
    out = jnp.concatenate([jnp.transpose(acc_s[h] / l_s[h]) for h in range(GROUP)], axis=1)
    o_ref[...] = out
    low_ref[...] = out.astype(jnp.bfloat16)
    logs = [m_s[h] + jnp.log(l_s[h]) for h in range(GROUP)]
    lse_ref[...] = jnp.concatenate(logs + [logs[0]] * (8 - GROUP), axis=0)


def attend(active, may, place, q, mine, theirs, q_seg, k_seg):
    rows, keys = q.shape[0], 2 * mine.shape[0]
    tall = pl.BlockSpec((CHUNK, GW), lambda i, *_: (i, 0))
    return pl.pallas_call(
        attend_kernel,
        out_shape=(
            jax.ShapeDtypeStruct((rows, GW), jnp.float32),
            jax.ShapeDtypeStruct((rows, GW), jnp.bfloat16),
            jax.ShapeDtypeStruct((8, rows), jnp.float32),
        ),
        grid_spec=pltpu.PrefetchScalarGridSpec(
            num_scalar_prefetch=3,
            grid=(rows // CHUNK,),
            in_specs=held(
                [whole_spec(a.shape) for a in (q, mine, theirs, q_seg, k_seg)], (q, mine, theirs, q_seg, k_seg)
            ),
            out_specs=[tall, tall, pl.BlockSpec((8, CHUNK), lambda i, *_: (0, i))],
            scratch_shapes=[
                pltpu.VMEM((GROUP, keys, HEAD_DIM), jnp.bfloat16),
                pltpu.VMEM((GROUP, HEAD_DIM, keys), jnp.bfloat16),
                pltpu.VMEM((keys, 1), jnp.float32),
                pltpu.VMEM((GROUP, 1, CHUNK), jnp.float32),
                pltpu.VMEM((GROUP, 1, CHUNK), jnp.float32),
                pltpu.VMEM((GROUP, HEAD_DIM, CHUNK), jnp.float32),
                pltpu.SMEM((keys // CHUNK + 1,), jnp.int32),
            ],
        ),
        compiler_params=pltpu.CompilerParams(vmem_limit_bytes=18 << 20),
        cost_estimate=pl.CostEstimate(
            flops=int(48 * rows * keys * GW), bytes_accessed=16 * keys * GW, transcendentals=4 * rows * keys
        ),
        name="attend",
    )(active, may, place, q, mine, theirs, q_seg, k_seg)


def attend_back_kernel(first, *refs):
    (act_ref, may_ref, place_ref, q_ref, d0_ref, d1_ref, d2_ref, d3_ref, kv_ref, lse_ref, qseg_ref,
     kseg_ref, from_ref, *refs) = refs
    if first:
        dqt_ref, delta_ref, dkv_ref, list_s, q_s, do_s, dk_s, dv_s = refs
    else:
        old_ref, dq_ref, dkv_ref, list_s, q_s, do_s, dk_s, dv_s, dqt_ref = refs
        delta_ref = from_ref
    step = pl.program_id(0)
    rows = q_ref.shape[0]
    z, c = place_ref[0], place_ref[1]
    j = 2 * step + (1 - c if first else c)

    @pl.when(step == 0)
    def _():
        for r, ref in enumerate((d0_ref, d1_ref, d2_ref, d3_ref)):
            at = pl.ds(pl.multiple_of(lax.rem(z - r + NZ, NZ) * CHUNK, CHUNK), CHUNK)
            for h in range(GROUP):
                do_s[h, at] = ref[:, HEAD_DIM * h : HEAD_DIM * (h + 1)]
        ones = jnp.ones((8, HEAD_DIM), jnp.bfloat16)
        for h in range(GROUP):
            lanes = slice(HEAD_DIM * h, HEAD_DIM * (h + 1))
            q_s[h] = q_ref[:, lanes]
            if first:
                both = do_s[h].astype(jnp.float32) * from_ref[:, lanes]
                high = both.astype(jnp.bfloat16)
                rest = (both - high.astype(jnp.float32)).astype(jnp.bfloat16)
                delta_ref[h : h + 1] = (dot_nt(ones, high) + dot_nt(ones, rest))[0:1]
        dqt_ref[...] = jnp.zeros(dqt_ref.shape, jnp.float32) if first else old_ref[...]
        if first:
            delta_ref[GROUP:] = jnp.zeros((8 - GROUP, rows), jnp.float32)

    dk_s[...] = jnp.zeros(dk_s.shape, jnp.float32)
    dv_s[...] = jnp.zeros(dv_s.shape, jnp.float32)
    here = pl.ds(pl.multiple_of(step * CHUNK, CHUNK), CHUNK)
    k_heads = [kv_ref[here, HEAD_DIM * h : HEAD_DIM * (h + 1)] for h in range(GROUP)]
    v_heads = [kv_ref[here, GW + HEAD_DIM * h : GW + HEAD_DIM * (h + 1)] for h in range(GROUP)]
    k_turned = [jnp.transpose(k) for k in k_heads]
    k_column = column_of(kseg_ref[pl.ds(j, 1)])

    count = list_live([act_ref[i, j] for i in range(rows // CHUNK)], list_s)

    def two_tiles(turn, carry):
        heads, pair, low = range(GROUP), pair_at(list_s, count, turn), jnp.bfloat16
        both = [(h, u) for h in heads for u in range(2)]
        at = [pl.ds(pl.multiple_of(i * CHUNK, CHUNK), CHUNK) for i, _ in pair]
        permit = [
            permit_of(may_ref, i, j, qseg_ref[pl.ds(i, 1)], k_column, alive) for i, alive in pair
        ]
        s = {(h, u): dot_nt(k_heads[h], q_s[h, at[u]]) for h, u in both}
        dp = {(h, u): dot_nt(v_heads[h], do_s[h, at[u]]) for h, u in both}
        p = {
            (h, u): jnp.where(permit[u], jnp.exp(s[h, u] - lse_ref[h : h + 1, at[u]]), 0.0) for h, u in both
        }
        ds = {(h, u): (p[h, u] * (dp[h, u] - delta_ref[h : h + 1, at[u]])).astype(low) for h, u in both}
        for h in heads:
            dv_s[h] += dot_nn(p[h, 0].astype(low), do_s[h, at[0]]) + dot_nn(p[h, 1].astype(low), do_s[h, at[1]])
            dk_s[h] += dot_nn(ds[h, 0], q_s[h, at[0]]) + dot_nn(ds[h, 1], q_s[h, at[1]])
            for u in range(2):
                dqt_ref[h, :, at[u]] += dot_nn(k_turned[h], ds[h, u])
        return carry

    lax.fori_loop(0, lax.div(count + 1, 2), two_tiles, 0)
    dkv_ref[...] = jnp.concatenate(
        [dk_s[h] for h in range(GROUP)] + [dv_s[h] for h in range(GROUP)], axis=1
    ).astype(jnp.bfloat16)
    if not first:

        @pl.when(step == pl.num_programs(0) - 1)
        def _():
            dq_ref[...] = jnp.concatenate(
                [jnp.transpose(dqt_ref[h] * SCORE_SCALE) for h in range(GROUP)], axis=1
            ).astype(jnp.bfloat16)


def attend_back(first, active, may, place, q, pieces, kv, lse, q_seg, k_seg, *carried):
    rows = q.shape[0]
    low, wide = jnp.bfloat16, jnp.float32
    tall = pl.BlockSpec((CHUNK, 2 * GW), lambda s, *_: (s, 0))
    turned = (GROUP, HEAD_DIM, rows)
    outs = [(turned, wide), ((8, rows), wide)] if first else [((rows, GW), low)]
    scratch = [pltpu.SMEM((rows // CHUNK + 1,), jnp.int32)] + [pltpu.VMEM((GROUP, rows, HEAD_DIM), low)] * 2 + [pltpu.VMEM((GROUP, CHUNK, HEAD_DIM), wide)] * 2
    if not first:
        scratch.append(pltpu.VMEM(turned, wide))
    return pl.pallas_call(
        functools.partial(attend_back_kernel, first),
        out_shape=tuple(jax.ShapeDtypeStruct(*o) for o in outs + [((rows, 2 * GW), low)]),
        grid_spec=pltpu.PrefetchScalarGridSpec(
            num_scalar_prefetch=3,
            grid=(rows // CHUNK,),
            in_specs=held(
                [
                    whole_spec((rows, GW)), *[whole_spec(p.shape) for p in pieces], whole_spec(kv.shape), whole_spec((8, rows)),
                    whole_spec(q_seg.shape), whole_spec(k_seg.shape), *[whole_spec(a.shape) for a in carried],
                ],
                (q, *pieces, kv, lse, q_seg, k_seg, *carried),
            ),
            out_specs=[whole_spec(shape) for shape, _ in outs] + [tall],
            scratch_shapes=scratch,
        ),
        compiler_params=pltpu.CompilerParams(vmem_limit_bytes=20 << 20),
        cost_estimate=pl.CostEstimate(
            flops=int(56 * rows * rows * GW), bytes_accessed=32 * rows * GW, transcendentals=4 * rows * rows
        ),
        name="attend_back_first" if first else "attend_back_last",
    )(active, may, place, q, *pieces, kv, lse, q_seg, k_seg, *carried)


def fast_local(
    tokens, segment_ids, live_blocks, norm1_gain, norm1_bias, qkv_weight, qv_bias, out_weight, out_bias,
    norm2_gain, norm2_bias, up_weight, up_bias, down_weight, down_bias, grad_out,
):
    y, x, z, c = (lax.axis_index(name) for name in ("y", "x", "z", "c"))
    place = jnp.stack([z, c, y, x]).astype(jnp.int32)
    wide, low = jnp.float32, jnp.bfloat16
    _, rows, width = tokens.shape
    own_rows, units = qkv_weight.shape[0], down_weight.shape[0]
    ff = up_weight.shape[1]
    half, pairs = ff // 2, ff // (2 * units)
    devices = width // own_rows
    seq_rows = rows * NZ
    keys = 2 * seq_rows
    blocks = keys // BLOCK
    per = CHUNK // BLOCK

    vectors = (norm1_gain, norm1_bias, qv_bias, out_bias, norm2_gain, norm2_bias, up_bias, down_bias)
    sizes = [v.shape[0] for v in vectors]
    cuts = [sum(sizes[:i]) for i in range(len(sizes) + 1)]
    span = width + 3 * GW
    tall = own_rows + 8
    parts = vectors + (segment_ids[0].astype(low),)
    extra = sum(
        jnp.pad(p, (start, span - start - p.shape[0])) for p, start in zip(parts, cuts)
    )
    extra = jnp.pad(extra[None], ((0, 7), (0, 0)))
    wz = qkv_weight.reshape(own_rows, 3, NZ, GW).transpose(2, 0, 1, 3).reshape(NZ, own_rows, 3 * GW)
    group1 = jnp.concatenate(
        [jnp.broadcast_to(out_weight[None], (NZ, own_rows, width)), wz], axis=2
    )
    group1 = jnp.concatenate([group1, jnp.broadcast_to(extra[None], (NZ, 8, span))], axis=1)
    pieces1 = z_exchange(group1, z, (2, 3, 1))

    up_sets = up_weight.reshape(own_rows, pairs, 2, units).transpose(2, 0, 1, 3)
    up_sets = up_sets.reshape(2, own_rows, half)
    up_chip = in_order(pick(up_sets, c), swap(pick(up_sets, 1 - c), "c"), c, 0)
    up_chip = up_chip.reshape(2 * own_rows, half)
    group2 = jnp.concatenate([up_chip[:, :width], up_chip[:, width:], down_weight], axis=0)
    pieces2 = z_pieces(group2, (3, 1, 2))

    own, pieces2[1], pieces2[3] = meet(tokens[0], pieces2[1], pieces2[3])
    line_pieces = z_pieces(own, (2, 1, 3))
    group1 = z_order(pieces1, z)
    own_seg = group1[:, own_rows, cuts[-1] : cuts[-1] + rows].astype(wide)
    seg = in_order(own_seg, swap(own_seg, "c"), c, 1).reshape(keys // CHUNK, CHUNK)
    group1 = jnp.concatenate([in_order(*half) for half in xy_gather(group1, y, x)], axis=2)
    group1 = in_order(group1, swap(group1, "c"), c, 3)
    wo = group1[..., :own_rows, :width].reshape(width, width)
    wz = group1[..., :own_rows, width:].reshape(width, 3 * GW)
    packed = group1[..., own_rows, : cuts[-1]].reshape(devices, cuts[-1])
    vec = kernel_call(
        unpack_kernel, place, (packed,), [whole_spec(packed.shape)], [((VEC_ROWS, width), wide)],
        [whole_spec((VEC_ROWS, width))], (1,), [], 1 << 20, "unpack",
    )[0]
    group2, vec = meet(z_order(pieces2, z), vec)
    group2 = xy_gather(group2, y, x)

    own_blocks = seq_rows // BLOCK
    ids = jnp.arange(blocks, dtype=jnp.int32)
    own_ids = pick(ids.reshape(NZ, 2, rows // BLOCK), c, 1).reshape(own_blocks)
    own_live = pick(live_blocks[0].reshape(NZ, 2, rows // BLOCK, blocks), c, 1)
    own_live = own_live.reshape(own_blocks, blocks)
    seg_blocks = seg.reshape(blocks, BLOCK)
    own_seg_blocks = own_seg.reshape(own_blocks, BLOCK)
    may = (own_live > 0) | (own_ids[:, None] == ids[None, :])
    touch = (
        may
        & (own_seg_blocks[:, :1] <= seg_blocks[:, -1][None])
        & (seg_blocks[:, 0][None] <= own_seg_blocks[:, -1:])
    )
    active = jnp.any(touch.reshape(own_blocks // per, per, blocks // per, per), axis=(1, 3))
    active, may = active.astype(jnp.int32), may.astype(jnp.int32)

    line, n1, q, kv = project(place, line_pieces, vec, wz)
    kv_theirs = swap(kv, "c")
    att_wide, att_low, lse = attend(active, may, place, q, kv, kv_theirs, own_seg, seg)
    att = z_exchange(att_low.reshape(NZ, rows, GW), z, (2, 1, 3))
    group2 = [in_order(own_half, after(other, att_low), at, axis) for own_half, other, at, axis in group2]
    group2 = jnp.concatenate(group2, axis=2)

    hidden, n2 = branch_call(place, att, wo, own, vec)
    go = grad_out[0]
    n2_theirs, go_theirs = swap(n2, "c"), swap(go, "c")
    up_bias_half = vec[8:10].reshape(1, half)
    chips = devices // 2
    group2 = group2.reshape(chips, 2 * units, width)
    activated, grad_before, out_part, m_part, sums, up_bias_part = feed(
        place, n2, n2_theirs, go, go_theirs, group2, up_bias_half
    )
    sums = swap(sums, "c")
    a_kept, a_sent, b_kept, b_sent = feed_weights(
        place, n2, n2_theirs, go, go_theirs, activated, grad_before, 2 * units
    )
    output, grad_hidden, grad_branch, *grad_att, mid = middle(
        place, m_part, out_part, sums, hidden, go, vec, wo
    )
    dout = [grad_att[0]] + hops(lambda hop: shift(grad_att[hop], "z", NZ, hop), (3, 1, 2))
    a, b = add_up(a_kept, a_sent, "y"), add_up(b_kept, b_sent, "x")

    dq_part, delta, dkv_theirs = attend_back(
        True, active, may, place, q, dout, kv_theirs, lse, own_seg, seg, att_wide
    )
    a, b, dq_part = meet(a, b, dq_part)
    a, b = halve(a, "x", x, low), halve(b, "y", y, low)
    dq, dkv_mine = attend_back(
        False, active, may, place, q, dout, kv, lse, own_seg, seg, delta, dq_part
    )
    dqkv, m1_own, *m1_sent, cols, dqkv_sum = inward(place, dq, dkv_mine, swap(dkv_theirs, "c"), line, wz)
    group2 = jnp.concatenate([a, b], axis=0)
    m1_up, m1_far, m1_down = z_reduce(m1_sent, z)

    mine, theirs = owners(
        place, att, grad_branch, n1, dqkv, cols, mid, dqkv_sum, up_bias_part, devices, tall
    )
    group1 = (mine.astype(wide) + swap(theirs, "c").astype(wide)).astype(low)
    group1 = group1.reshape(2, 2, NZ, tall, span)
    a = halve(group1[:, :, :2], "y", y, low)
    b = halve(group1[:, :, 2:].swapaxes(0, 1), "x", x, low)
    a, b = halve(a, "x", x, low), halve(b, "y", y, low)
    a, b, m1_far, m1_down = meet(a, b, m1_far, m1_down)
    grad_tokens = finish(place, m1_own, (m1_up, m1_far, m1_down), own, grad_hidden, vec)
    group1 = jnp.concatenate([a, b], axis=0)
    pieces = z_exchange(group1.astype(low), z, (1, 2, 3))
    arrays = (pick(group1, z), *pieces[1:])
    outs = [((own_rows, 3 * width), wide), ((own_rows, width), wide), ((tall - own_rows, span), wide)]
    grad_qkv, grad_wo, vec_sum = kernel_call(
        deliver_kernel, place, arrays, [whole_spec(a.shape) for a in arrays], outs,
        [whole_spec(shape) for shape, _ in outs], (1,), [], 1 << 20, "deliver",
    )
    v = [vec_sum[0, cuts[i] : cuts[i + 1]] for i in range(len(sizes))]

    group2_low = group2.astype(low)
    sent = [pick(group2_low, (z + j) % NZ) for j in range(1, NZ)]
    group2 = sum((piece.astype(wide) for piece in hops(lambda hop: shift(sent[hop - 1], "z", NZ, hop), (2, 3, 1))), pick(group2, z))
    grad_down = group2[units:]
    up_rows = jnp.concatenate([group2[: 2 * own_rows], group2[2 * own_rows : units]], axis=1)
    up_rows = up_rows.reshape(2, own_rows, half)
    arrays = (pick(up_rows, c), swap(pick(up_rows, 1 - c).astype(low), "c"))
    grad_up = kernel_call(
        weave_kernel, place, arrays, [whole_spec(a.shape) for a in arrays], [((own_rows, ff), wide)],
        [whole_spec((own_rows, ff))], (1,), [], 1 << 20, "weave",
    )[0]
    return (
        output[None], grad_tokens[None], v[0], v[1], grad_qkv, v[2], grad_wo, v[3],
        v[4], v[5], grad_up, v[6], grad_down, v[7],
    )


def build(body, mesh, dp, ctx):
    both = dp + ctx
    rows, vector, matrix = P(dp, ctx, None), P(both), P(both, None)
    return jax.shard_map(
        body,
        mesh=mesh,
        in_specs=(
            rows, P(dp, ctx), P(dp, None, None), vector, vector, matrix, vector, matrix, vector,
            vector, vector, matrix, vector, matrix, vector, rows,
        ),
        out_specs=(
            rows, rows, vector, vector, matrix, vector, matrix, vector, vector, vector, matrix,
            vector, matrix, vector,
        ),
        check_vma=False,
    )


def solution(mesh):
    if dict(mesh.shape) == {"dp": 4, "ctx": 2 * NZ}:
        grid = Mesh(mesh.devices.reshape(2, 2, NZ, 2), ("y", "x", "z", "c"))
        return build(fast_local, grid, ("y", "x"), ("z", "c"))
    return build(local, mesh, ("dp",), ("ctx",))
```

```python
import functools
import math

import jax
import jax.numpy as jnp
from jax import lax
from jax.experimental import pallas as pl
from jax.experimental.pallas import tpu as pltpu
from jax.sharding import Mesh, PartitionSpec as P

HEADS = 12
HEAD_DIM = 64
BLOCK = 128


NEG_FILL = -1e30
SCORE_SCALE = 0.125


def layer_norm(value_in, norm_gain, norm_shift):
    center = value_in - jnp.mean(value_in, axis=-1, keepdims=True)
    spread = jnp.mean(center * center, axis=-1, keepdims=True)
    return center * lax.rsqrt(spread + 1e-05) * norm_gain + norm_shift


def exact_gelu(value_in):
    return jax.nn.gelu(value_in, approximate=False)


def matmul_low(left_side, right_side):
    return jnp.dot(left_side, right_side, preferred_element_type=jnp.float32)


def inner_rows(left_side, right_side):
    return lax.dot_general(
        left_side, right_side, (((0,), (0,)), ((), ())), preferred_element_type=jnp.float32
    )


def times_transpose(left_side, right_side):
    return lax.dot_general(
        left_side, right_side, (((1,), (1,)), ((), ())), preferred_element_type=jnp.float32
    )


def sweep_blocks(count_rows, step_fn, carry_state):
    span_rows = math.gcd(count_rows, 512)
    return lax.fori_loop(
        0,
        count_rows // span_rows,
        lambda loop_index, loop_state: step_fn(loop_index * span_rows, span_rows, loop_state),
        carry_state,
    )


def allowed_pairs(live_table, query_pos, key_pos, query_seg, key_seg):
    block_slots = jnp.arange(live_table.shape[-1], dtype=jnp.int32)
    query_block = query_pos // BLOCK
    key_block = key_pos // BLOCK
    pick_query = (query_block[:, None] == block_slots[None, :]).astype(jnp.bfloat16)
    pick_key = (key_block[:, None] == block_slots[None, :]).astype(jnp.bfloat16)
    live_rows = jnp.einsum(
        "qa,sab->sqb", pick_query, live_table, preferred_element_type=jnp.float32
    )
    live_grid = jnp.einsum(
        "sqb,kb->sqk", live_rows.astype(jnp.bfloat16), pick_key, preferred_element_type=jnp.float32
    )
    same_block = query_block[:, None] == key_block[None, :]
    same_doc = query_seg[:, :, None] == key_seg[:, None, :]
    return same_doc & ((live_grid > 0.5) | same_block[None])


def pair_grads(
    live_table,
    query_heads,
    dout_heads,
    lse_heads,
    delta_heads,
    query_pos,
    query_seg,
    key_heads,
    value_heads,
    key_pos,
    key_seg,
):
    scores = (
        jnp.einsum("sqhd,skhd->shqk", query_heads, key_heads, preferred_element_type=jnp.float32)
        * SCORE_SCALE
    )
    permit = allowed_pairs(live_table, query_pos, key_pos, query_seg, key_seg)[:, None]
    attn_probs = jnp.where(permit, jnp.exp(scores - lse_heads[..., None]), 0.0)
    grad_prob = jnp.einsum(
        "sqhd,skhd->shqk", dout_heads, value_heads, preferred_element_type=jnp.float32
    )
    grad_score = (attn_probs * (grad_prob - delta_heads[..., None])).astype(jnp.bfloat16)
    grad_query = (
        jnp.einsum("shqk,skhd->sqhd", grad_score, key_heads, preferred_element_type=jnp.float32)
        * SCORE_SCALE
    )
    grad_key = (
        jnp.einsum("shqk,sqhd->skhd", grad_score, query_heads, preferred_element_type=jnp.float32)
        * SCORE_SCALE
    )
    grad_value = jnp.einsum(
        "shqk,sqhd->skhd",
        attn_probs.astype(jnp.bfloat16),
        dout_heads,
        preferred_element_type=jnp.float32,
    )
    return (grad_query, grad_key, grad_value)


def local(
    tokens,
    segment_ids,
    live_blocks,
    norm1_gain,
    norm1_bias,
    qkv_weight,
    qv_bias,
    out_weight,
    out_bias,
    norm2_gain,
    norm2_bias,
    up_weight,
    up_bias,
    down_weight,
    down_bias,
    grad_out,
):
    shards = (
        norm1_gain,
        norm1_bias,
        qkv_weight,
        qv_bias,
        out_weight,
        out_bias,
        norm2_gain,
        norm2_bias,
        up_weight,
        up_bias,
        down_weight,
        down_bias,
    )
    gathered = (
        lax.all_gather(shards[0], ("dp", "ctx"), axis=0, tiled=True),
        lax.all_gather(shards[1], ("dp", "ctx"), axis=0, tiled=True),
        lax.all_gather(shards[2], ("dp", "ctx"), axis=0, tiled=True),
        lax.all_gather(shards[3], ("dp", "ctx"), axis=0, tiled=True),
        lax.all_gather(shards[4], ("dp", "ctx"), axis=0, tiled=True),
        lax.all_gather(shards[5], ("dp", "ctx"), axis=0, tiled=True),
        lax.all_gather(shards[6], ("dp", "ctx"), axis=0, tiled=True),
        lax.all_gather(shards[7], ("dp", "ctx"), axis=0, tiled=True),
        lax.all_gather(shards[8], ("dp", "ctx"), axis=0, tiled=True),
        lax.all_gather(shards[9], ("dp", "ctx"), axis=0, tiled=True),
        lax.all_gather(shards[10], ("dp", "ctx"), axis=0, tiled=True),
        lax.all_gather(shards[11], ("dp", "ctx"), axis=0, tiled=True),
    )
    (
        gain_first,
        shift_first,
        full_qkv,
        bias_qv,
        full_out,
        bias_out,
        gain_second,
        shift_second,
        full_up,
        bias_up,
        full_down,
        bias_down,
    ) = gathered
    seq_count, tok_rows, model_width = tokens.shape
    head_count = HEADS
    head_size = HEAD_DIM
    flat_rows = seq_count * tok_rows
    query_pos = lax.axis_index("ctx") * tok_rows + jnp.arange(tok_rows, dtype=jnp.int32)
    live_table = live_blocks.astype(jnp.bfloat16)
    seg_low = segment_ids.astype(jnp.bfloat16)
    inputs_wide = tokens.reshape(flat_rows, model_width).astype(jnp.float32)
    normed_wide, norm_pull_one = jax.vjp(
        layer_norm, inputs_wide, gain_first.astype(jnp.float32), shift_first.astype(jnp.float32)
    )
    normed_one = normed_wide.astype(jnp.bfloat16)
    projected = matmul_low(normed_one, full_qkv)
    bias_wide = bias_qv.astype(jnp.float32)
    query_low = (projected[:, :model_width] + bias_wide[:model_width]).astype(jnp.bfloat16)
    key_low = projected[:, model_width : 2 * model_width].astype(jnp.bfloat16)
    value_low = (projected[:, 2 * model_width :] + bias_wide[model_width:]).astype(jnp.bfloat16)
    query_heads = query_low.reshape(seq_count, tok_rows, head_count, head_size)
    key_seq = key_low.reshape(seq_count, tok_rows, model_width)
    value_seq = value_low.reshape(seq_count, tok_rows, model_width)
    initial = (
        jnp.full((seq_count, head_count, tok_rows), NEG_FILL, jnp.float32),
        jnp.zeros((seq_count, head_count, tok_rows), jnp.float32),
        jnp.zeros((seq_count, tok_rows, head_count, head_size), jnp.float32),
    )
    key_part = lax.all_gather(key_seq, "ctx", axis=1, tiled=True)
    value_part = lax.all_gather(value_seq, "ctx", axis=1, tiled=True)
    seg_part = lax.all_gather(seg_low, "ctx", axis=1, tiled=True)

    def step_fn(offset, span_rows, inner_state):
        run_max, run_total, accum_out = inner_state
        key_heads = lax.dynamic_slice_in_dim(key_part, offset, span_rows, 1).reshape(
            seq_count, span_rows, head_count, head_size
        )
        value_heads = lax.dynamic_slice_in_dim(value_part, offset, span_rows, 1).reshape(
            seq_count, span_rows, head_count, head_size
        )
        key_seg = lax.dynamic_slice_in_dim(seg_part, offset, span_rows, 1)
        key_pos = offset + jnp.arange(span_rows, dtype=jnp.int32)
        scores = (
            jnp.einsum(
                "sqhd,skhd->shqk", query_heads, key_heads, preferred_element_type=jnp.float32
            )
            * SCORE_SCALE
        )
        permit = allowed_pairs(live_table, query_pos, key_pos, seg_low, key_seg)[:, None]
        scores = jnp.where(permit, scores, NEG_FILL)
        new_max = jnp.maximum(run_max, jnp.max(scores, axis=-1))
        exp_scores = jnp.where(permit, jnp.exp(scores - new_max[..., None]), 0.0)
        factor = jnp.exp(run_max - new_max)
        run_total = run_total * factor + jnp.sum(exp_scores, axis=-1)
        weighted = jnp.einsum(
            "shqk,skhd->sqhd",
            exp_scores.astype(jnp.bfloat16),
            value_heads,
            preferred_element_type=jnp.float32,
        )
        accum_out = accum_out * jnp.transpose(factor, (0, 2, 1))[..., None] + weighted
        return (new_max, run_total, accum_out)

    run_max, run_total, accum_out = sweep_blocks(key_part.shape[1], step_fn, initial)
    attn_wide = accum_out / jnp.transpose(run_total, (0, 2, 1))[..., None]
    lse_heads = run_max + jnp.log(run_total)
    attn_low = attn_wide.reshape(flat_rows, model_width).astype(jnp.bfloat16)
    hidden = inputs_wide + matmul_low(attn_low, full_out) + bias_out.astype(jnp.float32)
    normed_two_wide, norm_pull_two = jax.vjp(
        layer_norm, hidden, gain_second.astype(jnp.float32), shift_second.astype(jnp.float32)
    )
    normed_two = normed_two_wide.astype(jnp.bfloat16)
    before = matmul_low(normed_two, full_up) + bias_up.astype(jnp.float32)
    activated_wide, gelu_pull = jax.vjp(exact_gelu, before)
    activated = activated_wide.astype(jnp.bfloat16)
    output = (hidden + matmul_low(activated, full_down) + bias_down.astype(jnp.float32)).astype(
        jnp.bfloat16
    )
    back_params = (
        lax.all_gather(shards[0], ("dp", "ctx"), axis=0, tiled=True),
        lax.all_gather(shards[1], ("dp", "ctx"), axis=0, tiled=True),
        lax.all_gather(shards[2], ("dp", "ctx"), axis=0, tiled=True),
        lax.all_gather(shards[3], ("dp", "ctx"), axis=0, tiled=True),
        lax.all_gather(shards[4], ("dp", "ctx"), axis=0, tiled=True),
        lax.all_gather(shards[5], ("dp", "ctx"), axis=0, tiled=True),
        lax.all_gather(shards[6], ("dp", "ctx"), axis=0, tiled=True),
        lax.all_gather(shards[7], ("dp", "ctx"), axis=0, tiled=True),
        lax.all_gather(shards[8], ("dp", "ctx"), axis=0, tiled=True),
        lax.all_gather(shards[9], ("dp", "ctx"), axis=0, tiled=True),
        lax.all_gather(shards[10], ("dp", "ctx"), axis=0, tiled=True),
        lax.all_gather(shards[11], ("dp", "ctx"), axis=0, tiled=True),
    )
    back_qkv = back_params[2]
    back_out = back_params[4]
    back_up = back_params[8]
    back_down = back_params[10]
    grad_low = grad_out.reshape(flat_rows, model_width)
    grad_down = inner_rows(activated, grad_low)
    grad_bias_down = jnp.sum(grad_low.astype(jnp.float32), axis=0)
    grad_act = times_transpose(grad_low, back_down)
    grad_before = gelu_pull(grad_act)[0].astype(jnp.bfloat16)
    grad_up = inner_rows(normed_two, grad_before)
    grad_bias_up = jnp.sum(grad_before.astype(jnp.float32), axis=0)
    grad_normed_two = times_transpose(grad_before, back_up)
    grad_hidden_part, grad_gain_two, grad_shift_two = norm_pull_two(grad_normed_two)
    grad_hidden = grad_low.astype(jnp.float32) + grad_hidden_part
    grad_branch = grad_hidden.astype(jnp.bfloat16)
    grad_out_full = inner_rows(attn_low, grad_branch)
    grad_bias_out = jnp.sum(grad_branch.astype(jnp.float32), axis=0)
    grad_attn = times_transpose(grad_branch, back_out).astype(jnp.bfloat16)
    dout_heads = grad_attn.reshape(seq_count, tok_rows, head_count, head_size)
    delta_rows = jnp.sum(dout_heads.astype(jnp.float32) * attn_wide, axis=-1)
    delta_heads = jnp.transpose(delta_rows, (0, 2, 1))
    key_all, value_all, seg_all = (
        lax.all_gather(key_seq, "ctx", axis=1, tiled=True),
        lax.all_gather(value_seq, "ctx", axis=1, tiled=True),
        lax.all_gather(seg_low, "ctx", axis=1, tiled=True),
    )

    def key_step(offset, span_rows, inner_state):
        grad_query_acc, grad_key_all, grad_value_all = inner_state
        key_heads = lax.dynamic_slice_in_dim(key_all, offset, span_rows, 1).reshape(
            seq_count, span_rows, head_count, head_size
        )
        value_heads = lax.dynamic_slice_in_dim(value_all, offset, span_rows, 1).reshape(
            seq_count, span_rows, head_count, head_size
        )
        key_seg = lax.dynamic_slice_in_dim(seg_all, offset, span_rows, 1)
        key_pos = offset + jnp.arange(span_rows, dtype=jnp.int32)
        grad_query, grad_key, grad_value = pair_grads(
            live_table,
            query_heads,
            dout_heads,
            lse_heads,
            delta_heads,
            query_pos,
            seg_low,
            key_heads,
            value_heads,
            key_pos,
            key_seg,
        )
        grad_key_all = lax.dynamic_update_slice_in_dim(
            grad_key_all, grad_key.reshape(seq_count, span_rows, model_width), offset, 1
        )
        grad_value_all = lax.dynamic_update_slice_in_dim(
            grad_value_all, grad_value.reshape(seq_count, span_rows, model_width), offset, 1
        )
        return (grad_query_acc + grad_query, grad_key_all, grad_value_all)

    length_rows = key_all.shape[1]
    zero_query = jnp.zeros((seq_count, tok_rows, head_count, head_size), jnp.float32)
    zero_keys = jnp.zeros((seq_count, length_rows, model_width), jnp.float32)
    grad_query_heads, grad_key_all, grad_value_all = sweep_blocks(
        length_rows, key_step, (zero_query, zero_keys, zero_keys)
    )
    grad_key_seq, grad_value_seq = (
        lax.psum_scatter(
            grad_key_all.astype(jnp.bfloat16), "ctx", scatter_dimension=1, tiled=True
        ).astype(jnp.float32),
        lax.psum_scatter(
            grad_value_all.astype(jnp.bfloat16), "ctx", scatter_dimension=1, tiled=True
        ).astype(jnp.float32),
    )
    grad_query_low = grad_query_heads.reshape(flat_rows, model_width).astype(jnp.bfloat16)
    grad_key_low = grad_key_seq.reshape(flat_rows, model_width).astype(jnp.bfloat16)
    grad_value_low = grad_value_seq.reshape(flat_rows, model_width).astype(jnp.bfloat16)
    grad_proj_low = jnp.concatenate([grad_query_low, grad_key_low, grad_value_low], axis=1)
    grad_qkv_full = inner_rows(normed_one, grad_proj_low)
    grad_bias_qv = jnp.concatenate(
        [
            jnp.sum(grad_query_low.astype(jnp.float32), axis=0),
            jnp.sum(grad_value_low.astype(jnp.float32), axis=0),
        ]
    )
    grad_normed_one = times_transpose(grad_proj_low, back_qkv)
    grad_input_part, grad_gain_one, grad_shift_one = norm_pull_one(grad_normed_one)
    grad_tokens = (grad_hidden + grad_input_part).reshape(seq_count, tok_rows, model_width)
    summed = (
        lax.psum_scatter(grad_gain_one, ("dp", "ctx"), scatter_dimension=0, tiled=True),
        lax.psum_scatter(grad_shift_one, ("dp", "ctx"), scatter_dimension=0, tiled=True),
        lax.psum_scatter(grad_qkv_full.astype(jnp.bfloat16), ("dp", "ctx"), scatter_dimension=0, tiled=True).astype(jnp.float32),
        lax.psum_scatter(grad_bias_qv, ("dp", "ctx"), scatter_dimension=0, tiled=True),
        lax.psum_scatter(grad_out_full.astype(jnp.bfloat16), ("dp", "ctx"), scatter_dimension=0, tiled=True).astype(jnp.float32),
        lax.psum_scatter(grad_bias_out, ("dp", "ctx"), scatter_dimension=0, tiled=True),
        lax.psum_scatter(grad_gain_two, ("dp", "ctx"), scatter_dimension=0, tiled=True),
        lax.psum_scatter(grad_shift_two, ("dp", "ctx"), scatter_dimension=0, tiled=True),
        lax.psum_scatter(grad_up.astype(jnp.bfloat16), ("dp", "ctx"), scatter_dimension=0, tiled=True).astype(jnp.float32),
        lax.psum_scatter(grad_bias_up, ("dp", "ctx"), scatter_dimension=0, tiled=True),
        lax.psum_scatter(grad_down.astype(jnp.bfloat16), ("dp", "ctx"), scatter_dimension=0, tiled=True).astype(jnp.float32),
        lax.psum_scatter(grad_bias_down, ("dp", "ctx"), scatter_dimension=0, tiled=True),
    )
    return (
        output.reshape(seq_count, tok_rows, model_width),
        grad_tokens,
        summed[0],
        summed[1],
        summed[2],
        summed[3],
        summed[4],
        summed[5],
        summed[6],
        summed[7],
        summed[8],
        summed[9],
        summed[10],
        summed[11],
    )


NZ = 4
GROUP = HEADS // NZ
GW = GROUP * HEAD_DIM
CHUNK = 256


def pick(array, index, axis=0):
    return lax.dynamic_index_in_dim(array, index, axis, keepdims=False)


def shift(array, axis, size, hop):
    return lax.ppermute(array, axis, [(i, (i + hop) % size) for i in range(size)])


def swap(array, axis):
    return shift(array, axis, 2, 1)


def in_order(own, received, index, axis):
    first = jnp.where(index == 0, own, received)
    second = jnp.where(index == 0, received, own)
    return jnp.stack([first, second], axis=axis)


def hops(send, order):
    got = {hop: send(hop) for hop in order}
    return [got[hop] for hop in range(1, NZ)]


def z_pieces(block, order):
    return [block] + hops(lambda hop: shift(block, "z", NZ, hop), order)


def z_order(pieces, z):
    return jnp.stack([lax.select_n((z - a) % NZ, *pieces) for a in range(NZ)])


def z_exchange(array, z, order):
    return [pick(array, z)] + hops(lambda hop: shift(pick(array, (z + hop) % NZ), "z", NZ, hop), order)


def xy_gather(line, y, x):
    a, b = line[: NZ // 2], line[NZ // 2 :]
    a = in_order(a, swap(a, "x"), x, 0)
    b = in_order(b, swap(b, "y"), y, 0)
    return (a, swap(a, "y"), y, 0), (b, swap(b, "x"), x, 1)


def add_up(kept, sent, name):
    return kept.astype(jnp.float32) + swap(sent, name).astype(jnp.float32)


def halve(array, name, index, wire):
    return add_up(pick(array, index), pick(array, 1 - index).astype(wire), name)


def after(value, event):
    flag = event[(slice(0, 1),) * event.ndim].reshape(()).astype(jnp.float32)
    return jnp.where(flag != flag, jnp.zeros_like(value), value)


def meet(*values):
    return lax.optimization_barrier(values)


def z_reduce(sent, z):
    edge = jnp.where(z == 0, sent[2], sent[0])
    edge = lax.ppermute(edge, "z", [(0, 1), (NZ - 1, NZ - 2)])
    far = (sent[1].astype(jnp.float32) + edge.astype(jnp.float32)).astype(sent[1].dtype)
    far = shift(far, "z", NZ, 2)
    up = lax.ppermute(sent[0], "z", [(0, 1), (1, 2), (2, 3)])
    down = lax.ppermute(sent[2], "z", [(1, 0), (2, 1), (3, 2)])
    return up, far, down


def norm_back(grad, gain, unit, scale):
    c = grad * gain
    return scale * (
        c - jnp.mean(c, axis=-1, keepdims=True) - unit * jnp.mean(c * unit, axis=-1, keepdims=True)
    )


def dot_nt(a, b):
    return lax.dot_general(a, b, (((1,), (1,)), ((), ())), preferred_element_type=jnp.float32)


def dot_tn(a, b):
    return lax.dot_general(a, b, (((0,), (0,)), ((), ())), preferred_element_type=jnp.float32)


def dot_nn(a, b):
    return lax.dot_general(a, b, (((1,), (0,)), ((), ())), preferred_element_type=jnp.float32)


def column_of(row):
    return jnp.transpose(jnp.broadcast_to(row, (8, row.shape[1])))[:, 0:1]


def query_row(may_ref, tile, block, seg_row, alive):
    per = CHUNK // BLOCK
    lane = lax.broadcasted_iota(jnp.int32, (1, CHUNK), 1)
    flag = jnp.full((1, CHUNK), may_ref[tile * per, block] * alive, jnp.int32)
    for b in range(1, per):
        flag = jnp.where(lane >= b * BLOCK, may_ref[tile * per + b, block] * alive, flag)
    return jnp.where(flag > 0, seg_row, -1.0)


def permit_of(may_ref, tile, chunk, seg_row, key_column, alive):
    per = CHUNK // BLOCK
    return jnp.concatenate(
        [
            key_column[b * BLOCK : (b + 1) * BLOCK]
            == query_row(may_ref, tile, chunk * per + b, seg_row, alive)
            for b in range(per)
        ],
        axis=0,
    )


def list_live(live, list_ref):
    count = jnp.int32(0)
    for number, flag in enumerate(live):
        list_ref[count] = number
        count = count + flag
    list_ref[count] = list_ref[jnp.maximum(count - 1, 0)]
    return count


def pair_at(list_ref, count, step):
    return (
        (list_ref[2 * step], jnp.int32(1)),
        (list_ref[2 * step + 1], (2 * step + 1 < count).astype(jnp.int32)),
    )


def whole_spec(shape):
    return pl.BlockSpec(shape, lambda *_: (0,) * len(shape))


def held(specs, arrays):
    return [
        pl.BlockSpec(memory_space=pltpu.VMEM) if tuple(spec.block_shape) == a.shape else spec
        for spec, a in zip(specs, arrays)
    ]


VMEM_MIB = {
    "unpack": 4, "pack": 4, "project": 14, "branch": 10, "feed": 28, "feed_weights": 24, "middle": 16,
    "inward": 16, "owners": 20, "finish": 10, "deliver": 6, "weave": 6,
}


WEIGHT = {
    "project": 1, "branch": 3, "feed": 10, "feed_weights": 3, "middle": 3, "inward": 3, "owners": 3, "finish": 10, "deliver": 3, "weave": 3,
}


def kernel_call(body, place, arrays, in_specs, outs, out_specs, grid, scratch, flops, name, more=()):
    prefetch = (place,) + tuple(more)
    moved = sum(a.size * a.dtype.itemsize for a in arrays)
    return pl.pallas_call(
        body,
        out_shape=tuple(jax.ShapeDtypeStruct(shape, dtype) for shape, dtype in outs),
        grid_spec=pltpu.PrefetchScalarGridSpec(
            num_scalar_prefetch=len(prefetch),
            grid=grid,
            in_specs=held(in_specs, arrays),
            out_specs=out_specs,
            scratch_shapes=scratch,
        ),
        compiler_params=pltpu.CompilerParams(vmem_limit_bytes=VMEM_MIB[name] << 20),
        cost_estimate=pl.CostEstimate(
            flops=int(flops * WEIGHT.get(name, 1)), bytes_accessed=int(moved * WEIGHT.get(name, 1)), transcendentals=0
        ),
        name=name,
    )(*prefetch, *arrays)


def lane_groups(lanes, size):
    lane = lax.broadcasted_iota(jnp.int32, (1, lanes), 1).astype(jnp.float32)
    group = jnp.floor((lane + 0.5) * (1.0 / size))
    return group, lane - group * size


def one_hot_rows(place_row, count):
    rows = lax.broadcasted_iota(jnp.int32, (count, place_row.shape[1]), 0).astype(jnp.float32)
    return (rows == place_row).astype(jnp.float32).astype(jnp.bfloat16)


VEC_ROWS = 16


def unpack_kernel(place_ref, packed_ref, vec_ref):
    devices = packed_ref.shape[0]
    width = vec_ref.shape[1]
    size = width // devices
    c = place_ref[1]
    device = lax.broadcasted_iota(jnp.int32, (devices, 1), 0)
    parity = lax.rem(device, 2)
    pair = lax.div(device, 2).astype(jnp.float32)
    device = device.astype(jnp.float32)
    vec_ref[...] = jnp.zeros(vec_ref.shape, jnp.float32)

    def spread(start, n, lanes, owner, keep):
        group, at = lane_groups(lanes, n)
        tiled = dot_nn(packed_ref[:, start : start + n], one_hot_rows(at, n))
        mine = (owner == group) if keep is None else (owner == group) & keep
        return jnp.sum(jnp.where(mine, tiled, 0.0), axis=0, keepdims=True)

    vec_ref[0:1] = spread(0, size, width, device, None)
    vec_ref[1:2] = spread(size, size, width, device, None)
    qv = spread(2 * size, 2 * size, 2 * width, device, None)
    vec_ref[2:3] = qv[:, :width]
    vec_ref[3:4] = qv[:, width:]
    vec_ref[4:5] = spread(4 * size, size, width, device, None)
    vec_ref[5:6] = spread(5 * size, size, width, device, None)
    vec_ref[6:7] = spread(6 * size, size, width, device, None)
    up = spread(7 * size, 4 * size, 2 * width, pair, parity == c)
    vec_ref[8:9] = up[:, :width]
    vec_ref[9:10] = up[:, width:]
    vec_ref[7:8] = spread(11 * size, size, width, device, None)


def pack_kernel(place_ref, grads_ref, mid_ref, qkv_ref, up_ref, packed_ref):
    devices = packed_ref.shape[0]
    width = grads_ref.shape[1]
    size = width // devices
    z, c = place_ref[0], place_ref[1]
    device = lax.broadcasted_iota(jnp.int32, (devices, 1), 0)
    parity = lax.rem(device, 2)
    pair = lax.div(device, 2).astype(jnp.float32)
    device = device.astype(jnp.float32)
    packed_ref[...] = jnp.zeros(packed_ref.shape, jnp.bfloat16)

    def gather(row, n, owner, keep):
        group, at = lane_groups(row.shape[1], n)
        mine = (owner == group) if keep is None else (owner == group) & keep
        return dot_nt(jnp.where(mine, row, 0.0).astype(jnp.bfloat16), one_hot_rows(at, n))

    def place_group(row):
        wide = jnp.concatenate([row] * NZ, axis=1)
        group, _ = lane_groups(wide.shape[1], GW)
        return jnp.where(group == z.astype(jnp.float32), wide, 0.0)

    qkv = qkv_ref[0:1]
    qv = jnp.concatenate([place_group(qkv[:, :GW]), place_group(qkv[:, 2 * GW :])], axis=1)
    parts = [
        gather(grads_ref[0:1], size, device, None),
        gather(grads_ref[1:2], size, device, None),
        gather(qv, 2 * size, device, None),
        gather(mid_ref[2:3], size, device, None),
        gather(mid_ref[0:1], size, device, None),
        gather(mid_ref[1:2], size, device, None),
        gather(up_ref[0:1], 4 * size, pair, parity == c),
        gather(mid_ref[3:4], size, device, None),
    ]
    packed_ref[:, 0 : 12 * size] = jnp.concatenate(parts, axis=1).astype(jnp.bfloat16)


def norm_rows(x):
    center = x - jnp.mean(x, axis=-1, keepdims=True)
    scale = lax.rsqrt(jnp.mean(center * center, axis=-1, keepdims=True) + 1e-05)
    return center * scale, scale


def project_kernel(place_ref, t0_ref, t1_ref, t2_ref, t3_ref, vec_ref, wz_ref, line_ref, n1_ref, q_ref, kv_ref):
    a = pl.program_id(0)
    z = place_ref[0]
    away = lax.rem(z - a + NZ, NZ)
    x = t0_ref[...].astype(jnp.float32)
    for j, ref in enumerate((t1_ref, t2_ref, t3_ref), 1):
        x = jnp.where(away == j, ref[...].astype(jnp.float32), x)
    line_ref[...] = x.astype(jnp.bfloat16)
    unit, _ = norm_rows(x)
    n1 = (unit * vec_ref[0:1] + vec_ref[1:2]).astype(jnp.bfloat16)
    n1_ref[...] = n1
    y = dot_nn(n1, wz_ref[...])
    q_bias, v_bias = vec_ref[2:3, 0:GW], vec_ref[3:4, 0:GW]
    for g in range(1, NZ):
        q_bias = jnp.where(z == g, vec_ref[2:3, g * GW : (g + 1) * GW], q_bias)
        v_bias = jnp.where(z == g, vec_ref[3:4, g * GW : (g + 1) * GW], v_bias)
    q = (y[:, :GW] + q_bias).astype(jnp.bfloat16)
    q_ref[...] = q * jnp.asarray(SCORE_SCALE, jnp.bfloat16)
    kv_ref[:, :GW] = y[:, GW : 2 * GW].astype(jnp.bfloat16)
    kv_ref[:, GW:] = (y[:, 2 * GW :] + v_bias).astype(jnp.bfloat16)


def project(place, pieces, vec, wz):
    rows, width = pieces[0].shape
    low = jnp.bfloat16
    tall = lambda w: pl.BlockSpec((rows, w), lambda a, *_: (a, 0))
    return kernel_call(
        project_kernel, place, (*pieces, vec, wz),
        [whole_spec((rows, width))] * NZ + [whole_spec(vec.shape), whole_spec(wz.shape)],
        [((NZ * rows, width), low), ((NZ * rows, width), low), ((NZ * rows, GW), low), ((NZ * rows, 2 * GW), low)],
        [tall(width), tall(width), tall(GW), tall(2 * GW)],
        (NZ,), [], 8 * NZ * rows * width * 3 * GW, "project",
    )


def branch_kernel(place_ref, a0_ref, a1_ref, a2_ref, a3_ref, wo_ref, own_ref, vec_ref, hidden_ref, n2_ref):
    z = place_ref[0]
    total = own_ref[...].astype(jnp.float32) + vec_ref[4:5]
    branch = None
    for j, ref in enumerate((a0_ref, a1_ref, a2_ref, a3_ref)):
        start = pl.multiple_of(lax.rem(z - j + NZ, NZ) * GW, GW)
        part = dot_nn(ref[...], wo_ref[pl.ds(start, GW), :])
        branch = part if branch is None else branch + part
    hidden = total + branch
    hidden_ref[...] = hidden
    unit, _ = norm_rows(hidden)
    n2_ref[...] = (unit * vec_ref[5:6] + vec_ref[6:7]).astype(jnp.bfloat16)


def branch_call(place, pieces, wo, own, vec):
    rows, width = own.shape
    arrays = (*pieces, wo, own, vec)
    return kernel_call(
        branch_kernel, place, arrays, [whole_spec(a.shape) for a in arrays],
        [((rows, width), jnp.float32), ((rows, width), jnp.bfloat16)],
        [whole_spec((rows, width))] * 2, (1,), [], 8 * rows * width * width, "branch",
    )


def feed_kernel(
    place_ref, na_ref, nb_ref, ga_ref, gb_ref, up_ref, down_ref, bias_ref,
    act_ref, grad_ref, out_ref, m_ref, sums_ref, bias_out_ref, n_s, g_s, out_s, m_s,
):
    k = pl.program_id(0)
    rows, width = na_ref.shape

    @pl.when(k == 0)
    def _():
        n_s[:rows], n_s[rows:] = na_ref[...], nb_ref[...]
        g_s[:rows], g_s[rows:] = ga_ref[...], gb_ref[...]
        out_s[...] = jnp.zeros(out_s.shape, jnp.float32)
        m_s[...] = jnp.zeros(m_s.shape, jnp.float32)

    up, down = up_ref[...].reshape(width, width), down_ref[...].reshape(width, width)
    v = dot_nn(n_s[...], up) + bias_ref[...]
    cdf = 0.5 * (1.0 + lax.erf(v * 0.7071067811865476))
    slope = cdf + v * (0.3989422804014327 * jnp.exp(-0.5 * v * v))
    act = (v * cdf).astype(jnp.bfloat16)
    act_ref[...] = act
    grad = dot_nt(g_s[...], down) * slope
    grad = grad.astype(jnp.bfloat16)
    grad_ref[...] = grad
    bias_out_ref[...] = jnp.sum(grad.astype(jnp.float32), axis=0, keepdims=True)
    out_s[...] += dot_nn(act, down)
    m_s[...] += dot_nt(grad, up)

    @pl.when(k == pl.num_programs(0) - 1)
    def _():
        out_ref[...] = out_s[:rows]
        m_ref[...] = m_s[:rows]
        sums_ref[0] = m_s[rows:].astype(jnp.bfloat16)
        sums_ref[1] = out_s[rows:].astype(jnp.bfloat16)


def feed(place, na, nb, ga, gb, both, bias):
    rows, width = na.shape
    chips, tall, _ = both.shape
    half = bias.shape[1]
    low, wide = jnp.bfloat16, jnp.float32
    one = whole_spec((rows, width))
    across = lambda r: pl.BlockSpec((r, width), lambda k, *_: (0, k))
    return kernel_call(
        feed_kernel, place, (na, nb, ga, gb, both, both, bias),
        [one] * 4 + [
            pl.BlockSpec((chips, tall // 4, width), lambda k, *_: (0, k, 0)),
            pl.BlockSpec((chips // 2, tall // 2, width), lambda k, *_: (k, 1, 0)),
            across(1),
        ],
        [
            ((2 * rows, half), low), ((2 * rows, half), low), ((rows, width), wide), ((rows, width), wide),
            ((2, rows, width), low), ((1, half), wide),
        ],
        [across(2 * rows), across(2 * rows), one, one, whole_spec((2, rows, width)), across(1)],
        (2,),
        [
            pltpu.VMEM((2 * rows, width), low), pltpu.VMEM((2 * rows, width), low),
            pltpu.VMEM((2 * rows, width), wide), pltpu.VMEM((2 * rows, width), wide),
        ],
        32 * rows * width * half, "feed",
    )


def feed_weights_kernel(
    place_ref, na_ref, nb_ref, ga_ref, gb_ref, act_ref, grad_ref, ak_ref, as_ref, bk_ref, bs_ref, n_s, a_s, g_s
):
    rows, width = na_ref.shape
    y, x = place_ref[2], place_ref[3]
    n_s[:, :rows], n_s[:, rows:] = jnp.transpose(na_ref[...]), jnp.transpose(nb_ref[...])
    g_s[:rows], g_s[rows:] = ga_ref[...], gb_ref[...]
    for k in range(0, act_ref.shape[1], width):
        a_s[k : k + width] = jnp.transpose(act_ref[:, k : k + width])
    tall = ak_ref.shape[2]
    quarter = tall // 4
    span = NZ * quarter

    def put(py, px, pz, row, value):
        count = value.shape[0]
        near, far = (ak_ref, as_ref) if pz < NZ // 2 else (bk_ref, bs_ref)
        index, mine = (px, py == y) if pz < NZ // 2 else (py, px == x)

        @pl.when(mine)
        def _():
            near[index, pz % (NZ // 2), row : row + count] = value

        @pl.when(jnp.logical_not(mine))
        def _():
            far[index, pz % (NZ // 2), row : row + count] = value

    def one_column(column, carry):
        py, px = lax.div(column, 2), lax.rem(column, 2)
        at = pl.multiple_of(column * span, span)
        up = dot_nn(n_s[pl.ds(at, span)], grad_ref[...]).astype(jnp.bfloat16)
        down = dot_nn(a_s[pl.ds(pl.multiple_of(2 * at, 2 * span), 2 * span)], g_s[...]).astype(jnp.bfloat16)
        for pz in range(NZ):
            here = slice(pz * quarter, (pz + 1) * quarter)
            put(py, px, pz, 0, up[here, :width])
            put(py, px, pz, quarter, up[here, width:])
            put(py, px, pz, 2 * quarter, down[2 * pz * quarter : 2 * (pz + 1) * quarter])
        return carry

    lax.fori_loop(0, 4, one_column, 0)


def feed_weights(place, na, nb, ga, gb, act, grad, tall):
    rows, width = na.shape
    low = jnp.bfloat16
    arrays = (na, nb, ga, gb, act, grad)
    shape = (2, NZ // 2, tall, width)
    return kernel_call(
        feed_weights_kernel, place, arrays, [whole_spec(a.shape) for a in arrays], [(shape, low)] * 4,
        [whole_spec(shape)] * 4, (1,),
        [
            pltpu.VMEM((width, 2 * rows), low), pltpu.VMEM((act.shape[1], 2 * rows), low),
            pltpu.VMEM((2 * rows, width), low),
        ],
        8 * rows * width * act.shape[1], "feed_weights",
    )


def middle_kernel(
    place_ref, m_ref, out_ref, sums_ref, hidden_ref, go_ref, vec_ref, wo_ref,
    output_ref, gh_ref, branch_ref, d0_ref, d1_ref, d2_ref, d3_ref, cols_ref,
):
    z = place_ref[0]
    hidden, go = hidden_ref[...], go_ref[...].astype(jnp.float32)
    output_ref[...] = (hidden + out_ref[...] + sums_ref[1].astype(jnp.float32) + vec_ref[7:8]).astype(
        jnp.bfloat16
    )
    m = m_ref[...] + sums_ref[0].astype(jnp.float32)
    unit, scale = norm_rows(hidden)
    grad_hidden = go + norm_back(m, vec_ref[5:6], unit, scale)
    gh_ref[...] = grad_hidden
    branch = grad_hidden.astype(jnp.bfloat16)
    branch_ref[...] = branch
    for j, ref in enumerate((d0_ref, d1_ref, d2_ref, d3_ref)):
        start = pl.multiple_of(lax.rem(z + j, NZ) * GW, GW)
        ref[...] = dot_nt(branch, wo_ref[pl.ds(start, GW), :]).astype(jnp.bfloat16)
    cols_ref[...] = jnp.zeros(cols_ref.shape, jnp.float32)
    cols_ref[0:1] = jnp.sum(m * unit, axis=0, keepdims=True)
    cols_ref[1:2] = jnp.sum(m, axis=0, keepdims=True)
    cols_ref[2:3] = jnp.sum(branch.astype(jnp.float32), axis=0, keepdims=True)
    cols_ref[3:4] = jnp.sum(go, axis=0, keepdims=True)


def middle(place, m, out, sums, hidden, go, vec, wo):
    rows, width = m.shape
    arrays = (m, out, sums, hidden, go, vec, wo)
    low, wide = jnp.bfloat16, jnp.float32
    outs = [((rows, width), low), ((rows, width), wide), ((rows, width), low)]
    outs += [((rows, GW), low)] * NZ + [((8, width), wide)]
    return kernel_call(
        middle_kernel, place, arrays, [whole_spec(a.shape) for a in arrays], outs,
        [whole_spec(shape) for shape, _ in outs], (1,), [], 8 * rows * width * width, "middle",
    )


def inward_kernel(
    place_ref, dq_ref, mine_ref, theirs_ref, line_ref, wz_ref, dqkv_ref, keep_ref, s1_ref, s2_ref, s3_ref,
    cols_ref, sums_ref,
):
    j = pl.program_id(0)
    rows = keep_ref.shape[0]
    at = pl.ds(pl.multiple_of(lax.rem(place_ref[0] + 1 + j, NZ) * rows, rows), rows)
    dkv = (mine_ref[at].astype(jnp.float32) + theirs_ref[at].astype(jnp.float32)).astype(jnp.bfloat16)
    dqkv = jnp.concatenate([dq_ref[at], dkv], axis=1)
    dqkv_ref[at] = dqkv
    m1 = dot_nt(dqkv, wz_ref[...])
    unit, _ = norm_rows(line_ref[at].astype(jnp.float32))

    @pl.when(j == 0)
    def _():
        cols_ref[...] = jnp.zeros(cols_ref.shape, jnp.float32)
        sums_ref[...] = jnp.zeros(sums_ref.shape, jnp.float32)

    cols_ref[0:1] += jnp.sum(m1 * unit, axis=0, keepdims=True)
    cols_ref[1:2] += jnp.sum(m1, axis=0, keepdims=True)
    sums_ref[0:1] += jnp.sum(dqkv.astype(jnp.float32), axis=0, keepdims=True)

    for number, ref in enumerate((s1_ref, s2_ref, s3_ref)):

        @pl.when(j == number)
        def _():
            ref[...] = m1.astype(jnp.bfloat16)

    @pl.when(j == pl.num_programs(0) - 1)
    def _():
        keep_ref[...] = m1


def inward(place, dq, mine, theirs, line, wz):
    total, width = line.shape
    rows = total // NZ
    low, wide = jnp.bfloat16, jnp.float32
    arrays = (dq, mine, theirs, line, wz)
    outs = [((total, 3 * GW), low), ((rows, width), wide)] + [((rows, width), low)] * (NZ - 1)
    outs += [((8, width), wide), ((8, 3 * GW), wide)]
    return kernel_call(
        inward_kernel, place, arrays, [whole_spec(a.shape) for a in arrays], outs,
        [whole_spec(shape) for shape, _ in outs], (NZ,), [], 8 * total * width * 3 * GW, "inward",
    )


def finish_kernel(place_ref, m_ref, r1_ref, r2_ref, r3_ref, own_ref, gh_ref, vec_ref, out_ref):
    m = m_ref[...]
    for ref in (r1_ref, r2_ref, r3_ref):
        m = m + ref[...].astype(jnp.float32)
    unit, scale = norm_rows(own_ref[...].astype(jnp.float32))
    out_ref[...] = gh_ref[...] + norm_back(m, vec_ref[0:1], unit, scale)


def finish(place, m, pieces, own, grad_hidden, vec):
    rows, width = own.shape
    arrays = (m, *pieces, own, grad_hidden, vec)
    return kernel_call(
        finish_kernel, place, arrays, [whole_spec(a.shape) for a in arrays],
        [((rows, width), jnp.float32)], [whole_spec((rows, width))], (1,), [], 100 * rows * width, "finish",
    )[0]


def owners_kernel(
    place_ref, a0_ref, a1_ref, a2_ref, a3_ref, branch_ref, n1_ref, dqkv_ref, cols_ref, mid_ref, sums_ref, up_ref,
    mine_ref, theirs_ref, wo_s, wz_s, vec_s,
):
    z, c = place_ref[0], place_ref[1]
    width = branch_ref.shape[1]
    for j, ref in enumerate((a0_ref, a1_ref, a2_ref, a3_ref)):
        start = pl.multiple_of(lax.rem(z - j + NZ, NZ) * GW, GW)
        wo_s[pl.ds(start, GW), :] = dot_tn(ref[...], branch_ref[...]).astype(jnp.bfloat16)
    wz_s[...] = dot_tn(n1_ref[...], dqkv_ref[...]).astype(jnp.bfloat16)
    pack_kernel(place_ref, cols_ref, mid_ref, sums_ref, up_ref, vec_s)
    chips, tall, span = mine_ref.shape
    devices = 2 * chips
    rows = width // devices
    first_row = lax.broadcasted_iota(jnp.int32, (tall - rows, span), 0) == 0
    for pair in range(chips):
        tails = []
        for core in range(2):
            row = vec_s[2 * pair + core : 2 * pair + core + 1].astype(jnp.float32)
            tails.append(jnp.where(first_row, jnp.broadcast_to(row, first_row.shape), 0.0).astype(jnp.bfloat16))
        mine_ref[pair, rows:] = jnp.where(c == 0, tails[0], tails[1])
        theirs_ref[pair, rows:] = jnp.where(c == 0, tails[1], tails[0])

    def one_chip(pair, carry):
        at = pl.ds(pl.multiple_of(pair * (2 * rows), 2 * rows), 2 * rows)
        both = jnp.concatenate([wo_s[at], wz_s[at]], axis=1)
        mine_ref[pair, :rows] = jnp.where(c == 0, both[:rows], both[rows:])
        theirs_ref[pair, :rows] = jnp.where(c == 0, both[rows:], both[:rows])
        return carry

    lax.fori_loop(0, chips, one_chip, 0)


def owners(place, pieces, branch, n1, dqkv, cols, mid, sums, up, devices, tall):
    width, span = n1.shape[1], n1.shape[1] + dqkv.shape[1]
    low = jnp.bfloat16
    arrays = (*pieces, branch, n1, dqkv, cols, mid, sums, up)
    shape = (devices // 2, tall, span)
    return kernel_call(
        owners_kernel, place, arrays, [whole_spec(a.shape) for a in arrays], [(shape, low), (shape, low)],
        [whole_spec(shape)] * 2, (1,),
        [pltpu.VMEM((width, width), low), pltpu.VMEM((width, dqkv.shape[1]), low), pltpu.VMEM((devices, span), low)],
        1 << 20, "owners",
    )


def deliver_kernel(place_ref, own_ref, p1_ref, p2_ref, p3_ref, qkv_ref, wo_ref, vec_ref):
    z = place_ref[0]
    rows, width = wo_ref.shape
    own = own_ref[...]
    pieces = [own] + [ref[...].astype(jnp.float32) for ref in (p1_ref, p2_ref, p3_ref)]
    for g in range(NZ):
        away = lax.rem(z - g + NZ, NZ)
        part = pieces[0]
        for j in range(1, NZ):
            part = jnp.where(away == j, pieces[j], part)
        for k in range(3):
            lanes = slice(k * width + g * GW, k * width + (g + 1) * GW)
            qkv_ref[:, lanes] = part[:rows, width + k * GW : width + (k + 1) * GW]
    total = pieces[0] + pieces[1] + pieces[2] + pieces[3]
    wo_ref[...] = total[:rows, :width]
    vec_ref[...] = total[rows:]


def weave_kernel(place_ref, mine_ref, theirs_ref, out_ref):
    c = place_ref[1]
    mine, theirs = mine_ref[...], theirs_ref[...].astype(jnp.float32)
    even, odd = jnp.where(c == 0, mine, theirs), jnp.where(c == 0, theirs, mine)
    half = mine.shape[1]
    units = half // 16
    for pair in range(16):
        here = slice(pair * units, (pair + 1) * units)
        out_ref[:, 2 * pair * units : (2 * pair + 1) * units] = even[:, here]
        out_ref[:, (2 * pair + 1) * units : (2 * pair + 2) * units] = odd[:, here]


def attend_kernel(
    act_ref, may_ref, place_ref, q_ref, mine_ref, theirs_ref, qseg_ref, kseg_ref, o_ref, low_ref, lse_ref,
    k_s, vt_s, col_s, m_s, l_s, acc_s, list_s,
):
    i = pl.program_id(0)
    chunks = kseg_ref.shape[0]

    @pl.when(i == 0)
    def _():
        for line, ref in enumerate((mine_ref, theirs_ref)):
            core = place_ref[1] if line == 0 else 1 - place_ref[1]
            for a in range(chunks // 2):
                rows = slice(a * CHUNK, (a + 1) * CHUNK)
                at = pl.ds(pl.multiple_of((2 * a + core) * CHUNK, CHUNK), CHUNK)
                turned = jnp.transpose(ref[rows, :])
                for h in range(GROUP):
                    k_s[h, at] = ref[rows, HEAD_DIM * h : HEAD_DIM * (h + 1)]
                    vt_s[h, :, at] = turned[GW + HEAD_DIM * h : GW + HEAD_DIM * (h + 1)]
        for j in range(chunks):
            col_s[j * CHUNK : (j + 1) * CHUNK] = column_of(kseg_ref[j : j + 1])

    m_s[...] = jnp.full(m_s.shape, NEG_FILL, jnp.float32)
    l_s[...] = jnp.zeros(l_s.shape, jnp.float32)
    acc_s[...] = jnp.zeros(acc_s.shape, jnp.float32)
    here = pl.ds(pl.multiple_of(i * CHUNK, CHUNK), CHUNK)
    q_heads = [q_ref[here, HEAD_DIM * h : HEAD_DIM * (h + 1)] for h in range(GROUP)]
    q_seg = qseg_ref[pl.ds(i, 1)]

    count = list_live([act_ref[i, j] for j in range(chunks)], list_s)

    def two_chunks(step, carry):
        heads, pair = range(GROUP), pair_at(list_s, count, step)
        at = [pl.ds(pl.multiple_of(j * CHUNK, CHUNK), CHUNK) for j, _ in pair]
        permit = [permit_of(may_ref, i, j, q_seg, col_s[at[u]], alive) for u, (j, alive) in enumerate(pair)]
        s = [[jnp.where(permit[u], dot_nt(k_s[h, at[u]], q_heads[h]), NEG_FILL) for u in range(2)] for h in heads]
        old = [m_s[h] for h in heads]
        top = [[jnp.max(part, axis=0, keepdims=True) for part in s[h]] for h in heads]
        new = [jnp.maximum(old[h], jnp.maximum(*top[h])) for h in heads]
        p = [[jnp.exp(part - new[h]) for part in s[h]] for h in heads]
        fade = [jnp.exp(old[h] - new[h]) for h in heads]
        for h in heads:
            l_s[h] = l_s[h] * fade[h] + sum(jnp.sum(part, axis=0, keepdims=True) for part in p[h])
            added = [dot_nn(vt_s[h, :, at[u]], p[h][u].astype(jnp.bfloat16)) for u in range(2)]
            acc_s[h] = acc_s[h] * fade[h] + (added[0] + added[1])
            m_s[h] = new[h]
        return carry

    lax.fori_loop(0, lax.div(count + 1, 2), two_chunks, 0)
    out = jnp.concatenate([jnp.transpose(acc_s[h] / l_s[h]) for h in range(GROUP)], axis=1)
    o_ref[...] = out
    low_ref[...] = out.astype(jnp.bfloat16)
    logs = [m_s[h] + jnp.log(l_s[h]) for h in range(GROUP)]
    lse_ref[...] = jnp.concatenate(logs + [logs[0]] * (8 - GROUP), axis=0)


def attend(active, may, place, q, mine, theirs, q_seg, k_seg):
    rows, keys = q.shape[0], 2 * mine.shape[0]
    tall = pl.BlockSpec((CHUNK, GW), lambda i, *_: (i, 0))
    return pl.pallas_call(
        attend_kernel,
        out_shape=(
            jax.ShapeDtypeStruct((rows, GW), jnp.float32),
            jax.ShapeDtypeStruct((rows, GW), jnp.bfloat16),
            jax.ShapeDtypeStruct((8, rows), jnp.float32),
        ),
        grid_spec=pltpu.PrefetchScalarGridSpec(
            num_scalar_prefetch=3,
            grid=(rows // CHUNK,),
            in_specs=held(
                [whole_spec(a.shape) for a in (q, mine, theirs, q_seg, k_seg)], (q, mine, theirs, q_seg, k_seg)
            ),
            out_specs=[tall, tall, pl.BlockSpec((8, CHUNK), lambda i, *_: (0, i))],
            scratch_shapes=[
                pltpu.VMEM((GROUP, keys, HEAD_DIM), jnp.bfloat16),
                pltpu.VMEM((GROUP, HEAD_DIM, keys), jnp.bfloat16),
                pltpu.VMEM((keys, 1), jnp.float32),
                pltpu.VMEM((GROUP, 1, CHUNK), jnp.float32),
                pltpu.VMEM((GROUP, 1, CHUNK), jnp.float32),
                pltpu.VMEM((GROUP, HEAD_DIM, CHUNK), jnp.float32),
                pltpu.SMEM((keys // CHUNK + 1,), jnp.int32),
            ],
        ),
        compiler_params=pltpu.CompilerParams(vmem_limit_bytes=18 << 20),
        cost_estimate=pl.CostEstimate(
            flops=int(48 * rows * keys * GW), bytes_accessed=16 * keys * GW, transcendentals=4 * rows * keys
        ),
        name="attend",
    )(active, may, place, q, mine, theirs, q_seg, k_seg)


def attend_back_kernel(first, *refs):
    (act_ref, may_ref, place_ref, q_ref, d0_ref, d1_ref, d2_ref, d3_ref, kv_ref, lse_ref, qseg_ref,
     kseg_ref, from_ref, *refs) = refs
    if first:
        dqt_ref, delta_ref, dkv_ref, list_s, q_s, do_s, dk_s, dv_s = refs
    else:
        old_ref, dq_ref, dkv_ref, list_s, q_s, do_s, dk_s, dv_s, dqt_ref = refs
        delta_ref = from_ref
    step = pl.program_id(0)
    rows = q_ref.shape[0]
    z, c = place_ref[0], place_ref[1]
    j = 2 * step + (1 - c if first else c)

    @pl.when(step == 0)
    def _():
        for r, ref in enumerate((d0_ref, d1_ref, d2_ref, d3_ref)):
            at = pl.ds(pl.multiple_of(lax.rem(z - r + NZ, NZ) * CHUNK, CHUNK), CHUNK)
            for h in range(GROUP):
                do_s[h, at] = ref[:, HEAD_DIM * h : HEAD_DIM * (h + 1)]
        ones = jnp.ones((8, HEAD_DIM), jnp.bfloat16)
        for h in range(GROUP):
            lanes = slice(HEAD_DIM * h, HEAD_DIM * (h + 1))
            q_s[h] = q_ref[:, lanes]
            if first:
                both = do_s[h].astype(jnp.float32) * from_ref[:, lanes]
                high = both.astype(jnp.bfloat16)
                rest = (both - high.astype(jnp.float32)).astype(jnp.bfloat16)
                delta_ref[h : h + 1] = (dot_nt(ones, high) + dot_nt(ones, rest))[0:1]
        dqt_ref[...] = jnp.zeros(dqt_ref.shape, jnp.float32) if first else old_ref[...]
        if first:
            delta_ref[GROUP:] = jnp.zeros((8 - GROUP, rows), jnp.float32)

    dk_s[...] = jnp.zeros(dk_s.shape, jnp.float32)
    dv_s[...] = jnp.zeros(dv_s.shape, jnp.float32)
    here = pl.ds(pl.multiple_of(step * CHUNK, CHUNK), CHUNK)
    k_heads = [kv_ref[here, HEAD_DIM * h : HEAD_DIM * (h + 1)] for h in range(GROUP)]
    v_heads = [kv_ref[here, GW + HEAD_DIM * h : GW + HEAD_DIM * (h + 1)] for h in range(GROUP)]
    turned = jnp.transpose(kv_ref[here, :])
    k_turned = [turned[HEAD_DIM * h : HEAD_DIM * (h + 1)] for h in range(GROUP)]
    k_column = column_of(kseg_ref[pl.ds(j, 1)])

    count = list_live([act_ref[i, j] for i in range(rows // CHUNK)], list_s)

    def two_tiles(turn, carry):
        heads, pair, low = range(GROUP), pair_at(list_s, count, turn), jnp.bfloat16
        both = [(h, u) for h in heads for u in range(2)]
        at = [pl.ds(pl.multiple_of(i * CHUNK, CHUNK), CHUNK) for i, _ in pair]
        permit = [
            permit_of(may_ref, i, j, qseg_ref[pl.ds(i, 1)], k_column, alive) for i, alive in pair
        ]
        s = {(h, u): dot_nt(k_heads[h], q_s[h, at[u]]) for h, u in both}
        dp = {(h, u): dot_nt(v_heads[h], do_s[h, at[u]]) for h, u in both}
        p = {
            (h, u): jnp.where(permit[u], jnp.exp(s[h, u] - lse_ref[h : h + 1, at[u]]), 0.0) for h, u in both
        }
        ds = {(h, u): (p[h, u] * (dp[h, u] - delta_ref[h : h + 1, at[u]])).astype(low) for h, u in both}
        for h in heads:
            dv_s[h] += dot_nn(p[h, 0].astype(low), do_s[h, at[0]]) + dot_nn(p[h, 1].astype(low), do_s[h, at[1]])
            dk_s[h] += dot_nn(ds[h, 0], q_s[h, at[0]]) + dot_nn(ds[h, 1], q_s[h, at[1]])
            for u in range(2):
                dqt_ref[h, :, at[u]] += dot_nn(k_turned[h], ds[h, u])
        return carry

    lax.fori_loop(0, lax.div(count + 1, 2), two_tiles, 0)
    dkv_ref[...] = jnp.concatenate(
        [dk_s[h] for h in range(GROUP)] + [dv_s[h] for h in range(GROUP)], axis=1
    ).astype(jnp.bfloat16)
    if not first:

        @pl.when(step == pl.num_programs(0) - 1)
        def _():
            dq_ref[...] = jnp.concatenate(
                [jnp.transpose(dqt_ref[h] * SCORE_SCALE) for h in range(GROUP)], axis=1
            ).astype(jnp.bfloat16)


def attend_back(first, active, may, place, q, pieces, kv, lse, q_seg, k_seg, *carried):
    rows = q.shape[0]
    low, wide = jnp.bfloat16, jnp.float32
    tall = pl.BlockSpec((CHUNK, 2 * GW), lambda s, *_: (s, 0))
    turned = (GROUP, HEAD_DIM, rows)
    outs = [(turned, wide), ((8, rows), wide)] if first else [((rows, GW), low)]
    scratch = [pltpu.SMEM((rows // CHUNK + 1,), jnp.int32)] + [pltpu.VMEM((GROUP, rows, HEAD_DIM), low)] * 2 + [pltpu.VMEM((GROUP, CHUNK, HEAD_DIM), wide)] * 2
    if not first:
        scratch.append(pltpu.VMEM(turned, wide))
    return pl.pallas_call(
        functools.partial(attend_back_kernel, first),
        out_shape=tuple(jax.ShapeDtypeStruct(*o) for o in outs + [((rows, 2 * GW), low)]),
        grid_spec=pltpu.PrefetchScalarGridSpec(
            num_scalar_prefetch=3,
            grid=(rows // CHUNK,),
            in_specs=held(
                [
                    whole_spec((rows, GW)), *[whole_spec(p.shape) for p in pieces], whole_spec(kv.shape), whole_spec((8, rows)),
                    whole_spec(q_seg.shape), whole_spec(k_seg.shape), *[whole_spec(a.shape) for a in carried],
                ],
                (q, *pieces, kv, lse, q_seg, k_seg, *carried),
            ),
            out_specs=[whole_spec(shape) for shape, _ in outs] + [tall],
            scratch_shapes=scratch,
        ),
        compiler_params=pltpu.CompilerParams(vmem_limit_bytes=20 << 20),
        cost_estimate=pl.CostEstimate(
            flops=int(56 * rows * rows * GW), bytes_accessed=32 * rows * GW, transcendentals=4 * rows * rows
        ),
        name="attend_back_first" if first else "attend_back_last",
    )(active, may, place, q, *pieces, kv, lse, q_seg, k_seg, *carried)


def fast_local(
    tokens, segment_ids, live_blocks, norm1_gain, norm1_bias, qkv_weight, qv_bias, out_weight, out_bias,
    norm2_gain, norm2_bias, up_weight, up_bias, down_weight, down_bias, grad_out,
):
    y, x, z, c = (lax.axis_index(name) for name in ("y", "x", "z", "c"))
    place = jnp.stack([z, c, y, x]).astype(jnp.int32)
    wide, low = jnp.float32, jnp.bfloat16
    _, rows, width = tokens.shape
    own_rows, units = qkv_weight.shape[0], down_weight.shape[0]
    ff = up_weight.shape[1]
    half, pairs = ff // 2, ff // (2 * units)
    devices = width // own_rows
    seq_rows = rows * NZ
    keys = 2 * seq_rows
    blocks = keys // BLOCK
    per = CHUNK // BLOCK

    vectors = (norm1_gain, norm1_bias, qv_bias, out_bias, norm2_gain, norm2_bias, up_bias, down_bias)
    sizes = [v.shape[0] for v in vectors]
    cuts = [sum(sizes[:i]) for i in range(len(sizes) + 1)]
    span = width + 3 * GW
    tall = own_rows + 8
    parts = vectors + (segment_ids[0].astype(low),)
    extra = sum(
        jnp.pad(p, (start, span - start - p.shape[0])) for p, start in zip(parts, cuts)
    )
    extra = jnp.pad(extra[None], ((0, 7), (0, 0)))
    wz = qkv_weight.reshape(own_rows, 3, NZ, GW).transpose(2, 0, 1, 3).reshape(NZ, own_rows, 3 * GW)
    group1 = jnp.concatenate(
        [jnp.broadcast_to(out_weight[None], (NZ, own_rows, width)), wz], axis=2
    )
    group1 = jnp.concatenate([group1, jnp.broadcast_to(extra[None], (NZ, 8, span))], axis=1)
    pieces1 = z_exchange(group1, z, (2, 3, 1))

    up_sets = up_weight.reshape(own_rows, pairs, 2, units).transpose(2, 0, 1, 3)
    up_sets = up_sets.reshape(2, own_rows, half)
    up_chip = in_order(pick(up_sets, c), swap(pick(up_sets, 1 - c), "c"), c, 0)
    up_chip = up_chip.reshape(2 * own_rows, half)
    group2 = jnp.concatenate([up_chip[:, :width], up_chip[:, width:], down_weight], axis=0)
    pieces2 = z_pieces(group2, (3, 1, 2))

    own, pieces2[1], pieces2[3] = meet(tokens[0], pieces2[1], pieces2[3])
    line_pieces = z_pieces(own, (2, 1, 3))
    group1 = z_order(pieces1, z)
    own_seg = group1[:, own_rows, cuts[-1] : cuts[-1] + rows].astype(wide)
    seg = in_order(own_seg, swap(own_seg, "c"), c, 1).reshape(keys // CHUNK, CHUNK)
    group1 = jnp.concatenate([in_order(*half) for half in xy_gather(group1, y, x)], axis=2)
    group1 = in_order(group1, swap(group1, "c"), c, 3)
    wo = group1[..., :own_rows, :width].reshape(width, width)
    wz = group1[..., :own_rows, width:].reshape(width, 3 * GW)
    packed = group1[..., own_rows, : cuts[-1]].reshape(devices, cuts[-1])
    vec = kernel_call(
        unpack_kernel, place, (packed,), [whole_spec(packed.shape)], [((VEC_ROWS, width), wide)],
        [whole_spec((VEC_ROWS, width))], (1,), [], 1 << 20, "unpack",
    )[0]
    group2, vec = meet(z_order(pieces2, z), vec)
    group2 = xy_gather(group2, y, x)

    own_blocks = seq_rows // BLOCK
    ids = jnp.arange(blocks, dtype=jnp.int32)
    own_ids = pick(ids.reshape(NZ, 2, rows // BLOCK), c, 1).reshape(own_blocks)
    own_live = pick(live_blocks[0].reshape(NZ, 2, rows // BLOCK, blocks), c, 1)
    own_live = own_live.reshape(own_blocks, blocks)
    seg_blocks = seg.reshape(blocks, BLOCK)
    own_seg_blocks = own_seg.reshape(own_blocks, BLOCK)
    may = (own_live > 0) | (own_ids[:, None] == ids[None, :])
    touch = (
        may
        & (own_seg_blocks[:, :1] <= seg_blocks[:, -1][None])
        & (seg_blocks[:, 0][None] <= own_seg_blocks[:, -1:])
    )
    active = jnp.any(touch.reshape(own_blocks // per, per, blocks // per, per), axis=(1, 3))
    active, may = active.astype(jnp.int32), may.astype(jnp.int32)

    line, n1, q, kv = project(place, line_pieces, vec, wz)
    kv_theirs = swap(kv, "c")
    att_wide, att_low, lse = attend(active, may, place, q, kv, kv_theirs, own_seg, seg)
    att = z_exchange(att_low.reshape(NZ, rows, GW), z, (2, 1, 3))
    group2 = [in_order(own_half, after(other, att_low), at, axis) for own_half, other, at, axis in group2]
    group2 = jnp.concatenate(group2, axis=2)

    hidden, n2 = branch_call(place, att, wo, own, vec)
    go = grad_out[0]
    n2_theirs, go_theirs = swap(n2, "c"), swap(go, "c")
    up_bias_half = vec[8:10].reshape(1, half)
    chips = devices // 2
    group2 = group2.reshape(chips, 2 * units, width)
    activated, grad_before, out_part, m_part, sums, up_bias_part = feed(
        place, n2, n2_theirs, go, go_theirs, group2, up_bias_half
    )
    sums = swap(sums, "c")
    a_kept, a_sent, b_kept, b_sent = feed_weights(
        place, n2, n2_theirs, go, go_theirs, activated, grad_before, 2 * units
    )
    output, grad_hidden, grad_branch, *grad_att, mid = middle(
        place, m_part, out_part, sums, hidden, go, vec, wo
    )
    dout = [grad_att[0]] + hops(lambda hop: shift(grad_att[hop], "z", NZ, hop), (3, 1, 2))
    a, b = add_up(a_kept, a_sent, "y"), add_up(b_kept, b_sent, "x")

    dq_part, delta, dkv_theirs = attend_back(
        True, active, may, place, q, dout, kv_theirs, lse, own_seg, seg, att_wide
    )
    a, b, dq_part = meet(a, b, dq_part)
    a, b = halve(a, "x", x, low), halve(b, "y", y, low)
    dq, dkv_mine = attend_back(
        False, active, may, place, q, dout, kv, lse, own_seg, seg, delta, dq_part
    )
    dqkv, m1_own, *m1_sent, cols, dqkv_sum = inward(place, dq, dkv_mine, swap(dkv_theirs, "c"), line, wz)
    group2 = jnp.concatenate([a, b], axis=0)
    m1_up, m1_far, m1_down = z_reduce(m1_sent, z)

    mine, theirs = owners(
        place, att, grad_branch, n1, dqkv, cols, mid, dqkv_sum, up_bias_part, devices, tall
    )
    group1 = (mine.astype(wide) + swap(theirs, "c").astype(wide)).astype(low)
    group1 = group1.reshape(2, 2, NZ, tall, span)
    a = halve(group1[:, :, :2], "y", y, low)
    b = halve(group1[:, :, 2:].swapaxes(0, 1), "x", x, low)
    a, b = halve(a, "x", x, low), halve(b, "y", y, low)
    a, b, m1_far, m1_down = meet(a, b, m1_far, m1_down)
    grad_tokens = finish(place, m1_own, (m1_up, m1_far, m1_down), own, grad_hidden, vec)
    group1 = jnp.concatenate([a, b], axis=0)
    pieces = z_exchange(group1.astype(low), z, (1, 2, 3))
    arrays = (pick(group1, z), *pieces[1:])
    outs = [((own_rows, 3 * width), wide), ((own_rows, width), wide), ((tall - own_rows, span), wide)]
    grad_qkv, grad_wo, vec_sum = kernel_call(
        deliver_kernel, place, arrays, [whole_spec(a.shape) for a in arrays], outs,
        [whole_spec(shape) for shape, _ in outs], (1,), [], 1 << 20, "deliver",
    )
    v = [vec_sum[0, cuts[i] : cuts[i + 1]] for i in range(len(sizes))]

    group2_low = group2.astype(low)
    sent = [pick(group2_low, (z + j) % NZ) for j in range(1, NZ)]
    group2 = sum((piece.astype(wide) for piece in hops(lambda hop: shift(sent[hop - 1], "z", NZ, hop), (2, 3, 1))), pick(group2, z))
    grad_down = group2[units:]
    up_rows = jnp.concatenate([group2[: 2 * own_rows], group2[2 * own_rows : units]], axis=1)
    up_rows = up_rows.reshape(2, own_rows, half)
    arrays = (pick(up_rows, c), swap(pick(up_rows, 1 - c).astype(low), "c"))
    grad_up = kernel_call(
        weave_kernel, place, arrays, [whole_spec(a.shape) for a in arrays], [((own_rows, ff), wide)],
        [whole_spec((own_rows, ff))], (1,), [], 1 << 20, "weave",
    )[0]
    return (
        output[None], grad_tokens[None], v[0], v[1], grad_qkv, v[2], grad_wo, v[3],
        v[4], v[5], grad_up, v[6], grad_down, v[7],
    )


def build(body, mesh, dp, ctx):
    both = dp + ctx
    rows, vector, matrix = P(dp, ctx, None), P(both), P(both, None)
    return jax.shard_map(
        body,
        mesh=mesh,
        in_specs=(
            rows, P(dp, ctx), P(dp, None, None), vector, vector, matrix, vector, matrix, vector,
            vector, vector, matrix, vector, matrix, vector, rows,
        ),
        out_specs=(
            rows, rows, vector, vector, matrix, vector, matrix, vector, vector, vector, matrix,
            vector, matrix, vector,
        ),
        check_vma=False,
    )


def solution(mesh):
    if dict(mesh.shape) == {"dp": 4, "ctx": 2 * NZ}:
        grid = Mesh(mesh.devices.reshape(2, 2, NZ, 2), ("y", "x", "z", "c"))
        return build(fast_local, grid, ("y", "x"), ("z", "c"))
    return build(local, mesh, ("dp",), ("ctx",))
```
